32 devices in a mesh: dp: 4 (over y, x), expert: 8 (over z, core).
Axes of the slice: x: 2, y: 2, z: 4, core: 2. Of those that a mesh axis runs over, the one named last changes fastest.
Arguments:
- tokens: bfloat16 [2, 2048, 1536], P(None, ('dp', 'expert')), may hold values from -6 to 6
- segments: int32 [2, 32, 64], P(None, ('dp', 'expert')), may hold values from 0 to 3, never falling along the last dimension, each value on 1 to 32 neighbouring positions
- routes: int32 [2, 2, 2048, 6], P(None, None, ('dp', 'expert')), may hold values from 0 to 15, all different within a row; in each aligned block of 64 rows (0 to 63, 64 to 127, ..., all dimensions but the last counted through in order) at most 36 rows name the same one
- norm_mamba: bfloat16 [1536], P(('dp', 'expert')), may hold values from 0.5 to 1.5
- w_in: bfloat16 [1536, 6400], P(('dp', 'expert')), may hold values from -0.15625 to 0.15625
- w_dt: bfloat16 [1536, 48], P(('dp', 'expert')), may hold values from -0.15625 to 0.15625
- conv_w: bfloat16 [4, 3328], P(None, ('dp', 'expert')), may hold values from -3 to 3
- conv_b: bfloat16 [3328], P(('dp', 'expert')), may hold values from -3 to 3
- dt_bias: float32 [48], replicated, may hold values from -4.6 to -2.3
- a_log: float32 [48], replicated, may hold values from 0 to 2.5
- skip_scale: float32 [48], replicated, may hold values from 0.5 to 1.5
- gate_norm: bfloat16 [3072], P(('dp', 'expert')), may hold values from 0.5 to 1.5
- w_mix_out: bfloat16 [3072, 1536], P(None, ('dp', 'expert')), may hold values from -0.109375 to 0.109375
- norm_moe_m: bfloat16 [1536], P(('dp', 'expert')), may hold values from 0.5 to 1.5
- router_m: bfloat16 [1536, 16], P(('dp', 'expert')), may hold values from -0.078125 to 0.078125
- shared_in_m: bfloat16 [1536, 2048], P(('dp', 'expert')), may hold values from -0.15625 to 0.15625
- shared_down_m: bfloat16 [1024, 1536], P(None, ('dp', 'expert')), may hold values from -0.25 to 0.25
- expert_in_m: bfloat16 [16, 1536, 1024], P('expert', 'dp'), may hold values from -0.15625 to 0.15625
- expert_down_m: bfloat16 [16, 512, 1536], P('expert', 'dp'), may hold values from -0.5 to 0.5
- norm_attn: bfloat16 [1536], P(('dp', 'expert')), may hold values from 0.5 to 1.5
- w_qkv: bfloat16 [1536, 2560], P(('dp', 'expert')), may hold values from -0.15625 to 0.15625
- w_out: bfloat16 [1536, 1536], P(None, ('dp', 'expert')), may hold values from -0.625 to 0.625
- norm_moe: bfloat16 [1536], P(('dp', 'expert')), may hold values from 0.5 to 1.5
- router: bfloat16 [1536, 16], P(('dp', 'expert')), may hold values from -0.078125 to 0.078125
- shared_in: bfloat16 [1536, 2048], P(('dp', 'expert')), may hold values from -0.15625 to 0.15625
- shared_down: bfloat16 [1024, 1536], P(None, ('dp', 'expert')), may hold values from -0.25 to 0.25
- expert_in: bfloat16 [16, 1536, 1024], P('expert', 'dp'), may hold values from -0.15625 to 0.15625
- expert_down: bfloat16 [16, 512, 1536], P('expert', 'dp'), may hold values from -0.5 to 0.5
- cotangent: bfloat16 [2, 2048, 1536], P(None, ('dp', 'expert')), may hold values from -6 to 6
Outputs:
- output: bfloat16 [2, 2048, 1536], P(None, ('dp', 'expert'))
- input_grad: float32 [2, 2048, 1536], P(None, ('dp', 'expert'))
- grad_norm_mamba: float32 [1536], P(('dp', 'expert'))
- grad_w_in: float32 [1536, 6400], P(('dp', 'expert'))
- grad_w_dt: float32 [1536, 48], P(('dp', 'expert'))
- grad_conv_w: float32 [4, 3328], P(None, ('dp', 'expert'))
- grad_conv_b: float32 [3328], P(('dp', 'expert'))
- grad_dt_bias: float32 [48], replicated
- grad_a_log: float32 [48], replicated
- grad_skip_scale: float32 [48], replicated
- grad_gate_norm: float32 [3072], P(('dp', 'expert'))
- grad_w_mix_out: float32 [3072, 1536], P(None, ('dp', 'expert'))
- grad_norm_moe_m: float32 [1536], P(('dp', 'expert'))
- grad_router_m: float32 [1536, 16], P(('dp', 'expert'))
- grad_shared_in_m: float32 [1536, 2048], P(('dp', 'expert'))
- grad_shared_down_m: float32 [1024, 1536], P(None, ('dp', 'expert'))
- grad_expert_in_m: float32 [16, 1536, 1024], P('expert', 'dp')
- grad_expert_down_m: float32 [16, 512, 1536], P('expert', 'dp')
- grad_norm_attn: float32 [1536], P(('dp', 'expert'))
- grad_w_qkv: float32 [1536, 2560], P(('dp', 'expert'))
- grad_w_out: float32 [1536, 1536], P(None, ('dp', 'expert'))
- grad_norm_moe: float32 [1536], P(('dp', 'expert'))
- grad_router: float32 [1536, 16], P(('dp', 'expert'))
- grad_shared_in: float32 [1536, 2048], P(('dp', 'expert'))
- grad_shared_down: float32 [1024, 1536], P(None, ('dp', 'expert'))
- grad_expert_in: float32 [16, 1536, 1024], P('expert', 'dp')
- grad_expert_down: float32 [16, 512, 1536], P('expert', 'dp')
The draws below stay inside these ranges and needn't reach their ends.
Inputs may be any that keep to these rules, and one draw needn't show every extreme that they name: For each expert block, in each aligned block of 64 rows (one sequence) no expert is named by more than 36 routes, a bound that some block reaches. The 6 routes of a token differ. `segments`: within a sequence the numbers never fall; every segment has 1 to 32 positions.
All inputs are finite; a program needn't handle non-finite values.
Results may differ from the reference program's by a relative error of at most 0.039.
Values may be sent and summed in bfloat16 or wider, within the bound.
No kernel may reach another device: no remote copies, remote signals or barrier semaphores. Data moves between devices by JAX's collectives and lax.ppermute only.
A program may use at most 280 MiB of HBM per device.

```python
import math
import jax
import jax.numpy as jnp
import numpy as np
from jax import lax

D = 1536
QH = 12
KVH = 4
HEAD = 128
EXP_FF = 512
SH_FF = 1024
TOP = 6
MH = 48
HP = 64
STATE = 128
CK = 4
MB_TOK = 64
MICRO = 2
SEGS = 4
EXPERTS = 16
CAP = 36
SEQS = 32
ROWS = 2048
QW = 1536
QKV = 2560
DI = 3072
CONV = 3328
MIN = 6400
N_DP = 4
N_EXPERT = 8


def strengthened(result, own_key, source, target, blocks, factor):
    def block_of(position):
        return (jnp.arange(result.shape[position]) // (result.shape[position] // blocks)).reshape((-1,) + (1,) * (result.ndim - 1 - position))

    near = jax.random.permutation(own_key, blocks)[block_of(target)]
    other_side = (block_of(target) + blocks // 2) % blocks
    return jnp.where((block_of(source) == near) | (block_of(source) == other_side), factor * result, result)


def shard_levels(own_key, dims, cuts, low, top_value):
    level, own = 1.0, jax.random.fold_in(own_key, 6)
    for position, blocks in cuts:
        heights = jnp.exp(jax.random.uniform(jax.random.fold_in(own, position), (blocks,), jnp.float32, low / len(cuts), top_value / len(cuts)))
        level = level * jnp.repeat(heights, dims[position] // blocks).reshape([-1 if axis == position else 1 for axis in range(len(dims))])
    return level


def length_profile(number_of, total, bound, lean):
    weights = [(1 << 20) // math.isqrt(rank ** lean) + 1 for rank in range(2, number_of + 1)]
    rest, counts = total - bound - (number_of - 1), [1] * (number_of - 1)
    while rest > 0:
        candidates = [i for i in range(number_of - 1) if counts[i] < bound]
        whole, budget = sum([weights[i] for i in candidates]), rest
        for i in candidates:
            extra = min(bound - counts[i], max(1, budget * weights[i] // whole), rest)
            counts[i] = counts[i] + extra
            rest = rest - extra
    return np.array([bound] + counts)


def ragged_sizes(key, count, total, bound, slope):
    if count == 2:
        one = jax.random.randint(key, (), max(1, total - bound), min(bound, total - 1) + 1)
        return jnp.stack([one, total - one])
    sizes = jnp.asarray(length_profile(count, total, bound, slope), jnp.int32)
    pairs = (count - 1) // 2
    donor, taker = sizes[1:1 + 2 * pairs:2], sizes[2:2 + 2 * pairs:2]
    margin = jnp.minimum(donor - 1, bound - taker)
    moved = jax.random.randint(jax.random.fold_in(key, 1), (pairs,), 0, 1 << 20) % (margin + 1)
    sizes = sizes.at[1:1 + 2 * pairs:2].set(donor - moved).at[2:2 + 2 * pairs:2].set(taker + moved)
    return sizes[jax.random.permutation(jax.random.fold_in(key, 2), count)]


def assign_block(own_key, own, number, rows, amount, top, bound, skew):
    sequence = jax.random.permutation(own_key, amount)
    crowded, ordinary = shares(amount, rows * top, bound, skew, True), shares(amount, rows * top, bound, skew, False)
    places = jnp.arange(amount)

    def named(tallies, rotation):
        used = int((tallies > 0).sum())
        fixed = max(1, used // 4)
        moved = fixed + (places - fixed + rotation * (used - fixed)) % max(1, amount - fixed)
        return jnp.zeros((amount,), jnp.int32).at[sequence[jnp.where(places < fixed, places, moved)]].set(jnp.asarray(tallies, jnp.int32))

    tallies = jnp.where(number % 4 == 0, named(crowded, number // 4), named(ordinary, number - number // 4 - 1))
    mixed = jax.random.permutation(jax.random.fold_in(own, 3), amount)
    giver, sink = mixed[0:amount // 2 * 2:2], mixed[1:amount // 2 * 2:2]
    room = jnp.minimum(tallies[giver] - 1, bound - tallies[sink]) // 2
    room = jnp.where((giver == sequence[0]) | (sink == sequence[0]) | (tallies[sink] == 0), 0, jnp.maximum(room, 0))
    moved = jax.random.randint(jax.random.fold_in(own, 4), (amount // 2,), 0, 1 << 20) % (room + 1)
    tallies = tallies.at[giver].add(-moved).at[sink].add(moved)
    members = jnp.searchsorted(jnp.cumsum(tallies), jnp.arange(rows * top), side="right").astype(jnp.int32)
    table = members.reshape(top, rows).T
    table = table[jax.random.permutation(jax.random.fold_in(own, 1), rows)]
    rotation = jax.random.randint(jax.random.fold_in(own, 2), (rows, 1), 0, top)
    return jnp.take_along_axis(table, (jnp.arange(top)[None, :] + rotation) % top, axis=1)


def shares(amount, total, limit, skew, full):
    loads = [(1 << 20) // math.isqrt(grade ** skew) + 1 for grade in range(1, amount + 1)]
    largest = limit if full else min(limit, max(-(-total // amount), total * loads[0] // sum(loads)))
    least = 1 if total - largest >= amount - 1 else 0
    counts, spare = [largest] + [least] * (amount - 1), total - largest - least * (amount - 1)
    while spare > 0:
        free = [i for i in range(1, amount) if counts[i] < largest] or [i for i in range(1, amount) if counts[i] < limit]
        whole, budget = sum([loads[i] for i in free]), spare
        for i in free:
            more = min(limit - counts[i], max(1, budget * loads[i] // whole), spare)
            counts[i] = counts[i] + more
            spare = spare - more
    return np.array(counts)


def gaussian(own_key, extent, spread, reach, cuts=(), held_as=jnp.bfloat16):
    gain = shard_levels(own_key, extent, cuts, -0.22, 0.18) if cuts else 1.0
    values = jax.random.normal(own_key, extent, jnp.float32) * spread * gain
    return jnp.minimum(jnp.maximum(values, -reach), reach).astype(held_as)


def gaussian_with(rng, extent, width, bound, cuts, heavy, kind=jnp.bfloat16):
    values = width * jax.random.normal(rng, extent, jnp.float32)
    if cuts:
        values = values * shard_levels(rng, extent, cuts, -0.22, 0.18)
    return jnp.clip(strengthened(values, jax.random.fold_in(rng, 3), *heavy), -bound, bound).astype(kind)


def setup_inputs(seed: int = 0) -> dict:
    keys = jax.random.split(jax.random.key(seed), 30)
    tokens = gaussian_with(keys[0], (MICRO, ROWS, D), 1.0, 6.0, ((1, 32),), (1, 2, 32, 2.75))
    segments = jax.vmap(lambda own: jnp.searchsorted(jnp.cumsum(ragged_sizes(own, SEGS, MB_TOK, MB_TOK // 2, 2)), jnp.arange(MB_TOK), side="right"))(jax.random.split(keys[1], MICRO * SEQS)).reshape((MICRO, SEQS, MB_TOK)).astype(jnp.int32)
    routes_keys = jax.random.split(jax.random.fold_in(keys[2], 1), 2 * MICRO * ROWS // MB_TOK)
    routes_turns = jax.random.permutation(jax.random.fold_in(keys[2], 3), 2 * MICRO * ROWS // MB_TOK)
    routes = jax.vmap(lambda own, number: assign_block(jax.random.fold_in(keys[2], 2), own, number, MB_TOK, EXPERTS, TOP, CAP, 1))(routes_keys, routes_turns).reshape((2, MICRO, ROWS, TOP))
    norm_mamba = jnp.clip(1.0 + 0.1 * jax.random.normal(keys[3], (D,), jnp.float32), 0.5, 1.5).astype(jnp.bfloat16)
    w_in = gaussian(keys[4], (D, MIN), D ** -0.5, 0.15625, ((0, 32),))
    w_dt = gaussian(keys[5], (D, MH), D ** -0.5, 0.15625, ((0, 32),))
    conv_w = gaussian(keys[6], (CK, CONV), CK ** -0.5, 3.0, ((1, 32),))
    conv_b = gaussian(keys[7], (CONV,), 0.5, 3.0, ((0, 32),))
    dt_bias = jnp.clip(jax.random.uniform(keys[8], (MH,), jnp.float32, -4.6, -2.3), -4.6, -2.3)
    a_log = jnp.clip(jax.random.uniform(keys[9], (MH,), jnp.float32, 0.0, 2.5), 0.0, 2.5)
    skip_scale = jnp.clip(jax.random.uniform(keys[10], (MH,), jnp.float32, 0.5, 1.5), 0.5, 1.5)
    gate_norm = jnp.clip(1.0 + 0.1 * jax.random.normal(keys[11], (DI,), jnp.float32), 0.5, 1.5).astype(jnp.bfloat16)
    w_mix_out = gaussian(keys[12], (DI, D), DI ** -0.5, 0.109375, ((1, 32),))
    norm_moe_m = jnp.clip(1.0 + 0.1 * jax.random.normal(keys[13], (D,), jnp.float32), 0.5, 1.5).astype(jnp.bfloat16)
    router_m = gaussian(keys[14], (D, EXPERTS), (4 * D) ** -0.5, 0.078125, ((0, 32),))
    shared_in_m = gaussian(keys[15], (D, 2 * SH_FF), D ** -0.5, 0.15625, ((0, 32),))
    shared_down_m = gaussian(keys[16], (SH_FF, D), (SH_FF // 2) ** -0.5, 0.25, ((1, 32),))
    expert_in_m = gaussian(keys[17], (EXPERTS, D, 2 * EXP_FF), D ** -0.5, 0.15625, ((0, 8), (1, 4)))
    expert_down_m = gaussian(keys[18], (EXPERTS, EXP_FF, D), (EXP_FF // 4) ** -0.5, 0.5, ((0, 8), (1, 4)))
    norm_attn = jnp.clip(1.0 + 0.1 * jax.random.normal(keys[19], (D,), jnp.float32), 0.5, 1.5).astype(jnp.bfloat16)
    w_qkv = gaussian(keys[20], (D, QKV), D ** -0.5, 0.15625, ((0, 32),))
    w_out = gaussian(keys[21], (QW, D), (QW // 16) ** -0.5, 0.625, ((1, 32),))
    norm_moe = jnp.clip(1.0 + 0.1 * jax.random.normal(keys[22], (D,), jnp.float32), 0.5, 1.5).astype(jnp.bfloat16)
    router = gaussian(keys[23], (D, EXPERTS), (4 * D) ** -0.5, 0.078125, ((0, 32),))
    shared_in = gaussian(keys[24], (D, 2 * SH_FF), D ** -0.5, 0.15625, ((0, 32),))
    shared_down = gaussian(keys[25], (SH_FF, D), (SH_FF // 2) ** -0.5, 0.25, ((1, 32),))
    expert_in = gaussian(keys[26], (EXPERTS, D, 2 * EXP_FF), D ** -0.5, 0.15625, ((0, 8), (1, 4)))
    expert_down = gaussian(keys[27], (EXPERTS, EXP_FF, D), (EXP_FF // 4) ** -0.5, 0.5, ((0, 8), (1, 4)))
    cotangent = gaussian_with(keys[28], (MICRO, ROWS, D), 1.0, 6.0, ((1, 32),), (1, 2, 32, 2.75))
    return {"tokens": tokens, "segments": segments, "routes": routes, "norm_mamba": norm_mamba, "w_in": w_in, "w_dt": w_dt, "conv_w": conv_w, "conv_b": conv_b, "dt_bias": dt_bias, "a_log": a_log, "skip_scale": skip_scale, "gate_norm": gate_norm, "w_mix_out": w_mix_out, "norm_moe_m": norm_moe_m, "router_m": router_m, "shared_in_m": shared_in_m, "shared_down_m": shared_down_m, "expert_in_m": expert_in_m, "expert_down_m": expert_down_m, "norm_attn": norm_attn, "w_qkv": w_qkv, "w_out": w_out, "norm_moe": norm_moe, "router": router, "shared_in": shared_in, "shared_down": shared_down, "expert_in": expert_in, "expert_down": expert_down, "cotangent": cotangent}


@jax.custom_vjp
def low(v):
    return lax.optimization_barrier(v.astype(jnp.bfloat16)).astype(jnp.float32)

@jax.custom_vjp
def low_back(v):
    return v

def low_keep(v):
    return (low(v), None)

def low_pass(kept, grad):
    return (grad,)

def back_keep(v):
    return (v, None)

def back_low(kept, grad):
    return (low(grad),)
low.defvjp(low_keep, low_pass)
low_back.defvjp(back_keep, back_low)
epsilon = 1e-05
masked_value = -1e+30
highest = lax.Precision.HIGHEST

def rms_scale(values):
    return lax.rsqrt(lax.optimization_barrier(jnp.mean(values * values, axis=-1, keepdims=True)) + epsilon)

def ssd_piece(projected, dt_raw, seg_ids, conv_w, conv_b, dt_bias, a_log, skip_scale, gate_norm):
    length = projected.shape[0]
    gate_z = projected[:, :DI]
    conv_in = projected[:, DI:]
    positions = lax.broadcasted_iota(jnp.int32, (length,), 0)
    conv_sum = jnp.zeros_like(conv_in) + conv_b[None, :]
    for offset in range(CK):
        shifted = jnp.pad(conv_in, ((offset, 0), (0, 0)))[:length]
        seg_prev = jnp.pad(seg_ids, (offset, 0))[:length]
        usable = (positions >= offset) & (seg_prev == seg_ids)
        conv_sum = conv_sum + jnp.where(usable[:, None], conv_w[offset][None, :] * shifted, 0.0)
    conv_act = jax.nn.silu(conv_sum)
    head_inputs = conv_act[:, :DI].reshape(length, MH, HP)
    b_state = conv_act[:, DI:DI + STATE]
    c_state = conv_act[:, DI + STATE:]
    step_size = jax.nn.softplus(dt_raw + dt_bias[None, :])
    cum_decay = jnp.cumsum(step_size * (-jnp.exp(a_log))[None, :], axis=0)
    rows_pos = lax.broadcasted_iota(jnp.int32, (length, length), 0)
    cols_pos = lax.broadcasted_iota(jnp.int32, (length, length), 1)
    allowed = (seg_ids[:, None] == seg_ids[None, :]) & (cols_pos <= rows_pos)
    cum_heads = cum_decay.T
    log_gap = cum_heads[:, :, None] - cum_heads[:, None, :]
    decay_table = jnp.where(allowed[None], jnp.exp(jnp.where(allowed[None], log_gap, 0.0)), 0.0)
    c_dot_b = jnp.dot(c_state, b_state.T, precision=highest)
    mix_weight = decay_table * c_dot_b[None, :, :] * step_size.T[:, None, :]
    scan_out = jnp.einsum('hts,shp->thp', mix_weight, head_inputs, precision=highest) + skip_scale[None, :, None] * head_inputs
    gated_rows = scan_out.reshape(length, DI) * jax.nn.silu(gate_z)
    return gated_rows * rms_scale(gated_rows) * gate_norm[None, :]

def mamba_mix(mamba_in, seg_ids, w_in, w_dt, conv_w, conv_b, dt_bias, a_log, skip_scale, gate_norm, w_mix_out):
    projected = low_back(low(jnp.dot(mamba_in, w_in, precision=highest)))
    dt_raw = low_back(jnp.dot(mamba_in, w_dt, precision=highest))
    gated_out = ssd_piece(projected, dt_raw, seg_ids, conv_w, conv_b, dt_bias, a_log, skip_scale, gate_norm)
    gated_out = low_back(low(gated_out))
    return low_back(jnp.dot(gated_out, w_mix_out, precision=highest))

def attend(normed, seg_ids, w_qkv, w_out):
    length = normed.shape[0]
    group_size = QH // KVH
    packed = low_back(low(jnp.dot(normed, w_qkv, precision=highest)))
    queries = packed[:, :QH * HEAD].reshape(length, KVH, group_size, HEAD)
    key_heads = packed[:, QH * HEAD:(QH + KVH) * HEAD].reshape(length, KVH, HEAD)
    value_heads = packed[:, (QH + KVH) * HEAD:].reshape(length, KVH, HEAD)
    scores = low_back(jnp.einsum('qhgd,khd->hgqk', queries, key_heads, precision=highest) * HEAD ** (-0.5))
    rows_pos = lax.broadcasted_iota(jnp.int32, (length, length), 0)
    cols_pos = lax.broadcasted_iota(jnp.int32, (length, length), 1)
    allowed = (seg_ids[:, None] == seg_ids[None, :]) & (cols_pos <= rows_pos)
    probs = low(jax.nn.softmax(jnp.where(allowed, scores, masked_value), axis=-1))
    context = jnp.einsum('hgqk,khd->qhgd', probs, value_heads, precision=highest).reshape(length, QH * HEAD)
    context = low_back(low(context))
    return low_back(jnp.dot(context, w_out, precision=highest))

def route_slots(route_ids):
    flat_ids = route_ids.reshape(-1).astype(jnp.int32)
    onehot = (flat_ids[:, None] == jnp.arange(EXPERTS, dtype=jnp.int32)[None, :]).astype(jnp.int32)
    earlier = jnp.cumsum(onehot, axis=0).astype(jnp.int32) - onehot
    slot_index = lax.optimization_barrier(jnp.sum(earlier * onehot, axis=1)).astype(jnp.int32)
    return (flat_ids, slot_index)

def experts(normed, route_ids, expert_in, expert_down):
    length = normed.shape[0]
    flat_ids, slot_index = route_slots(route_ids)
    copies = low_back(jnp.repeat(normed, TOP, axis=0))
    buffer = jnp.zeros((EXPERTS, CAP, D), normed.dtype).at[flat_ids, slot_index].set(copies)
    gate_up = low_back(jnp.einsum('ecd,edf->ecf', buffer, expert_in, precision=highest))
    hidden_units = low_back(low(jax.nn.silu(gate_up[..., :EXP_FF]) * gate_up[..., EXP_FF:]))
    produced = low_back(low(jnp.einsum('ecf,efd->ecd', hidden_units, expert_down, precision=highest)))
    return produced[flat_ids, slot_index].reshape(length, TOP, D)

def moe_branch(moe_in, route_ids, router, shared_in, shared_down, expert_in, expert_down):
    logits = low_back(jnp.dot(moe_in, router, precision=highest))
    route_pick = (route_ids[:, :, None] == jnp.arange(EXPERTS, dtype=jnp.int32)[None, None, :]).astype(moe_in.dtype)
    chosen = jnp.einsum('tke,te->tk', route_pick, logits, precision=highest)
    gate_weights = jax.nn.softmax(chosen, axis=-1)
    expert_rows = experts(moe_in, route_ids, expert_in, expert_down)
    mixture = jnp.einsum('tk,tkd->td', gate_weights, expert_rows, precision=highest)
    shared_pre = low_back(jnp.dot(moe_in, shared_in, precision=highest))
    shared_hidden = low_back(low(jax.nn.silu(shared_pre[:, :SH_FF]) * shared_pre[:, SH_FF:]))
    shared_out = low_back(jnp.dot(shared_hidden, shared_down, precision=highest))
    return shared_out + mixture

def layer_pair(block_tokens, seg_ids, route_pair, weights):
    norm_mamba, w_in, w_dt, conv_w, conv_b, dt_bias, a_log, skip_scale, gate_norm, w_mix_out, norm_moe_m, router_m, shared_in_m, shared_down_m, expert_in_m, expert_down_m, norm_attn, w_qkv, w_out, norm_moe, router, shared_in, shared_down, expert_in, expert_down = weights
    mamba_in = low(block_tokens * rms_scale(block_tokens) * norm_mamba)
    hidden_one = block_tokens + mamba_mix(mamba_in, seg_ids, w_in, w_dt, conv_w, conv_b, dt_bias, a_log, skip_scale, gate_norm, w_mix_out)
    moe_one = low(hidden_one * rms_scale(hidden_one) * norm_moe_m)
    layer_one = hidden_one + moe_branch(moe_one, route_pair[0], router_m, shared_in_m, shared_down_m, expert_in_m, expert_down_m)
    attn_in = low(layer_one * rms_scale(layer_one) * norm_attn)
    hidden_two = layer_one + attend(attn_in, seg_ids, w_qkv, w_out)
    moe_two = low(hidden_two * rms_scale(hidden_two) * norm_moe)
    return hidden_two + moe_branch(moe_two, route_pair[1], router, shared_in, shared_down, expert_in, expert_down)

def reference(tokens, segments, routes, norm_mamba, w_in, w_dt, conv_w, conv_b, dt_bias, a_log, skip_scale, gate_norm, w_mix_out, norm_moe_m, router_m, shared_in_m, shared_down_m, expert_in_m, expert_down_m, norm_attn, w_qkv, w_out, norm_moe, router, shared_in, shared_down, expert_in, expert_down, cotangent):
    blocks = MICRO * N_DP * N_EXPERT
    group_size = math.gcd(blocks, max(1, 4096 // MB_TOK))
    step_count = blocks // group_size
    inputs = tokens.astype(jnp.float32).reshape(step_count, group_size, MB_TOK, D)
    seg_all = segments.reshape(step_count, group_size, MB_TOK).astype(jnp.int32)
    route_all = routes.astype(jnp.int32).reshape(2, blocks, MB_TOK, TOP).transpose(1, 0, 2, 3).reshape(step_count, group_size, 2, MB_TOK, TOP)
    weights = tuple((weight.astype(jnp.float32) for weight in (norm_mamba, w_in, w_dt, conv_w, conv_b, dt_bias, a_log, skip_scale, gate_norm, w_mix_out, norm_moe_m, router_m, shared_in_m, shared_down_m, expert_in_m, expert_down_m, norm_attn, w_qkv, w_out, norm_moe, router, shared_in, shared_down, expert_in, expert_down)))
    many_blocks = jax.vmap(jax.checkpoint(layer_pair), in_axes=(0, 0, 0, None))

    def forward(block_inputs, block_weights):

        def scan_step(carry, pieces):
            return (carry, many_blocks(pieces[0], pieces[1], pieces[2], block_weights))
        unused, results = lax.scan(scan_step, jnp.zeros((), jnp.float32), (block_inputs, seg_all, route_all))
        return results
    results, pullback = jax.vjp(forward, inputs, weights)
    grad_inputs, grad_weights = pullback(cotangent.astype(jnp.float32).reshape(results.shape))
    output = results.reshape(MICRO, ROWS, D).astype(jnp.bfloat16)
    input_grad = grad_inputs.reshape(MICRO, ROWS, D)
    return (output, input_grad, grad_weights[0], grad_weights[1], grad_weights[2], grad_weights[3], grad_weights[4], grad_weights[5], grad_weights[6], grad_weights[7], grad_weights[8], grad_weights[9], grad_weights[10], grad_weights[11], grad_weights[12], grad_weights[13], grad_weights[14], grad_weights[15], grad_weights[16], grad_weights[17], grad_weights[18], grad_weights[19], grad_weights[20], grad_weights[21], grad_weights[22], grad_weights[23], grad_weights[24])
```

```python
import jax
import jax.numpy as jnp
from jax import lax
from jax.sharding import Mesh, PartitionSpec as P

D = 1536
QH = 12
KVH = 4
HEAD = 128
EXP_FF = 512
SH_FF = 1024
TOP = 6
MH = 48
HP = 64
STATE = 128
CK = 4
DI = 3072

bf16 = jnp.bfloat16
f32 = jnp.float32
epsilon = 1e-05
masked_value = -1e30
highest = lax.Precision.HIGHEST
ALL = ("dp", "w", "z", "core")
EX = ("w", "z", "core")
TP = ("z", "core")
FS = ("dp", "w")
SWAP = [(0, 1), (1, 0)]


def dot(a, b, dims, out=f32):
    r = lax.dot_general(a, b, (dims, ((), ())), preferred_element_type=f32)
    return r if out == f32 else r.astype(out)


def nn(a, b, out=f32):
    return dot(a, b, ((1,), (0,)), out)


def nt(a, b, out=f32):
    return dot(a, b, ((1,), (1,)), out)


def tn(a, b, out=f32):
    return dot(a, b, ((0,), (0,)), out)


def ring(shift, axis="z"):
    n = lax.axis_size(axis)
    return [(i, (i + shift) % n) for i in range(n)]


def wide(x):
    parts = [x] + [lax.ppermute(x, "w", ring(s, "w")) for s in range(1, lax.axis_size("w"))]
    return parts[0] if len(parts) == 1 else jnp.concatenate(parts, axis=0)


def narrow(total):
    n = lax.axis_size("w")
    rows = total.shape[0] // n
    out = total[:rows]
    for s in range(1, n):
        part = total[s * rows : (s + 1) * rows].astype(bf16)
        out = out + lax.ppermute(part, "w", ring(-s, "w")).astype(f32)
    return out


def add_first(total, part):
    rows = part.shape[0]
    if rows == total.shape[0]:
        return total + part
    return jnp.concatenate([total[:rows] + part, total[rows:]], axis=0)


def fence(*trees):
    return lax.optimization_barrier(trees)


def gather_rows(x):
    n = lax.axis_size("z")
    parts = [x] + [lax.ppermute(x, "z", ring(s)) for s in range(1, n)]
    other = [lax.ppermute(p, "core", SWAP) for p in parts]
    return jnp.concatenate(parts + other, axis=0)


def return_rows(total):
    n = lax.axis_size("z")
    half = total.shape[0] // 2
    rows = half // n
    recv = lax.ppermute(total[half:].astype(bf16), "core", SWAP)
    mine = total[:half] + recv.astype(f32)
    out = mine[:rows]
    for s in range(1, n):
        part = mine[s * rows : (s + 1) * rows].astype(bf16)
        out = out + lax.ppermute(part, "z", ring(-s)).astype(f32)
    return out


def pair_gather(x):
    return jnp.concatenate([x, lax.ppermute(x, "core", SWAP)], axis=0)


def pair_return(total):
    half = total.shape[0] // 2
    recv = lax.ppermute(total[half:].astype(bf16), "core", SWAP)
    return total[:half] + recv.astype(f32)


def split_two(x):
    high = x.astype(bf16)
    return [high, (x - high.astype(f32)).astype(bf16)]


def row_scale(values):
    return lax.rsqrt(jnp.mean(values * values, axis=-1, keepdims=True) + epsilon)


def rms_forward(values, gain):
    scale = row_scale(values)
    normed = values * scale
    return normed, scale, (normed * gain).astype(bf16)


def rms_backward(grad_result, normed, scale, gain):
    grad_gain = jnp.sum(grad_result * normed, axis=0)
    grad_normed = grad_result * gain
    grad_values = scale * (
        grad_normed - normed * jnp.mean(grad_normed * normed, axis=-1, keepdims=True)
    )
    return grad_values, grad_gain


def lanes(parts, width):
    used = sum(p.shape[-1] for p in parts)
    rows = parts[0].shape[0]
    if used < width:
        parts = parts + [jnp.zeros((rows, width - used), bf16)]
    return jnp.concatenate(parts, axis=1)


def scan_piece(proj, dt_raw, seg, conv_w, conv_b, dt_bias, a_log, skip, heads):
    seqs, length, _ = proj.shape
    chan = heads * HP
    gate_z = proj[..., :chan]
    conv_in = proj[..., chan:]
    positions = lax.broadcasted_iota(jnp.int32, (length,), 0)
    conv_sum = jnp.zeros_like(conv_in) + conv_b
    for offset in range(CK):
        shifted = jnp.pad(conv_in, ((0, 0), (offset, 0), (0, 0)))[:, :length]
        seg_prev = jnp.pad(seg, ((0, 0), (offset, 0)))[:, :length]
        usable = (positions >= offset)[None] & (seg_prev == seg)
        conv_sum = conv_sum + jnp.where(usable[..., None], conv_w[offset] * shifted, 0.0)
    conv_act = jax.nn.silu(conv_sum)
    inputs = conv_act[..., :chan].reshape(seqs, length, heads, HP)
    b_state = conv_act[..., chan : chan + STATE]
    c_state = conv_act[..., chan + STATE :]
    step = jax.nn.softplus(dt_raw + dt_bias)
    rows_pos = lax.broadcasted_iota(jnp.int32, (length, length), 0)
    cols_pos = lax.broadcasted_iota(jnp.int32, (length, length), 1)
    lower = (cols_pos <= rows_pos).astype(f32)
    cum = jnp.einsum("ts,bsh->bht", lower, step * -jnp.exp(a_log), precision=highest)
    allowed = (seg[:, :, None] == seg[:, None, :]) & (cols_pos <= rows_pos)[None]
    allowed = allowed[:, None]
    gap = cum[..., :, None] - cum[..., None, :]
    decay = jnp.where(allowed, jnp.exp(jnp.where(allowed, gap, 0.0)), 0.0)
    cb = jnp.einsum("btn,bsn->bts", c_state, b_state, precision=highest)
    mix = decay * cb[:, None] * step.transpose(0, 2, 1)[:, :, None, :]
    scan = jnp.einsum("bhts,bshp->bthp", mix, inputs, precision=highest)
    scan = scan + skip[:, None] * inputs
    return scan.reshape(seqs, length, chan) * jax.nn.silu(gate_z)


def swiglu(gate, up):
    return gate * jax.nn.sigmoid(gate) * up


def swiglu_back(grad, gate, up):
    logistic = jax.nn.sigmoid(gate)
    grad_gate = grad * up * logistic * (1.0 + gate * (1.0 - logistic))
    return grad_gate.astype(bf16), (grad * gate * logistic).astype(bf16)


def gate_table(moe_in, mask, router):
    logits = nn(moe_in, router)
    picked = jnp.where(mask, logits, masked_value)
    peak = jnp.max(picked, axis=-1, keepdims=True)
    ex = jnp.where(mask, jnp.exp(picked - peak), 0.0)
    return ex / jnp.sum(ex, axis=-1, keepdims=True)


def moe_forward(own_in, mask, w):
    rows = own_in.shape[0]
    base_in = gather_rows(own_in)
    moe_in = wide(base_in)
    gates = gate_table(moe_in, mask, w["router"])
    count = w["expert_in"].shape[0]
    first = lax.axis_index(EX) * count
    local = lax.dynamic_slice(gates, (0, first), (gates.shape[0], count))
    pre = [nn(moe_in, w["expert_in"][e], bf16) for e in range(count)]
    pre_s = nn(base_in, w["shared_in"], bf16)
    total = None
    hidden = []
    for e in range(count):
        p = pre[e].astype(f32)
        act = swiglu(p[:, :EXP_FF], p[:, EXP_FF:])
        hid = (act * local[:, e : e + 1]).astype(bf16)
        hidden.append(hid)
        part = nn(hid, w["expert_down"][e])
        total = part if total is None else total + part
    half = pre_s.shape[1] // 2
    p = pre_s.astype(f32)
    hid_s = swiglu(p[:, :half], p[:, half:]).astype(bf16)
    total = add_first(total, nt(hid_s, w["shared_down_t"]))
    branch = return_rows(narrow(total))
    kept = (moe_in, base_in, gates[:rows], local, pre, pre_s, hidden, hid_s)
    return branch, kept


def moe_backward(base_z, kept, w, experts_total):
    moe_in, base_in, own_gates, local, pre, pre_s, hidden, hid_s = kept
    grad_z = wide(base_z)
    rows = own_gates.shape[0]
    count = len(pre)
    total = None
    first = lax.axis_index(EX) * count
    lane = lax.broadcasted_iota(jnp.int32, (1, experts_total), 1)
    table = jnp.zeros((grad_z.shape[0], experts_total), f32)
    pre_grads = []
    for e in range(count):
        p = pre[e].astype(f32)
        gate, up = p[:, :EXP_FF], p[:, EXP_FF:]
        grad_hid = nt(grad_z, w["expert_down"][e])
        share = local[:, e : e + 1]
        act = swiglu(gate, up)
        weighted = share * jnp.sum(grad_hid * act, axis=-1, keepdims=True)
        table = table + weighted * (lane == first + e).astype(f32)
        g_gate, g_up = swiglu_back(grad_hid * share, gate, up)
        g_pre = jnp.concatenate([g_gate, g_up], axis=1)
        pre_grads.append(g_pre)
        part = nt(g_pre, w["expert_in"][e])
        total = part if total is None else total + part
    half = pre_s.shape[1] // 2
    p = pre_s.astype(f32)
    grad_hid = nn(base_z, w["shared_down_t"])
    g_gate, g_up = swiglu_back(grad_hid, p[:, :half], p[:, half:])
    g_pre_s = jnp.concatenate([g_gate, g_up], axis=1)
    total = add_first(total, nt(g_pre_s, w["shared_in"]))
    extra = -(-experts_total // 128) * 128
    table = jnp.pad(table, ((0, 0), (0, extra - experts_total)))
    back = return_rows(narrow(jnp.concatenate([total, table], axis=1)))
    side = (moe_in, grad_z, hidden, hid_s, pre_grads, g_pre_s, base_in, base_z)
    return back, side


def moe_finish(back, kept, w, experts_total):
    own_gates = kept[2]
    weighted = back[:, D : D + experts_total]
    grad_logits = weighted - own_gates * jnp.sum(weighted, axis=-1, keepdims=True)
    grad_logits = grad_logits.astype(bf16)
    return back[:, :D] + nt(grad_logits, w["router"]), grad_logits


def cat(items):
    return jnp.concatenate(items, axis=0)


def moe_weight_grads(sides):
    moe_in = cat([s[0] for s in sides])
    grad_z = cat([s[1] for s in sides])
    count = len(sides[0][2])
    g_down = jnp.stack(
        [tn(cat([s[2][e] for s in sides]), grad_z, bf16) for e in range(count)]
    )
    g_in = jnp.stack([tn(moe_in, cat([s[4][e] for s in sides]), bf16) for e in range(count)])
    base_in = cat([s[6] for s in sides])
    g_sin = tn(base_in, cat([s[5] for s in sides]), bf16)
    g_sdown_t = tn(cat([s[7] for s in sides]), cat([s[3] for s in sides]), bf16)
    return g_in, g_down, g_sin, g_sdown_t


def attn_mask(seg):
    length = seg.shape[1]
    rows_pos = lax.broadcasted_iota(jnp.int32, (length, length), 0)
    cols_pos = lax.broadcasted_iota(jnp.int32, (length, length), 1)
    return (seg[:, :, None] == seg[:, None, :]) & (cols_pos <= rows_pos)[None]


def attn_forward(own_in, allowed, w_qkv, w_out_t):
    seqs, length, _ = allowed.shape
    kv = KVH // 2
    group = QH // KVH
    q_width = kv * group * HEAD
    kv_width = kv * HEAD
    attn_in = pair_gather(own_in)
    packed = nn(attn_in, w_qkv, bf16)
    q = packed[:, :q_width].reshape(seqs, length, kv, group, HEAD)
    k = packed[:, q_width : q_width + kv_width].reshape(seqs, length, kv, HEAD)
    v = packed[:, q_width + kv_width :].reshape(seqs, length, kv, HEAD)
    scores = jnp.einsum("bqhgd,bkhd->bhgqk", q, k, preferred_element_type=f32) * HEAD**-0.5
    scores = jnp.where(allowed[:, None, None], scores, masked_value)
    peak = jnp.max(scores, axis=-1, keepdims=True)
    ex = jnp.exp(scores - peak)
    probs = ex / jnp.sum(ex, axis=-1, keepdims=True)
    context = jnp.einsum("bhgqk,bkhd->bqhgd", probs.astype(bf16), v, preferred_element_type=f32)
    context = context.reshape(seqs * length, q_width).astype(bf16)
    branch = pair_return(nt(context, w_out_t))
    return branch, (attn_in, q, k, v, probs, context)


def attn_backward(own_grad, kept, w_qkv, w_out_t):
    attn_in, q, k, v, probs, context = kept
    seqs, length, kv, group, _ = q.shape
    grad = pair_gather(own_grad)
    grad_context = nn(grad, w_out_t, bf16).reshape(seqs, length, kv, group, HEAD)
    probs_low = probs.astype(bf16)
    grad_v = jnp.einsum("bhgqk,bqhgd->bkhd", probs_low, grad_context, preferred_element_type=f32)
    grad_p = jnp.einsum("bqhgd,bkhd->bhgqk", grad_context, v, preferred_element_type=f32)
    delta = jnp.sum(probs * grad_p, axis=-1, keepdims=True)
    grad_s = (probs * (grad_p - delta)).astype(bf16)
    scale = HEAD**-0.5
    grad_q = jnp.einsum("bhgqk,bkhd->bqhgd", grad_s, k, preferred_element_type=f32) * scale
    grad_k = jnp.einsum("bhgqk,bqhgd->bkhd", grad_s, q, preferred_element_type=f32) * scale
    rows = seqs * length
    grad_packed = jnp.concatenate(
        [grad_q.reshape(rows, -1), grad_k.reshape(rows, -1), grad_v.reshape(rows, -1)], axis=1
    ).astype(bf16)
    grad_in = pair_return(nt(grad_packed, w_qkv))
    return grad_in, (attn_in, grad_packed, context, grad)


def by_owner(x, count):
    return x.reshape(x.shape[0], count, x.shape[1] // count)


def body(
    tokens,
    segments,
    routes,
    norm_mamba,
    w_in,
    w_dt,
    conv_w,
    conv_b,
    dt_bias,
    a_log,
    skip_scale,
    gate_norm,
    w_mix_out,
    norm_moe_m,
    router_m,
    shared_in_m,
    shared_down_m,
    expert_in_m,
    expert_down_m,
    norm_attn,
    w_qkv,
    w_out,
    norm_moe,
    router,
    shared_in,
    shared_down,
    expert_in,
    expert_down,
    cotangent,
):
    micro, length, _ = tokens.shape
    n_tp = lax.axis_size("z") * lax.axis_size("core")
    n_ex = lax.axis_size("w") * n_tp
    n_all = lax.axis_size("dp") * n_ex
    rows = w_in.shape[0]
    local_experts = expert_in.shape[0]
    experts_total = local_experts * n_ex
    heads = MH // n_tp
    chan = heads * HP
    ff = SH_FF // n_tp
    slot = lax.axis_index(TP)
    conv_total = DI + 2 * STATE
    conv_here = conv_w.shape[1]
    gate_here = gate_norm.shape[0]
    vec_len = gate_here + (CK + 1) * conv_here
    vec_cols = -(-vec_len // rows)
    small_cols = 4 + 2 * experts_total + vec_cols
    step_width = -(-(heads + small_cols) // 128) * 128

    vec = jnp.concatenate([gate_norm, conv_b, conv_w.reshape(-1)])
    vec = jnp.pad(vec, (0, rows * vec_cols - vec_len)).reshape(rows, vec_cols)
    gains_own = jnp.stack([norm_mamba, norm_moe_m, norm_attn, norm_moe], axis=1)
    little = jnp.concatenate([gains_own, router_m, router, vec], axis=1)

    def for_all(x):
        return jnp.broadcast_to(x[:, None], (rows, n_tp, x.shape[1]))

    def columns(parts):
        packed = jnp.concatenate(parts, axis=2).transpose(1, 0, 2)
        moved = lax.all_to_all(packed, TP, split_axis=0, concat_axis=0, tiled=True)
        return lax.all_gather(moved.reshape(n_tp * rows, -1), FS, axis=0, tiled=True)

    def shared_pack(w_sin, w_sdown):
        return [
            by_owner(w_sin[:, :SH_FF], n_tp),
            by_owner(w_sin[:, SH_FF:], n_tp),
            by_owner(w_sdown.T, n_tp),
        ]

    blank = jnp.zeros((rows, n_tp, step_width - heads - small_cols), bf16)
    w_m = columns(
        [
            by_owner(w_in[:, :DI], n_tp),
            by_owner(w_in[:, DI : 2 * DI], n_tp),
            for_all(w_in[:, 2 * DI :]),
            by_owner(w_dt, n_tp),
            for_all(little),
            blank,
        ]
    )
    in_width = 2 * chan + 2 * STATE
    w_in_here = w_m[:, :in_width]
    w_step = w_m[:, in_width:]
    w_dt_here = w_step[:, :heads]
    small_all = w_step[:, heads : heads + small_cols]
    gain_mamba, gain_moe_m, gain_attn, gain_moe = [small_all[:, i].astype(f32) for i in range(4)]
    router_m_full = small_all[:, 4 : 4 + experts_total]
    router_full = small_all[:, 4 + experts_total : 4 + 2 * experts_total]
    vec_all = small_all[:, 4 + 2 * experts_total :].reshape(n_all, rows * vec_cols).astype(f32)
    gain_gate = vec_all[:, :gate_here].reshape(DI)
    bias_all = vec_all[:, gate_here : gate_here + conv_here].reshape(conv_total)
    taps_all = vec_all[:, gate_here + conv_here : vec_len].reshape(n_all, CK, conv_here)
    taps_all = taps_all.transpose(1, 0, 2).reshape(CK, conv_total)

    def channels(full_row):
        mine = lax.dynamic_slice_in_dim(full_row, slot * chan, chan, axis=-1)
        return jnp.concatenate([mine, full_row[..., DI:]], axis=-1)

    taps = channels(taps_all)
    bias = channels(bias_all)
    gain_here = lax.dynamic_slice_in_dim(gain_gate, slot * chan, chan)
    dt_here = lax.dynamic_slice_in_dim(dt_bias, slot * heads, heads)
    log_here = lax.dynamic_slice_in_dim(a_log, slot * heads, heads)
    skip_here = lax.dynamic_slice_in_dim(skip_scale, slot * heads, heads)

    w_s = columns(
        [by_owner(w_mix_out.T, n_tp)]
        + shared_pack(shared_in_m, shared_down_m)
        + shared_pack(shared_in, shared_down)
    )
    w_mix_t = w_s[:, :chan]
    at = chan

    moe_m = {
        "router": router_m_full,
        "shared_in": w_s[:, at : at + 2 * ff],
        "shared_down_t": w_s[:, at + 2 * ff : at + 3 * ff],
        "expert_in": lax.all_gather(expert_in_m, "dp", axis=1, tiled=True),
        "expert_down": lax.all_gather(expert_down_m, "dp", axis=1, tiled=True),
    }

    kv = KVH // 2
    q_width = QH // 2 * HEAD
    kv_width = kv * HEAD
    q_all, kv_all = QH * HEAD, KVH * HEAD
    attn_pack = jnp.concatenate(
        [
            by_owner(w_qkv[:, :q_all], 2),
            by_owner(w_qkv[:, q_all : q_all + kv_all], 2),
            by_owner(w_qkv[:, q_all + kv_all :], 2),
            by_owner(w_out.T, 2),
        ],
        axis=2,
    ).transpose(1, 0, 2)
    attn_pack = lax.all_to_all(attn_pack, "core", split_axis=0, concat_axis=0, tiled=True)
    attn_w = lax.all_gather(attn_pack.reshape(2 * rows, -1), "z", axis=0, tiled=True)
    attn_w = lax.all_gather(attn_w, FS, axis=0, tiled=True)
    w_qkv_here = attn_w[:, : q_width + 2 * kv_width]
    w_out_t = attn_w[:, q_width + 2 * kv_width :]

    moe_a = {
        "router": router_full,
        "shared_in": w_s[:, at + 3 * ff : at + 5 * ff],
        "shared_down_t": w_s[:, at + 5 * ff :],
        "expert_in": lax.all_gather(expert_in, "dp", axis=1, tiled=True),
        "expert_down": lax.all_gather(expert_down, "dp", axis=1, tiled=True),
    }

    expert_ids = jnp.arange(experts_total, dtype=jnp.int32)
    info_width = -(-(2 * experts_total + 1) // 128) * 128
    each = range(micro)
    x_own = [tokens[m].astype(f32) for m in each]
    seg_all, masks, allowed, mamba_kept, mix_kept, hidden_one = [], [], [], [], [], []
    for m in each:
        seg_own = segments[m, 0]
        hot = [
            jnp.any(routes[b, m][:, :, None] == expert_ids, axis=1).astype(bf16) for b in range(2)
        ]
        info = lanes(hot + [seg_own[:, None].astype(bf16)], info_width)
        rows_all = gather_rows(jnp.concatenate([tokens[m], info], axis=1))
        x_all = rows_all[:, :D].astype(f32)
        marks = wide(rows_all[:, D : D + 2 * experts_total]) > 0.5
        masks.append([marks[:, :experts_total], marks[:, experts_total:]])
        seg = rows_all[:, D + 2 * experts_total].astype(jnp.int32).reshape(n_tp, length)
        seg_all.append(seg)
        allowed.append(attn_mask(jnp.stack([seg[0], seg[n_tp // 2]])))

        normed_x, scale_x, mamba_in = rms_forward(x_all, gain_mamba)
        total_rows = mamba_in.shape[0]
        proj = nn(mamba_in, w_in_here, bf16)
        dt_raw = nn(mamba_in, w_dt_here)

        def piece(p, d, cw, cb, db, al, sk, seg=seg):
            return scan_piece(p, d, seg, cw, cb, db, al, sk, heads)

        gated, pullback = jax.vjp(
            piece,
            proj.astype(f32).reshape(n_tp, length, in_width),
            dt_raw.reshape(n_tp, length, heads),
            taps,
            bias,
            dt_here,
            log_here,
            skip_here,
        )
        gated = gated.reshape(total_rows, chan)
        gained = (gated * gain_here).astype(bf16)
        partial = nt(gained, w_mix_t)
        square = jnp.sum(gated * gated, axis=-1, keepdims=True)
        high = square.astype(bf16).astype(f32)
        extra = jnp.concatenate(
            [high, square - high, jnp.zeros((total_rows, 126), f32)], axis=1
        )
        back = return_rows(jnp.concatenate([partial, extra], axis=1))
        gate_scale = lax.rsqrt((back[:, D : D + 1] + back[:, D + 1 : D + 2]) / DI + epsilon)
        mix_branch = back[:, :D] * gate_scale
        hidden_one.append(x_own[m] + mix_branch)
        mamba_kept.append((normed_x[:length], scale_x[:length], mamba_in, pullback, gated, gained))
        mix_kept.append((mix_branch, gate_scale))

    one_kept, layer_one = [], []
    for m in each:
        normed, scale, own = rms_forward(hidden_one[m], gain_moe_m)
        branch, kept = moe_forward(own, masks[m][0], moe_m)
        layer_one.append(hidden_one[m] + branch)
        one_kept.append((normed, scale, kept))
    attn_kept, hidden_two = [], []
    for m in each:
        normed, scale, own = rms_forward(layer_one[m], gain_attn)
        branch, kept = attn_forward(own, allowed[m], w_qkv_here, w_out_t)
        hidden_two.append(layer_one[m] + branch)
        attn_kept.append((normed, scale, kept))
    cot_all = [gather_rows(cotangent[m]) for m in each]
    two_kept, results = [], []
    for m in each:
        normed, scale, own = rms_forward(hidden_two[m], gain_moe)
        branch, kept = moe_forward(own, masks[m][1], moe_a)
        results.append((hidden_two[m] + branch).astype(bf16))
        two_kept.append((normed, scale, kept))

    gains = [0.0, 0.0, 0.0, 0.0]

    def over_dp(g):
        return lax.psum_scatter(g, "dp", scatter_dimension=1, tiled=True).astype(f32)

    def moe_stage(grads, kept_all, w, gain):
        backs, sides = [], []
        for m in each:
            back, side = moe_backward(grads[m], kept_all[m][2], w, experts_total)
            backs.append(back)
            sides.append(side)
        weights = moe_weight_grads(sides)
        backs[-1], weights = fence(backs[-1], weights)
        grad_gain = 0.0
        values, logits = [], []
        for m in each:
            normed, scale, kept = kept_all[m]
            grad_in, grad_logits = moe_finish(backs[m], kept, w, experts_total)
            logits.append(grad_logits)
            grad_values, part = rms_backward(grad_in, normed, scale, gain)
            grad_gain = grad_gain + part
            values.append(grad_values)
        g_router = tn(cat([s[6][:length] for s in sides]), cat(logits))
        return values, weights, grad_gain, g_router

    values, (g_in_a, g_down_a, g_sin_a, g_sdown_a), gains[3], g_router = moe_stage(
        cot_all, two_kept, moe_a, gain_moe
    )
    out_expert_in = over_dp(g_in_a)
    out_expert_down = over_dp(g_down_a)
    grad_two = [cotangent[m].astype(f32) + values[m] for m in each]

    grad_layer, sides = [], []
    attn_back = []
    for m in each:
        grad_in, side = attn_backward(
            grad_two[m].astype(bf16), attn_kept[m][2], w_qkv_here, w_out_t
        )
        attn_back.append(grad_in)
        sides.append(side)
    attn_in = cat([s[0] for s in sides])
    grad_packed = cat([s[1] for s in sides])
    context = cat([s[2] for s in sides])
    grad_attn = cat([s[3] for s in sides])
    g_attn = jnp.concatenate([tn(attn_in, grad_packed, bf16), tn(grad_attn, context, bf16)], axis=1)
    attn_back[-1], g_attn = fence(attn_back[-1], g_attn)
    g_attn = lax.psum_scatter(g_attn, FS, scatter_dimension=0, tiled=True)
    g_attn = lax.psum_scatter(g_attn, "z", scatter_dimension=0, tiled=True)
    g_attn = lax.all_to_all(
        g_attn.reshape(2, rows, -1), "core", split_axis=0, concat_axis=0, tiled=True
    ).astype(f32)
    for m in each:
        normed, scale, _ = attn_kept[m]
        grad_values, part = rms_backward(attn_back[m], normed, scale, gain_attn)
        gains[2] = gains[2] + part
        grad_layer.append(grad_two[m] + grad_values)

    values, (g_in_m, g_down_m, g_sin_m, g_sdown_m), gains[1], g_router_m = moe_stage(
        [gather_rows(g.astype(bf16)) for g in grad_layer], one_kept, moe_m, gain_moe_m
    )
    out_expert_in_m = over_dp(g_in_m)
    out_expert_down_m = over_dp(g_down_m)
    grad_one = [grad_layer[m] + values[m] for m in each]

    small = None
    mamba_sides, mamba_back = [], []
    for m in each:
        mix_branch, gate_scale = mix_kept[m]
        normed_x, scale_x, mamba_in, pullback, gated, gained = mamba_kept[m]
        grad_mix = grad_one[m].astype(bf16)
        mean_term = jnp.sum(grad_mix.astype(f32) * mix_branch, axis=-1, keepdims=True) / DI
        extra = lanes(split_two(gate_scale) + split_two(mean_term), 128)
        rows_all = gather_rows(jnp.concatenate([grad_mix, extra], axis=1))
        mix_all = rows_all[:, :D]
        extra = rows_all[:, D:].astype(f32)
        scale_all = extra[:, 0:1] + extra[:, 1:2]
        mean_all = extra[:, 2:3] + extra[:, 3:4]
        grad_gated = nn(mix_all, w_mix_t, bf16).astype(f32)
        norm_gated = gated * scale_all
        grad_gate_norm = jnp.sum(grad_gated * norm_gated, axis=0)
        grad_rows = scale_all * (grad_gated * gain_here - norm_gated * mean_all)
        pulled = pullback(grad_rows.reshape(n_tp, length, chan))
        grad_proj = pulled[0].reshape(-1, in_width).astype(bf16)
        grad_step = pulled[1].reshape(-1, heads).astype(bf16)
        scaled_mix = (mix_all.astype(f32) * scale_all).astype(bf16)
        mamba_sides.append((mamba_in, grad_proj, grad_step, gained, scaled_mix))
        grads = (*pulled[2:], grad_gate_norm)
        small = grads if small is None else tuple(a + b for a, b in zip(small, grads))
        mamba_back.append(return_rows(nt(grad_proj, w_in_here) + nt(grad_step, w_dt_here)))

    def rows_back(packed):
        packed = lax.psum_scatter(packed, FS, scatter_dimension=0, tiled=True)
        return lax.all_to_all(
            packed.reshape(n_tp, rows, -1), TP, split_axis=0, concat_axis=0, tiled=True
        ).astype(f32)

    def owned(block):
        return block.transpose(1, 0, 2).reshape(rows, -1)

    g_mix = tn(
        cat([s[4] for s in mamba_sides]), cat([s[3] for s in mamba_sides]), bf16
    )
    g_s = rows_back(
        jnp.concatenate([g_mix, g_sin_m, g_sdown_m, g_sin_a, g_sdown_a], axis=1)
    )
    out_mix = owned(g_s[:, :, :chan]).T

    mamba_in = cat([s[0] for s in mamba_sides])
    g_proj = tn(mamba_in, cat([s[1] for s in mamba_sides]), bf16)
    g_step = tn(mamba_in, cat([s[2] for s in mamba_sides]), bf16)

    grads_in = []
    for m in each:
        normed_x, scale_x = mamba_kept[m][:2]
        grad_values, part = rms_backward(mamba_back[m], normed_x, scale_x, gain_mamba)
        gains[0] = gains[0] + part
        grads_in.append(grad_one[m] + grad_values)

    g_taps, g_bias, g_dt, g_log, g_skip, g_gate = small

    def spread(part, width):
        zeros = jnp.zeros(part.shape[:-1] + (width,), f32)
        return lax.dynamic_update_slice_in_dim(zeros, part[..., :chan], slot * chan, axis=-1)

    conv_grad = jnp.concatenate([g_bias[None], g_taps], axis=0)
    conv_grad = spread(conv_grad, conv_total) + jnp.pad(conv_grad[:, chan:], ((0, 0), (DI, 0)))
    conv_grad = conv_grad.reshape(CK + 1, n_all, conv_here).transpose(1, 0, 2).reshape(n_all, -1)
    vec_grad = jnp.concatenate([spread(g_gate, DI).reshape(n_all, gate_here), conv_grad], axis=1)
    vec_grad = jnp.pad(vec_grad, ((0, 0), (0, rows * vec_cols - vec_len))).reshape(D, vec_cols)
    little = jnp.concatenate(
        [g[:, None] for g in gains] + [g_router_m, g_router, vec_grad], axis=1
    ).astype(bf16)
    blank = jnp.zeros((D, step_width - heads - small_cols), bf16)
    g_m = rows_back(jnp.concatenate([g_proj, g_step, little, blank], axis=1))
    out_w_in = jnp.concatenate(
        [
            owned(g_m[:, :, :chan]),
            owned(g_m[:, :, chan : 2 * chan]),
            jnp.sum(g_m[:, :, 2 * chan : in_width], axis=0),
        ],
        axis=1,
    )
    out_w_dt = owned(g_m[:, :, in_width : in_width + heads])
    little = jnp.sum(g_m[:, :, in_width + heads : in_width + heads + small_cols], axis=0)
    vec = little[:, 4 + 2 * experts_total :].reshape(-1)
    out_gate = vec[:gate_here]
    out_conv_b = vec[gate_here : gate_here + conv_here]
    out_conv_w = vec[gate_here + conv_here : vec_len].reshape(CK, conv_here)

    head_grad = jnp.pad(jnp.stack([g_dt, g_log, g_skip]), ((0, 0), (0, 128 - heads)))[None]
    for axis in ("dp", "w"):
        own = head_grad
        for s in range(1, lax.axis_size(axis)):
            head_grad = head_grad + lax.ppermute(own, axis, ring(s, axis))
    for axis in ("z", "core"):
        n = lax.axis_size(axis)
        here = lax.axis_index(axis)
        parts = [head_grad] + [lax.ppermute(head_grad, axis, ring(s, axis)) for s in range(1, n)]
        ordered = 0.0
        for s, part in enumerate(parts):
            at_slot = jnp.arange(n)[:, None, None, None] == (here - s) % n
            ordered = ordered + jnp.where(at_slot, part[None], 0.0)
        head_grad = ordered.reshape((-1,) + ordered.shape[2:]) if axis == "z" else jnp.moveaxis(
            ordered, 0, 1
        ).reshape((-1,) + ordered.shape[2:])
    head_grad = head_grad[:, :, :heads].transpose(1, 0, 2).reshape(3, MH)

    cuts = (q_width, q_width + kv_width, q_width + 2 * kv_width)
    out_w_qkv = jnp.concatenate(
        [
            owned(g_attn[:, :, : cuts[0]]),
            owned(g_attn[:, :, cuts[0] : cuts[1]]),
            owned(g_attn[:, :, cuts[1] : cuts[2]]),
        ],
        axis=1,
    )
    out_w_out = owned(g_attn[:, :, cuts[2] :]).T

    def shared_out(block):
        g_sin = jnp.concatenate([owned(block[:, :, :ff]), owned(block[:, :, ff : 2 * ff])], axis=1)
        return g_sin, owned(block[:, :, 2 * ff :]).T

    out_sin_m, out_sdown_m = shared_out(g_s[:, :, chan : chan + 3 * ff])
    out_sin, out_sdown = shared_out(g_s[:, :, chan + 3 * ff :])

    return (
        jnp.stack(results),
        jnp.stack(grads_in),
        little[:, 0],
        out_w_in,
        out_w_dt,
        out_conv_w,
        out_conv_b,
        head_grad[0],
        head_grad[1],
        head_grad[2],
        out_gate,
        out_mix,
        little[:, 1],
        little[:, 4 : 4 + experts_total],
        out_sin_m,
        out_sdown_m,
        out_expert_in_m,
        out_expert_down_m,
        little[:, 2],
        out_w_qkv,
        out_w_out,
        little[:, 3],
        little[:, 4 + experts_total : 4 + 2 * experts_total],
        out_sin,
        out_sdown,
        out_expert_in,
        out_expert_down,
    )


def solution(mesh):
    n_dp, n_ex = mesh.shape["dp"], mesh.shape["expert"]
    outer = n_ex // 8
    fine = Mesh(mesh.devices.reshape(n_dp, outer, 4, 2), ALL)
    split = P(ALL)
    row = P(ALL, None)
    col = P(None, ALL)
    mid = P(None, ALL, None)
    part = P(EX, "dp", None)
    same = P()
    return jax.shard_map(
        body,
        mesh=fine,
        in_specs=(
            mid,
            mid,
            P(None, None, ALL, None),
            split,
            row,
            row,
            col,
            split,
            same,
            same,
            same,
            split,
            col,
            split,
            row,
            row,
            col,
            part,
            part,
            split,
            row,
            col,
            split,
            row,
            row,
            col,
            part,
            part,
            mid,
        ),
        out_specs=(
            mid,
            mid,
            split,
            row,
            row,
            col,
            split,
            same,
            same,
            same,
            split,
            col,
            split,
            row,
            row,
            col,
            part,
            part,
            split,
            row,
            col,
            split,
            row,
            row,
            col,
            part,
            part,
        ),
        check_vma=False,
    )
```

```python
import jax
import jax.numpy as jnp
from jax import lax
from jax.sharding import Mesh, PartitionSpec as P

D = 1536
QH = 12
KVH = 4
HEAD = 128
EXP_FF = 512
SH_FF = 1024
TOP = 6
MH = 48
HP = 64
STATE = 128
CK = 4
DI = 3072

bf16 = jnp.bfloat16
f32 = jnp.float32
epsilon = 1e-05
masked_value = -1e30
highest = lax.Precision.HIGHEST
ALL = ("dp", "w", "z", "core")
EX = ("w", "z", "core")
TP = ("z", "core")
FS = ("dp", "w")
SWAP = [(0, 1), (1, 0)]


def dot(a, b, dims, out=f32):
    r = lax.dot_general(a, b, (dims, ((), ())), preferred_element_type=f32)
    return r if out == f32 else r.astype(out)


def nn(a, b, out=f32):
    return dot(a, b, ((1,), (0,)), out)


def nt(a, b, out=f32):
    return dot(a, b, ((1,), (1,)), out)


def tn(a, b, out=f32):
    return dot(a, b, ((0,), (0,)), out)


def ring(shift, axis="z"):
    n = lax.axis_size(axis)
    return [(i, (i + shift) % n) for i in range(n)]


def wide(x):
    parts = [x] + [lax.ppermute(x, "w", ring(s, "w")) for s in range(1, lax.axis_size("w"))]
    return parts[0] if len(parts) == 1 else jnp.concatenate(parts, axis=0)


def narrow(total):
    n = lax.axis_size("w")
    rows = total.shape[0] // n
    out = total[:rows]
    for s in range(1, n):
        part = total[s * rows : (s + 1) * rows].astype(bf16)
        out = out + lax.ppermute(part, "w", ring(-s, "w")).astype(f32)
    return out


def add_first(total, part):
    rows = part.shape[0]
    if rows == total.shape[0]:
        return total + part
    return jnp.concatenate([total[:rows] + part, total[rows:]], axis=0)


def fence(*trees):
    if lax.axis_size("w") > 1:
        return trees
    return lax.optimization_barrier(trees)


def gather_rows(x):
    n = lax.axis_size("z")
    parts = [x] + [lax.ppermute(x, "z", ring(s)) for s in range(1, n)]
    other = [lax.ppermute(p, "core", SWAP) for p in parts]
    return jnp.concatenate(parts + other, axis=0)


def return_rows(total):
    n = lax.axis_size("z")
    half = total.shape[0] // 2
    rows = half // n
    recv = lax.ppermute(total[half:].astype(bf16), "core", SWAP)
    mine = total[:half] + recv.astype(f32)
    out = mine[:rows]
    for s in range(1, n):
        part = mine[s * rows : (s + 1) * rows].astype(bf16)
        out = out + lax.ppermute(part, "z", ring(-s)).astype(f32)
    return out


def pair_gather(x):
    return jnp.concatenate([x, lax.ppermute(x, "core", SWAP)], axis=0)


def pair_return(total):
    half = total.shape[0] // 2
    recv = lax.ppermute(total[half:].astype(bf16), "core", SWAP)
    return total[:half] + recv.astype(f32)


def split_two(x):
    high = x.astype(bf16)
    return [high, (x - high.astype(f32)).astype(bf16)]


def row_scale(values):
    return lax.rsqrt(jnp.mean(values * values, axis=-1, keepdims=True) + epsilon)


def rms_forward(values, gain):
    scale = row_scale(values)
    normed = values * scale
    return normed, scale, (normed * gain).astype(bf16)


def rms_backward(grad_result, normed, scale, gain):
    grad_gain = jnp.sum(grad_result * normed, axis=0)
    grad_normed = grad_result * gain
    grad_values = scale * (
        grad_normed - normed * jnp.mean(grad_normed * normed, axis=-1, keepdims=True)
    )
    return grad_values, grad_gain


def lanes(parts, width):
    used = sum(p.shape[-1] for p in parts)
    rows = parts[0].shape[0]
    if used < width:
        parts = parts + [jnp.zeros((rows, width - used), bf16)]
    return jnp.concatenate(parts, axis=1)


def scan_piece(proj, dt_raw, seg, conv_w, conv_b, dt_bias, a_log, skip, heads):
    seqs, length, _ = proj.shape
    chan = heads * HP
    gate_z = proj[..., :chan]
    conv_in = proj[..., chan:]
    positions = lax.broadcasted_iota(jnp.int32, (length,), 0)
    conv_sum = jnp.zeros_like(conv_in) + conv_b
    for offset in range(CK):
        shifted = jnp.pad(conv_in, ((0, 0), (offset, 0), (0, 0)))[:, :length]
        seg_prev = jnp.pad(seg, ((0, 0), (offset, 0)))[:, :length]
        usable = (positions >= offset)[None] & (seg_prev == seg)
        conv_sum = conv_sum + jnp.where(usable[..., None], conv_w[offset] * shifted, 0.0)
    conv_act = jax.nn.silu(conv_sum)
    inputs = conv_act[..., :chan].reshape(seqs, length, heads, HP)
    b_state = conv_act[..., chan : chan + STATE]
    c_state = conv_act[..., chan + STATE :]
    step = jax.nn.softplus(dt_raw + dt_bias)
    rows_pos = lax.broadcasted_iota(jnp.int32, (length, length), 0)
    cols_pos = lax.broadcasted_iota(jnp.int32, (length, length), 1)
    lower = (cols_pos <= rows_pos).astype(f32)
    cum = jnp.einsum("ts,bsh->bht", lower, step * -jnp.exp(a_log), precision=highest)
    allowed = (seg[:, :, None] == seg[:, None, :]) & (cols_pos <= rows_pos)[None]
    allowed = allowed[:, None]
    gap = cum[..., :, None] - cum[..., None, :]
    decay = jnp.where(allowed, jnp.exp(jnp.where(allowed, gap, 0.0)), 0.0)
    cb = jnp.einsum("btn,bsn->bts", c_state, b_state, precision=highest)
    mix = decay * cb[:, None] * step.transpose(0, 2, 1)[:, :, None, :]
    scan = jnp.einsum("bhts,bshp->bthp", mix, inputs, precision=highest)
    scan = scan + skip[:, None] * inputs
    return scan.reshape(seqs, length, chan) * jax.nn.silu(gate_z)


def swiglu(gate, up):
    return gate * jax.nn.sigmoid(gate) * up


def swiglu_back(grad, gate, up):
    logistic = jax.nn.sigmoid(gate)
    grad_gate = grad * up * logistic * (1.0 + gate * (1.0 - logistic))
    return grad_gate.astype(bf16), (grad * gate * logistic).astype(bf16)


def gate_table(moe_in, mask, router):
    logits = nn(moe_in, router)
    picked = jnp.where(mask, logits, masked_value)
    peak = jnp.max(picked, axis=-1, keepdims=True)
    ex = jnp.where(mask, jnp.exp(picked - peak), 0.0)
    return ex / jnp.sum(ex, axis=-1, keepdims=True)


def moe_forward(own_in, mask, w):
    rows = own_in.shape[0]
    base_in = gather_rows(own_in)
    moe_in = wide(base_in)
    gates = gate_table(moe_in, mask, w["router"])
    count = w["expert_in"].shape[0]
    first = lax.axis_index(EX) * count
    local = lax.dynamic_slice(gates, (0, first), (gates.shape[0], count))
    pre = [nn(moe_in, w["expert_in"][e], bf16) for e in range(count)]
    pre_s = nn(base_in, w["shared_in"], bf16)
    total = None
    for e in range(count):
        p = pre[e].astype(f32)
        act = swiglu(p[:, :EXP_FF], p[:, EXP_FF:])
        hid = (act * local[:, e : e + 1]).astype(bf16)
        part = nn(hid, w["expert_down"][e])
        total = part if total is None else total + part
    half = pre_s.shape[1] // 2
    p = pre_s.astype(f32)
    hid_s = swiglu(p[:, :half], p[:, half:]).astype(bf16)
    total = add_first(total, nt(hid_s, w["shared_down_t"]))
    branch = return_rows(narrow(total))
    kept = (moe_in, base_in, gates[:rows], local, pre, pre_s)
    return branch, kept


def moe_backward(base_z, kept, w, experts_total):
    moe_in, base_in, own_gates, local, pre, pre_s = kept
    pre, pre_s, _ = fence(pre, pre_s, base_z)
    grad_z = wide(base_z)
    rows = own_gates.shape[0]
    count = len(pre)
    total = None
    first = lax.axis_index(EX) * count
    lane = lax.broadcasted_iota(jnp.int32, (1, experts_total), 1)
    table = jnp.zeros((grad_z.shape[0], experts_total), f32)
    pre_grads, hidden = [], []
    for e in range(count):
        p = pre[e].astype(f32)
        gate, up = p[:, :EXP_FF], p[:, EXP_FF:]
        grad_hid = nt(grad_z, w["expert_down"][e])
        share = local[:, e : e + 1]
        act = swiglu(gate, up)
        hidden.append((act * share).astype(bf16))
        weighted = share * jnp.sum(grad_hid * act, axis=-1, keepdims=True)
        table = table + weighted * (lane == first + e).astype(f32)
        g_gate, g_up = swiglu_back(grad_hid * share, gate, up)
        g_pre = jnp.concatenate([g_gate, g_up], axis=1)
        pre_grads.append(g_pre)
        part = nt(g_pre, w["expert_in"][e])
        total = part if total is None else total + part
    half = pre_s.shape[1] // 2
    p = pre_s.astype(f32)
    grad_hid = nn(base_z, w["shared_down_t"])
    hid_s = swiglu(p[:, :half], p[:, half:]).astype(bf16)
    g_gate, g_up = swiglu_back(grad_hid, p[:, :half], p[:, half:])
    g_pre_s = jnp.concatenate([g_gate, g_up], axis=1)
    total = add_first(total, nt(g_pre_s, w["shared_in"]))
    extra = -(-experts_total // 128) * 128
    table = jnp.pad(table, ((0, 0), (0, extra - experts_total)))
    back = return_rows(narrow(jnp.concatenate([total, table], axis=1)))
    side = (moe_in, grad_z, hidden, hid_s, pre_grads, g_pre_s, base_in, base_z)
    return back, side


def moe_finish(back, kept, w, experts_total):
    own_gates = kept[2]
    weighted = back[:, D : D + experts_total]
    grad_logits = weighted - own_gates * jnp.sum(weighted, axis=-1, keepdims=True)
    grad_logits = grad_logits.astype(bf16)
    return back[:, :D] + nt(grad_logits, w["router"]), grad_logits


def tn_sum(pairs, out=bf16):
    if lax.axis_size("w") > 1:
        return tn(*[jnp.concatenate(side, axis=0) for side in zip(*pairs)], out)
    total = None
    for a, b in pairs:
        part = tn(a, b)
        total = part if total is None else total + part
    return total.astype(out)


def moe_weight_grads(sides):
    count = len(sides[0][2])
    g_down = jnp.stack([tn_sum([(s[2][e], s[1]) for s in sides]) for e in range(count)])
    g_in = jnp.stack([tn_sum([(s[0], s[4][e]) for s in sides]) for e in range(count)])
    g_sin = tn_sum([(s[6], s[5]) for s in sides])
    g_sdown_t = tn_sum([(s[7], s[3]) for s in sides])
    return g_in, g_down, g_sin, g_sdown_t


def attn_mask(seg):
    length = seg.shape[1]
    rows_pos = lax.broadcasted_iota(jnp.int32, (length, length), 0)
    cols_pos = lax.broadcasted_iota(jnp.int32, (length, length), 1)
    return (seg[:, :, None] == seg[:, None, :]) & (cols_pos <= rows_pos)[None]


def attn_forward(own_in, allowed, w_qkv, w_out_t):
    seqs, length, _ = allowed.shape
    kv = KVH // 2
    group = QH // KVH
    q_width = kv * group * HEAD
    kv_width = kv * HEAD
    attn_in = pair_gather(own_in)
    packed = nn(attn_in, w_qkv, bf16)
    q = packed[:, :q_width].reshape(seqs, length, kv, group, HEAD)
    k = packed[:, q_width : q_width + kv_width].reshape(seqs, length, kv, HEAD)
    v = packed[:, q_width + kv_width :].reshape(seqs, length, kv, HEAD)
    scores = jnp.einsum("bqhgd,bkhd->bhgqk", q, k, preferred_element_type=f32) * HEAD**-0.5
    scores = jnp.where(allowed[:, None, None], scores, masked_value)
    peak = jnp.max(scores, axis=-1, keepdims=True)
    ex = jnp.exp(scores - peak)
    probs = ex / jnp.sum(ex, axis=-1, keepdims=True)
    context = jnp.einsum("bhgqk,bkhd->bqhgd", probs.astype(bf16), v, preferred_element_type=f32)
    context = context.reshape(seqs * length, q_width).astype(bf16)
    branch = pair_return(nt(context, w_out_t))
    return branch, (attn_in, q, k, v, probs, context)


def attn_backward(own_grad, kept, w_qkv, w_out_t):
    attn_in, q, k, v, probs, context = kept
    seqs, length, kv, group, _ = q.shape
    grad = pair_gather(own_grad)
    grad_context = nn(grad, w_out_t, bf16).reshape(seqs, length, kv, group, HEAD)
    probs_low = probs.astype(bf16)
    grad_v = jnp.einsum("bhgqk,bqhgd->bkhd", probs_low, grad_context, preferred_element_type=f32)
    grad_p = jnp.einsum("bqhgd,bkhd->bhgqk", grad_context, v, preferred_element_type=f32)
    delta = jnp.sum(probs * grad_p, axis=-1, keepdims=True)
    grad_s = (probs * (grad_p - delta)).astype(bf16)
    scale = HEAD**-0.5
    grad_q = jnp.einsum("bhgqk,bkhd->bqhgd", grad_s, k, preferred_element_type=f32) * scale
    grad_k = jnp.einsum("bhgqk,bqhgd->bkhd", grad_s, q, preferred_element_type=f32) * scale
    rows = seqs * length
    grad_packed = jnp.concatenate(
        [grad_q.reshape(rows, -1), grad_k.reshape(rows, -1), grad_v.reshape(rows, -1)], axis=1
    ).astype(bf16)
    grad_in = pair_return(nt(grad_packed, w_qkv))
    return grad_in, (attn_in, grad_packed, context, grad)


def by_owner(x, count):
    return x.reshape(x.shape[0], count, x.shape[1] // count)


def body(
    tokens,
    segments,
    routes,
    norm_mamba,
    w_in,
    w_dt,
    conv_w,
    conv_b,
    dt_bias,
    a_log,
    skip_scale,
    gate_norm,
    w_mix_out,
    norm_moe_m,
    router_m,
    shared_in_m,
    shared_down_m,
    expert_in_m,
    expert_down_m,
    norm_attn,
    w_qkv,
    w_out,
    norm_moe,
    router,
    shared_in,
    shared_down,
    expert_in,
    expert_down,
    cotangent,
):
    micro, length, _ = tokens.shape
    n_tp = lax.axis_size("z") * lax.axis_size("core")
    n_ex = lax.axis_size("w") * n_tp
    n_all = lax.axis_size("dp") * n_ex
    rows = w_in.shape[0]
    local_experts = expert_in.shape[0]
    experts_total = local_experts * n_ex
    heads = MH // n_tp
    chan = heads * HP
    ff = SH_FF // n_tp
    slot = lax.axis_index(TP)
    conv_total = DI + 2 * STATE
    conv_here = conv_w.shape[1]
    gate_here = gate_norm.shape[0]
    vec_len = gate_here + (CK + 1) * conv_here
    vec_cols = -(-vec_len // rows)
    small_cols = 4 + 2 * experts_total + vec_cols
    step_width = -(-(heads + small_cols) // 128) * 128

    vec = jnp.concatenate([gate_norm, conv_b, conv_w.reshape(-1)])
    vec = jnp.pad(vec, (0, rows * vec_cols - vec_len)).reshape(rows, vec_cols)
    gains_own = jnp.stack([norm_mamba, norm_moe_m, norm_attn, norm_moe], axis=1)
    little = jnp.concatenate([gains_own, router_m, router, vec], axis=1)

    def for_all(x):
        return jnp.broadcast_to(x[:, None], (rows, n_tp, x.shape[1]))

    def moved_columns(parts, *after):
        packed = jnp.concatenate(parts, axis=2).transpose(1, 0, 2)
        packed = fence(packed, *after)[0]
        moved = lax.all_to_all(packed, TP, split_axis=0, concat_axis=0, tiled=True)
        return moved.reshape(n_tp * rows, -1)

    def whole_rows(moved):
        return lax.all_gather(moved, FS, axis=0, tiled=True)

    def shared_pack(w_sin, w_sdown):
        return [
            by_owner(w_sin[:, :SH_FF], n_tp),
            by_owner(w_sin[:, SH_FF:], n_tp),
            by_owner(w_sdown.T, n_tp),
        ]

    blank = jnp.zeros((rows, n_tp, step_width - heads - small_cols), bf16)
    moved_m = moved_columns(
        [
            by_owner(w_in[:, :DI], n_tp),
            by_owner(w_in[:, DI : 2 * DI], n_tp),
            for_all(w_in[:, 2 * DI :]),
            by_owner(w_dt, n_tp),
            for_all(little),
            blank,
        ]
    )
    w_m = whole_rows(moved_m)
    moved_s = moved_columns(
        [by_owner(w_mix_out.T, n_tp)]
        + shared_pack(shared_in_m, shared_down_m)
        + shared_pack(shared_in, shared_down),
        moved_m,
    )
    w_s = whole_rows(moved_s)
    in_width = 2 * chan + 2 * STATE
    w_in_here = w_m[:, :in_width]
    w_step = w_m[:, in_width:]
    w_dt_here = w_step[:, :heads]
    small_all = w_step[:, heads : heads + small_cols]
    gain_mamba, gain_moe_m, gain_attn, gain_moe = [small_all[:, i].astype(f32) for i in range(4)]
    router_m_full = small_all[:, 4 : 4 + experts_total]
    router_full = small_all[:, 4 + experts_total : 4 + 2 * experts_total]
    vec_all = small_all[:, 4 + 2 * experts_total :].reshape(n_all, rows * vec_cols).astype(f32)
    gain_gate = vec_all[:, :gate_here].reshape(DI)
    bias_all = vec_all[:, gate_here : gate_here + conv_here].reshape(conv_total)
    taps_all = vec_all[:, gate_here + conv_here : vec_len].reshape(n_all, CK, conv_here)
    taps_all = taps_all.transpose(1, 0, 2).reshape(CK, conv_total)

    def channels(full_row):
        mine = lax.dynamic_slice_in_dim(full_row, slot * chan, chan, axis=-1)
        return jnp.concatenate([mine, full_row[..., DI:]], axis=-1)

    taps = channels(taps_all)
    bias = channels(bias_all)
    gain_here = lax.dynamic_slice_in_dim(gain_gate, slot * chan, chan)
    dt_here = lax.dynamic_slice_in_dim(dt_bias, slot * heads, heads)
    log_here = lax.dynamic_slice_in_dim(a_log, slot * heads, heads)
    skip_here = lax.dynamic_slice_in_dim(skip_scale, slot * heads, heads)

    w_mix_t = w_s[:, :chan]
    at = chan

    moe_m = {
        "router": router_m_full,
        "shared_in": w_s[:, at : at + 2 * ff],
        "shared_down_t": w_s[:, at + 2 * ff : at + 3 * ff],
        "expert_in": lax.all_gather(expert_in_m, "dp", axis=1, tiled=True),
        "expert_down": lax.all_gather(expert_down_m, "dp", axis=1, tiled=True),
    }

    kv = KVH // 2
    q_width = QH // 2 * HEAD
    kv_width = kv * HEAD
    q_all, kv_all = QH * HEAD, KVH * HEAD
    attn_pack = jnp.concatenate(
        [
            by_owner(w_qkv[:, :q_all], 2),
            by_owner(w_qkv[:, q_all : q_all + kv_all], 2),
            by_owner(w_qkv[:, q_all + kv_all :], 2),
            by_owner(w_out.T, 2),
        ],
        axis=2,
    ).transpose(1, 0, 2)
    attn_pack, _ = fence(attn_pack, (w_m, moved_s))
    attn_pack = lax.all_to_all(attn_pack, "core", split_axis=0, concat_axis=0, tiled=True)
    attn_w = lax.all_gather(attn_pack.reshape(2 * rows, -1), "z", axis=0, tiled=True)
    attn_w = lax.all_gather(attn_w, FS, axis=0, tiled=True)
    w_qkv_here = attn_w[:, : q_width + 2 * kv_width]
    w_out_t = attn_w[:, q_width + 2 * kv_width :]

    moe_a = {
        "router": router_full,
        "shared_in": w_s[:, at + 3 * ff : at + 5 * ff],
        "shared_down_t": w_s[:, at + 5 * ff :],
        "expert_in": lax.all_gather(expert_in, "dp", axis=1, tiled=True),
        "expert_down": lax.all_gather(expert_down, "dp", axis=1, tiled=True),
    }

    expert_ids = jnp.arange(experts_total, dtype=jnp.int32)
    info_width = -(-(2 * experts_total + 1) // 128) * 128
    each = range(micro)
    x_own = [tokens[m].astype(f32) for m in each]
    seg_all, masks, allowed, mamba_kept, mix_kept, hidden_one = [], [], [], [], [], []
    for m in each:
        seg_own = segments[m, 0]
        hot = [
            jnp.any(routes[b, m][:, :, None] == expert_ids, axis=1).astype(bf16) for b in range(2)
        ]
        info = lanes(hot + [seg_own[:, None].astype(bf16)], info_width)
        x_info, _ = fence(jnp.concatenate([tokens[m], info], axis=1), moved_m)
        rows_all = gather_rows(x_info)
        x_all = rows_all[:, :D].astype(f32)
        marks = wide(rows_all[:, D : D + 2 * experts_total]) > 0.5
        masks.append([marks[:, :experts_total], marks[:, experts_total:]])
        seg = rows_all[:, D + 2 * experts_total].astype(jnp.int32).reshape(n_tp, length)
        seg_all.append(seg)
        allowed.append(attn_mask(jnp.stack([seg[0], seg[n_tp // 2]])))

        normed_x, scale_x, mamba_in = rms_forward(x_all, gain_mamba)
        total_rows = mamba_in.shape[0]
        proj = nn(mamba_in, w_in_here, bf16)
        dt_raw = nn(mamba_in, w_dt_here)

        def piece(p, d, cw, cb, db, al, sk, seg=seg):
            return scan_piece(p, d, seg, cw, cb, db, al, sk, heads)

        gated, pullback = jax.vjp(
            piece,
            proj.astype(f32).reshape(n_tp, length, in_width),
            dt_raw.reshape(n_tp, length, heads),
            taps,
            bias,
            dt_here,
            log_here,
            skip_here,
        )
        gated = gated.reshape(total_rows, chan)
        gained = (gated * gain_here).astype(bf16)
        partial = nt(gained, w_mix_t)
        square = jnp.sum(gated * gated, axis=-1, keepdims=True)
        high = square.astype(bf16).astype(f32)
        extra = jnp.concatenate(
            [high, square - high, jnp.zeros((total_rows, 126), f32)], axis=1
        )
        back = return_rows(jnp.concatenate([partial, extra], axis=1))
        gate_scale = lax.rsqrt((back[:, D : D + 1] + back[:, D + 1 : D + 2]) / DI + epsilon)
        mix_branch = back[:, :D] * gate_scale
        hidden_one.append(x_own[m] + mix_branch)
        mamba_kept.append((rows_all, scale_x[:length], mamba_in, pullback, gated, gained))
        mix_kept.append((mix_branch, gate_scale))

    cot_all = [gather_rows(cotangent[m]) for m in each]
    hidden_one[-1], cot_all = fence(hidden_one[-1], cot_all)
    one_kept, layer_one = [], []
    for m in each:
        normed, scale, own = rms_forward(hidden_one[m], gain_moe_m)
        branch, kept = moe_forward(own, masks[m][0], moe_m)
        layer_one.append(hidden_one[m] + branch)
        one_kept.append((normed, scale, kept))
    attn_kept, hidden_two = [], []
    for m in each:
        normed, scale, own = rms_forward(layer_one[m], gain_attn)
        branch, kept = attn_forward(own, allowed[m], w_qkv_here, w_out_t)
        hidden_two.append(layer_one[m] + branch)
        attn_kept.append((normed, scale, kept))
    two_kept, results = [], []
    for m in each:
        normed, scale, own = rms_forward(hidden_two[m], gain_moe)
        branch, kept = moe_forward(own, masks[m][1], moe_a)
        results.append((hidden_two[m] + branch).astype(bf16))
        two_kept.append((normed, scale, kept))

    gains = [0.0, 0.0, 0.0, 0.0]

    def over_dp(g):
        return lax.psum_scatter(g, "dp", scatter_dimension=1, tiled=True)

    def moe_stage(grads, kept_all, w, gain, *before):
        backs, sides, own_rows = [], [], []
        for m in each:
            back, side = moe_backward(grads[m], kept_all[m][2], w, experts_total)
            backs.append(back)
            sides.append(side)
            own_rows.append(side[6][:length])
        weights = moe_weight_grads(sides)
        backs[-1], weights = lax.optimization_barrier((backs[-1], weights))
        backs[-1], before = fence(backs[-1], before)
        grad_gain = 0.0
        values, logits = [], []
        for m in each:
            normed, scale, kept = kept_all[m]
            grad_in, grad_logits = moe_finish(backs[m], kept, w, experts_total)
            logits.append(grad_logits)
            grad_values, part = rms_backward(grad_in, normed, scale, gain)
            grad_gain = grad_gain + part
            values.append(grad_values)
        g_router = tn_sum(list(zip(own_rows, logits)), f32)
        return values, weights, grad_gain, g_router, before

    values, (g_in_a, g_down_a, g_sin_a, g_sdown_a), gains[3], g_router, _ = moe_stage(
        cot_all, two_kept, moe_a, gain_moe
    )
    sum_in_a = over_dp(g_in_a)
    sum_down_a = over_dp(g_down_a)
    grad_two = [cotangent[m].astype(f32) + values[m] for m in each]

    grad_layer, sides = [], []
    attn_back = []
    for m in each:
        grad_in, side = attn_backward(
            grad_two[m].astype(bf16), attn_kept[m][2], w_qkv_here, w_out_t
        )
        attn_back.append(grad_in)
        sides.append(side)
    g_attn = jnp.concatenate(
        [tn_sum([(s[0], s[1]) for s in sides]), tn_sum([(s[3], s[2]) for s in sides])], axis=1
    )
    attn_back[-1], g_attn = lax.optimization_barrier((attn_back[-1], g_attn))
    attn_back[-1], sum_in_a = fence(attn_back[-1], sum_in_a)
    g_attn = lax.psum_scatter(g_attn, FS, scatter_dimension=0, tiled=True)
    g_part = g_attn
    g_attn = lax.psum_scatter(g_attn, "z", scatter_dimension=0, tiled=True)
    g_attn = lax.all_to_all(
        g_attn.reshape(2, rows, -1), "core", split_axis=0, concat_axis=0, tiled=True
    ).astype(f32)
    for m in each:
        normed, scale, _ = attn_kept[m]
        grad_values, part = rms_backward(attn_back[m], normed, scale, gain_attn)
        gains[2] = gains[2] + part
        grad_layer.append(grad_two[m] + grad_values)

    values, (g_in_m, g_down_m, g_sin_m, g_sdown_m), gains[1], g_router_m, before = moe_stage(
        [gather_rows(g.astype(bf16)) for g in grad_layer],
        one_kept,
        moe_m,
        gain_moe_m,
        sum_down_a,
        g_part,
    )
    sum_down_a = before[0]
    sum_in_m = over_dp(g_in_m)
    sum_down_m = over_dp(g_down_m)
    grad_one = [grad_layer[m] + values[m] for m in each]

    small = None
    mamba_sides, mamba_back, mixes, own_normed = [], [], [], []
    for m in each:
        mix_branch, gate_scale = mix_kept[m]
        x_rows, _, mamba_in, pullback, gated, gained = mamba_kept[m]
        x_rows, _ = fence(x_rows, grad_one[m])
        x_rows = x_rows[:, :D].astype(f32)
        normed_x = x_rows * row_scale(x_rows)
        own_normed.append(normed_x[:length])
        grad_mix = grad_one[m].astype(bf16)
        mean_term = jnp.sum(grad_mix.astype(f32) * mix_branch, axis=-1, keepdims=True) / DI
        extra = lanes(split_two(gate_scale) + split_two(mean_term), 128)
        rows_all = gather_rows(jnp.concatenate([grad_mix, extra], axis=1))
        mix_all = rows_all[:, :D]
        extra = rows_all[:, D:].astype(f32)
        scale_all = extra[:, 0:1] + extra[:, 1:2]
        mean_all = extra[:, 2:3] + extra[:, 3:4]
        scaled_mix = (mix_all.astype(f32) * scale_all).astype(bf16)
        mixes.append(scaled_mix)
        if m == micro - 1:
            g_mix = tn_sum([(x, k[5]) for x, k in zip(mixes, mamba_kept)])
            mix_all, g_mix = fence(mix_all, g_mix)
        grad_gated = nn(mix_all, w_mix_t, bf16).astype(f32)
        norm_gated = gated * scale_all
        grad_gate_norm = jnp.sum(grad_gated * norm_gated, axis=0)
        grad_rows = scale_all * (grad_gated * gain_here - norm_gated * mean_all)
        pulled = pullback(grad_rows.reshape(n_tp, length, chan))
        grad_proj = pulled[0].reshape(-1, in_width).astype(bf16)
        grad_step = pulled[1].reshape(-1, heads).astype(bf16)
        mamba_sides.append((mamba_in, grad_proj, grad_step))
        grads = (*pulled[2:], grad_gate_norm)
        small = grads if small is None else tuple(a + b for a, b in zip(small, grads))
        total = nt(grad_proj, w_in_here) + nt(grad_step, w_dt_here)
        gains[0] = gains[0] + jnp.sum(total * normed_x, axis=0)
        mamba_back.append(return_rows(total))

    def rows_back(packed):
        packed = lax.psum_scatter(packed, FS, scatter_dimension=0, tiled=True)
        return lax.all_to_all(
            packed.reshape(n_tp, rows, -1), TP, split_axis=0, concat_axis=0, tiled=True
        ).astype(f32)

    def owned(block):
        return block.transpose(1, 0, 2).reshape(rows, -1)

    g_s = rows_back(
        jnp.concatenate([g_mix, g_sin_m, g_sdown_m, g_sin_a, g_sdown_a], axis=1)
    )
    out_mix = owned(g_s[:, :, :chan]).T

    g_proj = tn_sum([(s[0], s[1]) for s in mamba_sides])
    g_step = tn_sum([(s[0], s[2]) for s in mamba_sides])
    g_proj, sum_in_m = fence(g_proj, sum_in_m)
    out_expert_in = sum_in_a.astype(f32)
    out_expert_down = sum_down_a.astype(f32)
    out_expert_in_m = sum_in_m.astype(f32)
    out_expert_down_m = sum_down_m.astype(f32)

    grads_in = []
    for m in each:
        scale_x = mamba_kept[m][1]
        grad_values, _ = rms_backward(mamba_back[m], own_normed[m], scale_x, gain_mamba)
        grads_in.append(grad_one[m] + grad_values)

    g_taps, g_bias, g_dt, g_log, g_skip, g_gate = small

    def spread(part, width):
        zeros = jnp.zeros(part.shape[:-1] + (width,), f32)
        return lax.dynamic_update_slice_in_dim(zeros, part[..., :chan], slot * chan, axis=-1)

    conv_grad = jnp.concatenate([g_bias[None], g_taps], axis=0)
    conv_grad = spread(conv_grad, conv_total) + jnp.pad(conv_grad[:, chan:], ((0, 0), (DI, 0)))
    conv_grad = conv_grad.reshape(CK + 1, n_all, conv_here).transpose(1, 0, 2).reshape(n_all, -1)
    vec_grad = jnp.concatenate([spread(g_gate, DI).reshape(n_all, gate_here), conv_grad], axis=1)
    vec_grad = jnp.pad(vec_grad, ((0, 0), (0, rows * vec_cols - vec_len))).reshape(D, vec_cols)
    little = jnp.concatenate(
        [g[:, None] for g in gains] + [g_router_m, g_router, vec_grad], axis=1
    ).astype(bf16)
    blank = jnp.zeros((D, step_width - heads - small_cols), bf16)
    g_m = rows_back(jnp.concatenate([g_proj, g_step, little, blank], axis=1))
    out_w_in = jnp.concatenate(
        [
            owned(g_m[:, :, :chan]),
            owned(g_m[:, :, chan : 2 * chan]),
            jnp.sum(g_m[:, :, 2 * chan : in_width], axis=0),
        ],
        axis=1,
    )
    out_w_dt = owned(g_m[:, :, in_width : in_width + heads])
    little = jnp.sum(g_m[:, :, in_width + heads : in_width + heads + small_cols], axis=0)
    vec = little[:, 4 + 2 * experts_total :].reshape(-1)
    out_gate = vec[:gate_here]
    out_conv_b = vec[gate_here : gate_here + conv_here]
    out_conv_w = vec[gate_here + conv_here : vec_len].reshape(CK, conv_here)

    head_grad = jnp.pad(jnp.stack([g_dt, g_log, g_skip]), ((0, 0), (0, 128 - heads)))[None]
    for axis in ("dp", "w"):
        own = head_grad
        for s in range(1, lax.axis_size(axis)):
            head_grad = head_grad + lax.ppermute(own, axis, ring(s, axis))
    for axis in ("z", "core"):
        n = lax.axis_size(axis)
        here = lax.axis_index(axis)
        parts = [head_grad] + [lax.ppermute(head_grad, axis, ring(s, axis)) for s in range(1, n)]
        ordered = 0.0
        for s, part in enumerate(parts):
            at_slot = jnp.arange(n)[:, None, None, None] == (here - s) % n
            ordered = ordered + jnp.where(at_slot, part[None], 0.0)
        head_grad = ordered.reshape((-1,) + ordered.shape[2:]) if axis == "z" else jnp.moveaxis(
            ordered, 0, 1
        ).reshape((-1,) + ordered.shape[2:])
    head_grad = head_grad[:, :, :heads].transpose(1, 0, 2).reshape(3, MH)

    cuts = (q_width, q_width + kv_width, q_width + 2 * kv_width)
    out_w_qkv = jnp.concatenate(
        [
            owned(g_attn[:, :, : cuts[0]]),
            owned(g_attn[:, :, cuts[0] : cuts[1]]),
            owned(g_attn[:, :, cuts[1] : cuts[2]]),
        ],
        axis=1,
    )
    out_w_out = owned(g_attn[:, :, cuts[2] :]).T

    def shared_out(block):
        g_sin = jnp.concatenate([owned(block[:, :, :ff]), owned(block[:, :, ff : 2 * ff])], axis=1)
        return g_sin, owned(block[:, :, 2 * ff :]).T

    out_sin_m, out_sdown_m = shared_out(g_s[:, :, chan : chan + 3 * ff])
    out_sin, out_sdown = shared_out(g_s[:, :, chan + 3 * ff :])

    return (
        jnp.stack(results),
        jnp.stack(grads_in),
        little[:, 0],
        out_w_in,
        out_w_dt,
        out_conv_w,
        out_conv_b,
        head_grad[0],
        head_grad[1],
        head_grad[2],
        out_gate,
        out_mix,
        little[:, 1],
        little[:, 4 : 4 + experts_total],
        out_sin_m,
        out_sdown_m,
        out_expert_in_m,
        out_expert_down_m,
        little[:, 2],
        out_w_qkv,
        out_w_out,
        little[:, 3],
        little[:, 4 + experts_total : 4 + 2 * experts_total],
        out_sin,
        out_sdown,
        out_expert_in,
        out_expert_down,
    )


def solution(mesh):
    n_dp, n_ex = mesh.shape["dp"], mesh.shape["expert"]
    outer = n_ex // 8
    fine = Mesh(mesh.devices.reshape(n_dp, outer, 4, 2), ALL)
    split = P(ALL)
    row = P(ALL, None)
    col = P(None, ALL)
    mid = P(None, ALL, None)
    part = P(EX, "dp", None)
    same = P()
    return jax.shard_map(
        body,
        mesh=fine,
        in_specs=(
            mid,
            mid,
            P(None, None, ALL, None),
            split,
            row,
            row,
            col,
            split,
            same,
            same,
            same,
            split,
            col,
            split,
            row,
            row,
            col,
            part,
            part,
            split,
            row,
            col,
            split,
            row,
            row,
            col,
            part,
            part,
            mid,
        ),
        out_specs=(
            mid,
            mid,
            split,
            row,
            row,
            col,
            split,
            same,
            same,
            same,
            split,
            col,
            split,
            row,
            row,
            col,
            part,
            part,
            split,
            row,
            col,
            split,
            row,
            row,
            col,
            part,
            part,
        ),
        check_vma=False,
    )
```

```python
import jax
import jax.numpy as jnp
from jax import lax
from jax.experimental.layout import Layout, with_layout_constraint
from jax.sharding import Mesh, PartitionSpec as P

D = 1536
QH = 12
KVH = 4
HEAD = 128
EXP_FF = 512
SH_FF = 1024
TOP = 6
MH = 48
HP = 64
STATE = 128
CK = 4
DI = 3072

bf16 = jnp.bfloat16
f32 = jnp.float32
epsilon = 1e-05
masked_value = -1e30
highest = lax.Precision.HIGHEST
ALL = ("dp", "w", "z", "core")
EX = ("w", "z", "core")
TP = ("z", "core")
FS = ("dp", "w")
SWAP = [(0, 1), (1, 0)]


def dot(a, b, dims, out=f32):
    r = lax.dot_general(a, b, (dims, ((), ())), preferred_element_type=f32)
    return r if out == f32 else r.astype(out)


def nn(a, b, out=f32):
    return dot(a, b, ((1,), (0,)), out)


def nt(a, b, out=f32):
    return dot(a, b, ((1,), (1,)), out)


def tn(a, b, out=f32):
    return dot(a, b, ((0,), (0,)), out)


def ring(shift, axis="z"):
    n = lax.axis_size(axis)
    return [(i, (i + shift) % n) for i in range(n)]


def wide(x):
    parts = [x] + [lax.ppermute(x, "w", ring(s, "w")) for s in range(1, lax.axis_size("w"))]
    return parts[0] if len(parts) == 1 else jnp.concatenate(parts, axis=0)


def narrow(total):
    n = lax.axis_size("w")
    rows = total.shape[0] // n
    out = total[:rows]
    for s in range(1, n):
        part = total[s * rows : (s + 1) * rows].astype(bf16)
        out = out + lax.ppermute(part, "w", ring(-s, "w")).astype(f32)
    return out


def add_first(total, part):
    rows = part.shape[0]
    if rows == total.shape[0]:
        return total + part
    return jnp.concatenate([total[:rows] + part, total[rows:]], axis=0)


def fence(*trees):
    if lax.axis_size("w") > 1:
        return trees
    return lax.optimization_barrier(trees)


def by_rows(x):
    if lax.axis_size("w") > 1:
        return x
    return with_layout_constraint(x, Layout(major_to_minor=tuple(range(x.ndim))))


def send(x, axis, pairs):
    return by_rows(lax.ppermute(by_rows(x), axis, pairs))


def gather_rows(x):
    n = lax.axis_size("z")
    parts = [x] + [send(x, "z", ring(s)) for s in range(1, n)]
    other = [send(p, "core", SWAP) for p in parts]
    return by_rows(jnp.concatenate(parts + other, axis=0))


def return_rows(total):
    n = lax.axis_size("z")
    half = total.shape[0] // 2
    rows = half // n
    recv = send(total[half:].astype(bf16), "core", SWAP)
    mine = total[:half] + recv.astype(f32)
    out = mine[:rows]
    for s in range(1, n):
        part = mine[s * rows : (s + 1) * rows].astype(bf16)
        out = out + send(part, "z", ring(-s)).astype(f32)
    return out


def pair_gather(x):
    return by_rows(jnp.concatenate([x, send(x, "core", SWAP)], axis=0))


def pair_return(total):
    half = total.shape[0] // 2
    recv = send(total[half:].astype(bf16), "core", SWAP)
    return total[:half] + recv.astype(f32)


def split_two(x):
    high = x.astype(bf16)
    return [high, (x - high.astype(f32)).astype(bf16)]


def row_scale(values):
    return lax.rsqrt(jnp.mean(values * values, axis=-1, keepdims=True) + epsilon)


def rms_forward(values, gain):
    scale = row_scale(values)
    normed = values * scale
    return normed, scale, (normed * gain).astype(bf16)


def rms_backward(grad_result, normed, scale, gain):
    grad_gain = jnp.sum(grad_result * normed, axis=0)
    grad_normed = grad_result * gain
    grad_values = scale * (
        grad_normed - normed * jnp.mean(grad_normed * normed, axis=-1, keepdims=True)
    )
    return grad_values, grad_gain


def lanes(parts, width):
    used = sum(p.shape[-1] for p in parts)
    rows = parts[0].shape[0]
    if used < width:
        parts = parts + [jnp.zeros((rows, width - used), bf16)]
    return jnp.concatenate(parts, axis=1)


def scan_piece(proj, dt_raw, seg, conv_w, conv_b, dt_bias, a_log, skip, heads):
    seqs, length, _ = proj.shape
    chan = heads * HP
    gate_z = proj[..., :chan]
    conv_in = proj[..., chan:]
    positions = lax.broadcasted_iota(jnp.int32, (length,), 0)
    conv_sum = jnp.zeros_like(conv_in) + conv_b
    for offset in range(CK):
        shifted = jnp.pad(conv_in, ((0, 0), (offset, 0), (0, 0)))[:, :length]
        seg_prev = jnp.pad(seg, ((0, 0), (offset, 0)))[:, :length]
        usable = (positions >= offset)[None] & (seg_prev == seg)
        conv_sum = conv_sum + jnp.where(usable[..., None], conv_w[offset] * shifted, 0.0)
    conv_act = jax.nn.silu(conv_sum)
    inputs = conv_act[..., :chan].reshape(seqs, length, heads, HP)
    b_state = conv_act[..., chan : chan + STATE]
    c_state = conv_act[..., chan + STATE :]
    step = jax.nn.softplus(dt_raw + dt_bias)
    rows_pos = lax.broadcasted_iota(jnp.int32, (length, length), 0)
    cols_pos = lax.broadcasted_iota(jnp.int32, (length, length), 1)
    lower = (cols_pos <= rows_pos).astype(f32)
    cum = jnp.einsum("ts,bsh->bht", lower, step * -jnp.exp(a_log), precision=highest)
    allowed = (seg[:, :, None] == seg[:, None, :]) & (cols_pos <= rows_pos)[None]
    allowed = allowed[:, None]
    gap = cum[..., :, None] - cum[..., None, :]
    decay = jnp.where(allowed, jnp.exp(jnp.where(allowed, gap, 0.0)), 0.0)
    cb = jnp.einsum("btn,bsn->bts", c_state, b_state, precision=highest)
    mix = decay * cb[:, None] * step.transpose(0, 2, 1)[:, :, None, :]
    scan = jnp.einsum("bhts,bshp->bthp", mix, inputs, precision=highest)
    scan = scan + skip[:, None] * inputs
    return scan.reshape(seqs, length, chan) * jax.nn.silu(gate_z)


def swiglu(gate, up):
    return gate * jax.nn.sigmoid(gate) * up


def swiglu_back(grad, gate, up):
    logistic = jax.nn.sigmoid(gate)
    grad_gate = grad * up * logistic * (1.0 + gate * (1.0 - logistic))
    return grad_gate.astype(bf16), (grad * gate * logistic).astype(bf16)


def gate_table(moe_in, mask, router):
    logits = nn(moe_in, router)
    picked = jnp.where(mask, logits, masked_value)
    peak = jnp.max(picked, axis=-1, keepdims=True)
    ex = jnp.where(mask, jnp.exp(picked - peak), 0.0)
    return ex / jnp.sum(ex, axis=-1, keepdims=True)


def moe_forward(own_in, mask, w):
    rows = own_in.shape[0]
    base_in = gather_rows(own_in)
    moe_in = wide(base_in)
    gates = gate_table(moe_in, mask, w["router"])
    count = w["expert_in"].shape[0]
    first = lax.axis_index(EX) * count
    local = lax.dynamic_slice(gates, (0, first), (gates.shape[0], count))
    pre = [nn(moe_in, w["expert_in"][e], bf16) for e in range(count)]
    pre_s = nn(base_in, w["shared_in"], bf16)
    total = None
    for e in range(count):
        p = pre[e].astype(f32)
        act = swiglu(p[:, :EXP_FF], p[:, EXP_FF:])
        hid = (act * local[:, e : e + 1]).astype(bf16)
        part = nn(hid, w["expert_down"][e])
        total = part if total is None else total + part
    half = pre_s.shape[1] // 2
    p = pre_s.astype(f32)
    hid_s = swiglu(p[:, :half], p[:, half:]).astype(bf16)
    total = add_first(total, nt(hid_s, w["shared_down_t"]))
    branch = return_rows(narrow(total))
    kept = (moe_in, base_in, gates[:rows], local, pre, pre_s)
    return branch, kept


def moe_backward(base_z, kept, w, experts_total):
    moe_in, base_in, own_gates, local, pre, pre_s = kept
    pre, pre_s, _ = fence(pre, pre_s, base_z)
    grad_z = wide(base_z)
    rows = own_gates.shape[0]
    count = len(pre)
    total = None
    first = lax.axis_index(EX) * count
    lane = lax.broadcasted_iota(jnp.int32, (1, experts_total), 1)
    table = jnp.zeros((grad_z.shape[0], experts_total), f32)
    pre_grads, hidden = [], []
    for e in range(count):
        p = pre[e].astype(f32)
        gate, up = p[:, :EXP_FF], p[:, EXP_FF:]
        grad_hid = nt(grad_z, w["expert_down"][e])
        share = local[:, e : e + 1]
        act = swiglu(gate, up)
        hidden.append((act * share).astype(bf16))
        weighted = share * jnp.sum(grad_hid * act, axis=-1, keepdims=True)
        table = table + weighted * (lane == first + e).astype(f32)
        g_gate, g_up = swiglu_back(grad_hid * share, gate, up)
        g_pre = jnp.concatenate([g_gate, g_up], axis=1)
        pre_grads.append(g_pre)
        part = nt(g_pre, w["expert_in"][e])
        total = part if total is None else total + part
    half = pre_s.shape[1] // 2
    p = pre_s.astype(f32)
    grad_hid = nn(base_z, w["shared_down_t"])
    hid_s = swiglu(p[:, :half], p[:, half:]).astype(bf16)
    g_gate, g_up = swiglu_back(grad_hid, p[:, :half], p[:, half:])
    g_pre_s = jnp.concatenate([g_gate, g_up], axis=1)
    total = add_first(total, nt(g_pre_s, w["shared_in"]))
    extra = -(-experts_total // 128) * 128
    table = jnp.pad(table, ((0, 0), (0, extra - experts_total)))
    back = return_rows(narrow(jnp.concatenate([total, table], axis=1)))
    side = (moe_in, grad_z, hidden, hid_s, pre_grads, g_pre_s, base_in, base_z)
    return back, side


def moe_finish(back, kept, w, experts_total):
    own_gates = kept[2]
    weighted = back[:, D : D + experts_total]
    grad_logits = weighted - own_gates * jnp.sum(weighted, axis=-1, keepdims=True)
    grad_logits = grad_logits.astype(bf16)
    return back[:, :D] + nt(grad_logits, w["router"]), grad_logits


def tn_sum(pairs, out=bf16):
    if lax.axis_size("w") > 1:
        return tn(*[jnp.concatenate(side, axis=0) for side in zip(*pairs)], out)
    total = None
    for a, b in pairs:
        part = tn(a, b)
        total = part if total is None else total + part
    return total.astype(out)


def moe_weight_grads(sides):
    count = len(sides[0][2])
    g_down = jnp.stack([tn_sum([(s[2][e], s[1]) for s in sides]) for e in range(count)])
    g_in = jnp.stack([tn_sum([(s[0], s[4][e]) for s in sides]) for e in range(count)])
    g_sin = tn_sum([(s[6], s[5]) for s in sides])
    g_sdown_t = tn_sum([(s[7], s[3]) for s in sides])
    return g_in, g_down, g_sin, g_sdown_t


def attn_mask(seg):
    length = seg.shape[1]
    rows_pos = lax.broadcasted_iota(jnp.int32, (length, length), 0)
    cols_pos = lax.broadcasted_iota(jnp.int32, (length, length), 1)
    return (seg[:, :, None] == seg[:, None, :]) & (cols_pos <= rows_pos)[None]


def attn_forward(own_in, allowed, w_qkv, w_out_t):
    seqs, length, _ = allowed.shape
    kv = KVH // 2
    group = QH // KVH
    q_width = kv * group * HEAD
    kv_width = kv * HEAD
    attn_in = pair_gather(own_in)
    packed = nn(attn_in, w_qkv, bf16)
    q = packed[:, :q_width].reshape(seqs, length, kv, group, HEAD)
    k = packed[:, q_width : q_width + kv_width].reshape(seqs, length, kv, HEAD)
    v = packed[:, q_width + kv_width :].reshape(seqs, length, kv, HEAD)
    scores = jnp.einsum("bqhgd,bkhd->bhgqk", q, k, preferred_element_type=f32) * HEAD**-0.5
    scores = jnp.where(allowed[:, None, None], scores, masked_value)
    peak = jnp.max(scores, axis=-1, keepdims=True)
    ex = jnp.exp(scores - peak)
    probs = ex / jnp.sum(ex, axis=-1, keepdims=True)
    context = jnp.einsum("bhgqk,bkhd->bqhgd", probs.astype(bf16), v, preferred_element_type=f32)
    context = context.reshape(seqs * length, q_width).astype(bf16)
    branch = pair_return(nt(context, w_out_t))
    return branch, (attn_in, q, k, v, probs, context)


def attn_backward(own_grad, kept, w_qkv, w_out_t):
    attn_in, q, k, v, probs, context = kept
    seqs, length, kv, group, _ = q.shape
    grad = pair_gather(own_grad)
    grad_context = nn(grad, w_out_t, bf16).reshape(seqs, length, kv, group, HEAD)
    probs_low = probs.astype(bf16)
    grad_v = jnp.einsum("bhgqk,bqhgd->bkhd", probs_low, grad_context, preferred_element_type=f32)
    grad_p = jnp.einsum("bqhgd,bkhd->bhgqk", grad_context, v, preferred_element_type=f32)
    delta = jnp.sum(probs * grad_p, axis=-1, keepdims=True)
    grad_s = (probs * (grad_p - delta)).astype(bf16)
    scale = HEAD**-0.5
    grad_q = jnp.einsum("bhgqk,bkhd->bqhgd", grad_s, k, preferred_element_type=f32) * scale
    grad_k = jnp.einsum("bhgqk,bqhgd->bkhd", grad_s, q, preferred_element_type=f32) * scale
    rows = seqs * length
    grad_packed = jnp.concatenate(
        [grad_q.reshape(rows, -1), grad_k.reshape(rows, -1), grad_v.reshape(rows, -1)], axis=1
    ).astype(bf16)
    grad_in = pair_return(nt(grad_packed, w_qkv))
    return grad_in, (attn_in, grad_packed, context, grad)


def by_owner(x, count):
    return x.reshape(x.shape[0], count, x.shape[1] // count)


def body(
    tokens,
    segments,
    routes,
    norm_mamba,
    w_in,
    w_dt,
    conv_w,
    conv_b,
    dt_bias,
    a_log,
    skip_scale,
    gate_norm,
    w_mix_out,
    norm_moe_m,
    router_m,
    shared_in_m,
    shared_down_m,
    expert_in_m,
    expert_down_m,
    norm_attn,
    w_qkv,
    w_out,
    norm_moe,
    router,
    shared_in,
    shared_down,
    expert_in,
    expert_down,
    cotangent,
):
    micro, length, _ = tokens.shape
    n_tp = lax.axis_size("z") * lax.axis_size("core")
    n_ex = lax.axis_size("w") * n_tp
    n_all = lax.axis_size("dp") * n_ex
    rows = w_in.shape[0]
    local_experts = expert_in.shape[0]
    experts_total = local_experts * n_ex
    heads = MH // n_tp
    chan = heads * HP
    ff = SH_FF // n_tp
    slot = lax.axis_index(TP)
    conv_total = DI + 2 * STATE
    conv_here = conv_w.shape[1]
    gate_here = gate_norm.shape[0]
    vec_len = gate_here + (CK + 1) * conv_here
    vec_cols = -(-vec_len // rows)
    small_cols = 4 + 2 * experts_total + vec_cols
    step_width = -(-(heads + small_cols) // 128) * 128

    vec = jnp.concatenate([gate_norm, conv_b, conv_w.reshape(-1)])
    vec = jnp.pad(vec, (0, rows * vec_cols - vec_len)).reshape(rows, vec_cols)
    gains_own = jnp.stack([norm_mamba, norm_moe_m, norm_attn, norm_moe], axis=1)
    little = jnp.concatenate([gains_own, router_m, router, vec], axis=1)

    def for_all(x):
        return jnp.broadcast_to(x[:, None], (rows, n_tp, x.shape[1]))

    def moved_columns(parts, *after):
        packed = jnp.concatenate(parts, axis=2).transpose(1, 0, 2)
        packed = fence(packed, *after)[0]
        moved = lax.all_to_all(packed, TP, split_axis=0, concat_axis=0, tiled=True)
        return moved.reshape(n_tp * rows, -1)

    def whole_rows(moved):
        return lax.all_gather(moved, FS, axis=0, tiled=True)

    def shared_pack(w_sin, w_sdown):
        return [
            by_owner(w_sin[:, :SH_FF], n_tp),
            by_owner(w_sin[:, SH_FF:], n_tp),
            by_owner(w_sdown.T, n_tp),
        ]

    blank = jnp.zeros((rows, n_tp, step_width - heads - small_cols), bf16)
    moved_m = moved_columns(
        [
            by_owner(w_in[:, :DI], n_tp),
            by_owner(w_in[:, DI : 2 * DI], n_tp),
            for_all(w_in[:, 2 * DI :]),
            by_owner(w_dt, n_tp),
            for_all(little),
            blank,
        ]
    )
    w_m = whole_rows(moved_m)
    moved_s = moved_columns(
        [by_owner(w_mix_out.T, n_tp)]
        + shared_pack(shared_in_m, shared_down_m)
        + shared_pack(shared_in, shared_down),
        moved_m,
    )
    w_s = whole_rows(moved_s)
    in_width = 2 * chan + 2 * STATE
    w_in_here = w_m[:, :in_width]
    w_step = w_m[:, in_width:]
    w_dt_here = w_step[:, :heads]
    small_all = w_step[:, heads : heads + small_cols]
    gain_mamba, gain_moe_m, gain_attn, gain_moe = [small_all[:, i].astype(f32) for i in range(4)]
    router_m_full = small_all[:, 4 : 4 + experts_total]
    router_full = small_all[:, 4 + experts_total : 4 + 2 * experts_total]
    vec_all = small_all[:, 4 + 2 * experts_total :].reshape(n_all, rows * vec_cols).astype(f32)
    gain_gate = vec_all[:, :gate_here].reshape(DI)
    bias_all = vec_all[:, gate_here : gate_here + conv_here].reshape(conv_total)
    taps_all = vec_all[:, gate_here + conv_here : vec_len].reshape(n_all, CK, conv_here)
    taps_all = taps_all.transpose(1, 0, 2).reshape(CK, conv_total)

    def channels(full_row):
        mine = lax.dynamic_slice_in_dim(full_row, slot * chan, chan, axis=-1)
        return jnp.concatenate([mine, full_row[..., DI:]], axis=-1)

    taps = channels(taps_all)
    bias = channels(bias_all)
    gain_here = lax.dynamic_slice_in_dim(gain_gate, slot * chan, chan)
    dt_here = lax.dynamic_slice_in_dim(dt_bias, slot * heads, heads)
    log_here = lax.dynamic_slice_in_dim(a_log, slot * heads, heads)
    skip_here = lax.dynamic_slice_in_dim(skip_scale, slot * heads, heads)

    w_mix_t = w_s[:, :chan]
    at = chan

    moe_m = {
        "router": router_m_full,
        "shared_in": w_s[:, at : at + 2 * ff],
        "shared_down_t": w_s[:, at + 2 * ff : at + 3 * ff],
        "expert_in": lax.all_gather(expert_in_m, "dp", axis=1, tiled=True),
        "expert_down": lax.all_gather(expert_down_m, "dp", axis=1, tiled=True),
    }

    kv = KVH // 2
    q_width = QH // 2 * HEAD
    kv_width = kv * HEAD
    q_all, kv_all = QH * HEAD, KVH * HEAD
    attn_pack = jnp.concatenate(
        [
            by_owner(w_qkv[:, :q_all], 2),
            by_owner(w_qkv[:, q_all : q_all + kv_all], 2),
            by_owner(w_qkv[:, q_all + kv_all :], 2),
            by_owner(w_out.T, 2),
        ],
        axis=2,
    ).transpose(1, 0, 2)
    attn_pack, _ = fence(attn_pack, (w_m, moved_s))
    attn_pack = lax.all_to_all(attn_pack, "core", split_axis=0, concat_axis=0, tiled=True)
    attn_w = lax.all_gather(attn_pack.reshape(2 * rows, -1), "z", axis=0, tiled=True)
    attn_w = lax.all_gather(attn_w, FS, axis=0, tiled=True)
    w_qkv_here = attn_w[:, : q_width + 2 * kv_width]
    w_out_t = attn_w[:, q_width + 2 * kv_width :]

    moe_a = {
        "router": router_full,
        "shared_in": w_s[:, at + 3 * ff : at + 5 * ff],
        "shared_down_t": w_s[:, at + 5 * ff :],
        "expert_in": lax.all_gather(expert_in, "dp", axis=1, tiled=True),
        "expert_down": lax.all_gather(expert_down, "dp", axis=1, tiled=True),
    }

    expert_ids = jnp.arange(experts_total, dtype=jnp.int32)
    info_width = -(-(2 * experts_total + 1) // 128) * 128
    each = range(micro)
    x_own = [tokens[m].astype(f32) for m in each]
    seg_all, masks, allowed, mamba_kept, mix_kept, hidden_one = [], [], [], [], [], []
    for m in each:
        seg_own = segments[m, 0]
        hot = [
            jnp.any(routes[b, m][:, :, None] == expert_ids, axis=1).astype(bf16) for b in range(2)
        ]
        info = lanes(hot + [seg_own[:, None].astype(bf16)], info_width)
        x_info, _ = fence(jnp.concatenate([tokens[m], info], axis=1), moved_m)
        rows_all = gather_rows(x_info)
        x_all = rows_all[:, :D].astype(f32)
        marks = wide(rows_all[:, D : D + 2 * experts_total]) > 0.5
        masks.append([marks[:, :experts_total], marks[:, experts_total:]])
        seg = rows_all[:, D + 2 * experts_total].astype(jnp.int32).reshape(n_tp, length)
        seg_all.append(seg)
        allowed.append(attn_mask(jnp.stack([seg[0], seg[n_tp // 2]])))

        normed_x, scale_x, mamba_in = rms_forward(x_all, gain_mamba)
        total_rows = mamba_in.shape[0]
        proj = nn(mamba_in, w_in_here, bf16)
        dt_raw = nn(mamba_in, w_dt_here)

        def piece(p, d, cw, cb, db, al, sk, seg=seg):
            return scan_piece(p, d, seg, cw, cb, db, al, sk, heads)

        gated, pullback = jax.vjp(
            piece,
            proj.astype(f32).reshape(n_tp, length, in_width),
            dt_raw.reshape(n_tp, length, heads),
            taps,
            bias,
            dt_here,
            log_here,
            skip_here,
        )
        gated = gated.reshape(total_rows, chan)
        gained = (gated * gain_here).astype(bf16)
        partial = nt(gained, w_mix_t)
        square = jnp.sum(gated * gated, axis=-1, keepdims=True)
        high = square.astype(bf16).astype(f32)
        extra = jnp.concatenate(
            [high, square - high, jnp.zeros((total_rows, 126), f32)], axis=1
        )
        back = return_rows(jnp.concatenate([partial, extra], axis=1))
        gate_scale = lax.rsqrt((back[:, D : D + 1] + back[:, D + 1 : D + 2]) / DI + epsilon)
        mix_branch = back[:, :D] * gate_scale
        hidden_one.append(x_own[m] + mix_branch)
        mamba_kept.append((rows_all, scale_x[:length], mamba_in, pullback, gated, gained))
        mix_kept.append((mix_branch, gate_scale))

    cot_all = [gather_rows(cotangent[m]) for m in each]
    hidden_one[-1], cot_all = fence(hidden_one[-1], cot_all)
    one_kept, layer_one = [], []
    for m in each:
        normed, scale, own = rms_forward(hidden_one[m], gain_moe_m)
        branch, kept = moe_forward(own, masks[m][0], moe_m)
        layer_one.append(hidden_one[m] + branch)
        one_kept.append((normed, scale, kept))
    attn_kept, hidden_two = [], []
    for m in each:
        normed, scale, own = rms_forward(layer_one[m], gain_attn)
        branch, kept = attn_forward(own, allowed[m], w_qkv_here, w_out_t)
        hidden_two.append(layer_one[m] + branch)
        attn_kept.append((normed, scale, kept))
    two_kept, results = [], []
    for m in each:
        normed, scale, own = rms_forward(hidden_two[m], gain_moe)
        branch, kept = moe_forward(own, masks[m][1], moe_a)
        results.append((hidden_two[m] + branch).astype(bf16))
        two_kept.append((normed, scale, kept))

    gains = [0.0, 0.0, 0.0, 0.0]

    def over_dp(g):
        return lax.psum_scatter(g, "dp", scatter_dimension=1, tiled=True)

    def moe_stage(grads, kept_all, w, gain, *before):
        backs, sides, own_rows = [], [], []
        for m in each:
            back, side = moe_backward(grads[m], kept_all[m][2], w, experts_total)
            backs.append(back)
            sides.append(side)
            own_rows.append(side[6][:length])
        weights = moe_weight_grads(sides)
        backs[-1], weights = lax.optimization_barrier((backs[-1], weights))
        backs[-1], before = fence(backs[-1], before)
        grad_gain = 0.0
        values, logits = [], []
        for m in each:
            normed, scale, kept = kept_all[m]
            grad_in, grad_logits = moe_finish(backs[m], kept, w, experts_total)
            logits.append(grad_logits)
            grad_values, part = rms_backward(grad_in, normed, scale, gain)
            grad_gain = grad_gain + part
            values.append(grad_values)
        g_router = tn_sum(list(zip(own_rows, logits)), f32)
        return values, weights, grad_gain, g_router, before

    values, (g_in_a, g_down_a, g_sin_a, g_sdown_a), gains[3], g_router, _ = moe_stage(
        cot_all, two_kept, moe_a, gain_moe
    )
    sum_in_a = over_dp(g_in_a)
    sum_down_a = over_dp(g_down_a)
    grad_two = [cotangent[m].astype(f32) + values[m] for m in each]

    grad_layer, sides = [], []
    attn_back = []
    for m in each:
        grad_in, side = attn_backward(
            grad_two[m].astype(bf16), attn_kept[m][2], w_qkv_here, w_out_t
        )
        attn_back.append(grad_in)
        sides.append(side)
    g_attn = jnp.concatenate(
        [tn_sum([(s[0], s[1]) for s in sides]), tn_sum([(s[3], s[2]) for s in sides])], axis=1
    )
    attn_back[-1], g_attn = lax.optimization_barrier((attn_back[-1], g_attn))
    attn_back[-1], sum_in_a = fence(attn_back[-1], sum_in_a)
    g_attn = lax.psum_scatter(g_attn, FS, scatter_dimension=0, tiled=True)
    g_part = g_attn
    g_attn = lax.psum_scatter(g_attn, "z", scatter_dimension=0, tiled=True)
    g_attn = lax.all_to_all(
        g_attn.reshape(2, rows, -1), "core", split_axis=0, concat_axis=0, tiled=True
    ).astype(f32)
    for m in each:
        normed, scale, _ = attn_kept[m]
        grad_values, part = rms_backward(attn_back[m], normed, scale, gain_attn)
        gains[2] = gains[2] + part
        grad_layer.append(grad_two[m] + grad_values)

    values, (g_in_m, g_down_m, g_sin_m, g_sdown_m), gains[1], g_router_m, before = moe_stage(
        [gather_rows(g.astype(bf16)) for g in grad_layer],
        one_kept,
        moe_m,
        gain_moe_m,
        sum_down_a,
        g_part,
    )
    sum_down_a = before[0]
    sum_in_m = over_dp(g_in_m)
    sum_down_m = over_dp(g_down_m)
    grad_one = [grad_layer[m] + values[m] for m in each]

    small = None
    mamba_sides, mamba_back, mixes, own_normed = [], [], [], []
    for m in each:
        mix_branch, gate_scale = mix_kept[m]
        x_rows, _, mamba_in, pullback, gated, gained = mamba_kept[m]
        x_rows, _ = fence(x_rows, grad_one[m])
        x_rows = x_rows[:, :D].astype(f32)
        normed_x = x_rows * row_scale(x_rows)
        own_normed.append(normed_x[:length])
        grad_mix = grad_one[m].astype(bf16)
        mean_term = jnp.sum(grad_mix.astype(f32) * mix_branch, axis=-1, keepdims=True) / DI
        extra = lanes(split_two(gate_scale) + split_two(mean_term), 128)
        rows_all = gather_rows(jnp.concatenate([grad_mix, extra], axis=1))
        mix_all = rows_all[:, :D]
        extra = rows_all[:, D:].astype(f32)
        scale_all = extra[:, 0:1] + extra[:, 1:2]
        mean_all = extra[:, 2:3] + extra[:, 3:4]
        scaled_mix = (mix_all.astype(f32) * scale_all).astype(bf16)
        mixes.append(scaled_mix)
        if m == micro - 1:
            g_mix = tn_sum([(x, k[5]) for x, k in zip(mixes, mamba_kept)])
            mix_all, g_mix = fence(mix_all, g_mix)
        grad_gated = nn(mix_all, w_mix_t, bf16).astype(f32)
        norm_gated = gated * scale_all
        grad_gate_norm = jnp.sum(grad_gated * norm_gated, axis=0)
        grad_rows = scale_all * (grad_gated * gain_here - norm_gated * mean_all)
        pulled = pullback(grad_rows.reshape(n_tp, length, chan))
        grad_proj = pulled[0].reshape(-1, in_width).astype(bf16)
        grad_step = pulled[1].reshape(-1, heads).astype(bf16)
        mamba_sides.append((mamba_in, grad_proj, grad_step))
        grads = (*pulled[2:], grad_gate_norm)
        small = grads if small is None else tuple(a + b for a, b in zip(small, grads))
        total = nt(grad_proj, w_in_here) + nt(grad_step, w_dt_here)
        gains[0] = gains[0] + jnp.sum(total * normed_x, axis=0)
        mamba_back.append(return_rows(total))

    def rows_back(packed):
        packed = lax.psum_scatter(packed, FS, scatter_dimension=0, tiled=True)
        return lax.all_to_all(
            packed.reshape(n_tp, rows, -1), TP, split_axis=0, concat_axis=0, tiled=True
        ).astype(f32)

    def owned(block):
        return block.transpose(1, 0, 2).reshape(rows, -1)

    g_s = rows_back(
        jnp.concatenate([g_mix, g_sin_m, g_sdown_m, g_sin_a, g_sdown_a], axis=1)
    )
    out_mix = owned(g_s[:, :, :chan]).T

    g_proj = tn_sum([(s[0], s[1]) for s in mamba_sides])
    g_step = tn_sum([(s[0], s[2]) for s in mamba_sides])
    g_proj, sum_in_m = fence(g_proj, sum_in_m)
    out_expert_in = sum_in_a.astype(f32)
    out_expert_down = sum_down_a.astype(f32)
    out_expert_in_m = sum_in_m.astype(f32)
    out_expert_down_m = sum_down_m.astype(f32)

    grads_in = []
    for m in each:
        scale_x = mamba_kept[m][1]
        grad_values, _ = rms_backward(mamba_back[m], own_normed[m], scale_x, gain_mamba)
        grads_in.append(grad_one[m] + grad_values)

    g_taps, g_bias, g_dt, g_log, g_skip, g_gate = small

    def spread(part, width):
        zeros = jnp.zeros(part.shape[:-1] + (width,), f32)
        return lax.dynamic_update_slice_in_dim(zeros, part[..., :chan], slot * chan, axis=-1)

    conv_grad = jnp.concatenate([g_bias[None], g_taps], axis=0)
    conv_grad = spread(conv_grad, conv_total) + jnp.pad(conv_grad[:, chan:], ((0, 0), (DI, 0)))
    conv_grad = conv_grad.reshape(CK + 1, n_all, conv_here).transpose(1, 0, 2).reshape(n_all, -1)
    vec_grad = jnp.concatenate([spread(g_gate, DI).reshape(n_all, gate_here), conv_grad], axis=1)
    vec_grad = jnp.pad(vec_grad, ((0, 0), (0, rows * vec_cols - vec_len))).reshape(D, vec_cols)
    little = jnp.concatenate(
        [g[:, None] for g in gains] + [g_router_m, g_router, vec_grad], axis=1
    ).astype(bf16)
    blank = jnp.zeros((D, step_width - heads - small_cols), bf16)
    g_m = rows_back(jnp.concatenate([g_proj, g_step, little, blank], axis=1))
    out_w_in = jnp.concatenate(
        [
            owned(g_m[:, :, :chan]),
            owned(g_m[:, :, chan : 2 * chan]),
            jnp.sum(g_m[:, :, 2 * chan : in_width], axis=0),
        ],
        axis=1,
    )
    out_w_dt = owned(g_m[:, :, in_width : in_width + heads])
    little = jnp.sum(g_m[:, :, in_width + heads : in_width + heads + small_cols], axis=0)
    vec = little[:, 4 + 2 * experts_total :].reshape(-1)
    out_gate = vec[:gate_here]
    out_conv_b = vec[gate_here : gate_here + conv_here]
    out_conv_w = vec[gate_here + conv_here : vec_len].reshape(CK, conv_here)

    head_grad = jnp.pad(jnp.stack([g_dt, g_log, g_skip]), ((0, 0), (0, 128 - heads)))[None]
    for axis in ("dp", "w"):
        own = head_grad
        for s in range(1, lax.axis_size(axis)):
            head_grad = head_grad + lax.ppermute(own, axis, ring(s, axis))
    for axis in ("z", "core"):
        n = lax.axis_size(axis)
        here = lax.axis_index(axis)
        parts = [head_grad] + [lax.ppermute(head_grad, axis, ring(s, axis)) for s in range(1, n)]
        ordered = 0.0
        for s, part in enumerate(parts):
            at_slot = jnp.arange(n)[:, None, None, None] == (here - s) % n
            ordered = ordered + jnp.where(at_slot, part[None], 0.0)
        head_grad = ordered.reshape((-1,) + ordered.shape[2:]) if axis == "z" else jnp.moveaxis(
            ordered, 0, 1
        ).reshape((-1,) + ordered.shape[2:])
    head_grad = head_grad[:, :, :heads].transpose(1, 0, 2).reshape(3, MH)

    cuts = (q_width, q_width + kv_width, q_width + 2 * kv_width)
    out_w_qkv = jnp.concatenate(
        [
            owned(g_attn[:, :, : cuts[0]]),
            owned(g_attn[:, :, cuts[0] : cuts[1]]),
            owned(g_attn[:, :, cuts[1] : cuts[2]]),
        ],
        axis=1,
    )
    out_w_out = owned(g_attn[:, :, cuts[2] :]).T

    def shared_out(block):
        g_sin = jnp.concatenate([owned(block[:, :, :ff]), owned(block[:, :, ff : 2 * ff])], axis=1)
        return g_sin, owned(block[:, :, 2 * ff :]).T

    out_sin_m, out_sdown_m = shared_out(g_s[:, :, chan : chan + 3 * ff])
    out_sin, out_sdown = shared_out(g_s[:, :, chan + 3 * ff :])

    return (
        jnp.stack(results),
        jnp.stack(grads_in),
        little[:, 0],
        out_w_in,
        out_w_dt,
        out_conv_w,
        out_conv_b,
        head_grad[0],
        head_grad[1],
        head_grad[2],
        out_gate,
        out_mix,
        little[:, 1],
        little[:, 4 : 4 + experts_total],
        out_sin_m,
        out_sdown_m,
        out_expert_in_m,
        out_expert_down_m,
        little[:, 2],
        out_w_qkv,
        out_w_out,
        little[:, 3],
        little[:, 4 + experts_total : 4 + 2 * experts_total],
        out_sin,
        out_sdown,
        out_expert_in,
        out_expert_down,
    )


def solution(mesh):
    n_dp, n_ex = mesh.shape["dp"], mesh.shape["expert"]
    outer = n_ex // 8
    fine = Mesh(mesh.devices.reshape(n_dp, outer, 4, 2), ALL)
    split = P(ALL)
    row = P(ALL, None)
    col = P(None, ALL)
    mid = P(None, ALL, None)
    part = P(EX, "dp", None)
    same = P()
    return jax.shard_map(
        body,
        mesh=fine,
        in_specs=(
            mid,
            mid,
            P(None, None, ALL, None),
            split,
            row,
            row,
            col,
            split,
            same,
            same,
            same,
            split,
            col,
            split,
            row,
            row,
            col,
            part,
            part,
            split,
            row,
            col,
            split,
            row,
            row,
            col,
            part,
            part,
            mid,
        ),
        out_specs=(
            mid,
            mid,
            split,
            row,
            row,
            col,
            split,
            same,
            same,
            same,
            split,
            col,
            split,
            row,
            row,
            col,
            part,
            part,
            split,
            row,
            col,
            split,
            row,
            row,
            col,
            part,
            part,
        ),
        check_vma=False,
    )
```

```python
import functools

import jax
import jax.numpy as jnp
from jax import lax
from jax.experimental import pallas as pl
from jax.experimental.pallas import tpu as pltpu
from jax.experimental.layout import Layout, with_layout_constraint
from jax.sharding import Mesh, PartitionSpec as P

D = 1536
QH = 12
KVH = 4
HEAD = 128
EXP_FF = 512
SH_FF = 1024
TOP = 6
MH = 48
HP = 64
STATE = 128
CK = 4
DI = 3072

bf16 = jnp.bfloat16
f32 = jnp.float32
epsilon = 1e-05
masked_value = -1e30
highest = lax.Precision.HIGHEST
ALL = ("dp", "w", "z", "core")
EX = ("w", "z", "core")
TP = ("z", "core")
FS = ("dp", "w")
SWAP = [(0, 1), (1, 0)]


def dot(a, b, dims, out=f32):
    r = lax.dot_general(a, b, (dims, ((), ())), preferred_element_type=f32)
    return r if out == f32 else r.astype(out)


def nn(a, b, out=f32):
    return dot(a, b, ((1,), (0,)), out)


def nt(a, b, out=f32):
    return dot(a, b, ((1,), (1,)), out)


def tn(a, b, out=f32):
    return dot(a, b, ((0,), (0,)), out)


def ring(shift, axis="z"):
    n = lax.axis_size(axis)
    return [(i, (i + shift) % n) for i in range(n)]


def wide(x):
    parts = [x] + [lax.ppermute(x, "w", ring(s, "w")) for s in range(1, lax.axis_size("w"))]
    return parts[0] if len(parts) == 1 else jnp.concatenate(parts, axis=0)


def narrow(total):
    n = lax.axis_size("w")
    rows = total.shape[0] // n
    out = total[:rows]
    for s in range(1, n):
        part = total[s * rows : (s + 1) * rows].astype(bf16)
        out = out + lax.ppermute(part, "w", ring(-s, "w")).astype(f32)
    return out


def add_first(total, part):
    rows = part.shape[0]
    if rows == total.shape[0]:
        return total + part
    return jnp.concatenate([total[:rows] + part, total[rows:]], axis=0)


def fence(*trees):
    if lax.axis_size("w") > 1:
        return trees
    return lax.optimization_barrier(trees)


def by_rows(x):
    if lax.axis_size("w") > 1:
        return x
    return with_layout_constraint(x, Layout(major_to_minor=tuple(range(x.ndim))))


def send(x, axis, pairs):
    return by_rows(lax.ppermute(by_rows(x), axis, pairs))


def gather_rows(x):
    n = lax.axis_size("z")
    parts = [x] + [send(x, "z", ring(s)) for s in range(1, n)]
    other = [send(p, "core", SWAP) for p in parts]
    return by_rows(jnp.concatenate(parts + other, axis=0))


def return_rows(total):
    n = lax.axis_size("z")
    half = total.shape[0] // 2
    rows = half // n
    recv = send(total[half:].astype(bf16), "core", SWAP)
    mine = total[:half] + recv.astype(f32)
    out = mine[:rows]
    for s in range(1, n):
        part = mine[s * rows : (s + 1) * rows].astype(bf16)
        out = out + send(part, "z", ring(-s)).astype(f32)
    return out


def pair_gather(x):
    return by_rows(jnp.concatenate([x, send(x, "core", SWAP)], axis=0))


def pair_return(total):
    half = total.shape[0] // 2
    recv = send(total[half:].astype(bf16), "core", SWAP)
    return total[:half] + recv.astype(f32)


def split_two(x):
    high = x.astype(bf16)
    return [high, (x - high.astype(f32)).astype(bf16)]


def row_scale(values):
    return lax.rsqrt(jnp.mean(values * values, axis=-1, keepdims=True) + epsilon)


def rms_forward(values, gain):
    scale = row_scale(values)
    normed = values * scale
    return normed, scale, (normed * gain).astype(bf16)


def rms_backward(grad_result, normed, scale, gain):
    grad_gain = jnp.sum(grad_result * normed, axis=0)
    grad_normed = grad_result * gain
    grad_values = scale * (
        grad_normed - normed * jnp.mean(grad_normed * normed, axis=-1, keepdims=True)
    )
    return grad_values, grad_gain


def lanes(parts, width):
    used = sum(p.shape[-1] for p in parts)
    rows = parts[0].shape[0]
    if used < width:
        parts = parts + [jnp.zeros((rows, width - used), bf16)]
    return jnp.concatenate(parts, axis=1)


def scan_core(proj, step_raw, seg_col, seg_row, taps, bias, heads_par):
    length = proj.shape[0]
    chan = proj.shape[1] - 2 * STATE
    chan = chan // 2
    z = proj[:, :chan].astype(f32)
    conv_in = proj[:, chan:].astype(f32)
    place = lax.broadcasted_iota(jnp.int32, (length, 1), 0)
    shifted, masks = [], []
    conv_sum = bias
    for k in range(CK):
        if k == 0:
            moved, mask = conv_in, None
            conv_sum = conv_sum + taps[0:1] * moved
        else:
            same = pltpu.roll(seg_col, k, 0) == seg_col
            mask = jnp.where(same & (place >= k), 1.0, 0.0)
            moved = pltpu.roll(conv_in, k, 0) * mask
            conv_sum = conv_sum + taps[k : k + 1] * moved
        shifted.append(moved)
        masks.append(mask)
    logistic = jax.nn.sigmoid(conv_sum)
    act = conv_sum * logistic
    pre = step_raw + heads_par[0:1]
    step = jnp.maximum(pre, 0.0) + jnp.log1p(jnp.exp(-jnp.abs(pre)))
    decay_rate = heads_par[1:2]
    rows_pos = lax.broadcasted_iota(jnp.int32, (length, length), 0)
    cols_pos = lax.broadcasted_iota(jnp.int32, (length, length), 1)
    lower = jnp.where(cols_pos <= rows_pos, 1.0, 0.0)
    cum = lax.dot_general(
        lower, step * decay_rate, (((1,), (0,)), ((), ())), precision=highest, preferred_element_type=f32
    )
    allowed = (seg_col == seg_row) & (cols_pos <= rows_pos)
    b_low = act[:, chan : chan + STATE].astype(bf16)
    c_low = act[:, chan + STATE :].astype(bf16)
    cb = nt(c_low, b_low)
    return dict(
        chan=chan, z=z, conv_in=conv_in, shifted=shifted, masks=masks, conv_sum=conv_sum,
        logistic=logistic, act=act, pre=pre, step=step, rate=decay_rate, lower=lower, cum=cum,
        cum_t=cum.T, step_t=step.T, allowed=allowed, b=b_low, c=c_low, cb=cb,
    )


def head_table(s, h):
    gap = s["cum"][:, h : h + 1] - s["cum_t"][h : h + 1, :]
    decay = jnp.exp(jnp.where(s["allowed"], gap, masked_value))
    return decay, s["step_t"][h : h + 1, :]


def pair_scan(s, heads, low):
    lane = lax.broadcasted_iota(jnp.int32, (1, 2 * HP), 1)
    blocks, mixes, tables = [], [], []
    for j in range(heads // 2):
        both = low[:, j * 2 * HP : (j + 1) * 2 * HP]
        outs = []
        for h in (2 * j, 2 * j + 1):
            decay, step_row = head_table(s, h)
            mix = (decay * s["cb"] * step_row).astype(bf16)
            outs.append(nn(mix, both))
            mixes.append(mix)
            tables.append((decay, step_row))
        blocks.append(jnp.where(lane < HP, outs[0], outs[1]))
    return jnp.concatenate(blocks, axis=1), mixes, tables


def scan_forward_kernel(heads, proj_ref, step_ref, col_ref, row_ref, conv_ref, chan_ref, head_ref, gained_ref, square_ref):
    s = scan_core(
        proj_ref[...], step_ref[...], col_ref[...], row_ref[0], conv_ref[0:CK], conv_ref[CK : CK + 1], head_ref[...]
    )
    chan = s["chan"]
    inputs = s["act"][:, :chan]
    scan, _, _ = pair_scan(s, heads, inputs.astype(bf16))
    scan = scan + chan_ref[1:2] * inputs
    gated = scan * s["z"] * jax.nn.sigmoid(s["z"])
    gained_ref[...] = (gated * chan_ref[0:1]).astype(bf16)
    square_ref[...] = jnp.broadcast_to(jnp.sum(gated * gated, axis=1, keepdims=True), square_ref.shape)


def scan_backward_kernel(
    heads, proj_ref, step_ref, col_ref, row_ref, conv_ref, chan_ref, head_ref, grad_ref, extra_ref,
    dproj_ref, dstep_ref, dconv_ref, dchan_ref, dhead_ref, flat_ref,
):
    @pl.when(pl.program_id(0) == 0)
    def _():
        dconv_ref[...] = jnp.zeros_like(dconv_ref)
        dchan_ref[...] = jnp.zeros_like(dchan_ref)
        dhead_ref[...] = jnp.zeros_like(dhead_ref)

    taps = conv_ref[0:CK]
    s = scan_core(proj_ref[...], step_ref[...], col_ref[...], row_ref[0], taps, conv_ref[CK : CK + 1], head_ref[...])
    chan, length = s["chan"], s["z"].shape[0]
    gain, skip = chan_ref[0:1], chan_ref[1:2]
    inputs = s["act"][:, :chan]
    low = inputs.astype(bf16)
    scan, mixes, tables = pair_scan(s, heads, low)
    scan = scan + skip * inputs
    z = s["z"]
    sig = jax.nn.sigmoid(z)
    silu = z * sig
    gated = scan * silu
    extra = extra_ref[...].astype(f32)
    scale = extra[:, 0:1] + extra[:, 1:2]
    mean = extra[:, 2:3] + extra[:, 3:4]
    grad = grad_ref[...].astype(f32)
    normed = gated * scale
    d_gated = scale * (grad * gain - normed * mean)
    d_scan = d_gated * silu
    d_z = d_gated * scan * sig * (1.0 + z * (1.0 - sig))
    d_low = d_scan.astype(bf16)
    lane = lax.broadcasted_iota(jnp.int32, (1, 2 * HP), 1)
    spot = lax.broadcasted_iota(jnp.int32, (1, s["step"].shape[1]), 1)
    d_cb = jnp.zeros((length, length), f32)
    d_cum = jnp.zeros(s["step"].shape, f32)
    flat_ref[...] = jnp.zeros_like(flat_ref)
    blocks = []
    for j in range(heads // 2):
        cut = slice(j * 2 * HP, (j + 1) * 2 * HP)
        both, d_both = low[:, cut], d_low[:, cut]
        outs = []
        for i, h in enumerate((2 * j, 2 * j + 1)):
            decay, step_row = tables[h]
            outs.append(tn(mixes[h], d_both))
            keep = (lane < HP) if i == 0 else (lane >= HP)
            d_mix = nt(jnp.where(keep, d_both, jnp.zeros_like(d_both)), both)
            part = d_mix * decay
            d_cb = d_cb + part * step_row
            part = part * s["cb"]
            flat_ref[h : h + 1, 0:length] = jnp.sum(part, axis=0, keepdims=True)
            column = jnp.sum(part * step_row, axis=1, keepdims=True)
            d_cum = d_cum + jnp.where(spot == h, column, 0.0)
        blocks.append(jnp.where(lane < HP, outs[0], outs[1]))
    d_inputs = jnp.concatenate(blocks, axis=1) + skip * d_scan
    from_rows = flat_ref[...].T[0:length]
    d_cum = d_cum - s["step"] * from_rows
    d_rate = lax.dot_general(
        s["lower"], d_cum, (((0,), (0,)), ((), ())), precision=highest, preferred_element_type=f32
    )
    d_step = from_rows + d_rate * s["rate"]
    d_pre = jnp.where(spot < heads, d_step * jax.nn.sigmoid(s["pre"]), 0.0)
    d_cb_low = d_cb.astype(bf16)
    d_act = jnp.concatenate([d_inputs, tn(d_cb_low, s["c"]), nn(d_cb_low, s["b"])], axis=1)
    logistic = s["logistic"]
    d_sum = d_act * logistic * (1.0 + s["conv_sum"] * (1.0 - logistic))
    d_in = taps[0:1] * d_sum
    for k in range(1, CK):
        back = d_sum * s["masks"][k] * taps[k : k + 1]
        d_in = d_in + pltpu.roll(back, length - k, 0)
    dproj_ref[...] = jnp.concatenate([d_z, d_in], axis=1).astype(bf16)
    dstep_ref[...] = d_pre.astype(bf16)
    for k in range(CK):
        dconv_ref[k : k + 1] += jnp.sum(d_sum * s["shifted"][k], axis=0, keepdims=True)
    dconv_ref[CK : CK + 1] += jnp.sum(d_sum, axis=0, keepdims=True)
    dchan_ref[0:1] += jnp.sum(grad * normed, axis=0, keepdims=True)
    dchan_ref[1:2] += jnp.sum(d_scan * inputs, axis=0, keepdims=True)
    dhead_ref[0:1] += jnp.sum(d_pre, axis=0, keepdims=True)
    dhead_ref[1:2] += jnp.sum(d_rate * s["step"] * s["rate"], axis=0, keepdims=True)


def scan_specs(length, width, lanes_, conv, chan):
    def whole(shape):
        return pl.BlockSpec(shape, lambda i: (0,) * len(shape))

    rows = lambda w: pl.BlockSpec((length, w), lambda i: (i, 0))
    return rows, whole, [
        rows(width), rows(lanes_), rows(1), pl.BlockSpec((1, 1, length), lambda i: (i, 0, 0)),
        whole((8, conv)), whole((8, chan)), whole((8, lanes_)),
    ]


def scan_forward(heads, length, proj, step, seg_col, seg_row, conv_par, chan_par, head_par):
    total, width = proj.shape
    chan = heads * HP
    rows, whole, specs = scan_specs(length, width, step.shape[1], width - chan, chan)
    return pl.pallas_call(
        functools.partial(scan_forward_kernel, heads),
        grid=(total // length,),
        in_specs=specs,
        out_specs=[rows(chan), rows(128)],
        out_shape=[jax.ShapeDtypeStruct((total, chan), bf16), jax.ShapeDtypeStruct((total, 128), f32)],
        compiler_params=pltpu.CompilerParams(vmem_limit_bytes=32 << 20),
        name="scan_forward",
    )(proj, step, seg_col, seg_row, conv_par, chan_par, head_par)


def scan_backward(heads, length, proj, step, seg_col, seg_row, conv_par, chan_par, head_par, grad, extra):
    total, width = proj.shape
    chan = heads * HP
    lanes_ = step.shape[1]
    rows, whole, specs = scan_specs(length, width, lanes_, width - chan, chan)
    return pl.pallas_call(
        functools.partial(scan_backward_kernel, heads),
        grid=(total // length,),
        in_specs=specs + [rows(chan), rows(128)],
        out_specs=[rows(width), rows(lanes_), whole((8, width - chan)), whole((8, chan)), whole((8, lanes_))],
        out_shape=[
            jax.ShapeDtypeStruct((total, width), bf16),
            jax.ShapeDtypeStruct((total, lanes_), bf16),
            jax.ShapeDtypeStruct((8, width - chan), f32),
            jax.ShapeDtypeStruct((8, chan), f32),
            jax.ShapeDtypeStruct((8, lanes_), f32),
        ],
        scratch_shapes=[pltpu.VMEM((128, 128), f32)],
        compiler_params=pltpu.CompilerParams(vmem_limit_bytes=32 << 20),
        name="scan_backward",
    )(proj, step, seg_col, seg_row, conv_par, chan_par, head_par, grad, extra)


def swiglu(gate, up):
    return gate * jax.nn.sigmoid(gate) * up


def swiglu_back(grad, gate, up):
    logistic = jax.nn.sigmoid(gate)
    grad_gate = grad * up * logistic * (1.0 + gate * (1.0 - logistic))
    return grad_gate.astype(bf16), (grad * gate * logistic).astype(bf16)


def gate_table(moe_in, mask, router):
    logits = nn(moe_in, router)
    picked = jnp.where(mask, logits, masked_value)
    peak = jnp.max(picked, axis=-1, keepdims=True)
    ex = jnp.where(mask, jnp.exp(picked - peak), 0.0)
    return ex / jnp.sum(ex, axis=-1, keepdims=True)


def moe_forward(own_in, mask, w):
    rows = own_in.shape[0]
    base_in = gather_rows(own_in)
    moe_in = wide(base_in)
    gates = gate_table(moe_in, mask, w["router"])
    count = w["expert_in"].shape[0]
    first = lax.axis_index(EX) * count
    local = lax.dynamic_slice(gates, (0, first), (gates.shape[0], count))
    pre = [nn(moe_in, w["expert_in"][e], bf16) for e in range(count)]
    pre_s = nn(base_in, w["shared_in"], bf16)
    if lax.axis_size("w") > 1:
        pre, pre_s = lax.optimization_barrier((pre, pre_s))
    total = None
    for e in range(count):
        p = pre[e].astype(f32)
        act = swiglu(p[:, :EXP_FF], p[:, EXP_FF:])
        hid = (act * local[:, e : e + 1]).astype(bf16)
        part = nn(hid, w["expert_down"][e])
        total = part if total is None else total + part
    half = pre_s.shape[1] // 2
    p = pre_s.astype(f32)
    hid_s = swiglu(p[:, :half], p[:, half:]).astype(bf16)
    total = add_first(total, nt(hid_s, w["shared_down_t"]))
    branch = return_rows(narrow(total))
    kept = (moe_in, base_in, gates[:rows], local, pre, pre_s)
    return branch, kept


def moe_backward(base_z, kept, w, experts_total):
    moe_in, base_in, own_gates, local, pre, pre_s = kept
    pre, pre_s, _ = lax.optimization_barrier((pre, pre_s, base_z))
    grad_z = wide(base_z)
    rows = own_gates.shape[0]
    count = len(pre)
    total = None
    first = lax.axis_index(EX) * count
    lane = lax.broadcasted_iota(jnp.int32, (1, experts_total), 1)
    table = jnp.zeros((grad_z.shape[0], experts_total), f32)
    pre_grads, hidden = [], []
    for e in range(count):
        p = pre[e].astype(f32)
        gate, up = p[:, :EXP_FF], p[:, EXP_FF:]
        grad_hid = nt(grad_z, w["expert_down"][e])
        share = local[:, e : e + 1]
        act = swiglu(gate, up)
        hidden.append((act * share).astype(bf16))
        weighted = share * jnp.sum(grad_hid * act, axis=-1, keepdims=True)
        table = table + weighted * (lane == first + e).astype(f32)
        g_gate, g_up = swiglu_back(grad_hid * share, gate, up)
        g_pre = jnp.concatenate([g_gate, g_up], axis=1)
        pre_grads.append(g_pre)
        part = nt(g_pre, w["expert_in"][e])
        total = part if total is None else total + part
    half = pre_s.shape[1] // 2
    p = pre_s.astype(f32)
    grad_hid = nn(base_z, w["shared_down_t"])
    hid_s = swiglu(p[:, :half], p[:, half:]).astype(bf16)
    g_gate, g_up = swiglu_back(grad_hid, p[:, :half], p[:, half:])
    g_pre_s = jnp.concatenate([g_gate, g_up], axis=1)
    total = add_first(total, nt(g_pre_s, w["shared_in"]))
    extra = -(-experts_total // 128) * 128
    table = jnp.pad(table, ((0, 0), (0, extra - experts_total)))
    back = return_rows(narrow(jnp.concatenate([total, table], axis=1)))
    side = (moe_in, grad_z, hidden, hid_s, pre_grads, g_pre_s, base_in, base_z)
    return back, side


def moe_finish(back, kept, w, experts_total):
    own_gates = kept[2]
    weighted = back[:, D : D + experts_total]
    grad_logits = weighted - own_gates * jnp.sum(weighted, axis=-1, keepdims=True)
    grad_logits = grad_logits.astype(bf16)
    return back[:, :D] + nt(grad_logits, w["router"]), grad_logits


def tn_sum(pairs, out=bf16):
    if lax.axis_size("w") > 1:
        return tn(*[jnp.concatenate(side, axis=0) for side in zip(*pairs)], out)
    total = None
    for a, b in pairs:
        part = tn(a, b)
        total = part if total is None else total + part
    return total.astype(out)


def moe_weight_grads(sides):
    count = len(sides[0][2])
    g_down = jnp.stack([tn_sum([(s[2][e], s[1]) for s in sides]) for e in range(count)])
    g_in = jnp.stack([tn_sum([(s[0], s[4][e]) for s in sides]) for e in range(count)])
    g_sin = tn_sum([(s[6], s[5]) for s in sides])
    g_sdown_t = tn_sum([(s[7], s[3]) for s in sides])
    return g_in, g_down, g_sin, g_sdown_t


def attn_mask(seg):
    length = seg.shape[1]
    rows_pos = lax.broadcasted_iota(jnp.int32, (length, length), 0)
    cols_pos = lax.broadcasted_iota(jnp.int32, (length, length), 1)
    return (seg[:, :, None] == seg[:, None, :]) & (cols_pos <= rows_pos)[None]


def attn_forward(own_in, allowed, w_qkv, w_out_t):
    seqs, length, _ = allowed.shape
    kv = KVH // 2
    group = QH // KVH
    q_width = kv * group * HEAD
    kv_width = kv * HEAD
    attn_in = pair_gather(own_in)
    packed = nn(attn_in, w_qkv, bf16)
    q = packed[:, :q_width].reshape(seqs, length, kv, group, HEAD)
    k = packed[:, q_width : q_width + kv_width].reshape(seqs, length, kv, HEAD)
    v = packed[:, q_width + kv_width :].reshape(seqs, length, kv, HEAD)
    scores = jnp.einsum("bqhgd,bkhd->bhgqk", q, k, preferred_element_type=f32) * HEAD**-0.5
    scores = jnp.where(allowed[:, None, None], scores, masked_value)
    peak = jnp.max(scores, axis=-1, keepdims=True)
    ex = jnp.exp(scores - peak)
    probs = ex / jnp.sum(ex, axis=-1, keepdims=True)
    context = jnp.einsum("bhgqk,bkhd->bqhgd", probs.astype(bf16), v, preferred_element_type=f32)
    context = context.reshape(seqs * length, q_width).astype(bf16)
    branch = pair_return(nt(context, w_out_t))
    return branch, (attn_in, q, k, v, probs, context)


def attn_backward(own_grad, kept, w_qkv, w_out_t):
    attn_in, q, k, v, probs, context = kept
    seqs, length, kv, group, _ = q.shape
    grad = pair_gather(own_grad)
    grad_context = nn(grad, w_out_t, bf16).reshape(seqs, length, kv, group, HEAD)
    probs_low = probs.astype(bf16)
    grad_v = jnp.einsum("bhgqk,bqhgd->bkhd", probs_low, grad_context, preferred_element_type=f32)
    grad_p = jnp.einsum("bqhgd,bkhd->bhgqk", grad_context, v, preferred_element_type=f32)
    delta = jnp.sum(probs * grad_p, axis=-1, keepdims=True)
    grad_s = (probs * (grad_p - delta)).astype(bf16)
    scale = HEAD**-0.5
    grad_q = jnp.einsum("bhgqk,bkhd->bqhgd", grad_s, k, preferred_element_type=f32) * scale
    grad_k = jnp.einsum("bhgqk,bqhgd->bkhd", grad_s, q, preferred_element_type=f32) * scale
    rows = seqs * length
    grad_packed = jnp.concatenate(
        [grad_q.reshape(rows, -1), grad_k.reshape(rows, -1), grad_v.reshape(rows, -1)], axis=1
    ).astype(bf16)
    grad_in = pair_return(nt(grad_packed, w_qkv))
    return grad_in, (attn_in, grad_packed, context, grad)


def by_owner(x, count):
    return x.reshape(x.shape[0], count, x.shape[1] // count)


def body(
    tokens,
    segments,
    routes,
    norm_mamba,
    w_in,
    w_dt,
    conv_w,
    conv_b,
    dt_bias,
    a_log,
    skip_scale,
    gate_norm,
    w_mix_out,
    norm_moe_m,
    router_m,
    shared_in_m,
    shared_down_m,
    expert_in_m,
    expert_down_m,
    norm_attn,
    w_qkv,
    w_out,
    norm_moe,
    router,
    shared_in,
    shared_down,
    expert_in,
    expert_down,
    cotangent,
):
    micro, length, _ = tokens.shape
    n_tp = lax.axis_size("z") * lax.axis_size("core")
    n_ex = lax.axis_size("w") * n_tp
    n_all = lax.axis_size("dp") * n_ex
    rows = w_in.shape[0]
    local_experts = expert_in.shape[0]
    experts_total = local_experts * n_ex
    heads = MH // n_tp
    chan = heads * HP
    ff = SH_FF // n_tp
    slot = lax.axis_index(TP)
    conv_total = DI + 2 * STATE
    conv_here = conv_w.shape[1]
    gate_here = gate_norm.shape[0]
    vec_len = gate_here + (CK + 1) * conv_here
    vec_cols = -(-vec_len // rows)
    small_cols = 4 + 2 * experts_total + vec_cols
    step_width = -(-(heads + small_cols) // 128) * 128

    vec = jnp.concatenate([gate_norm, conv_b, conv_w.reshape(-1)])
    vec = jnp.pad(vec, (0, rows * vec_cols - vec_len)).reshape(rows, vec_cols)
    gains_own = jnp.stack([norm_mamba, norm_moe_m, norm_attn, norm_moe], axis=1)
    little = jnp.concatenate([gains_own, router_m, router, vec], axis=1)

    def for_all(x):
        return jnp.broadcast_to(x[:, None], (rows, n_tp, x.shape[1]))

    def moved_columns(parts, *after):
        packed = jnp.concatenate(parts, axis=2).transpose(1, 0, 2)
        packed = fence(packed, *after)[0]
        moved = lax.all_to_all(packed, TP, split_axis=0, concat_axis=0, tiled=True)
        return moved.reshape(n_tp * rows, -1)

    def whole_rows(moved):
        return lax.all_gather(moved, FS, axis=0, tiled=True)

    def shared_pack(w_sin, w_sdown):
        return [
            by_owner(w_sin[:, :SH_FF], n_tp),
            by_owner(w_sin[:, SH_FF:], n_tp),
            by_owner(w_sdown.T, n_tp),
        ]

    blank = jnp.zeros((rows, n_tp, step_width - heads - small_cols), bf16)
    moved_m = moved_columns(
        [
            by_owner(w_in[:, :DI], n_tp),
            by_owner(w_in[:, DI : 2 * DI], n_tp),
            for_all(w_in[:, 2 * DI :]),
            by_owner(w_dt, n_tp),
            for_all(little),
            blank,
        ]
    )
    w_m = whole_rows(moved_m)

    expert_ids = jnp.arange(experts_total, dtype=jnp.int32)
    info_width = -(-(2 * experts_total + 1) // 128) * 128
    each = range(micro)
    rows_in = []
    for m in each:
        hot = [
            jnp.any(routes[b, m][:, :, None] == expert_ids, axis=1).astype(bf16) for b in range(2)
        ]
        info = lanes(hot + [segments[m, 0][:, None].astype(bf16)], info_width)
        x_info, _ = fence(jnp.concatenate([tokens[m], info], axis=1), moved_m)
        rows_in.append(gather_rows(x_info))
    moved_s = moved_columns(
        [by_owner(w_mix_out.T, n_tp)]
        + shared_pack(shared_in_m, shared_down_m)
        + shared_pack(shared_in, shared_down),
        rows_in[0],
    )
    w_s = whole_rows(moved_s)
    in_width = 2 * chan + 2 * STATE
    w_in_here = w_m[:, :in_width]
    w_step = w_m[:, in_width:]
    w_dt_here = w_step[:, :128]
    small_all = w_step[:, heads : heads + small_cols]
    gain_mamba, gain_moe_m, gain_attn, gain_moe = [small_all[:, i].astype(f32) for i in range(4)]
    router_m_full = small_all[:, 4 : 4 + experts_total]
    router_full = small_all[:, 4 + experts_total : 4 + 2 * experts_total]
    vec_all = small_all[:, 4 + 2 * experts_total :].reshape(n_all, rows * vec_cols).astype(f32)
    gain_gate = vec_all[:, :gate_here].reshape(DI)
    bias_all = vec_all[:, gate_here : gate_here + conv_here].reshape(conv_total)
    taps_all = vec_all[:, gate_here + conv_here : vec_len].reshape(n_all, CK, conv_here)
    taps_all = taps_all.transpose(1, 0, 2).reshape(CK, conv_total)

    def channels(full_row):
        mine = lax.dynamic_slice_in_dim(full_row, slot * chan, chan, axis=-1)
        return jnp.concatenate([mine, full_row[..., DI:]], axis=-1)

    taps = channels(taps_all)
    bias = channels(bias_all)
    gain_here = lax.dynamic_slice_in_dim(gain_gate, slot * chan, chan)
    dt_here = lax.dynamic_slice_in_dim(dt_bias, slot * heads, heads)
    log_here = lax.dynamic_slice_in_dim(a_log, slot * heads, heads)
    skip_here = lax.dynamic_slice_in_dim(skip_scale, slot * heads, heads)

    w_mix_t = w_s[:, :chan]
    expert_in_m, expert_down_m, _ = fence(expert_in_m, expert_down_m, moved_s)
    at = chan

    moe_m = {
        "router": router_m_full,
        "shared_in": w_s[:, at : at + 2 * ff],
        "shared_down_t": w_s[:, at + 2 * ff : at + 3 * ff],
        "expert_in": lax.all_gather(expert_in_m, "dp", axis=1, tiled=True),
        "expert_down": lax.all_gather(expert_down_m, "dp", axis=1, tiled=True),
    }

    kv = KVH // 2
    q_width = QH // 2 * HEAD
    kv_width = kv * HEAD
    q_all, kv_all = QH * HEAD, KVH * HEAD
    moe_a = {
        "router": router_full,
        "shared_in": w_s[:, at + 3 * ff : at + 5 * ff],
        "shared_down_t": w_s[:, at + 5 * ff :],
        "expert_in": lax.all_gather(expert_in, "dp", axis=1, tiled=True),
        "expert_down": lax.all_gather(expert_down, "dp", axis=1, tiled=True),
    }

    def eight(parts):
        block = jnp.concatenate([p.reshape(-1, p.shape[-1]) for p in parts], axis=0)
        return jnp.pad(block, ((0, 8 - block.shape[0]), (0, 0)))

    conv_par = eight([taps, bias])
    chan_par = eight([gain_here, jnp.repeat(skip_here, HP)])
    head_par = jnp.pad(eight([dt_here, -jnp.exp(log_here)]), ((0, 0), (0, 128 - heads)))
    x_own = [tokens[m].astype(f32) for m in each]
    masks, allowed, mamba_kept, mix_kept, hidden_one = [], [], [], [], []
    proj_all, cot_all = [], []
    for m in each:
        rows_all = rows_in[m]
        x_all = rows_all[:, :D].astype(f32)
        marks = wide(rows_all[:, D : D + 2 * experts_total]) > 0.5
        masks.append([marks[:, :experts_total], marks[:, experts_total:]])
        seg_col = rows_all[:, D + 2 * experts_total :][:, :1].astype(f32)
        seg_row = seg_col.reshape(n_tp, 1, length)
        seg = seg_row[:, 0].astype(jnp.int32)
        allowed.append(attn_mask(jnp.stack([seg[0], seg[n_tp // 2]])))

        _, scale_x, mamba_in = rms_forward(x_all, gain_mamba)
        total_rows = mamba_in.shape[0]
        proj = nn(mamba_in, w_in_here, bf16)
        dt_raw = nn(mamba_in, w_dt_here)
        proj_all.append(proj)
        cot, _ = fence(cotangent[m], proj)
        cot_all.append(gather_rows(cot))
        pars = (seg_col, seg_row, conv_par, chan_par, head_par)
        gained, square = scan_forward(heads, length, proj, dt_raw, *pars)
        partial = nt(gained, w_mix_t)
        high = square.astype(bf16).astype(f32)
        lane = lax.broadcasted_iota(jnp.int32, square.shape, 1)
        extra = jnp.where(lane == 0, high, jnp.where(lane == 1, square - high, 0.0))
        back = return_rows(jnp.concatenate([partial, extra], axis=1))
        gate_scale = lax.rsqrt((back[:, D : D + 1] + back[:, D + 1 : D + 2]) / DI + epsilon)
        mix_branch = back[:, :D] * gate_scale
        hidden_one.append(x_own[m] + mix_branch)
        mamba_kept.append((rows_all, scale_x[:length], mamba_in, (proj, dt_raw, *pars), gained))
        mix_kept.append((mix_branch, gate_scale))

    attn_pack = jnp.concatenate(
        [
            by_owner(w_qkv[:, :q_all], 2),
            by_owner(w_qkv[:, q_all : q_all + kv_all], 2),
            by_owner(w_qkv[:, q_all + kv_all :], 2),
            by_owner(w_out.T, 2),
        ],
        axis=2,
    ).transpose(1, 0, 2)
    attn_pack, _ = fence(attn_pack, hidden_one[0])
    attn_pack = lax.all_to_all(attn_pack, "core", split_axis=0, concat_axis=0, tiled=True)
    attn_w = lax.all_gather(attn_pack.reshape(2 * rows, -1), "z", axis=0, tiled=True)
    attn_w = lax.all_gather(attn_w, FS, axis=0, tiled=True)
    w_qkv_here = attn_w[:, : q_width + 2 * kv_width]
    w_out_t = attn_w[:, q_width + 2 * kv_width :]

    hidden_one[-1], cot_all = fence(hidden_one[-1], cot_all)
    one_kept, layer_one = [], []
    for m in each:
        normed, scale, own = rms_forward(hidden_one[m], gain_moe_m)
        branch, kept = moe_forward(own, masks[m][0], moe_m)
        layer_one.append(hidden_one[m] + branch)
        one_kept.append((normed, scale, kept))
    attn_kept, hidden_two = [], []
    for m in each:
        normed, scale, own = rms_forward(layer_one[m], gain_attn)
        branch, kept = attn_forward(own, allowed[m], w_qkv_here, w_out_t)
        hidden_two.append(layer_one[m] + branch)
        attn_kept.append((normed, scale, kept))
    two_kept, results = [], []
    for m in each:
        normed, scale, own = rms_forward(hidden_two[m], gain_moe)
        branch, kept = moe_forward(own, masks[m][1], moe_a)
        results.append((hidden_two[m] + branch).astype(bf16))
        two_kept.append((normed, scale, kept))

    gains = [0.0, 0.0, 0.0, 0.0]

    def over_dp(g):
        return lax.psum_scatter(g, "dp", scatter_dimension=1, tiled=True)

    saving = lax.axis_size("w") > 1

    def moe_stage(grads, kept_all, w, gain, *before):
        grads = list(grads)
        backs, sides, own_rows = [], [], []
        for m in each:
            back, side = moe_backward(grads[m], kept_all[m][2], w, experts_total)
            backs.append(back)
            sides.append(side)
            own_rows.append(side[6][:length])
            if saving:
                newer = moe_weight_grads(sides[-1:])
                hold = (back, newer, grads[m + 1 :])
                backs[-1], newer, grads[m + 1 :] = lax.optimization_barrier(hold)
                weights = newer if m == 0 else [a + b for a, b in zip(weights, newer)]
        if not saving:
            weights = moe_weight_grads(sides)
            backs[-1], weights = lax.optimization_barrier((backs[-1], weights))
        backs[-1], before = fence(backs[-1], before)
        grad_gain = 0.0
        values, logits = [], []
        for m in each:
            normed, scale, kept = kept_all[m]
            grad_in, grad_logits = moe_finish(backs[m], kept, w, experts_total)
            logits.append(grad_logits)
            grad_values, part = rms_backward(grad_in, normed, scale, gain)
            grad_gain = grad_gain + part
            values.append(grad_values)
        g_router = tn_sum(list(zip(own_rows, logits)), f32)
        return values, weights, grad_gain, g_router, before

    values, (g_in_a, g_down_a, g_sin_a, g_sdown_a), gains[3], g_router, _ = moe_stage(
        cot_all, two_kept, moe_a, gain_moe
    )
    sum_in_a = over_dp(g_in_a)
    sum_down_a = over_dp(g_down_a)
    grad_two = [cotangent[m].astype(f32) + values[m] for m in each]

    grad_layer, sides = [], []
    attn_back = []
    for m in each:
        grad_in, side = attn_backward(
            grad_two[m].astype(bf16), attn_kept[m][2], w_qkv_here, w_out_t
        )
        attn_back.append(grad_in)
        sides.append(side)
    g_attn = jnp.concatenate(
        [tn_sum([(s[0], s[1]) for s in sides]), tn_sum([(s[3], s[2]) for s in sides])], axis=1
    )
    attn_back[-1], g_attn = lax.optimization_barrier((attn_back[-1], g_attn))
    attn_back[-1], sum_in_a = fence(attn_back[-1], sum_in_a)
    g_attn = lax.psum_scatter(g_attn, FS, scatter_dimension=0, tiled=True)
    g_part = g_attn
    g_attn = lax.psum_scatter(g_attn, "z", scatter_dimension=0, tiled=True)
    g_attn = lax.all_to_all(
        g_attn.reshape(2, rows, -1), "core", split_axis=0, concat_axis=0, tiled=True
    ).astype(f32)
    for m in each:
        normed, scale, _ = attn_kept[m]
        grad_values, part = rms_backward(attn_back[m], normed, scale, gain_attn)
        gains[2] = gains[2] + part
        grad_layer.append(grad_two[m] + grad_values)

    values, (g_in_m, g_down_m, g_sin_m, g_sdown_m), gains[1], g_router_m, before = moe_stage(
        [gather_rows(g.astype(bf16)) for g in grad_layer],
        one_kept,
        moe_m,
        gain_moe_m,
        sum_down_a,
        g_part,
    )
    sum_down_a = before[0]
    sum_in_m = over_dp(g_in_m)
    sum_down_m = over_dp(g_down_m)
    grad_one = [grad_layer[m] + values[m] for m in each]

    small = None
    mamba_sides, mamba_back, mixes, own_normed = [], [], [], []
    for m in each:
        mix_branch, gate_scale = mix_kept[m]
        x_rows, _, mamba_in, scan_args, _ = mamba_kept[m]
        x_rows, _ = fence(x_rows, grad_one[m])
        x_rows = x_rows[:, :D].astype(f32)
        normed_x = x_rows * row_scale(x_rows)
        own_normed.append(normed_x[:length])
        grad_mix = grad_one[m].astype(bf16)
        mean_term = jnp.sum(grad_mix.astype(f32) * mix_branch, axis=-1, keepdims=True) / DI
        extra = lanes(split_two(gate_scale) + split_two(mean_term), 128)
        rows_all = gather_rows(jnp.concatenate([grad_mix, extra], axis=1))
        mix_all = rows_all[:, :D]
        extra_all = rows_all[:, D:]
        scale_all = extra_all[:, 0:1].astype(f32) + extra_all[:, 1:2].astype(f32)
        scaled_mix = (mix_all.astype(f32) * scale_all).astype(bf16)
        mixes.append(scaled_mix)
        if m == micro - 1:
            g_mix = tn_sum([(x, k[4]) for x, k in zip(mixes, mamba_kept)])
            mix_all, g_mix = fence(mix_all, g_mix)
        grad_gated = nn(mix_all, w_mix_t, bf16)
        grad_proj, grad_step, *grads = scan_backward(
            heads, length, *scan_args, grad_gated, extra_all
        )
        mamba_sides.append((mamba_in, grad_proj, grad_step))
        small = grads if small is None else [a + b for a, b in zip(small, grads)]
        total = nt(grad_proj, w_in_here) + nt(grad_step, w_dt_here)
        gains[0] = gains[0] + jnp.sum(total * normed_x, axis=0)
        mamba_back.append(return_rows(total))

    def rows_back(packed):
        packed = lax.psum_scatter(packed, FS, scatter_dimension=0, tiled=True)
        return lax.all_to_all(
            packed.reshape(n_tp, rows, -1), TP, split_axis=0, concat_axis=0, tiled=True
        ).astype(f32)

    def owned(block):
        return block.transpose(1, 0, 2).reshape(rows, -1)

    g_s = rows_back(
        jnp.concatenate([g_mix, g_sin_m, g_sdown_m, g_sin_a, g_sdown_a], axis=1)
    )
    out_mix = owned(g_s[:, :, :chan]).T

    g_proj = tn_sum([(s[0], s[1]) for s in mamba_sides])
    g_step = tn_sum([(s[0], s[2]) for s in mamba_sides])[:, :heads]
    g_proj, sum_in_m = fence(g_proj, sum_in_m)
    out_expert_in = sum_in_a.astype(f32)
    out_expert_down = sum_down_a.astype(f32)
    out_expert_in_m = sum_in_m.astype(f32)
    out_expert_down_m = sum_down_m.astype(f32)

    grads_in = []
    for m in each:
        scale_x = mamba_kept[m][1]
        grad_values, _ = rms_backward(mamba_back[m], own_normed[m], scale_x, gain_mamba)
        grads_in.append(grad_one[m] + grad_values)

    conv_sums, chan_sums, head_sums = small
    g_gate = chan_sums[0]
    g_skip = jnp.sum(chan_sums[1].reshape(heads, HP), axis=1)
    head_grad = jnp.stack([head_sums[0, :heads], head_sums[1, :heads], g_skip])

    def spread(part, width):
        zeros = jnp.zeros(part.shape[:-1] + (width,), f32)
        return lax.dynamic_update_slice_in_dim(zeros, part[..., :chan], slot * chan, axis=-1)

    conv_grad = jnp.concatenate([conv_sums[CK : CK + 1], conv_sums[:CK]], axis=0)
    conv_grad = spread(conv_grad, conv_total) + jnp.pad(conv_grad[:, chan:], ((0, 0), (DI, 0)))
    conv_grad = conv_grad.reshape(CK + 1, n_all, conv_here).transpose(1, 0, 2).reshape(n_all, -1)
    vec_grad = jnp.concatenate([spread(g_gate, DI).reshape(n_all, gate_here), conv_grad], axis=1)
    vec_grad = jnp.pad(vec_grad, ((0, 0), (0, rows * vec_cols - vec_len))).reshape(D, vec_cols)
    little = jnp.concatenate(
        [g[:, None] for g in gains] + [g_router_m, g_router, vec_grad], axis=1
    ).astype(bf16)
    blank = jnp.zeros((D, step_width - heads - small_cols), bf16)
    g_m = rows_back(jnp.concatenate([g_proj, g_step, little, blank], axis=1))
    out_w_in = jnp.concatenate(
        [
            owned(g_m[:, :, :chan]),
            owned(g_m[:, :, chan : 2 * chan]),
            jnp.sum(g_m[:, :, 2 * chan : in_width], axis=0),
        ],
        axis=1,
    )
    out_w_dt = owned(g_m[:, :, in_width : in_width + heads])
    little = jnp.sum(g_m[:, :, in_width + heads : in_width + heads + small_cols], axis=0)
    vec = little[:, 4 + 2 * experts_total :].reshape(-1)
    out_gate = vec[:gate_here]
    out_conv_b = vec[gate_here : gate_here + conv_here]
    out_conv_w = vec[gate_here + conv_here : vec_len].reshape(CK, conv_here)

    head_grad = lax.dynamic_update_slice(jnp.zeros((8, 128), f32), head_grad, (0, slot * heads))
    for axis in ALL:
        size = lax.axis_size(axis)
        step = 1
        while step < size:
            pairs = [(i, i ^ step) for i in range(size)]
            head_grad = head_grad + send(head_grad, axis, pairs)
            step *= 2
    head_grad = head_grad[:3, :MH]

    cuts = (q_width, q_width + kv_width, q_width + 2 * kv_width)
    out_w_qkv = jnp.concatenate(
        [
            owned(g_attn[:, :, : cuts[0]]),
            owned(g_attn[:, :, cuts[0] : cuts[1]]),
            owned(g_attn[:, :, cuts[1] : cuts[2]]),
        ],
        axis=1,
    )
    out_w_out = owned(g_attn[:, :, cuts[2] :]).T

    def shared_out(block):
        g_sin = jnp.concatenate([owned(block[:, :, :ff]), owned(block[:, :, ff : 2 * ff])], axis=1)
        return g_sin, owned(block[:, :, 2 * ff :]).T

    out_sin_m, out_sdown_m = shared_out(g_s[:, :, chan : chan + 3 * ff])
    out_sin, out_sdown = shared_out(g_s[:, :, chan + 3 * ff :])

    return (
        jnp.stack(results),
        jnp.stack(grads_in),
        little[:, 0],
        out_w_in,
        out_w_dt,
        out_conv_w,
        out_conv_b,
        head_grad[0],
        head_grad[1],
        head_grad[2],
        out_gate,
        out_mix,
        little[:, 1],
        little[:, 4 : 4 + experts_total],
        out_sin_m,
        out_sdown_m,
        out_expert_in_m,
        out_expert_down_m,
        little[:, 2],
        out_w_qkv,
        out_w_out,
        little[:, 3],
        little[:, 4 + experts_total : 4 + 2 * experts_total],
        out_sin,
        out_sdown,
        out_expert_in,
        out_expert_down,
    )


def solution(mesh):
    n_dp, n_ex = mesh.shape["dp"], mesh.shape["expert"]
    outer = n_ex // 8
    fine = Mesh(mesh.devices.reshape(n_dp, outer, 4, 2), ALL)
    split = P(ALL)
    row = P(ALL, None)
    col = P(None, ALL)
    mid = P(None, ALL, None)
    part = P(EX, "dp", None)
    same = P()
    return jax.shard_map(
        body,
        mesh=fine,
        in_specs=(
            mid,
            mid,
            P(None, None, ALL, None),
            split,
            row,
            row,
            col,
            split,
            same,
            same,
            same,
            split,
            col,
            split,
            row,
            row,
            col,
            part,
            part,
            split,
            row,
            col,
            split,
            row,
            row,
            col,
            part,
            part,
            mid,
        ),
        out_specs=(
            mid,
            mid,
            split,
            row,
            row,
            col,
            split,
            same,
            same,
            same,
            split,
            col,
            split,
            row,
            row,
            col,
            part,
            part,
            split,
            row,
            col,
            split,
            row,
            row,
            col,
            part,
            part,
        ),
        check_vma=False,
    )
```

```python
import functools

import jax
import jax.numpy as jnp
from jax import lax
from jax.experimental import pallas as pl
from jax.experimental.pallas import tpu as pltpu
from jax.experimental.layout import Layout, with_layout_constraint
from jax.sharding import Mesh, PartitionSpec as P

D = 1536
QH = 12
KVH = 4
HEAD = 128
EXP_FF = 512
SH_FF = 1024
TOP = 6
MH = 48
HP = 64
STATE = 128
CK = 4
DI = 3072

bf16 = jnp.bfloat16
f32 = jnp.float32
epsilon = 1e-05
masked_value = -1e30
highest = lax.Precision.HIGHEST
ALL = ("dp", "w", "z", "core")
EX = ("w", "z", "core")
TP = ("z", "core")
FS = ("dp", "w")
SWAP = [(0, 1), (1, 0)]


def dot(a, b, dims, out=f32):
    r = lax.dot_general(a, b, (dims, ((), ())), preferred_element_type=f32)
    return r if out == f32 else r.astype(out)


def nn(a, b, out=f32):
    return dot(a, b, ((1,), (0,)), out)


def nt(a, b, out=f32):
    return dot(a, b, ((1,), (1,)), out)


def tn(a, b, out=f32):
    return dot(a, b, ((0,), (0,)), out)


def ring(shift, axis="z"):
    n = lax.axis_size(axis)
    return [(i, (i + shift) % n) for i in range(n)]


def wide(x):
    parts = [x] + [lax.ppermute(x, "w", ring(s, "w")) for s in range(1, lax.axis_size("w"))]
    return parts[0] if len(parts) == 1 else jnp.concatenate(parts, axis=0)


def narrow(total):
    n = lax.axis_size("w")
    rows = total.shape[0] // n
    out = total[:rows]
    for s in range(1, n):
        part = total[s * rows : (s + 1) * rows].astype(bf16)
        out = out + lax.ppermute(part, "w", ring(-s, "w")).astype(f32)
    return out


def add_first(total, part):
    rows = part.shape[0]
    if rows == total.shape[0]:
        return total + part
    return jnp.concatenate([total[:rows] + part, total[rows:]], axis=0)


def fence(*trees):
    if lax.axis_size("w") > 1:
        return trees
    return lax.optimization_barrier(trees)


def by_rows(x):
    if lax.axis_size("w") > 1:
        return x
    return with_layout_constraint(x, Layout(major_to_minor=tuple(range(x.ndim))))


def send(x, axis, pairs):
    return by_rows(lax.ppermute(by_rows(x), axis, pairs))


def gather_rows(x):
    n = lax.axis_size("z")
    parts = [x] + [send(x, "z", ring(s)) for s in range(1, n)]
    other = [send(p, "core", SWAP) for p in parts]
    return by_rows(jnp.concatenate(parts + other, axis=0))


def return_rows(total):
    n = lax.axis_size("z")
    half = total.shape[0] // 2
    rows = half // n
    recv = send(total[half:].astype(bf16), "core", SWAP)
    mine = total[:half] + recv.astype(f32)
    out = mine[:rows]
    for s in range(1, n):
        part = mine[s * rows : (s + 1) * rows].astype(bf16)
        out = out + send(part, "z", ring(-s)).astype(f32)
    return out


def pair_gather(x):
    return by_rows(jnp.concatenate([x, send(x, "core", SWAP)], axis=0))


def pair_return(total):
    half = total.shape[0] // 2
    recv = send(total[half:].astype(bf16), "core", SWAP)
    return total[:half] + recv.astype(f32)


def split_two(x):
    high = x.astype(bf16)
    return [high, (x - high.astype(f32)).astype(bf16)]


def row_scale(values):
    return lax.rsqrt(jnp.mean(values * values, axis=-1, keepdims=True) + epsilon)


def rms_forward(values, gain):
    scale = row_scale(values)
    normed = values * scale
    return normed, scale, (normed * gain).astype(bf16)


def rms_backward(grad_result, normed, scale, gain):
    grad_gain = jnp.sum(grad_result * normed, axis=0)
    grad_normed = grad_result * gain
    grad_values = scale * (
        grad_normed - normed * jnp.mean(grad_normed * normed, axis=-1, keepdims=True)
    )
    return grad_values, grad_gain


def lanes(parts, width):
    used = sum(p.shape[-1] for p in parts)
    rows = parts[0].shape[0]
    if used < width:
        parts = parts + [jnp.zeros((rows, width - used), bf16)]
    return jnp.concatenate(parts, axis=1)


def scan_core(proj, step_raw, seg_col, seg_row, taps, bias, heads_par):
    length = proj.shape[0]
    chan = proj.shape[1] - 2 * STATE
    chan = chan // 2
    z = proj[:, :chan].astype(f32)
    conv_in = proj[:, chan:].astype(f32)
    place = lax.broadcasted_iota(jnp.int32, (length, 1), 0)
    shifted, masks = [], []
    conv_sum = bias
    for k in range(CK):
        if k == 0:
            moved, mask = conv_in, None
            conv_sum = conv_sum + taps[0:1] * moved
        else:
            same = pltpu.roll(seg_col, k, 0) == seg_col
            mask = jnp.where(same & (place >= k), 1.0, 0.0)
            moved = pltpu.roll(conv_in, k, 0) * mask
            conv_sum = conv_sum + taps[k : k + 1] * moved
        shifted.append(moved)
        masks.append(mask)
    logistic = jax.nn.sigmoid(conv_sum)
    act = conv_sum * logistic
    pre = step_raw + heads_par[0:1]
    step = jnp.maximum(pre, 0.0) + jnp.log1p(jnp.exp(-jnp.abs(pre)))
    decay_rate = heads_par[1:2]
    rows_pos = lax.broadcasted_iota(jnp.int32, (length, length), 0)
    cols_pos = lax.broadcasted_iota(jnp.int32, (length, length), 1)
    lower = jnp.where(cols_pos <= rows_pos, 1.0, 0.0)
    cum = lax.dot_general(
        lower, step * decay_rate, (((1,), (0,)), ((), ())), precision=highest, preferred_element_type=f32
    )
    allowed = (seg_col == seg_row) & (cols_pos <= rows_pos)
    b_low = act[:, chan : chan + STATE].astype(bf16)
    c_low = act[:, chan + STATE :].astype(bf16)
    cb = nt(c_low, b_low)
    return dict(
        chan=chan, z=z, conv_in=conv_in, shifted=shifted, masks=masks, conv_sum=conv_sum,
        logistic=logistic, act=act, pre=pre, step=step, rate=decay_rate, lower=lower, cum=cum,
        cum_t=cum.T, step_t=step.T, allowed=allowed, b=b_low, c=c_low, cb=cb,
    )


def head_table(s, h):
    gap = s["cum"][:, h : h + 1] - s["cum_t"][h : h + 1, :]
    decay = jnp.exp(jnp.where(s["allowed"], gap, masked_value))
    return decay, s["step_t"][h : h + 1, :]


def pair_scan(s, heads, low):
    lane = lax.broadcasted_iota(jnp.int32, (1, 2 * HP), 1)
    blocks, mixes, tables = [], [], []
    for j in range(heads // 2):
        both = low[:, j * 2 * HP : (j + 1) * 2 * HP]
        outs = []
        for h in (2 * j, 2 * j + 1):
            decay, step_row = head_table(s, h)
            mix = (decay * s["cb"] * step_row).astype(bf16)
            outs.append(nn(mix, both))
            mixes.append(mix)
            tables.append((decay, step_row))
        blocks.append(jnp.where(lane < HP, outs[0], outs[1]))
    return jnp.concatenate(blocks, axis=1), mixes, tables


def scan_forward_kernel(heads, proj_ref, step_ref, col_ref, row_ref, conv_ref, chan_ref, head_ref, gained_ref, square_ref):
    s = scan_core(
        proj_ref[...], step_ref[...], col_ref[...], row_ref[0], conv_ref[0:CK], conv_ref[CK : CK + 1], head_ref[...]
    )
    chan = s["chan"]
    inputs = s["act"][:, :chan]
    scan, _, _ = pair_scan(s, heads, inputs.astype(bf16))
    scan = scan + chan_ref[1:2] * inputs
    gated = scan * s["z"] * jax.nn.sigmoid(s["z"])
    gained_ref[...] = (gated * chan_ref[0:1]).astype(bf16)
    square_ref[...] = jnp.broadcast_to(jnp.sum(gated * gated, axis=1, keepdims=True), square_ref.shape)


def scan_backward_kernel(
    heads, proj_ref, step_ref, col_ref, row_ref, conv_ref, chan_ref, head_ref, grad_ref, extra_ref,
    dproj_ref, dconv_ref, dchan_ref, dhead_ref, flat_ref,
):
    @pl.when(pl.program_id(0) == 0)
    def _():
        dconv_ref[...] = jnp.zeros_like(dconv_ref)
        dchan_ref[...] = jnp.zeros_like(dchan_ref)
        dhead_ref[...] = jnp.zeros_like(dhead_ref)

    taps = conv_ref[0:CK]
    s = scan_core(proj_ref[...], step_ref[...], col_ref[...], row_ref[0], taps, conv_ref[CK : CK + 1], head_ref[...])
    chan, length = s["chan"], s["z"].shape[0]
    gain, skip = chan_ref[0:1], chan_ref[1:2]
    inputs = s["act"][:, :chan]
    low = inputs.astype(bf16)
    scan, mixes, tables = pair_scan(s, heads, low)
    scan = scan + skip * inputs
    z = s["z"]
    sig = jax.nn.sigmoid(z)
    silu = z * sig
    gated = scan * silu
    extra = extra_ref[...].astype(f32)
    scale = extra[:, 0:1] + extra[:, 1:2]
    mean = extra[:, 2:3] + extra[:, 3:4]
    grad = grad_ref[...].astype(f32)
    normed = gated * scale
    d_gated = scale * (grad * gain - normed * mean)
    d_scan = d_gated * silu
    d_z = d_gated * scan * sig * (1.0 + z * (1.0 - sig))
    d_low = d_scan.astype(bf16)
    lane = lax.broadcasted_iota(jnp.int32, (1, 2 * HP), 1)
    spot = lax.broadcasted_iota(jnp.int32, (1, s["step"].shape[1]), 1)
    d_cb = jnp.zeros((length, length), f32)
    d_cum = jnp.zeros(s["step"].shape, f32)
    flat_ref[...] = jnp.zeros_like(flat_ref)
    blocks = []
    for j in range(heads // 2):
        cut = slice(j * 2 * HP, (j + 1) * 2 * HP)
        both, d_both = low[:, cut], d_low[:, cut]
        outs = []
        for i, h in enumerate((2 * j, 2 * j + 1)):
            decay, step_row = tables[h]
            outs.append(tn(mixes[h], d_both))
            keep = (lane < HP) if i == 0 else (lane >= HP)
            d_mix = nt(jnp.where(keep, d_both, jnp.zeros_like(d_both)), both)
            part = d_mix * decay
            d_cb = d_cb + part * step_row
            part = part * s["cb"]
            flat_ref[h : h + 1, 0:length] = jnp.sum(part, axis=0, keepdims=True)
            column = jnp.sum(part * step_row, axis=1, keepdims=True)
            d_cum = d_cum + jnp.where(spot == h, column, 0.0)
        blocks.append(jnp.where(lane < HP, outs[0], outs[1]))
    d_inputs = jnp.concatenate(blocks, axis=1) + skip * d_scan
    from_rows = flat_ref[...].T[0:length]
    d_cum = d_cum - s["step"] * from_rows
    d_rate = lax.dot_general(
        s["lower"], d_cum, (((0,), (0,)), ((), ())), precision=highest, preferred_element_type=f32
    )
    d_step = from_rows + d_rate * s["rate"]
    d_pre = jnp.where(spot < heads, d_step * jax.nn.sigmoid(s["pre"]), 0.0)
    d_cb_low = d_cb.astype(bf16)
    d_act = jnp.concatenate([d_inputs, tn(d_cb_low, s["c"]), nn(d_cb_low, s["b"])], axis=1)
    logistic = s["logistic"]
    d_sum = d_act * logistic * (1.0 + s["conv_sum"] * (1.0 - logistic))
    d_in = taps[0:1] * d_sum
    for k in range(1, CK):
        back = d_sum * s["masks"][k] * taps[k : k + 1]
        d_in = d_in + pltpu.roll(back, length - k, 0)
    dproj_ref[...] = jnp.concatenate([d_z, d_in, d_pre], axis=1).astype(bf16)
    for k in range(CK):
        dconv_ref[k : k + 1] += jnp.sum(d_sum * s["shifted"][k], axis=0, keepdims=True)
    dconv_ref[CK : CK + 1] += jnp.sum(d_sum, axis=0, keepdims=True)
    dchan_ref[0:1] += jnp.sum(grad * normed, axis=0, keepdims=True)
    dchan_ref[1:2] += jnp.sum(d_scan * inputs, axis=0, keepdims=True)
    dhead_ref[0:1] += jnp.sum(d_pre, axis=0, keepdims=True)
    dhead_ref[1:2] += jnp.sum(d_rate * s["step"] * s["rate"], axis=0, keepdims=True)


def scan_specs(length, width, lanes_, conv, chan):
    def whole(shape):
        return pl.BlockSpec(shape, lambda i: (0,) * len(shape))

    rows = lambda w: pl.BlockSpec((length, w), lambda i: (i, 0))
    return rows, whole, [
        rows(width), rows(lanes_), rows(1), pl.BlockSpec((1, 1, length), lambda i: (i, 0, 0)),
        whole((8, conv)), whole((8, chan)), whole((8, lanes_)),
    ]


def scan_forward(heads, length, proj, step, seg_col, seg_row, conv_par, chan_par, head_par):
    total, width = proj.shape
    chan = heads * HP
    rows, whole, specs = scan_specs(length, width, step.shape[1], width - chan, chan)
    return pl.pallas_call(
        functools.partial(scan_forward_kernel, heads),
        grid=(total // length,),
        in_specs=specs,
        out_specs=[rows(chan), rows(128)],
        out_shape=[jax.ShapeDtypeStruct((total, chan), bf16), jax.ShapeDtypeStruct((total, 128), f32)],
        compiler_params=pltpu.CompilerParams(vmem_limit_bytes=32 << 20),
        name="scan_forward",
    )(proj, step, seg_col, seg_row, conv_par, chan_par, head_par)


def scan_backward(heads, length, proj, step, seg_col, seg_row, conv_par, chan_par, head_par, grad, extra):
    total, width = proj.shape
    chan = heads * HP
    lanes_ = step.shape[1]
    rows, whole, specs = scan_specs(length, width, lanes_, width - chan, chan)
    return pl.pallas_call(
        functools.partial(scan_backward_kernel, heads),
        grid=(total // length,),
        in_specs=specs + [rows(chan), rows(128)],
        out_specs=[rows(width + lanes_), whole((8, width - chan)), whole((8, chan)), whole((8, lanes_))],
        out_shape=[
            jax.ShapeDtypeStruct((total, width + lanes_), bf16),
            jax.ShapeDtypeStruct((8, width - chan), f32),
            jax.ShapeDtypeStruct((8, chan), f32),
            jax.ShapeDtypeStruct((8, lanes_), f32),
        ],
        scratch_shapes=[pltpu.VMEM((128, 128), f32)],
        compiler_params=pltpu.CompilerParams(vmem_limit_bytes=32 << 20),
        name="scan_backward",
    )(proj, step, seg_col, seg_row, conv_par, chan_par, head_par, grad, extra)


def swiglu(gate, up):
    return gate * jax.nn.sigmoid(gate) * up


def swiglu_back(grad, gate, up):
    logistic = jax.nn.sigmoid(gate)
    grad_gate = grad * up * logistic * (1.0 + gate * (1.0 - logistic))
    return grad_gate.astype(bf16), (grad * gate * logistic).astype(bf16)


def gate_table(moe_in, mask, router):
    logits = nn(moe_in, router)
    picked = jnp.where(mask, logits, masked_value)
    peak = jnp.max(picked, axis=-1, keepdims=True)
    ex = jnp.where(mask, jnp.exp(picked - peak), 0.0)
    return ex / jnp.sum(ex, axis=-1, keepdims=True)


def unit_gates(local, units):
    count = local.shape[1]
    inner = EXP_FF // lax.axis_size("dp")
    owner = lax.broadcasted_iota(jnp.int32, (1, units), 1) // inner % count
    spread = local[:, count - 1 :]
    for e in range(count - 1):
        spread = jnp.where(owner == e, local[:, e : e + 1], spread)
    return spread, owner


def moe_forward(own_in, mask, w):
    rows = own_in.shape[0]
    base_in = gather_rows(own_in)
    moe_in = wide(base_in)
    gates = gate_table(moe_in, mask, w["router"])
    units = w["expert_down"].shape[0]
    count = units // EXP_FF
    first = lax.axis_index(EX) * count
    local = lax.dynamic_slice(gates, (0, first), (gates.shape[0], count))
    pre = nn(moe_in, w["expert_in"], bf16)
    pre_s = nn(base_in, w["shared_in"], bf16)
    pre, pre_s = lax.optimization_barrier((pre, pre_s))
    p = pre.astype(f32)
    spread, _ = unit_gates(local, units)
    hid = (swiglu(p[:, :units], p[:, units:]) * spread).astype(bf16)
    half = pre_s.shape[1] // 2
    p = pre_s.astype(f32)
    hid_s = swiglu(p[:, :half], p[:, half:]).astype(bf16)
    total = add_first(nn(hid, w["expert_down"]), nt(hid_s, w["shared_down_t"]))
    return total, (moe_in, base_in, gates[:rows], local, pre, pre_s)


def moe_backward(base_z, kept, w, experts_total):
    moe_in, base_in, own_gates, local, pre, pre_s = kept
    pre, pre_s, _ = lax.optimization_barrier((pre, pre_s, base_z))
    grad_z = wide(base_z)
    units = w["expert_down"].shape[0]
    count = units // EXP_FF
    first = lax.axis_index(EX) * count
    spread, owner = unit_gates(local, units)
    p = pre.astype(f32)
    gate, up = p[:, :units], p[:, units:]
    grad_hid = nt(grad_z, w["expert_down"])
    act = swiglu(gate, up)
    hidden = (act * spread).astype(bf16)
    product = grad_hid * act
    lane = lax.broadcasted_iota(jnp.int32, (1, experts_total), 1)
    table = jnp.zeros((grad_z.shape[0], experts_total), f32)
    for e in range(count):
        mine = jnp.sum(jnp.where(owner == e, product, 0.0), axis=-1, keepdims=True)
        table = table + local[:, e : e + 1] * mine * (lane == first + e).astype(f32)
    g_gate, g_up = swiglu_back(grad_hid * spread, gate, up)
    g_pre = jnp.concatenate([g_gate, g_up], axis=1)
    total = nt(g_pre, w["expert_in"])
    half = pre_s.shape[1] // 2
    p = pre_s.astype(f32)
    grad_hid = nn(base_z, w["shared_down_t"])
    hid_s = swiglu(p[:, :half], p[:, half:]).astype(bf16)
    g_gate, g_up = swiglu_back(grad_hid, p[:, :half], p[:, half:])
    g_pre_s = jnp.concatenate([g_gate, g_up], axis=1)
    total = add_first(total, nt(g_pre_s, w["shared_in"]))
    extra = -(-experts_total // 128) * 128
    table = jnp.pad(table, ((0, 0), (0, extra - experts_total)))
    back = return_rows(narrow(jnp.concatenate([total, table], axis=1)))
    side = (moe_in, grad_z, hidden, hid_s, g_pre, g_pre_s, base_in, base_z)
    return back, side


def moe_finish(back, kept, w, experts_total):
    own_gates = kept[2]
    weighted = back[:, D : D + experts_total]
    grad_logits = weighted - own_gates * jnp.sum(weighted, axis=-1, keepdims=True)
    grad_logits = grad_logits.astype(bf16)
    return back[:, :D] + nt(grad_logits, w["router"]), grad_logits


def tn_sum(pairs, out=bf16):
    if lax.axis_size("w") > 1:
        return tn(*[jnp.concatenate(side, axis=0) for side in zip(*pairs)], out)
    total = None
    for a, b in pairs:
        part = tn(a, b)
        total = part if total is None else total + part
    return total.astype(out)


def moe_weight_grads(sides):
    g_down = tn_sum([(s[2], s[1]) for s in sides])
    g_in = tn_sum([(s[0], s[4]) for s in sides])
    g_sin = tn_sum([(s[6], s[5]) for s in sides])
    g_sdown_t = tn_sum([(s[7], s[3]) for s in sides])
    return g_in, g_down, g_sin, g_sdown_t


def attn_mask(seg):
    length = seg.shape[1]
    rows_pos = lax.broadcasted_iota(jnp.int32, (length, length), 0)
    cols_pos = lax.broadcasted_iota(jnp.int32, (length, length), 1)
    return (seg[:, :, None] == seg[:, None, :]) & (cols_pos <= rows_pos)[None]


def attn_forward(own_in, allowed, w_qkv, w_out_t):
    seqs, length, _ = allowed.shape
    kv = KVH // 2
    group = QH // KVH
    q_width = kv * group * HEAD
    kv_width = kv * HEAD
    attn_in = pair_gather(own_in)
    packed = nn(attn_in, w_qkv, bf16)
    q = packed[:, :q_width].reshape(seqs, length, kv, group, HEAD)
    k = packed[:, q_width : q_width + kv_width].reshape(seqs, length, kv, HEAD)
    v = packed[:, q_width + kv_width :].reshape(seqs, length, kv, HEAD)
    scores = jnp.einsum("bqhgd,bkhd->bhgqk", q, k, preferred_element_type=f32) * HEAD**-0.5
    scores = jnp.where(allowed[:, None, None], scores, masked_value)
    peak = jnp.max(scores, axis=-1, keepdims=True)
    ex = jnp.exp(scores - peak)
    probs = ex / jnp.sum(ex, axis=-1, keepdims=True)
    context = jnp.einsum("bhgqk,bkhd->bqhgd", probs.astype(bf16), v, preferred_element_type=f32)
    context = context.reshape(seqs * length, q_width).astype(bf16)
    branch = pair_return(nt(context, w_out_t))
    return branch, (attn_in, q, k, v, probs, context)


def attn_backward(own_grad, kept, w_qkv, w_out_t):
    attn_in, q, k, v, probs, context = kept
    seqs, length, kv, group, _ = q.shape
    grad = pair_gather(own_grad)
    grad_context = nn(grad, w_out_t, bf16).reshape(seqs, length, kv, group, HEAD)
    probs_low = probs.astype(bf16)
    grad_v = jnp.einsum("bhgqk,bqhgd->bkhd", probs_low, grad_context, preferred_element_type=f32)
    grad_p = jnp.einsum("bqhgd,bkhd->bhgqk", grad_context, v, preferred_element_type=f32)
    delta = jnp.sum(probs * grad_p, axis=-1, keepdims=True)
    grad_s = (probs * (grad_p - delta)).astype(bf16)
    scale = HEAD**-0.5
    grad_q = jnp.einsum("bhgqk,bkhd->bqhgd", grad_s, k, preferred_element_type=f32) * scale
    grad_k = jnp.einsum("bhgqk,bqhgd->bkhd", grad_s, q, preferred_element_type=f32) * scale
    rows = seqs * length
    grad_packed = jnp.concatenate(
        [grad_q.reshape(rows, -1), grad_k.reshape(rows, -1), grad_v.reshape(rows, -1)], axis=1
    ).astype(bf16)
    grad_in = pair_return(nt(grad_packed, w_qkv))
    return grad_in, (attn_in, grad_packed, context, grad)


def by_owner(x, count):
    return x.reshape(x.shape[0], count, x.shape[1] // count)


def body(
    tokens,
    segments,
    routes,
    norm_mamba,
    w_in,
    w_dt,
    conv_w,
    conv_b,
    dt_bias,
    a_log,
    skip_scale,
    gate_norm,
    w_mix_out,
    norm_moe_m,
    router_m,
    shared_in_m,
    shared_down_m,
    expert_in_m,
    expert_down_m,
    norm_attn,
    w_qkv,
    w_out,
    norm_moe,
    router,
    shared_in,
    shared_down,
    expert_in,
    expert_down,
    cotangent,
):
    micro, length, _ = tokens.shape
    n_tp = lax.axis_size("z") * lax.axis_size("core")
    n_ex = lax.axis_size("w") * n_tp
    n_all = lax.axis_size("dp") * n_ex
    rows = w_in.shape[0]
    local_experts = expert_in.shape[0]
    experts_total = local_experts * n_ex
    heads = MH // n_tp
    chan = heads * HP
    ff = SH_FF // n_tp
    slot = lax.axis_index(TP)
    conv_total = DI + 2 * STATE
    conv_here = conv_w.shape[1]
    gate_here = gate_norm.shape[0]
    vec_len = gate_here + (CK + 1) * conv_here
    vec_cols = -(-vec_len // rows)
    small_cols = 4 + 2 * experts_total + vec_cols
    step_width = -(-(heads + small_cols) // 128) * 128

    vec = jnp.concatenate([gate_norm, conv_b, conv_w.reshape(-1)])
    vec = jnp.pad(vec, (0, rows * vec_cols - vec_len)).reshape(rows, vec_cols)
    gains_own = jnp.stack([norm_mamba, norm_moe_m, norm_attn, norm_moe], axis=1)
    little = jnp.concatenate([gains_own, router_m, router, vec], axis=1)

    def for_all(x):
        return jnp.broadcast_to(x[:, None], (rows, n_tp, x.shape[1]))

    def moved_columns(parts, *after):
        packed = jnp.concatenate(parts, axis=2).transpose(1, 0, 2)
        packed = fence(packed, *after)[0]
        moved = lax.all_to_all(packed, TP, split_axis=0, concat_axis=0, tiled=True)
        return moved.reshape(n_tp * rows, -1)

    def whole_rows(moved):
        return lax.all_gather(moved, FS, axis=0, tiled=True)

    def shared_pack(w_sin, w_sdown):
        return [
            by_owner(w_sin[:, :SH_FF], n_tp),
            by_owner(w_sin[:, SH_FF:], n_tp),
            by_owner(w_sdown.T, n_tp),
        ]

    blank = jnp.zeros((rows, n_tp, step_width - heads - small_cols), bf16)
    moved_m = moved_columns(
        [
            by_owner(w_in[:, :DI], n_tp),
            by_owner(w_in[:, DI : 2 * DI], n_tp),
            for_all(w_in[:, 2 * DI :]),
            by_owner(w_dt, n_tp),
            for_all(little),
            blank,
            by_owner(w_mix_out.T, n_tp),
        ]
        + shared_pack(shared_in_m, shared_down_m)
        + shared_pack(shared_in, shared_down)
    )
    w_m = whole_rows(moved_m)

    expert_ids = jnp.arange(experts_total, dtype=jnp.int32)
    info_width = -(-(2 * experts_total + 1) // 128) * 128
    each = range(micro)
    rows_in = []
    for m in each:
        hot = [
            jnp.any(routes[b, m][:, :, None] == expert_ids, axis=1).astype(bf16) for b in range(2)
        ]
        info = lanes(hot + [segments[m, 0][:, None].astype(bf16)], info_width)
        x_info, _ = fence(jnp.concatenate([tokens[m], info], axis=1), moved_m)
        rows_in.append(gather_rows(x_info))
    in_width = 2 * chan + 2 * STATE
    w_in_here = w_m[:, :in_width]
    at = in_width + step_width
    w_step = w_m[:, in_width:at]
    w_dt_here = w_step[:, :128]
    small_all = w_step[:, heads : heads + small_cols]
    gain_mamba, gain_moe_m, gain_attn, gain_moe = [small_all[:, i].astype(f32) for i in range(4)]
    router_m_full = small_all[:, 4 : 4 + experts_total]
    router_full = small_all[:, 4 + experts_total : 4 + 2 * experts_total]
    vec_all = small_all[:, 4 + 2 * experts_total :].reshape(n_all, rows * vec_cols).astype(f32)
    gain_gate = vec_all[:, :gate_here].reshape(DI)
    bias_all = vec_all[:, gate_here : gate_here + conv_here].reshape(conv_total)
    taps_all = vec_all[:, gate_here + conv_here : vec_len].reshape(n_all, CK, conv_here)
    taps_all = taps_all.transpose(1, 0, 2).reshape(CK, conv_total)

    def channels(full_row):
        mine = lax.dynamic_slice_in_dim(full_row, slot * chan, chan, axis=-1)
        return jnp.concatenate([mine, full_row[..., DI:]], axis=-1)

    taps = channels(taps_all)
    bias = channels(bias_all)
    gain_here = lax.dynamic_slice_in_dim(gain_gate, slot * chan, chan)
    dt_here = lax.dynamic_slice_in_dim(dt_bias, slot * heads, heads)
    log_here = lax.dynamic_slice_in_dim(a_log, slot * heads, heads)
    skip_here = lax.dynamic_slice_in_dim(skip_scale, slot * heads, heads)

    w_scan = w_m[:, : in_width + 128]
    w_mix_t = w_m[:, at : at + chan]
    at += chan

    n_dp = lax.axis_size("dp")

    def expert_weights(w_up, w_low):
        count, depth, width = w_up.shape
        cols = w_up.reshape(count, depth, 2, n_dp, EXP_FF // n_dp).transpose(1, 2, 3, 0, 4)
        return (
            by_rows(lax.all_gather(by_rows(cols.reshape(depth, -1)), "dp", axis=0, tiled=True)),
            lax.all_gather(w_low.reshape(-1, D), "dp", axis=0, tiled=True),
        )

    expert_in_m, expert_down_m, _ = fence(expert_in_m, expert_down_m, moved_m)
    up_m, low_m = expert_weights(expert_in_m, expert_down_m)
    moe_m = {
        "router": router_m_full,
        "shared_in": w_m[:, at : at + 2 * ff],
        "shared_down_t": w_m[:, at + 2 * ff : at + 3 * ff],
        "expert_in": up_m,
        "expert_down": low_m,
    }

    kv = KVH // 2
    q_width = QH // 2 * HEAD
    kv_width = kv * HEAD
    q_all, kv_all = QH * HEAD, KVH * HEAD
    up_a, low_a = expert_weights(expert_in, expert_down)
    moe_a = {
        "router": router_full,
        "shared_in": w_m[:, at + 3 * ff : at + 5 * ff],
        "shared_down_t": w_m[:, at + 5 * ff :],
        "expert_in": up_a,
        "expert_down": low_a,
    }

    def eight(parts):
        block = jnp.concatenate([p.reshape(-1, p.shape[-1]) for p in parts], axis=0)
        return jnp.pad(block, ((0, 8 - block.shape[0]), (0, 0)))

    conv_par = eight([taps, bias])
    chan_par = eight([gain_here, jnp.repeat(skip_here, HP)])
    head_par = jnp.pad(eight([dt_here, -jnp.exp(log_here)]), ((0, 0), (0, 128 - heads)))
    x_own = [tokens[m].astype(f32) for m in each]
    masks, allowed, mamba_kept, mix_kept, hidden_one = [], [], [], [], []
    proj_all, cot_all = [], []
    for m in each:
        rows_all = rows_in[m]
        x_all = rows_all[:, :D].astype(f32)
        marks = wide(rows_all[:, D : D + 2 * experts_total]) > 0.5
        masks.append([marks[:, :experts_total], marks[:, experts_total:]])
        seg_col = rows_all[:, D + 2 * experts_total :][:, :1].astype(f32)
        seg_row = seg_col.reshape(n_tp, 1, length)
        seg = seg_row[:, 0].astype(jnp.int32)
        allowed.append(attn_mask(jnp.stack([seg[0], seg[n_tp // 2]])))

        x_all, _ = fence(x_all, w_m)
        _, scale_x, mamba_in = rms_forward(x_all, gain_mamba)
        total_rows = mamba_in.shape[0]
        proj = nn(mamba_in, w_in_here, bf16)
        dt_raw = nn(mamba_in, w_dt_here)
        proj_all.append(proj)
        cot, _ = fence(cotangent[m], proj)
        cot_all.append(gather_rows(cot))
        pars = (seg_col, seg_row, conv_par, chan_par, head_par)
        gained, square = scan_forward(heads, length, proj, dt_raw, *pars)
        partial = nt(gained, w_mix_t)
        high = square.astype(bf16).astype(f32)
        lane = lax.broadcasted_iota(jnp.int32, square.shape, 1)
        extra = jnp.where(lane == 0, high, jnp.where(lane == 1, square - high, 0.0))
        back = return_rows(jnp.concatenate([partial, extra], axis=1))
        gate_scale = lax.rsqrt((back[:, D : D + 1] + back[:, D + 1 : D + 2]) / DI + epsilon)
        mix_branch = back[:, :D] * gate_scale
        hidden_one.append(x_own[m] + mix_branch)
        mamba_kept.append((rows_all, scale_x[:length], mamba_in, (proj, dt_raw, *pars), gained))
        mix_kept.append((mix_branch, gate_scale))

    attn_pack = jnp.concatenate(
        [
            by_owner(w_qkv[:, :q_all], 2),
            by_owner(w_qkv[:, q_all : q_all + kv_all], 2),
            by_owner(w_qkv[:, q_all + kv_all :], 2),
            by_owner(w_out.T, 2),
        ],
        axis=2,
    ).transpose(1, 0, 2)
    attn_pack, _ = fence(attn_pack, rows_in)
    attn_pack = lax.all_to_all(attn_pack, "core", split_axis=0, concat_axis=0, tiled=True)
    own = attn_pack.reshape(2 * rows, -1)
    n_z = lax.axis_size("z")
    parts = [send(own, "z", ring(s)) for s in range(n_z - 1, 0, -1)] + [own]
    twice = jnp.concatenate(parts + parts, axis=0)
    start = (n_z - 1 - lax.axis_index("z")) * 2 * rows
    attn_w = lax.dynamic_slice(twice, (start, 0), (n_z * 2 * rows, own.shape[1]))
    attn_w = lax.all_gather(attn_w, FS, axis=0, tiled=True)
    w_qkv_here = attn_w[:, : q_width + 2 * kv_width]
    w_out_t = attn_w[:, q_width + 2 * kv_width :]

    hidden_one[-1], cot_all = fence(hidden_one[-1], cot_all)
    one_kept, layer_one = [], []
    for m in each:
        normed, scale, own = rms_forward(hidden_one[m], gain_moe_m)
        total, kept = moe_forward(own, masks[m][0], moe_m)
        layer_one.append(hidden_one[m] + return_rows(narrow(total)))
        one_kept.append((normed, scale, kept))
    attn_kept, hidden_two = [], []
    for m in each:
        normed, scale, own = rms_forward(layer_one[m], gain_attn)
        branch, kept = attn_forward(own, allowed[m], w_qkv_here, w_out_t)
        hidden_two.append(layer_one[m] + branch)
        attn_kept.append((normed, scale, kept))
    two_kept, results = [], []
    for m in each:
        normed, scale, own = rms_forward(hidden_two[m], gain_moe)
        total, kept = moe_forward(own, masks[m][1], moe_a)
        results.append(total)
        two_kept.append((normed, scale, kept))

    gains = [0.0, 0.0, 0.0, 0.0]

    def over_dp(g):
        return lax.psum_scatter(g, "dp", scatter_dimension=0, tiled=True)

    def expert_out(g_up, g_low):
        depth = g_up.shape[0]
        cols = g_up.reshape(depth, 2, n_dp, local_experts, EXP_FF // n_dp)
        cols = cols.transpose(3, 0, 1, 2, 4).reshape(local_experts, depth, 2 * EXP_FF)
        return cols.astype(f32), g_low.reshape(local_experts, -1, D).astype(f32)

    saving = lax.axis_size("w") > 1

    def moe_stage(grads, kept_all, w, gain, *before):
        grads = list(grads)
        backs, sides, own_rows = [], [], []
        for m in each:
            back, side = moe_backward(grads[m], kept_all[m][2], w, experts_total)
            backs.append(back)
            sides.append(side)
            own_rows.append(side[6][:length])
            if saving:
                newer = moe_weight_grads(sides[-1:])
                hold = (back, newer, grads[m + 1 :])
                backs[-1], newer, grads[m + 1 :] = lax.optimization_barrier(hold)
                weights = newer if m == 0 else [a + b for a, b in zip(weights, newer)]
        if not saving:
            weights = moe_weight_grads(sides)
            backs[-1], weights = lax.optimization_barrier((backs[-1], weights))
        backs[-1], before = fence(backs[-1], before)
        grad_gain = 0.0
        values, logits = [], []
        for m in each:
            normed, scale, kept = kept_all[m]
            grad_in, grad_logits = moe_finish(backs[m], kept, w, experts_total)
            logits.append(grad_logits)
            grad_values, part = rms_backward(grad_in, normed, scale, gain)
            grad_gain = grad_gain + part
            values.append(grad_values)
        g_router = tn_sum(list(zip(own_rows, logits)), f32)
        return values, weights, grad_gain, g_router, before

    values, (g_in_a, g_down_a, g_sin_a, g_sdown_a), gains[3], g_router, _ = moe_stage(
        cot_all, two_kept, moe_a, gain_moe
    )
    sum_in_a = over_dp(g_in_a)
    sum_down_a = over_dp(g_down_a)
    grad_two = [cotangent[m].astype(f32) + values[m] for m in each]
    for m in each:
        total, _ = fence(results[m], grad_two[m])
        results[m] = (hidden_two[m] + return_rows(narrow(total))).astype(bf16)

    grad_layer, sides = [], []
    attn_back = []
    for m in each:
        grad_in, side = attn_backward(
            grad_two[m].astype(bf16), attn_kept[m][2], w_qkv_here, w_out_t
        )
        attn_back.append(grad_in)
        sides.append(side)
    g_attn = jnp.concatenate(
        [tn_sum([(s[0], s[1]) for s in sides]), tn_sum([(s[3], s[2]) for s in sides])], axis=1
    )
    attn_back[-1], g_attn = lax.optimization_barrier((attn_back[-1], g_attn))
    attn_back[-1], sum_in_a = fence(attn_back[-1], sum_in_a)
    g_attn = lax.psum_scatter(g_attn, FS, scatter_dimension=0, tiled=True)
    g_part = g_attn
    g_attn = lax.psum_scatter(g_attn, "z", scatter_dimension=0, tiled=True)
    g_attn = lax.all_to_all(
        g_attn.reshape(2, rows, -1), "core", split_axis=0, concat_axis=0, tiled=True
    ).astype(f32)
    for m in each:
        normed, scale, _ = attn_kept[m]
        grad_values, part = rms_backward(attn_back[m], normed, scale, gain_attn)
        gains[2] = gains[2] + part
        grad_layer.append(grad_two[m] + grad_values)

    values, (g_in_m, g_down_m, g_sin_m, g_sdown_m), gains[1], g_router_m, before = moe_stage(
        [gather_rows(g.astype(bf16)) for g in grad_layer],
        one_kept,
        moe_m,
        gain_moe_m,
        sum_down_a,
        g_part,
    )
    sum_down_a = before[0]
    sum_in_m = over_dp(g_in_m)
    sum_down_m = over_dp(g_down_m)
    grad_one = [grad_layer[m] + values[m] for m in each]

    small = None
    mamba_sides, mamba_back, mixes, own_normed = [], [], [], []
    for m in each:
        mix_branch, gate_scale = mix_kept[m]
        x_rows, _, mamba_in, scan_args, _ = mamba_kept[m]
        x_rows, _ = fence(x_rows, grad_one[m])
        x_rows = x_rows[:, :D].astype(f32)
        normed_x = x_rows * row_scale(x_rows)
        own_normed.append(normed_x[:length])
        grad_mix = grad_one[m].astype(bf16)
        mean_term = jnp.sum(grad_mix.astype(f32) * mix_branch, axis=-1, keepdims=True) / DI
        extra = lanes(split_two(gate_scale) + split_two(mean_term), 128)
        rows_all = gather_rows(jnp.concatenate([grad_mix, extra], axis=1))
        mix_all = rows_all[:, :D]
        extra_all = rows_all[:, D:]
        scale_all = extra_all[:, 0:1].astype(f32) + extra_all[:, 1:2].astype(f32)
        scaled_mix = (mix_all.astype(f32) * scale_all).astype(bf16)
        mixes.append(scaled_mix)
        if m == micro - 1:
            g_mix = tn_sum([(x, k[4]) for x, k in zip(mixes, mamba_kept)])
            mix_all, g_mix = fence(mix_all, g_mix)
        grad_gated = nn(mix_all, w_mix_t, bf16)
        grad_scan, *grads = scan_backward(
            heads, length, *scan_args, grad_gated, extra_all
        )
        mamba_sides.append((mamba_in, grad_scan))
        small = grads if small is None else [a + b for a, b in zip(small, grads)]
        total = nt(grad_scan, w_scan)
        gains[0] = gains[0] + jnp.sum(total * normed_x, axis=0)
        mamba_back.append(return_rows(total))

    def rows_back(packed):
        packed = lax.psum_scatter(packed, FS, scatter_dimension=0, tiled=True)
        return lax.all_to_all(
            packed.reshape(n_tp, rows, -1), TP, split_axis=0, concat_axis=0, tiled=True
        ).astype(f32)

    def owned(block):
        return block.transpose(1, 0, 2).reshape(rows, -1)

    g_s = rows_back(
        jnp.concatenate([g_mix, g_sin_m, g_sdown_m, g_sin_a, g_sdown_a], axis=1)
    )

    g_scan = tn_sum(mamba_sides, f32)
    g_scan, sum_in_m, sum_down_m = fence(g_scan, sum_in_m, sum_down_m)
    out_expert_in, out_expert_down = expert_out(sum_in_a, sum_down_a)
    out_expert_in_m, out_expert_down_m = expert_out(sum_in_m, sum_down_m)

    conv_sums, chan_sums, head_sums = small
    g_gate = chan_sums[0]
    g_skip = jnp.sum(chan_sums[1].reshape(heads, HP), axis=1)
    head_grad = jnp.stack([head_sums[0, :heads], head_sums[1, :heads], g_skip])

    def spread(part, width):
        zeros = jnp.zeros(part.shape[:-1] + (width,), f32)
        return lax.dynamic_update_slice_in_dim(zeros, part[..., :chan], slot * chan, axis=-1)

    conv_grad = jnp.concatenate([conv_sums[CK : CK + 1], conv_sums[:CK]], axis=0)
    conv_grad = spread(conv_grad, conv_total) + jnp.pad(conv_grad[:, chan:], ((0, 0), (DI, 0)))
    conv_grad = conv_grad.reshape(CK + 1, n_all, conv_here).transpose(1, 0, 2).reshape(n_all, -1)
    vec_grad = jnp.concatenate([spread(g_gate, DI).reshape(n_all, gate_here), conv_grad], axis=1)
    vec_grad = jnp.pad(vec_grad, ((0, 0), (0, rows * vec_cols - vec_len))).reshape(D, vec_cols)
    little = jnp.concatenate([g[:, None] for g in gains] + [g_router_m, g_router, vec_grad], axis=1)
    after = step_width - heads - small_cols
    g_scan = jnp.pad(g_scan, ((0, 0), (0, step_width - 128)))
    g_m = rows_back((g_scan + jnp.pad(little, ((0, 0), (in_width + heads, after)))).astype(bf16))
    mamba_back[-1], g_s = fence(mamba_back[-1], g_s)
    grads_in = []
    for m in each:
        scale_x = mamba_kept[m][1]
        grad_values, _ = rms_backward(mamba_back[m], own_normed[m], scale_x, gain_mamba)
        grads_in.append(grad_one[m] + grad_values)

    out_w_in = jnp.concatenate(
        [
            owned(g_m[:, :, :chan]),
            owned(g_m[:, :, chan : 2 * chan]),
            jnp.sum(g_m[:, :, 2 * chan : in_width], axis=0),
        ],
        axis=1,
    )
    out_mix = owned(g_s[:, :, :chan]).T
    out_w_dt = owned(g_m[:, :, in_width : in_width + heads])
    little = jnp.sum(g_m[:, :, in_width + heads : in_width + heads + small_cols], axis=0)
    vec = little[:, 4 + 2 * experts_total :].reshape(-1)
    out_gate = vec[:gate_here]
    out_conv_b = vec[gate_here : gate_here + conv_here]
    out_conv_w = vec[gate_here + conv_here : vec_len].reshape(CK, conv_here)

    head_grad = lax.dynamic_update_slice(jnp.zeros((8, 128), f32), head_grad, (0, slot * heads))
    for axis in ALL:
        size = lax.axis_size(axis)
        step = 1
        while step < size:
            pairs = [(i, i ^ step) for i in range(size)]
            head_grad = head_grad + send(head_grad, axis, pairs)
            step *= 2
    head_grad = head_grad[:3, :MH]

    cuts = (q_width, q_width + kv_width, q_width + 2 * kv_width)
    out_w_qkv = jnp.concatenate(
        [
            owned(g_attn[:, :, : cuts[0]]),
            owned(g_attn[:, :, cuts[0] : cuts[1]]),
            owned(g_attn[:, :, cuts[1] : cuts[2]]),
        ],
        axis=1,
    )
    out_w_out = owned(g_attn[:, :, cuts[2] :]).T

    def shared_out(block):
        g_sin = jnp.concatenate([owned(block[:, :, :ff]), owned(block[:, :, ff : 2 * ff])], axis=1)
        return g_sin, owned(block[:, :, 2 * ff :]).T

    out_sin_m, out_sdown_m = shared_out(g_s[:, :, chan : chan + 3 * ff])
    out_sin, out_sdown = shared_out(g_s[:, :, chan + 3 * ff :])

    return (
        jnp.stack(results),
        jnp.stack(grads_in),
        little[:, 0],
        out_w_in,
        out_w_dt,
        out_conv_w,
        out_conv_b,
        head_grad[0],
        head_grad[1],
        head_grad[2],
        out_gate,
        out_mix,
        little[:, 1],
        little[:, 4 : 4 + experts_total],
        out_sin_m,
        out_sdown_m,
        out_expert_in_m,
        out_expert_down_m,
        little[:, 2],
        out_w_qkv,
        out_w_out,
        little[:, 3],
        little[:, 4 + experts_total : 4 + 2 * experts_total],
        out_sin,
        out_sdown,
        out_expert_in,
        out_expert_down,
    )


def solution(mesh):
    n_dp, n_ex = mesh.shape["dp"], mesh.shape["expert"]
    outer = n_ex // 8
    fine = Mesh(mesh.devices.reshape(n_dp, outer, 4, 2), ALL)
    split = P(ALL)
    row = P(ALL, None)
    col = P(None, ALL)
    mid = P(None, ALL, None)
    part = P(EX, "dp", None)
    same = P()
    return jax.shard_map(
        body,
        mesh=fine,
        in_specs=(
            mid,
            mid,
            P(None, None, ALL, None),
            split,
            row,
            row,
            col,
            split,
            same,
            same,
            same,
            split,
            col,
            split,
            row,
            row,
            col,
            part,
            part,
            split,
            row,
            col,
            split,
            row,
            row,
            col,
            part,
            part,
            mid,
        ),
        out_specs=(
            mid,
            mid,
            split,
            row,
            row,
            col,
            split,
            same,
            same,
            same,
            split,
            col,
            split,
            row,
            row,
            col,
            part,
            part,
            split,
            row,
            col,
            split,
            row,
            row,
            col,
            part,
            part,
        ),
        check_vma=False,
    )
```

```python
import functools

import jax
import jax.numpy as jnp
from jax import lax
from jax.experimental import pallas as pl
from jax.experimental.pallas import tpu as pltpu
from jax.experimental.layout import Layout, with_layout_constraint
from jax.sharding import Mesh, PartitionSpec as P

D = 1536
QH = 12
KVH = 4
HEAD = 128
EXP_FF = 512
SH_FF = 1024
TOP = 6
MH = 48
HP = 64
STATE = 128
CK = 4
DI = 3072

bf16 = jnp.bfloat16
f32 = jnp.float32
epsilon = 1e-05
masked_value = -1e30
highest = lax.Precision.HIGHEST
ALL = ("dp", "w", "z", "core")
EX = ("w", "z", "core")
TP = ("z", "core")
FS = ("dp", "w")
SWAP = [(0, 1), (1, 0)]


def dot(a, b, dims, out=f32):
    r = lax.dot_general(a, b, (dims, ((), ())), preferred_element_type=f32)
    return r if out == f32 else r.astype(out)


def nn(a, b, out=f32):
    return dot(a, b, ((1,), (0,)), out)


def nt(a, b, out=f32):
    return dot(a, b, ((1,), (1,)), out)


def tn(a, b, out=f32):
    return dot(a, b, ((0,), (0,)), out)


def ring(shift, axis="z"):
    n = lax.axis_size(axis)
    return [(i, (i + shift) % n) for i in range(n)]


def wide(x):
    parts = [x] + [lax.ppermute(x, "w", ring(s, "w")) for s in range(1, lax.axis_size("w"))]
    return parts[0] if len(parts) == 1 else jnp.concatenate(parts, axis=0)


def narrow(total):
    n = lax.axis_size("w")
    rows = total.shape[0] // n
    out = total[:rows]
    for s in range(1, n):
        part = total[s * rows : (s + 1) * rows].astype(bf16)
        out = out + lax.ppermute(part, "w", ring(-s, "w")).astype(f32)
    return out


def add_first(total, part):
    rows = part.shape[0]
    if rows == total.shape[0]:
        return total + part
    return jnp.concatenate([total[:rows] + part, total[rows:]], axis=0)


def fence(*trees):
    if lax.axis_size("w") > 1:
        return trees
    return lax.optimization_barrier(trees)


def by_rows(x):
    if lax.axis_size("w") > 1:
        return x
    return with_layout_constraint(x, Layout(major_to_minor=tuple(range(x.ndim))))


def send(x, axis, pairs):
    return by_rows(lax.ppermute(by_rows(x), axis, pairs))


def gather_rows(x):
    n = lax.axis_size("z")
    parts = [x] + [send(x, "z", ring(s)) for s in range(1, n)]
    other = [send(p, "core", SWAP) for p in parts]
    return by_rows(jnp.concatenate(parts + other, axis=0))


def return_rows(total):
    n = lax.axis_size("z")
    half = total.shape[0] // 2
    rows = half // n
    recv = send(total[half:].astype(bf16), "core", SWAP)
    mine = total[:half] + recv.astype(f32)
    out = mine[:rows]
    for s in range(1, n):
        part = mine[s * rows : (s + 1) * rows].astype(bf16)
        out = out + send(part, "z", ring(-s)).astype(f32)
    return out


def pair_gather(x):
    return by_rows(jnp.concatenate([x, send(x, "core", SWAP)], axis=0))


def pair_return(total):
    half = total.shape[0] // 2
    recv = send(total[half:].astype(bf16), "core", SWAP)
    return total[:half] + recv.astype(f32)


def split_two(x):
    high = x.astype(bf16)
    return [high, (x - high.astype(f32)).astype(bf16)]


def row_scale(values):
    return lax.rsqrt(jnp.mean(values * values, axis=-1, keepdims=True) + epsilon)


def rms_forward(values, gain):
    scale = row_scale(values)
    normed = values * scale
    return normed, scale, (normed * gain).astype(bf16)


def rms_backward(grad_result, normed, scale, gain):
    grad_gain = jnp.sum(grad_result * normed, axis=0)
    grad_normed = grad_result * gain
    grad_values = scale * (
        grad_normed - normed * jnp.mean(grad_normed * normed, axis=-1, keepdims=True)
    )
    return grad_values, grad_gain


def lanes(parts, width):
    used = sum(p.shape[-1] for p in parts)
    rows = parts[0].shape[0]
    if used < width:
        parts = parts + [jnp.zeros((rows, width - used), bf16)]
    return jnp.concatenate(parts, axis=1)


def scan_core(proj, step_raw, seg_col, seg_row, taps, bias, heads_par):
    length = proj.shape[0]
    chan = proj.shape[1] - 2 * STATE
    chan = chan // 2
    z = proj[:, :chan].astype(f32)
    conv_in = proj[:, chan:].astype(f32)
    place = lax.broadcasted_iota(jnp.int32, (length, 1), 0)
    shifted, masks = [], []
    conv_sum = bias
    for k in range(CK):
        if k == 0:
            moved, mask = conv_in, None
            conv_sum = conv_sum + taps[0:1] * moved
        else:
            same = pltpu.roll(seg_col, k, 0) == seg_col
            mask = jnp.where(same & (place >= k), 1.0, 0.0)
            moved = pltpu.roll(conv_in, k, 0) * mask
            conv_sum = conv_sum + taps[k : k + 1] * moved
        shifted.append(moved)
        masks.append(mask)
    logistic = jax.nn.sigmoid(conv_sum)
    act = conv_sum * logistic
    pre = step_raw + heads_par[0:1]
    step = jnp.maximum(pre, 0.0) + jnp.log1p(jnp.exp(-jnp.abs(pre)))
    decay_rate = heads_par[1:2]
    rows_pos = lax.broadcasted_iota(jnp.int32, (length, length), 0)
    cols_pos = lax.broadcasted_iota(jnp.int32, (length, length), 1)
    lower = jnp.where(cols_pos <= rows_pos, 1.0, 0.0)
    cum = lax.dot_general(
        lower, step * decay_rate, (((1,), (0,)), ((), ())), precision=highest, preferred_element_type=f32
    )
    allowed = (seg_col == seg_row) & (cols_pos <= rows_pos)
    b_low = act[:, chan : chan + STATE].astype(bf16)
    c_low = act[:, chan + STATE :].astype(bf16)
    cb = nt(c_low, b_low)
    return dict(
        chan=chan, z=z, conv_in=conv_in, shifted=shifted, masks=masks, conv_sum=conv_sum,
        logistic=logistic, act=act, pre=pre, step=step, rate=decay_rate, lower=lower, cum=cum,
        cum_t=cum.T, step_t=step.T, allowed=allowed, b=b_low, c=c_low, cb=cb,
    )


def head_table(s, h):
    gap = s["cum"][:, h : h + 1] - s["cum_t"][h : h + 1, :]
    decay = jnp.exp(jnp.where(s["allowed"], gap, masked_value))
    return decay, s["step_t"][h : h + 1, :]


def pair_scan(s, heads, low):
    lane = lax.broadcasted_iota(jnp.int32, (1, 2 * HP), 1)
    blocks, mixes, tables = [], [], []
    for j in range(heads // 2):
        both = low[:, j * 2 * HP : (j + 1) * 2 * HP]
        outs = []
        for h in (2 * j, 2 * j + 1):
            decay, step_row = head_table(s, h)
            mix = (decay * s["cb"] * step_row).astype(bf16)
            outs.append(nn(mix, both))
            mixes.append(mix)
            tables.append((decay, step_row))
        blocks.append(jnp.where(lane < HP, outs[0], outs[1]))
    return jnp.concatenate(blocks, axis=1), mixes, tables


def scan_forward_kernel(heads, proj_ref, step_ref, col_ref, row_ref, conv_ref, chan_ref, head_ref, gained_ref, square_ref):
    s = scan_core(
        proj_ref[...], step_ref[...], col_ref[...], row_ref[0], conv_ref[0:CK], conv_ref[CK : CK + 1], head_ref[...]
    )
    chan = s["chan"]
    inputs = s["act"][:, :chan]
    scan, _, _ = pair_scan(s, heads, inputs.astype(bf16))
    scan = scan + chan_ref[1:2] * inputs
    gated = scan * s["z"] * jax.nn.sigmoid(s["z"])
    gained_ref[...] = (gated * chan_ref[0:1]).astype(bf16)
    square_ref[...] = jnp.broadcast_to(jnp.sum(gated * gated, axis=1, keepdims=True), square_ref.shape)


def scan_backward_kernel(
    heads, proj_ref, step_ref, col_ref, row_ref, conv_ref, chan_ref, head_ref, grad_ref, extra_ref,
    dproj_ref, dconv_ref, dchan_ref, dhead_ref, flat_ref,
):
    @pl.when(pl.program_id(0) == 0)
    def _():
        dconv_ref[...] = jnp.zeros_like(dconv_ref)
        dchan_ref[...] = jnp.zeros_like(dchan_ref)
        dhead_ref[...] = jnp.zeros_like(dhead_ref)

    taps = conv_ref[0:CK]
    s = scan_core(proj_ref[...], step_ref[...], col_ref[...], row_ref[0], taps, conv_ref[CK : CK + 1], head_ref[...])
    chan, length = s["chan"], s["z"].shape[0]
    gain, skip = chan_ref[0:1], chan_ref[1:2]
    inputs = s["act"][:, :chan]
    low = inputs.astype(bf16)
    scan, mixes, tables = pair_scan(s, heads, low)
    scan = scan + skip * inputs
    z = s["z"]
    sig = jax.nn.sigmoid(z)
    silu = z * sig
    gated = scan * silu
    extra = extra_ref[...].astype(f32)
    scale = extra[:, 0:1] + extra[:, 1:2]
    mean = extra[:, 2:3] + extra[:, 3:4]
    grad = grad_ref[...].astype(f32)
    normed = gated * scale
    d_gated = scale * (grad * gain - normed * mean)
    d_scan = d_gated * silu
    d_z = d_gated * scan * sig * (1.0 + z * (1.0 - sig))
    d_low = d_scan.astype(bf16)
    lane = lax.broadcasted_iota(jnp.int32, (1, 2 * HP), 1)
    spot = lax.broadcasted_iota(jnp.int32, (1, s["step"].shape[1]), 1)
    d_cb = jnp.zeros((length, length), f32)
    d_cum = jnp.zeros(s["step"].shape, f32)
    flat_ref[...] = jnp.zeros_like(flat_ref)
    blocks = []
    for j in range(heads // 2):
        cut = slice(j * 2 * HP, (j + 1) * 2 * HP)
        both, d_both = low[:, cut], d_low[:, cut]
        outs = []
        for i, h in enumerate((2 * j, 2 * j + 1)):
            decay, step_row = tables[h]
            outs.append(tn(mixes[h], d_both))
            keep = (lane < HP) if i == 0 else (lane >= HP)
            d_mix = nt(jnp.where(keep, d_both, jnp.zeros_like(d_both)), both)
            part = d_mix * decay
            d_cb = d_cb + part * step_row
            part = part * s["cb"]
            flat_ref[h : h + 1, 0:length] = jnp.sum(part, axis=0, keepdims=True)
            column = jnp.sum(part * step_row, axis=1, keepdims=True)
            d_cum = d_cum + jnp.where(spot == h, column, 0.0)
        blocks.append(jnp.where(lane < HP, outs[0], outs[1]))
    d_inputs = jnp.concatenate(blocks, axis=1) + skip * d_scan
    from_rows = flat_ref[...].T[0:length]
    d_cum = d_cum - s["step"] * from_rows
    d_rate = lax.dot_general(
        s["lower"], d_cum, (((0,), (0,)), ((), ())), precision=highest, preferred_element_type=f32
    )
    d_step = from_rows + d_rate * s["rate"]
    d_pre = jnp.where(spot < heads, d_step * jax.nn.sigmoid(s["pre"]), 0.0)
    d_cb_low = d_cb.astype(bf16)
    d_act = jnp.concatenate([d_inputs, tn(d_cb_low, s["c"]), nn(d_cb_low, s["b"])], axis=1)
    logistic = s["logistic"]
    d_sum = d_act * logistic * (1.0 + s["conv_sum"] * (1.0 - logistic))
    d_in = taps[0:1] * d_sum
    for k in range(1, CK):
        back = d_sum * s["masks"][k] * taps[k : k + 1]
        d_in = d_in + pltpu.roll(back, length - k, 0)
    dproj_ref[...] = jnp.concatenate([d_z, d_in, d_pre], axis=1).astype(bf16)
    for k in range(CK):
        dconv_ref[k : k + 1] += jnp.sum(d_sum * s["shifted"][k], axis=0, keepdims=True)
    dconv_ref[CK : CK + 1] += jnp.sum(d_sum, axis=0, keepdims=True)
    dchan_ref[0:1] += jnp.sum(grad * normed, axis=0, keepdims=True)
    dchan_ref[1:2] += jnp.sum(d_scan * inputs, axis=0, keepdims=True)
    dhead_ref[0:1] += jnp.sum(d_pre, axis=0, keepdims=True)
    dhead_ref[1:2] += jnp.sum(d_rate * s["step"] * s["rate"], axis=0, keepdims=True)


def scan_specs(length, width, lanes_, conv, chan):
    def whole(shape):
        return pl.BlockSpec(shape, lambda i: (0,) * len(shape))

    rows = lambda w: pl.BlockSpec((length, w), lambda i: (i, 0))
    return rows, whole, [
        rows(width), rows(lanes_), rows(1), pl.BlockSpec((1, 1, length), lambda i: (i, 0, 0)),
        whole((8, conv)), whole((8, chan)), whole((8, lanes_)),
    ]


def scan_forward(heads, length, proj, step, seg_col, seg_row, conv_par, chan_par, head_par):
    total, width = proj.shape
    chan = heads * HP
    rows, whole, specs = scan_specs(length, width, step.shape[1], width - chan, chan)
    return pl.pallas_call(
        functools.partial(scan_forward_kernel, heads),
        grid=(total // length,),
        in_specs=specs,
        out_specs=[rows(chan), rows(128)],
        out_shape=[jax.ShapeDtypeStruct((total, chan), bf16), jax.ShapeDtypeStruct((total, 128), f32)],
        compiler_params=pltpu.CompilerParams(vmem_limit_bytes=32 << 20),
        name="scan_forward",
    )(proj, step, seg_col, seg_row, conv_par, chan_par, head_par)


def scan_backward(heads, length, proj, step, seg_col, seg_row, conv_par, chan_par, head_par, grad, extra):
    total, width = proj.shape
    chan = heads * HP
    lanes_ = step.shape[1]
    rows, whole, specs = scan_specs(length, width, lanes_, width - chan, chan)
    return pl.pallas_call(
        functools.partial(scan_backward_kernel, heads),
        grid=(total // length,),
        in_specs=specs + [rows(chan), rows(128)],
        out_specs=[rows(width + lanes_), whole((8, width - chan)), whole((8, chan)), whole((8, lanes_))],
        out_shape=[
            jax.ShapeDtypeStruct((total, width + lanes_), bf16),
            jax.ShapeDtypeStruct((8, width - chan), f32),
            jax.ShapeDtypeStruct((8, chan), f32),
            jax.ShapeDtypeStruct((8, lanes_), f32),
        ],
        scratch_shapes=[pltpu.VMEM((128, 128), f32)],
        compiler_params=pltpu.CompilerParams(vmem_limit_bytes=32 << 20),
        name="scan_backward",
    )(proj, step, seg_col, seg_row, conv_par, chan_par, head_par, grad, extra)


def swiglu(gate, up):
    return gate * jax.nn.sigmoid(gate) * up


def swiglu_back(grad, gate, up):
    logistic = jax.nn.sigmoid(gate)
    grad_gate = grad * up * logistic * (1.0 + gate * (1.0 - logistic))
    return grad_gate.astype(bf16), (grad * gate * logistic).astype(bf16)


def gate_table(moe_in, mask, router):
    logits = nn(moe_in, router)
    picked = jnp.where(mask, logits, masked_value)
    peak = jnp.max(picked, axis=-1, keepdims=True)
    ex = jnp.where(mask, jnp.exp(picked - peak), 0.0)
    return ex / jnp.sum(ex, axis=-1, keepdims=True)


def unit_gates(local, units):
    count = local.shape[1]
    inner = EXP_FF // lax.axis_size("dp")
    owner = lax.broadcasted_iota(jnp.int32, (1, units), 1) // inner % count
    spread = local[:, count - 1 :]
    for e in range(count - 1):
        spread = jnp.where(owner == e, local[:, e : e + 1], spread)
    return spread, owner


def moe_forward(own_in, mask, w):
    rows = own_in.shape[0]
    base_in = gather_rows(own_in)
    moe_in = wide(base_in)
    gates = gate_table(moe_in, mask, w["router"])
    units = w["expert_down"].shape[0]
    count = units // EXP_FF
    first = lax.axis_index(EX) * count
    local = lax.dynamic_slice(gates, (0, first), (gates.shape[0], count))
    pre = nn(moe_in, w["expert_in"], bf16)
    pre_s = nn(base_in, w["shared_in"], bf16)
    pre, pre_s = lax.optimization_barrier((pre, pre_s))
    p = pre.astype(f32)
    spread, _ = unit_gates(local, units)
    hid = (swiglu(p[:, :units], p[:, units:]) * spread).astype(bf16)
    half = pre_s.shape[1] // 2
    p = pre_s.astype(f32)
    hid_s = swiglu(p[:, :half], p[:, half:]).astype(bf16)
    total = add_first(nn(hid, w["expert_down"]), nt(hid_s, w["shared_down_t"]))
    return total, (moe_in, base_in, gates[:rows], local, pre, pre_s)


def moe_backward(base_z, kept, w, experts_total):
    moe_in, base_in, own_gates, local, pre, pre_s = kept
    pre, pre_s, _ = lax.optimization_barrier((pre, pre_s, base_z))
    grad_z = wide(base_z)
    units = w["expert_down"].shape[0]
    count = units // EXP_FF
    first = lax.axis_index(EX) * count
    spread, owner = unit_gates(local, units)
    p = pre.astype(f32)
    gate, up = p[:, :units], p[:, units:]
    grad_hid = nt(grad_z, w["expert_down"])
    act = swiglu(gate, up)
    hidden = (act * spread).astype(bf16)
    product = grad_hid * act
    lane = lax.broadcasted_iota(jnp.int32, (1, experts_total), 1)
    table = jnp.zeros((grad_z.shape[0], experts_total), f32)
    for e in range(count):
        mine = jnp.sum(jnp.where(owner == e, product, 0.0), axis=-1, keepdims=True)
        table = table + local[:, e : e + 1] * mine * (lane == first + e).astype(f32)
    g_gate, g_up = swiglu_back(grad_hid * spread, gate, up)
    g_pre = jnp.concatenate([g_gate, g_up], axis=1)
    total = nt(g_pre, w["expert_in"])
    half = pre_s.shape[1] // 2
    p = pre_s.astype(f32)
    grad_hid = nn(base_z, w["shared_down_t"])
    hid_s = swiglu(p[:, :half], p[:, half:]).astype(bf16)
    g_gate, g_up = swiglu_back(grad_hid, p[:, :half], p[:, half:])
    g_pre_s = jnp.concatenate([g_gate, g_up], axis=1)
    total = add_first(total, nt(g_pre_s, w["shared_in"]))
    extra = -(-experts_total // 128) * 128
    table = jnp.pad(table, ((0, 0), (0, extra - experts_total)))
    back = return_rows(narrow(jnp.concatenate([total, table], axis=1)))
    side = (moe_in, grad_z, hidden, hid_s, g_pre, g_pre_s, base_in, base_z)
    return back, side


def moe_finish(back, kept, w, experts_total):
    own_gates = kept[2]
    weighted = back[:, D : D + experts_total]
    grad_logits = weighted - own_gates * jnp.sum(weighted, axis=-1, keepdims=True)
    grad_logits = grad_logits.astype(bf16)
    return back[:, :D] + nt(grad_logits, w["router"]), grad_logits


def tn_sum(pairs, out=bf16):
    if lax.axis_size("w") > 1:
        return tn(*[jnp.concatenate(side, axis=0) for side in zip(*pairs)], out)
    total = None
    for a, b in pairs:
        part = tn(a, b)
        total = part if total is None else total + part
    return total.astype(out)


def moe_weight_grads(sides):
    g_down = tn_sum([(s[2], s[1]) for s in sides])
    g_in = tn_sum([(s[0], s[4]) for s in sides])
    g_sin = tn_sum([(s[6], s[5]) for s in sides])
    g_sdown_t = tn_sum([(s[7], s[3]) for s in sides])
    return g_in, g_down, g_sin, g_sdown_t


def attn_mask(seg):
    length = seg.shape[1]
    rows_pos = lax.broadcasted_iota(jnp.int32, (length, length), 0)
    cols_pos = lax.broadcasted_iota(jnp.int32, (length, length), 1)
    return (seg[:, :, None] == seg[:, None, :]) & (cols_pos <= rows_pos)[None]


def attn_forward(own_in, allowed, w_qkv, w_out_t):
    seqs, length, _ = allowed.shape
    kv = KVH // 2
    group = QH // KVH
    q_width = kv * group * HEAD
    kv_width = kv * HEAD
    attn_in = pair_gather(own_in)
    packed = nn(attn_in, w_qkv, bf16)
    q = packed[:, :q_width].reshape(seqs, length, kv, group, HEAD)
    k = packed[:, q_width : q_width + kv_width].reshape(seqs, length, kv, HEAD)
    v = packed[:, q_width + kv_width :].reshape(seqs, length, kv, HEAD)
    scores = jnp.einsum("bqhgd,bkhd->bhgqk", q, k, preferred_element_type=f32) * HEAD**-0.5
    scores = jnp.where(allowed[:, None, None], scores, masked_value)
    peak = jnp.max(scores, axis=-1, keepdims=True)
    ex = jnp.exp(scores - peak)
    probs = ex / jnp.sum(ex, axis=-1, keepdims=True)
    context = jnp.einsum("bhgqk,bkhd->bqhgd", probs.astype(bf16), v, preferred_element_type=f32)
    context = context.reshape(seqs * length, q_width).astype(bf16)
    branch = pair_return(nt(context, w_out_t))
    return branch, (attn_in, q, k, v, probs, context)


def attn_backward(own_grad, kept, w_qkv, w_out_t):
    attn_in, q, k, v, probs, context = kept
    seqs, length, kv, group, _ = q.shape
    grad = pair_gather(own_grad)
    grad_context = nn(grad, w_out_t, bf16).reshape(seqs, length, kv, group, HEAD)
    probs_low = probs.astype(bf16)
    grad_v = jnp.einsum("bhgqk,bqhgd->bkhd", probs_low, grad_context, preferred_element_type=f32)
    grad_p = jnp.einsum("bqhgd,bkhd->bhgqk", grad_context, v, preferred_element_type=f32)
    delta = jnp.sum(probs * grad_p, axis=-1, keepdims=True)
    grad_s = (probs * (grad_p - delta)).astype(bf16)
    scale = HEAD**-0.5
    grad_q = jnp.einsum("bhgqk,bkhd->bqhgd", grad_s, k, preferred_element_type=f32) * scale
    grad_k = jnp.einsum("bhgqk,bqhgd->bkhd", grad_s, q, preferred_element_type=f32) * scale
    rows = seqs * length
    grad_packed = jnp.concatenate(
        [grad_q.reshape(rows, -1), grad_k.reshape(rows, -1), grad_v.reshape(rows, -1)], axis=1
    ).astype(bf16)
    grad_in = pair_return(nt(grad_packed, w_qkv))
    return grad_in, (attn_in, grad_packed, context, grad)


def by_owner(x, count):
    return x.reshape(x.shape[0], count, x.shape[1] // count)


def body(
    tokens,
    segments,
    routes,
    norm_mamba,
    w_in,
    w_dt,
    conv_w,
    conv_b,
    dt_bias,
    a_log,
    skip_scale,
    gate_norm,
    w_mix_out,
    norm_moe_m,
    router_m,
    shared_in_m,
    shared_down_m,
    expert_in_m,
    expert_down_m,
    norm_attn,
    w_qkv,
    w_out,
    norm_moe,
    router,
    shared_in,
    shared_down,
    expert_in,
    expert_down,
    cotangent,
):
    micro, length, _ = tokens.shape
    n_tp = lax.axis_size("z") * lax.axis_size("core")
    n_ex = lax.axis_size("w") * n_tp
    n_all = lax.axis_size("dp") * n_ex
    rows = w_in.shape[0]
    local_experts = expert_in.shape[0]
    experts_total = local_experts * n_ex
    heads = MH // n_tp
    chan = heads * HP
    ff = SH_FF // n_tp
    slot = lax.axis_index(TP)
    conv_total = DI + 2 * STATE
    conv_here = conv_w.shape[1]
    gate_here = gate_norm.shape[0]
    vec_len = gate_here + (CK + 1) * conv_here
    vec_cols = -(-vec_len // rows)
    small_cols = 4 + 2 * experts_total + vec_cols
    step_width = -(-(heads + small_cols) // 128) * 128

    vec = jnp.concatenate([gate_norm, conv_b, conv_w.reshape(-1)])
    vec = jnp.pad(vec, (0, rows * vec_cols - vec_len)).reshape(rows, vec_cols)
    gains_own = jnp.stack([norm_mamba, norm_moe_m, norm_attn, norm_moe], axis=1)
    little = jnp.concatenate([gains_own, router_m, router, vec], axis=1)

    def for_all(x):
        return jnp.broadcast_to(x[:, None], (rows, n_tp, x.shape[1]))

    def moved_columns(parts, *after):
        packed = jnp.concatenate(parts, axis=2).transpose(1, 0, 2)
        packed = fence(packed, *after)[0]
        moved = lax.all_to_all(packed, TP, split_axis=0, concat_axis=0, tiled=True)
        return moved.reshape(n_tp * rows, -1)

    def whole_rows(moved):
        return lax.all_gather(moved, FS, axis=0, tiled=True)

    def shared_pack(w_sin, w_sdown):
        return [
            by_owner(w_sin[:, :SH_FF], n_tp),
            by_owner(w_sin[:, SH_FF:], n_tp),
            by_owner(w_sdown.T, n_tp),
        ]

    blank = jnp.zeros((rows, n_tp, step_width - heads - small_cols), bf16)
    moved_m = moved_columns(
        [
            by_owner(w_in[:, :DI], n_tp),
            by_owner(w_in[:, DI : 2 * DI], n_tp),
            for_all(w_in[:, 2 * DI :]),
            by_owner(w_dt, n_tp),
            for_all(little),
            blank,
            by_owner(w_mix_out.T, n_tp),
        ]
    )
    w_m = whole_rows(moved_m)

    expert_ids = jnp.arange(experts_total, dtype=jnp.int32)
    info_width = -(-(2 * experts_total + 1) // 128) * 128
    each = range(micro)
    rows_in = []
    for m in each:
        hot = [
            jnp.any(routes[b, m][:, :, None] == expert_ids, axis=1).astype(bf16) for b in range(2)
        ]
        info = lanes(hot + [segments[m, 0][:, None].astype(bf16)], info_width)
        x_info, _ = fence(jnp.concatenate([tokens[m], info], axis=1), moved_m)
        rows_in.append(gather_rows(x_info))
    in_width = 2 * chan + 2 * STATE
    w_in_here = w_m[:, :in_width]
    moved_s = moved_columns(
        shared_pack(shared_in_m, shared_down_m) + shared_pack(shared_in, shared_down), rows_in
    )
    w_s = whole_rows(moved_s)
    at = in_width + step_width
    w_step = w_m[:, in_width:at]
    w_dt_here = w_step[:, :128]
    small_all = w_step[:, heads : heads + small_cols]
    gain_mamba, gain_moe_m, gain_attn, gain_moe = [small_all[:, i].astype(f32) for i in range(4)]
    router_m_full = small_all[:, 4 : 4 + experts_total]
    router_full = small_all[:, 4 + experts_total : 4 + 2 * experts_total]
    vec_all = small_all[:, 4 + 2 * experts_total :].reshape(n_all, rows * vec_cols).astype(f32)
    gain_gate = vec_all[:, :gate_here].reshape(DI)
    bias_all = vec_all[:, gate_here : gate_here + conv_here].reshape(conv_total)
    taps_all = vec_all[:, gate_here + conv_here : vec_len].reshape(n_all, CK, conv_here)
    taps_all = taps_all.transpose(1, 0, 2).reshape(CK, conv_total)

    def channels(full_row):
        mine = lax.dynamic_slice_in_dim(full_row, slot * chan, chan, axis=-1)
        return jnp.concatenate([mine, full_row[..., DI:]], axis=-1)

    taps = channels(taps_all)
    bias = channels(bias_all)
    gain_here = lax.dynamic_slice_in_dim(gain_gate, slot * chan, chan)
    dt_here = lax.dynamic_slice_in_dim(dt_bias, slot * heads, heads)
    log_here = lax.dynamic_slice_in_dim(a_log, slot * heads, heads)
    skip_here = lax.dynamic_slice_in_dim(skip_scale, slot * heads, heads)

    w_scan = w_m[:, : in_width + 128]
    w_mix_t = w_m[:, at:]

    n_dp = lax.axis_size("dp")

    def expert_weights(w_up, w_low):
        count, depth, width = w_up.shape
        cols = w_up.reshape(count, depth, 2, n_dp, EXP_FF // n_dp).transpose(1, 2, 3, 0, 4)
        return (
            by_rows(lax.all_gather(by_rows(cols.reshape(depth, -1)), "dp", axis=0, tiled=True)),
            lax.all_gather(w_low.reshape(-1, D), "dp", axis=0, tiled=True),
        )

    expert_in_m, expert_down_m, _ = fence(expert_in_m, expert_down_m, moved_m)
    up_m, low_m = expert_weights(expert_in_m, expert_down_m)
    moe_m = {
        "router": router_m_full,
        "shared_in": w_s[:, : 2 * ff],
        "shared_down_t": w_s[:, 2 * ff : 3 * ff],
        "expert_in": up_m,
        "expert_down": low_m,
    }

    kv = KVH // 2
    q_width = QH // 2 * HEAD
    kv_width = kv * HEAD
    q_all, kv_all = QH * HEAD, KVH * HEAD
    up_a, low_a = expert_weights(expert_in, expert_down)
    moe_a = {
        "router": router_full,
        "shared_in": w_s[:, 3 * ff : 5 * ff],
        "shared_down_t": w_s[:, 5 * ff :],
        "expert_in": up_a,
        "expert_down": low_a,
    }

    def eight(parts):
        block = jnp.concatenate([p.reshape(-1, p.shape[-1]) for p in parts], axis=0)
        return jnp.pad(block, ((0, 8 - block.shape[0]), (0, 0)))

    conv_par = eight([taps, bias])
    chan_par = eight([gain_here, jnp.repeat(skip_here, HP)])
    head_par = jnp.pad(eight([dt_here, -jnp.exp(log_here)]), ((0, 0), (0, 128 - heads)))
    x_own = [tokens[m].astype(f32) for m in each]
    masks, allowed, mamba_kept, mix_kept, hidden_one = [], [], [], [], []
    proj_all, cot_all = [], []
    for m in each:
        rows_all = rows_in[m]
        x_all = rows_all[:, :D].astype(f32)
        marks = wide(rows_all[:, D : D + 2 * experts_total]) > 0.5
        masks.append([marks[:, :experts_total], marks[:, experts_total:]])
        seg_col = rows_all[:, D + 2 * experts_total :][:, :1].astype(f32)
        seg_row = seg_col.reshape(n_tp, 1, length)
        seg = seg_row[:, 0].astype(jnp.int32)
        allowed.append(attn_mask(jnp.stack([seg[0], seg[n_tp // 2]])))

        x_all, _ = fence(x_all, w_m)
        _, scale_x, mamba_in = rms_forward(x_all, gain_mamba)
        total_rows = mamba_in.shape[0]
        proj = nn(mamba_in, w_in_here, bf16)
        dt_raw = nn(mamba_in, w_dt_here)
        proj_all.append(proj)
        pars = (seg_col, seg_row, conv_par, chan_par, head_par)
        gained, square = scan_forward(heads, length, proj, dt_raw, *pars)
        partial = nt(gained, w_mix_t)
        high = square.astype(bf16).astype(f32)
        lane = lax.broadcasted_iota(jnp.int32, square.shape, 1)
        extra = jnp.where(lane == 0, high, jnp.where(lane == 1, square - high, 0.0))
        back = return_rows(jnp.concatenate([partial, extra], axis=1))
        gate_scale = lax.rsqrt((back[:, D : D + 1] + back[:, D + 1 : D + 2]) / DI + epsilon)
        mix_branch = back[:, :D] * gate_scale
        hidden_one.append(x_own[m] + mix_branch)
        mamba_kept.append((rows_all, scale_x[:length], mamba_in, (proj, dt_raw, *pars), gained))
        mix_kept.append((mix_branch, gate_scale))

    attn_pack = jnp.concatenate(
        [
            by_owner(w_qkv[:, :q_all], 2),
            by_owner(w_qkv[:, q_all : q_all + kv_all], 2),
            by_owner(w_qkv[:, q_all + kv_all :], 2),
            by_owner(w_out.T, 2),
        ],
        axis=2,
    ).transpose(1, 0, 2)
    attn_pack, _ = fence(attn_pack, moved_s)
    attn_pack = lax.all_to_all(attn_pack, "core", split_axis=0, concat_axis=0, tiled=True)
    own = attn_pack.reshape(2 * rows, -1)
    n_z = lax.axis_size("z")
    parts = [send(own, "z", ring(s)) for s in range(n_z - 1, 0, -1)] + [own]
    twice = jnp.concatenate(parts + parts, axis=0)
    start = (n_z - 1 - lax.axis_index("z")) * 2 * rows
    attn_w = lax.dynamic_slice(twice, (start, 0), (n_z * 2 * rows, own.shape[1]))
    attn_w, _ = fence(attn_w, mamba_kept[-1][-1])
    attn_w = lax.all_gather(attn_w, FS, axis=0, tiled=True)
    w_qkv_here = attn_w[:, : q_width + 2 * kv_width]
    w_out_t = attn_w[:, q_width + 2 * kv_width :]

    one_kept, layer_one = [], []
    for m in each:
        normed, scale, own = rms_forward(hidden_one[m], gain_moe_m)
        total, kept = moe_forward(own, masks[m][0], moe_m)
        layer_one.append(hidden_one[m] + return_rows(narrow(total)))
        one_kept.append((normed, scale, kept))
    attn_kept, hidden_two = [], []
    for m in each:
        cot, _ = fence(cotangent[m], layer_one[m])
        cot_all.append(gather_rows(cot))
        normed, scale, own = rms_forward(layer_one[m], gain_attn)
        branch, kept = attn_forward(own, allowed[m], w_qkv_here, w_out_t)
        hidden_two.append(layer_one[m] + branch)
        attn_kept.append((normed, scale, kept))
    two_kept, results = [], []
    for m in each:
        hidden_two[m], cot_all[m] = fence(hidden_two[m], cot_all[m])
        normed, scale, own = rms_forward(hidden_two[m], gain_moe)
        total, kept = moe_forward(own, masks[m][1], moe_a)
        results.append(total)
        two_kept.append((normed, scale, kept))

    gains = [0.0, 0.0, 0.0, 0.0]

    def over_dp(g):
        return lax.psum_scatter(g, "dp", scatter_dimension=0, tiled=True)

    def expert_out(g_up, g_low):
        depth = g_up.shape[0]
        cols = g_up.reshape(depth, 2, n_dp, local_experts, EXP_FF // n_dp)
        cols = cols.transpose(3, 0, 1, 2, 4).reshape(local_experts, depth, 2 * EXP_FF)
        return cols.astype(f32), g_low.reshape(local_experts, -1, D).astype(f32)

    saving = lax.axis_size("w") > 1

    def moe_stage(grads, kept_all, w, gain, *before):
        grads = list(grads)
        backs, sides, own_rows = [], [], []
        for m in each:
            back, side = moe_backward(grads[m], kept_all[m][2], w, experts_total)
            backs.append(back)
            sides.append(side)
            own_rows.append(side[6][:length])
            if saving:
                newer = moe_weight_grads(sides[-1:])
                hold = (back, newer, grads[m + 1 :])
                backs[-1], newer, grads[m + 1 :] = lax.optimization_barrier(hold)
                weights = newer if m == 0 else [a + b for a, b in zip(weights, newer)]
        if not saving:
            weights = moe_weight_grads(sides)
            backs[-1], weights = lax.optimization_barrier((backs[-1], weights))
        backs[-1], before = fence(backs[-1], before)
        grad_gain = 0.0
        values, logits = [], []
        for m in each:
            normed, scale, kept = kept_all[m]
            grad_in, grad_logits = moe_finish(backs[m], kept, w, experts_total)
            logits.append(grad_logits)
            grad_values, part = rms_backward(grad_in, normed, scale, gain)
            grad_gain = grad_gain + part
            values.append(grad_values)
        g_router = tn_sum(list(zip(own_rows, logits)), f32)
        return values, weights, grad_gain, g_router, before

    values, (g_in_a, g_down_a, g_sin_a, g_sdown_a), gains[3], g_router, _ = moe_stage(
        cot_all, two_kept, moe_a, gain_moe
    )
    sum_in_a = over_dp(g_in_a)
    sum_down_a = over_dp(g_down_a)
    grad_two = [cotangent[m].astype(f32) + values[m] for m in each]
    for m in each:
        total, _ = fence(results[m], grad_two[m])
        results[m] = (hidden_two[m] + return_rows(narrow(total))).astype(bf16)

    grad_layer, sides = [], []
    attn_back = []
    for m in each:
        grad_in, side = attn_backward(
            grad_two[m].astype(bf16), attn_kept[m][2], w_qkv_here, w_out_t
        )
        attn_back.append(grad_in)
        sides.append(side)
    g_attn = by_rows(
        jnp.concatenate(
            [
                by_rows(tn_sum([(s[0], s[1]) for s in sides])),
                by_rows(tn_sum([(s[3], s[2]) for s in sides])),
            ],
            axis=1,
        )
    )
    attn_back[-1], g_attn = lax.optimization_barrier((attn_back[-1], g_attn))
    g_attn = lax.psum_scatter(g_attn, FS, scatter_dimension=0, tiled=True)
    g_part = g_attn
    for m in each:
        normed, scale, _ = attn_kept[m]
        grad_values, part = rms_backward(attn_back[m], normed, scale, gain_attn)
        gains[2] = gains[2] + part
        grad_layer.append(grad_two[m] + grad_values)
    grad_layer[-1], sum_in_a = fence(grad_layer[-1], sum_in_a)

    values, (g_in_m, g_down_m, g_sin_m, g_sdown_m), gains[1], g_router_m, before = moe_stage(
        [gather_rows(g.astype(bf16)) for g in grad_layer],
        one_kept,
        moe_m,
        gain_moe_m,
        sum_down_a,
        g_part,
    )
    sum_down_a, g_part = before
    out_expert_in, out_expert_down = expert_out(sum_in_a, sum_down_a)
    sum_in_m = over_dp(g_in_m)
    sum_down_m = over_dp(g_down_m)
    grad_one = [grad_layer[m] + values[m] for m in each]

    small = None
    mamba_sides, mamba_back, mixes, own_normed = [], [], [], []
    for m in each:
        mix_branch, gate_scale = mix_kept[m]
        x_rows, _, mamba_in, scan_args, _ = mamba_kept[m]
        x_rows, _ = fence(x_rows, grad_one[m])
        x_rows = x_rows[:, :D].astype(f32)
        normed_x = x_rows * row_scale(x_rows)
        own_normed.append(normed_x[:length])
        grad_mix = grad_one[m].astype(bf16)
        mean_term = jnp.sum(grad_mix.astype(f32) * mix_branch, axis=-1, keepdims=True) / DI
        extra = lanes(split_two(gate_scale) + split_two(mean_term), 128)
        rows_all = gather_rows(jnp.concatenate([grad_mix, extra], axis=1))
        if m == micro - 1:
            rows_all, out_expert_in, out_expert_down = fence(
                rows_all, out_expert_in, out_expert_down
            )
        mix_all = rows_all[:, :D]
        extra_all = rows_all[:, D:]
        scale_all = extra_all[:, 0:1].astype(f32) + extra_all[:, 1:2].astype(f32)
        scaled_mix = (mix_all.astype(f32) * scale_all).astype(bf16)
        mixes.append(scaled_mix)
        if m == micro - 1:
            g_mix = tn_sum([(x, k[4]) for x, k in zip(mixes, mamba_kept)])
            mix_all, g_mix = fence(mix_all, by_rows(g_mix))
        grad_gated = nn(mix_all, w_mix_t, bf16)
        grad_scan, *grads = scan_backward(
            heads, length, *scan_args, grad_gated, extra_all
        )
        mamba_sides.append((mamba_in, grad_scan))
        small = grads if small is None else [a + b for a, b in zip(small, grads)]
        total = nt(grad_scan, w_scan)
        gains[0] = gains[0] + jnp.sum(total * normed_x, axis=0)
        mamba_back.append(return_rows(total))

    g_part, _ = fence(g_part, mixes)
    blocks = g_part.reshape(n_z, 2 * rows, -1)
    here = lax.axis_index("z")
    g_attn = lax.dynamic_index_in_dim(blocks, here, 0, keepdims=False).astype(f32)
    for shift in range(1, n_z):
        block = lax.dynamic_index_in_dim(blocks, (here + shift) % n_z, 0, keepdims=False)
        g_attn = g_attn + send(block, "z", ring(shift)).astype(f32)
    g_attn = lax.all_to_all(
        g_attn.astype(bf16).reshape(2, rows, -1), "core", split_axis=0, concat_axis=0, tiled=True
    ).astype(f32)

    def rows_back(packed):
        packed = lax.psum_scatter(packed, FS, scatter_dimension=0, tiled=True)
        return lax.all_to_all(
            packed.reshape(n_tp, rows, -1), TP, split_axis=0, concat_axis=0, tiled=True
        ).astype(f32)

    def owned(block):
        return block.transpose(1, 0, 2).reshape(rows, -1)

    g_s = rows_back(
        jnp.concatenate([g_mix, g_sin_m, g_sdown_m, g_sin_a, g_sdown_a], axis=1)
    )

    g_scan = by_rows(tn_sum(mamba_sides, f32))
    g_scan, sum_in_m, sum_down_m = fence(g_scan, sum_in_m, sum_down_m)
    out_expert_in_m, out_expert_down_m = expert_out(sum_in_m, sum_down_m)

    conv_sums, chan_sums, head_sums = small
    g_gate = chan_sums[0]
    g_skip = jnp.sum(chan_sums[1].reshape(heads, HP), axis=1)
    head_grad = jnp.stack([head_sums[0, :heads], head_sums[1, :heads], g_skip])

    def spread(part, width):
        zeros = jnp.zeros(part.shape[:-1] + (width,), f32)
        return lax.dynamic_update_slice_in_dim(zeros, part[..., :chan], slot * chan, axis=-1)

    conv_grad = jnp.concatenate([conv_sums[CK : CK + 1], conv_sums[:CK]], axis=0)
    conv_grad = spread(conv_grad, conv_total) + jnp.pad(conv_grad[:, chan:], ((0, 0), (DI, 0)))
    conv_grad = conv_grad.reshape(CK + 1, n_all, conv_here).transpose(1, 0, 2).reshape(n_all, -1)
    vec_grad = jnp.concatenate([spread(g_gate, DI).reshape(n_all, gate_here), conv_grad], axis=1)
    vec_grad = jnp.pad(vec_grad, ((0, 0), (0, rows * vec_cols - vec_len))).reshape(D, vec_cols)
    little = jnp.concatenate([g[:, None] for g in gains] + [g_router_m, g_router, vec_grad], axis=1)
    after = step_width - heads - small_cols
    g_scan = jnp.pad(g_scan, ((0, 0), (0, step_width - 128)))
    g_m = rows_back((g_scan + jnp.pad(little, ((0, 0), (in_width + heads, after)))).astype(bf16))
    mamba_back[-1], g_s = fence(mamba_back[-1], g_s)
    grads_in = []
    for m in each:
        scale_x = mamba_kept[m][1]
        grad_values, _ = rms_backward(mamba_back[m], own_normed[m], scale_x, gain_mamba)
        grads_in.append(grad_one[m] + grad_values)

    out_w_in = jnp.concatenate(
        [
            owned(g_m[:, :, :chan]),
            owned(g_m[:, :, chan : 2 * chan]),
            jnp.sum(g_m[:, :, 2 * chan : in_width], axis=0),
        ],
        axis=1,
    )
    out_mix = owned(g_s[:, :, :chan]).T
    out_w_dt = owned(g_m[:, :, in_width : in_width + heads])
    little = jnp.sum(g_m[:, :, in_width + heads : in_width + heads + small_cols], axis=0)
    vec = little[:, 4 + 2 * experts_total :].reshape(-1)
    out_gate = vec[:gate_here]
    out_conv_b = vec[gate_here : gate_here + conv_here]
    out_conv_w = vec[gate_here + conv_here : vec_len].reshape(CK, conv_here)

    head_grad = lax.dynamic_update_slice(jnp.zeros((8, 128), f32), head_grad, (0, slot * heads))
    for axis in ALL:
        size = lax.axis_size(axis)
        step = 1
        while step < size:
            pairs = [(i, i ^ step) for i in range(size)]
            head_grad = head_grad + send(head_grad, axis, pairs)
            step *= 2
    head_grad = head_grad[:3, :MH]

    cuts = (q_width, q_width + kv_width, q_width + 2 * kv_width)
    out_w_qkv = jnp.concatenate(
        [
            owned(g_attn[:, :, : cuts[0]]),
            owned(g_attn[:, :, cuts[0] : cuts[1]]),
            owned(g_attn[:, :, cuts[1] : cuts[2]]),
        ],
        axis=1,
    )
    out_w_out = owned(g_attn[:, :, cuts[2] :]).T

    def shared_out(block):
        g_sin = jnp.concatenate([owned(block[:, :, :ff]), owned(block[:, :, ff : 2 * ff])], axis=1)
        return g_sin, owned(block[:, :, 2 * ff :]).T

    out_sin_m, out_sdown_m = shared_out(g_s[:, :, chan : chan + 3 * ff])
    out_sin, out_sdown = shared_out(g_s[:, :, chan + 3 * ff :])

    return (
        jnp.stack(results),
        jnp.stack(grads_in),
        little[:, 0],
        out_w_in,
        out_w_dt,
        out_conv_w,
        out_conv_b,
        head_grad[0],
        head_grad[1],
        head_grad[2],
        out_gate,
        out_mix,
        little[:, 1],
        little[:, 4 : 4 + experts_total],
        out_sin_m,
        out_sdown_m,
        out_expert_in_m,
        out_expert_down_m,
        little[:, 2],
        out_w_qkv,
        out_w_out,
        little[:, 3],
        little[:, 4 + experts_total : 4 + 2 * experts_total],
        out_sin,
        out_sdown,
        out_expert_in,
        out_expert_down,
    )


def solution(mesh):
    n_dp, n_ex = mesh.shape["dp"], mesh.shape["expert"]
    outer = n_ex // 8
    fine = Mesh(mesh.devices.reshape(n_dp, outer, 4, 2), ALL)
    split = P(ALL)
    row = P(ALL, None)
    col = P(None, ALL)
    mid = P(None, ALL, None)
    part = P(EX, "dp", None)
    same = P()
    return jax.shard_map(
        body,
        mesh=fine,
        in_specs=(
            mid,
            mid,
            P(None, None, ALL, None),
            split,
            row,
            row,
            col,
            split,
            same,
            same,
            same,
            split,
            col,
            split,
            row,
            row,
            col,
            part,
            part,
            split,
            row,
            col,
            split,
            row,
            row,
            col,
            part,
            part,
            mid,
        ),
        out_specs=(
            mid,
            mid,
            split,
            row,
            row,
            col,
            split,
            same,
            same,
            same,
            split,
            col,
            split,
            row,
            row,
            col,
            part,
            part,
            split,
            row,
            col,
            split,
            row,
            row,
            col,
            part,
            part,
        ),
        check_vma=False,
    )
```

```python
import functools

import jax
import jax.numpy as jnp
from jax import lax
from jax.experimental import pallas as pl
from jax.experimental.pallas import tpu as pltpu
from jax.experimental.layout import Layout, with_layout_constraint
from jax.sharding import Mesh, PartitionSpec as P

D = 1536
QH = 12
KVH = 4
HEAD = 128
EXP_FF = 512
SH_FF = 1024
TOP = 6
MH = 48
HP = 64
STATE = 128
CK = 4
DI = 3072

bf16 = jnp.bfloat16
f32 = jnp.float32
epsilon = 1e-05
masked_value = -1e30
highest = lax.Precision.HIGHEST
ALL = ("dp", "w", "z", "core")
EX = ("w", "z", "core")
TP = ("z", "core")
FS = ("dp", "w")
SWAP = [(0, 1), (1, 0)]


def dot(a, b, dims, out=f32):
    r = lax.dot_general(a, b, (dims, ((), ())), preferred_element_type=f32)
    return r if out == f32 else r.astype(out)


def nn(a, b, out=f32):
    return dot(a, b, ((1,), (0,)), out)


def nt(a, b, out=f32):
    return dot(a, b, ((1,), (1,)), out)


def tn(a, b, out=f32):
    return dot(a, b, ((0,), (0,)), out)


def ring(shift, axis="z"):
    n = lax.axis_size(axis)
    return [(i, (i + shift) % n) for i in range(n)]


def wide(x):
    parts = [x] + [lax.ppermute(x, "w", ring(s, "w")) for s in range(1, lax.axis_size("w"))]
    return parts[0] if len(parts) == 1 else jnp.concatenate(parts, axis=0)


def narrow(total):
    n = lax.axis_size("w")
    rows = total.shape[0] // n
    out = total[:rows]
    for s in range(1, n):
        part = total[s * rows : (s + 1) * rows].astype(bf16)
        out = out + lax.ppermute(part, "w", ring(-s, "w")).astype(f32)
    return out


def add_first(total, part):
    rows = part.shape[0]
    if rows == total.shape[0]:
        return total + part
    return jnp.concatenate([total[:rows] + part, total[rows:]], axis=0)


def fence(*trees):
    if lax.axis_size("w") > 1:
        return trees
    return lax.optimization_barrier(trees)


def by_rows(x):
    if lax.axis_size("w") > 1:
        return x
    return with_layout_constraint(x, Layout(major_to_minor=tuple(range(x.ndim))))


def send(x, axis, pairs):
    return by_rows(lax.ppermute(by_rows(x), axis, pairs))


def gather_rows(x):
    n = lax.axis_size("z")
    parts = [x] + [send(x, "z", ring(s)) for s in range(1, n)]
    mine = by_rows(jnp.concatenate(parts, axis=0))
    return by_rows(jnp.concatenate([mine, send(mine, "core", SWAP)], axis=0))


def return_rows(total):
    n = lax.axis_size("z")
    half = total.shape[0] // 2
    rows = half // n
    recv = send(total[half:].astype(bf16), "core", SWAP)
    mine = total[:half] + recv.astype(f32)
    out = mine[:rows]
    for s in range(1, n):
        part = mine[s * rows : (s + 1) * rows].astype(bf16)
        out = out + send(part, "z", ring(-s)).astype(f32)
    return out


def pair_gather(x):
    return by_rows(jnp.concatenate([x, send(x, "core", SWAP)], axis=0))


def pair_return(total):
    half = total.shape[0] // 2
    recv = send(total[half:].astype(bf16), "core", SWAP)
    return total[:half] + recv.astype(f32)


def split_two(x):
    high = x.astype(bf16)
    return [high, (x - high.astype(f32)).astype(bf16)]


def row_scale(values):
    return lax.rsqrt(jnp.mean(values * values, axis=-1, keepdims=True) + epsilon)


def rms_forward(values, gain):
    scale = row_scale(values)
    normed = values * scale
    return normed, scale, (normed * gain).astype(bf16)


def rms_backward(grad_result, normed, scale, gain):
    grad_gain = jnp.sum(grad_result * normed, axis=0)
    grad_normed = grad_result * gain
    grad_values = scale * (
        grad_normed - normed * jnp.mean(grad_normed * normed, axis=-1, keepdims=True)
    )
    return grad_values, grad_gain


def lanes(parts, width):
    used = sum(p.shape[-1] for p in parts)
    rows = parts[0].shape[0]
    if used < width:
        parts = parts + [jnp.zeros((rows, width - used), bf16)]
    return jnp.concatenate(parts, axis=1)


def scan_core(proj, step_raw, seg_col, seg_row, taps, bias, heads_par):
    length = proj.shape[0]
    chan = proj.shape[1] - 2 * STATE
    chan = chan // 2
    z = proj[:, :chan].astype(f32)
    conv_in = proj[:, chan:].astype(f32)
    place = lax.broadcasted_iota(jnp.int32, (length, 1), 0)
    shifted, masks = [], []
    conv_sum = bias
    for k in range(CK):
        if k == 0:
            moved, mask = conv_in, None
            conv_sum = conv_sum + taps[0:1] * moved
        else:
            same = pltpu.roll(seg_col, k, 0) == seg_col
            mask = jnp.where(same & (place >= k), 1.0, 0.0)
            moved = pltpu.roll(conv_in, k, 0) * mask
            conv_sum = conv_sum + taps[k : k + 1] * moved
        shifted.append(moved)
        masks.append(mask)
    logistic = jax.nn.sigmoid(conv_sum)
    act = conv_sum * logistic
    pre = step_raw + heads_par[0:1]
    step = jnp.maximum(pre, 0.0) + jnp.log1p(jnp.exp(-jnp.abs(pre)))
    decay_rate = heads_par[1:2]
    rows_pos = lax.broadcasted_iota(jnp.int32, (length, length), 0)
    cols_pos = lax.broadcasted_iota(jnp.int32, (length, length), 1)
    lower = jnp.where(cols_pos <= rows_pos, 1.0, 0.0)
    cum = lax.dot_general(
        lower, step * decay_rate, (((1,), (0,)), ((), ())), precision=highest, preferred_element_type=f32
    )
    allowed = (seg_col == seg_row) & (cols_pos <= rows_pos)
    b_low = act[:, chan : chan + STATE].astype(bf16)
    c_low = act[:, chan + STATE :].astype(bf16)
    cb = nt(c_low, b_low)
    return dict(
        chan=chan, z=z, conv_in=conv_in, shifted=shifted, masks=masks, conv_sum=conv_sum,
        logistic=logistic, act=act, pre=pre, step=step, rate=decay_rate, lower=lower, cum=cum,
        cum_t=cum.T, step_t=step.T, allowed=allowed, b=b_low, c=c_low, cb=cb,
    )


def head_table(s, h):
    gap = s["cum"][:, h : h + 1] - s["cum_t"][h : h + 1, :]
    decay = jnp.exp(jnp.where(s["allowed"], gap, masked_value))
    return decay, s["step_t"][h : h + 1, :]


def pair_scan(s, heads, low):
    lane = lax.broadcasted_iota(jnp.int32, (1, 2 * HP), 1)
    blocks, mixes, tables = [], [], []
    for j in range(heads // 2):
        both = low[:, j * 2 * HP : (j + 1) * 2 * HP]
        outs = []
        for h in (2 * j, 2 * j + 1):
            decay, step_row = head_table(s, h)
            mix = (decay * s["cb"] * step_row).astype(bf16)
            outs.append(nn(mix, both))
            mixes.append(mix)
            tables.append((decay, step_row))
        blocks.append(jnp.where(lane < HP, outs[0], outs[1]))
    return jnp.concatenate(blocks, axis=1), mixes, tables


def scan_forward_kernel(heads, proj_ref, step_ref, col_ref, row_ref, conv_ref, chan_ref, head_ref, gained_ref, square_ref):
    s = scan_core(
        proj_ref[...], step_ref[...], col_ref[...], row_ref[0], conv_ref[0:CK], conv_ref[CK : CK + 1], head_ref[...]
    )
    chan = s["chan"]
    inputs = s["act"][:, :chan]
    scan, _, _ = pair_scan(s, heads, inputs.astype(bf16))
    scan = scan + chan_ref[1:2] * inputs
    gated = scan * s["z"] * jax.nn.sigmoid(s["z"])
    gained_ref[...] = (gated * chan_ref[0:1]).astype(bf16)
    square_ref[...] = jnp.broadcast_to(jnp.sum(gated * gated, axis=1, keepdims=True), square_ref.shape)


def scan_backward_kernel(
    heads, proj_ref, step_ref, col_ref, row_ref, conv_ref, chan_ref, head_ref, grad_ref, extra_ref,
    dproj_ref, dconv_ref, dchan_ref, dhead_ref, flat_ref,
):
    @pl.when(pl.program_id(0) == 0)
    def _():
        dconv_ref[...] = jnp.zeros_like(dconv_ref)
        dchan_ref[...] = jnp.zeros_like(dchan_ref)
        dhead_ref[...] = jnp.zeros_like(dhead_ref)

    taps = conv_ref[0:CK]
    s = scan_core(proj_ref[...], step_ref[...], col_ref[...], row_ref[0], taps, conv_ref[CK : CK + 1], head_ref[...])
    chan, length = s["chan"], s["z"].shape[0]
    gain, skip = chan_ref[0:1], chan_ref[1:2]
    inputs = s["act"][:, :chan]
    low = inputs.astype(bf16)
    scan, mixes, tables = pair_scan(s, heads, low)
    scan = scan + skip * inputs
    z = s["z"]
    sig = jax.nn.sigmoid(z)
    silu = z * sig
    gated = scan * silu
    extra = extra_ref[...].astype(f32)
    scale = extra[:, 0:1] + extra[:, 1:2]
    mean = extra[:, 2:3] + extra[:, 3:4]
    grad = grad_ref[...].astype(f32)
    normed = gated * scale
    d_gated = scale * (grad * gain - normed * mean)
    d_scan = d_gated * silu
    d_z = d_gated * scan * sig * (1.0 + z * (1.0 - sig))
    d_low = d_scan.astype(bf16)
    lane = lax.broadcasted_iota(jnp.int32, (1, 2 * HP), 1)
    spot = lax.broadcasted_iota(jnp.int32, (1, s["step"].shape[1]), 1)
    d_cb = jnp.zeros((length, length), f32)
    d_cum = jnp.zeros(s["step"].shape, f32)
    flat_ref[...] = jnp.zeros_like(flat_ref)
    blocks = []
    for j in range(heads // 2):
        cut = slice(j * 2 * HP, (j + 1) * 2 * HP)
        both, d_both = low[:, cut], d_low[:, cut]
        outs = []
        for i, h in enumerate((2 * j, 2 * j + 1)):
            decay, step_row = tables[h]
            outs.append(tn(mixes[h], d_both))
            keep = (lane < HP) if i == 0 else (lane >= HP)
            d_mix = nt(jnp.where(keep, d_both, jnp.zeros_like(d_both)), both)
            part = d_mix * decay
            d_cb = d_cb + part * step_row
            part = part * s["cb"]
            flat_ref[h : h + 1, 0:length] = jnp.sum(part, axis=0, keepdims=True)
            column = jnp.sum(part * step_row, axis=1, keepdims=True)
            d_cum = d_cum + jnp.where(spot == h, column, 0.0)
        blocks.append(jnp.where(lane < HP, outs[0], outs[1]))
    d_inputs = jnp.concatenate(blocks, axis=1) + skip * d_scan
    from_rows = flat_ref[...].T[0:length]
    d_cum = d_cum - s["step"] * from_rows
    d_rate = lax.dot_general(
        s["lower"], d_cum, (((0,), (0,)), ((), ())), precision=highest, preferred_element_type=f32
    )
    d_step = from_rows + d_rate * s["rate"]
    d_pre = jnp.where(spot < heads, d_step * jax.nn.sigmoid(s["pre"]), 0.0)
    d_cb_low = d_cb.astype(bf16)
    d_act = jnp.concatenate([d_inputs, tn(d_cb_low, s["c"]), nn(d_cb_low, s["b"])], axis=1)
    logistic = s["logistic"]
    d_sum = d_act * logistic * (1.0 + s["conv_sum"] * (1.0 - logistic))
    d_in = taps[0:1] * d_sum
    for k in range(1, CK):
        back = d_sum * s["masks"][k] * taps[k : k + 1]
        d_in = d_in + pltpu.roll(back, length - k, 0)
    dproj_ref[...] = jnp.concatenate([d_z, d_in, d_pre], axis=1).astype(bf16)
    for k in range(CK):
        dconv_ref[k : k + 1] += jnp.sum(d_sum * s["shifted"][k], axis=0, keepdims=True)
    dconv_ref[CK : CK + 1] += jnp.sum(d_sum, axis=0, keepdims=True)
    dchan_ref[0:1] += jnp.sum(grad * normed, axis=0, keepdims=True)
    dchan_ref[1:2] += jnp.sum(d_scan * inputs, axis=0, keepdims=True)
    dhead_ref[0:1] += jnp.sum(d_pre, axis=0, keepdims=True)
    dhead_ref[1:2] += jnp.sum(d_rate * s["step"] * s["rate"], axis=0, keepdims=True)


def scan_specs(length, width, lanes_, conv, chan):
    def whole(shape):
        return pl.BlockSpec(shape, lambda i: (0,) * len(shape))

    rows = lambda w: pl.BlockSpec((length, w), lambda i: (i, 0))
    return rows, whole, [
        rows(width), rows(lanes_), rows(1), pl.BlockSpec((1, 1, length), lambda i: (i, 0, 0)),
        whole((8, conv)), whole((8, chan)), whole((8, lanes_)),
    ]


def scan_forward(heads, length, proj, step, seg_col, seg_row, conv_par, chan_par, head_par):
    total, width = proj.shape
    chan = heads * HP
    rows, whole, specs = scan_specs(length, width, step.shape[1], width - chan, chan)
    return pl.pallas_call(
        functools.partial(scan_forward_kernel, heads),
        grid=(total // length,),
        in_specs=specs,
        out_specs=[rows(chan), rows(128)],
        out_shape=[jax.ShapeDtypeStruct((total, chan), bf16), jax.ShapeDtypeStruct((total, 128), f32)],
        compiler_params=pltpu.CompilerParams(vmem_limit_bytes=32 << 20),
        name="scan_forward",
    )(proj, step, seg_col, seg_row, conv_par, chan_par, head_par)


def scan_backward(heads, length, proj, step, seg_col, seg_row, conv_par, chan_par, head_par, grad, extra):
    total, width = proj.shape
    chan = heads * HP
    lanes_ = step.shape[1]
    rows, whole, specs = scan_specs(length, width, lanes_, width - chan, chan)
    return pl.pallas_call(
        functools.partial(scan_backward_kernel, heads),
        grid=(total // length,),
        in_specs=specs + [rows(chan), rows(128)],
        out_specs=[rows(width + lanes_), whole((8, width - chan)), whole((8, chan)), whole((8, lanes_))],
        out_shape=[
            jax.ShapeDtypeStruct((total, width + lanes_), bf16),
            jax.ShapeDtypeStruct((8, width - chan), f32),
            jax.ShapeDtypeStruct((8, chan), f32),
            jax.ShapeDtypeStruct((8, lanes_), f32),
        ],
        scratch_shapes=[pltpu.VMEM((128, 128), f32)],
        compiler_params=pltpu.CompilerParams(vmem_limit_bytes=32 << 20),
        name="scan_backward",
    )(proj, step, seg_col, seg_row, conv_par, chan_par, head_par, grad, extra)


def swiglu(gate, up):
    return gate * jax.nn.sigmoid(gate) * up


def swiglu_back(grad, gate, up):
    logistic = jax.nn.sigmoid(gate)
    grad_gate = grad * up * logistic * (1.0 + gate * (1.0 - logistic))
    return grad_gate.astype(bf16), (grad * gate * logistic).astype(bf16)


def gate_table(moe_in, mask, router):
    logits = nn(moe_in, router)
    picked = jnp.where(mask, logits, masked_value)
    peak = jnp.max(picked, axis=-1, keepdims=True)
    ex = jnp.where(mask, jnp.exp(picked - peak), 0.0)
    return ex / jnp.sum(ex, axis=-1, keepdims=True)


def unit_gates(local, units):
    count = local.shape[1]
    owner = lax.broadcasted_iota(jnp.int32, (1, units), 1) // EXP_FF
    spread = local[:, count - 1 :]
    for e in range(count - 1):
        spread = jnp.where(owner == e, local[:, e : e + 1], spread)
    return spread, owner


def moe_forward(own_in, mask, w):
    rows = own_in.shape[0]
    base_in = gather_rows(own_in)
    moe_in = wide(base_in)
    gates = gate_table(moe_in, mask, w["router"])
    units = w["expert_down"].shape[0]
    count = units // EXP_FF
    first = lax.axis_index(EX) * count
    local = lax.dynamic_slice(gates, (0, first), (gates.shape[0], count))
    pre = nn(moe_in, w["expert_in"], bf16)
    pre_s = nn(base_in, w["shared_in"], bf16)
    pre, pre_s = lax.optimization_barrier((pre, pre_s))
    p = pre.astype(f32)
    spread, _ = unit_gates(local, units)
    hid = (swiglu(p[:, :units], p[:, units:]) * spread).astype(bf16)
    half = pre_s.shape[1] // 2
    p = pre_s.astype(f32)
    hid_s = swiglu(p[:, :half], p[:, half:]).astype(bf16)
    total = add_first(nn(hid, w["expert_down"]), nt(hid_s, w["shared_down_t"]))
    return total, (moe_in, base_in, gates[:rows], local, pre, pre_s)


def moe_backward(base_z, kept, w, experts_total):
    moe_in, base_in, own_gates, local, pre, pre_s = kept
    pre, pre_s, _ = lax.optimization_barrier((pre, pre_s, base_z))
    grad_z = wide(base_z)
    units = w["expert_down"].shape[0]
    count = units // EXP_FF
    first = lax.axis_index(EX) * count
    spread, owner = unit_gates(local, units)
    p = pre.astype(f32)
    gate, up = p[:, :units], p[:, units:]
    grad_hid = nt(grad_z, w["expert_down"])
    act = swiglu(gate, up)
    hidden = (act * spread).astype(bf16)
    product = grad_hid * act
    lane = lax.broadcasted_iota(jnp.int32, (1, experts_total), 1)
    table = jnp.zeros((grad_z.shape[0], experts_total), f32)
    for e in range(count):
        mine = jnp.sum(jnp.where(owner == e, product, 0.0), axis=-1, keepdims=True)
        table = table + local[:, e : e + 1] * mine * (lane == first + e).astype(f32)
    g_gate, g_up = swiglu_back(grad_hid * spread, gate, up)
    g_pre = jnp.concatenate([g_gate, g_up], axis=1)
    total = nt(g_pre, w["expert_in"])
    half = pre_s.shape[1] // 2
    p = pre_s.astype(f32)
    grad_hid = nn(base_z, w["shared_down_t"])
    hid_s = swiglu(p[:, :half], p[:, half:]).astype(bf16)
    g_gate, g_up = swiglu_back(grad_hid, p[:, :half], p[:, half:])
    g_pre_s = jnp.concatenate([g_gate, g_up], axis=1)
    total = add_first(total, nt(g_pre_s, w["shared_in"]))
    extra = -(-experts_total // 128) * 128
    table = jnp.pad(table, ((0, 0), (0, extra - experts_total)))
    back = return_rows(narrow(jnp.concatenate([total, table], axis=1)))
    side = (moe_in, grad_z, hidden, hid_s, g_pre, g_pre_s, base_in, base_z)
    return back, side


def moe_finish(back, kept, w, experts_total):
    own_gates = kept[2]
    weighted = back[:, D : D + experts_total]
    grad_logits = weighted - own_gates * jnp.sum(weighted, axis=-1, keepdims=True)
    grad_logits = grad_logits.astype(bf16)
    return back[:, :D] + nt(grad_logits, w["router"]), grad_logits


def tn_sum(pairs, out=bf16):
    if lax.axis_size("w") > 1:
        return tn(*[jnp.concatenate(side, axis=0) for side in zip(*pairs)], out)
    total = None
    for a, b in pairs:
        part = tn(a, b)
        total = part if total is None else total + part
    return total.astype(out)


def moe_weight_grads(sides):
    g_down = tn_sum([(s[2], s[1]) for s in sides])
    g_in = tn_sum([(s[0], s[4]) for s in sides])
    g_sin = tn_sum([(s[6], s[5]) for s in sides])
    g_sdown_t = tn_sum([(s[7], s[3]) for s in sides])
    return g_in, g_down, g_sin, g_sdown_t


def attn_mask(seg):
    length = seg.shape[1]
    rows_pos = lax.broadcasted_iota(jnp.int32, (length, length), 0)
    cols_pos = lax.broadcasted_iota(jnp.int32, (length, length), 1)
    return (seg[:, :, None] == seg[:, None, :]) & (cols_pos <= rows_pos)[None]


def attn_forward(own_in, allowed, w_qkv, w_out_t):
    seqs, length, _ = allowed.shape
    kv = KVH // 2
    group = QH // KVH
    q_width = kv * group * HEAD
    kv_width = kv * HEAD
    attn_in = pair_gather(own_in)
    packed = nn(attn_in, w_qkv, bf16)
    q = packed[:, :q_width].reshape(seqs, length, kv, group, HEAD)
    k = packed[:, q_width : q_width + kv_width].reshape(seqs, length, kv, HEAD)
    v = packed[:, q_width + kv_width :].reshape(seqs, length, kv, HEAD)
    scores = jnp.einsum("bqhgd,bkhd->bhgqk", q, k, preferred_element_type=f32) * HEAD**-0.5
    scores = jnp.where(allowed[:, None, None], scores, masked_value)
    peak = jnp.max(scores, axis=-1, keepdims=True)
    ex = jnp.exp(scores - peak)
    probs = ex / jnp.sum(ex, axis=-1, keepdims=True)
    context = jnp.einsum("bhgqk,bkhd->bqhgd", probs.astype(bf16), v, preferred_element_type=f32)
    context = context.reshape(seqs * length, q_width).astype(bf16)
    branch = pair_return(nt(context, w_out_t))
    return branch, (attn_in, q, k, v, probs, context)


def attn_backward(own_grad, kept, w_qkv, w_out_t):
    attn_in, q, k, v, probs, context = kept
    seqs, length, kv, group, _ = q.shape
    grad = pair_gather(own_grad)
    grad_context = nn(grad, w_out_t, bf16).reshape(seqs, length, kv, group, HEAD)
    probs_low = probs.astype(bf16)
    grad_v = jnp.einsum("bhgqk,bqhgd->bkhd", probs_low, grad_context, preferred_element_type=f32)
    grad_p = jnp.einsum("bqhgd,bkhd->bhgqk", grad_context, v, preferred_element_type=f32)
    delta = jnp.sum(probs * grad_p, axis=-1, keepdims=True)
    grad_s = (probs * (grad_p - delta)).astype(bf16)
    scale = HEAD**-0.5
    grad_q = jnp.einsum("bhgqk,bkhd->bqhgd", grad_s, k, preferred_element_type=f32) * scale
    grad_k = jnp.einsum("bhgqk,bqhgd->bkhd", grad_s, q, preferred_element_type=f32) * scale
    rows = seqs * length
    grad_packed = jnp.concatenate(
        [grad_q.reshape(rows, -1), grad_k.reshape(rows, -1), grad_v.reshape(rows, -1)], axis=1
    ).astype(bf16)
    grad_in = pair_return(nt(grad_packed, w_qkv))
    return grad_in, (attn_in, grad_packed, context, grad)


def by_owner(x, count):
    return x.reshape(x.shape[0], count, x.shape[1] // count)


def body(
    tokens,
    segments,
    routes,
    norm_mamba,
    w_in,
    w_dt,
    conv_w,
    conv_b,
    dt_bias,
    a_log,
    skip_scale,
    gate_norm,
    w_mix_out,
    norm_moe_m,
    router_m,
    shared_in_m,
    shared_down_m,
    expert_in_m,
    expert_down_m,
    norm_attn,
    w_qkv,
    w_out,
    norm_moe,
    router,
    shared_in,
    shared_down,
    expert_in,
    expert_down,
    cotangent,
):
    batches, length, _ = tokens.shape
    micro = batches if lax.axis_size("w") > 1 else 1
    seqs = batches // micro
    own_rows = seqs * length
    tokens = tokens.reshape(micro, own_rows, D)
    cotangent = cotangent.reshape(micro, own_rows, D)
    routes = routes.reshape(2, micro, own_rows, TOP)
    segments = segments.reshape(micro, own_rows)
    n_tp = lax.axis_size("z") * lax.axis_size("core")
    n_ex = lax.axis_size("w") * n_tp
    n_all = lax.axis_size("dp") * n_ex
    rows = w_in.shape[0]
    local_experts = expert_in.shape[0]
    experts_total = local_experts * n_ex
    heads = MH // n_tp
    chan = heads * HP
    ff = SH_FF // n_tp
    slot = lax.axis_index(TP)
    conv_total = DI + 2 * STATE
    conv_here = conv_w.shape[1]
    gate_here = gate_norm.shape[0]
    vec_len = gate_here + (CK + 1) * conv_here
    vec_cols = -(-vec_len // rows)
    small_cols = 4 + 2 * experts_total + vec_cols
    step_width = -(-(heads + small_cols) // 128) * 128

    vec = jnp.concatenate([gate_norm, conv_b, conv_w.reshape(-1)])
    vec = jnp.pad(vec, (0, rows * vec_cols - vec_len)).reshape(rows, vec_cols)
    gains_own = jnp.stack([norm_mamba, norm_moe_m, norm_attn, norm_moe], axis=1)
    little = jnp.concatenate([gains_own, router_m, router, vec], axis=1)

    def for_all(x):
        return jnp.broadcast_to(x[:, None], (rows, n_tp, x.shape[1]))

    def moved_columns(parts, *after):
        packed = jnp.concatenate(parts, axis=2).transpose(1, 0, 2)
        packed = fence(packed, *after)[0]
        moved = lax.all_to_all(packed, TP, split_axis=0, concat_axis=0, tiled=True)
        return moved.reshape(n_tp * rows, -1)

    def whole_rows(moved):
        return lax.all_gather(moved, FS, axis=0, tiled=True)

    def shared_pack(w_sin, w_sdown):
        return [
            by_owner(w_sin[:, :SH_FF], n_tp),
            by_owner(w_sin[:, SH_FF:], n_tp),
            by_owner(w_sdown.T, n_tp),
        ]

    blank = jnp.zeros((rows, n_tp, step_width - heads - small_cols), bf16)
    moved_m = moved_columns(
        [
            by_owner(w_in[:, :DI], n_tp),
            by_owner(w_in[:, DI : 2 * DI], n_tp),
            for_all(w_in[:, 2 * DI :]),
            by_owner(w_dt, n_tp),
            for_all(little),
            blank,
            by_owner(w_mix_out.T, n_tp),
        ]
    )
    w_m = whole_rows(moved_m)

    expert_ids = jnp.arange(experts_total, dtype=jnp.int32)
    info_width = -(-(2 * experts_total + 1) // 128) * 128
    each = range(micro)
    rows_in = []
    for m in each:
        hot = [
            jnp.any(routes[b, m][:, :, None] == expert_ids, axis=1).astype(bf16) for b in range(2)
        ]
        info = lanes(hot + [segments[m][:, None].astype(bf16)], info_width)
        x_info, _ = fence(jnp.concatenate([tokens[m], info], axis=1), moved_m)
        rows_in.append(gather_rows(x_info))
    in_width = 2 * chan + 2 * STATE
    w_in_here = w_m[:, :in_width]
    moved_s = moved_columns(
        shared_pack(shared_in_m, shared_down_m) + shared_pack(shared_in, shared_down), rows_in
    )
    w_s = whole_rows(moved_s)
    at = in_width + step_width
    w_step = w_m[:, in_width:at]
    w_dt_here = w_step[:, :128]
    small_all = w_step[:, heads : heads + small_cols]
    gain_mamba, gain_moe_m, gain_attn, gain_moe = [small_all[:, i].astype(f32) for i in range(4)]
    router_m_full = small_all[:, 4 : 4 + experts_total]
    router_full = small_all[:, 4 + experts_total : 4 + 2 * experts_total]
    vec_all = small_all[:, 4 + 2 * experts_total :].reshape(n_all, rows * vec_cols).astype(f32)
    gain_gate = vec_all[:, :gate_here].reshape(DI)
    bias_all = vec_all[:, gate_here : gate_here + conv_here].reshape(conv_total)
    taps_all = vec_all[:, gate_here + conv_here : vec_len].reshape(n_all, CK, conv_here)
    taps_all = taps_all.transpose(1, 0, 2).reshape(CK, conv_total)

    def channels(full_row):
        mine = lax.dynamic_slice_in_dim(full_row, slot * chan, chan, axis=-1)
        return jnp.concatenate([mine, full_row[..., DI:]], axis=-1)

    taps = channels(taps_all)
    bias = channels(bias_all)
    gain_here = lax.dynamic_slice_in_dim(gain_gate, slot * chan, chan)
    dt_here = lax.dynamic_slice_in_dim(dt_bias, slot * heads, heads)
    log_here = lax.dynamic_slice_in_dim(a_log, slot * heads, heads)
    skip_here = lax.dynamic_slice_in_dim(skip_scale, slot * heads, heads)

    w_scan = w_m[:, : in_width + 128]
    w_mix_t = w_m[:, at:]

    def expert_weights(w_up, w_low):
        count = w_up.shape[0]
        cols = [w_up[e, :, :EXP_FF] for e in range(count)] + [w_up[e, :, EXP_FF:] for e in range(count)]
        cols = by_rows(jnp.concatenate(cols, axis=1))
        return (
            by_rows(lax.all_gather(cols, "dp", axis=0, tiled=True)),
            lax.all_gather(w_low, "dp", axis=1, tiled=True).reshape(-1, D),
        )

    expert_in_m, expert_down_m, _ = fence(expert_in_m, expert_down_m, moved_m)
    up_m, low_m = expert_weights(expert_in_m, expert_down_m)
    moe_m = {
        "router": router_m_full,
        "shared_in": w_s[:, : 2 * ff],
        "shared_down_t": w_s[:, 2 * ff : 3 * ff],
        "expert_in": up_m,
        "expert_down": low_m,
    }

    kv = KVH // 2
    q_width = QH // 2 * HEAD
    kv_width = kv * HEAD
    q_all, kv_all = QH * HEAD, KVH * HEAD
    up_a, low_a = expert_weights(expert_in, expert_down)
    moe_a = {
        "router": router_full,
        "shared_in": w_s[:, 3 * ff : 5 * ff],
        "shared_down_t": w_s[:, 5 * ff :],
        "expert_in": up_a,
        "expert_down": low_a,
    }

    def eight(parts):
        block = jnp.concatenate([p.reshape(-1, p.shape[-1]) for p in parts], axis=0)
        return jnp.pad(block, ((0, 8 - block.shape[0]), (0, 0)))

    conv_par = eight([taps, bias])
    chan_par = eight([gain_here, jnp.repeat(skip_here, HP)])
    head_par = jnp.pad(eight([dt_here, -jnp.exp(log_here)]), ((0, 0), (0, 128 - heads)))
    x_own = [tokens[m].astype(f32) for m in each]
    masks, allowed, mamba_kept, mix_kept, hidden_one = [], [], [], [], []
    proj_all, cot_all = [], []
    for m in each:
        rows_all = rows_in[m]
        x_all = rows_all[:, :D].astype(f32)
        marks = wide(rows_all[:, D : D + 2 * experts_total]) > 0.5
        masks.append([marks[:, :experts_total], marks[:, experts_total:]])
        seg_col = rows_all[:, D + 2 * experts_total :][:, :1].astype(f32)
        seg_row = seg_col.reshape(n_tp * seqs, 1, length)
        seg = seg_row[:, 0].astype(jnp.int32)
        middle = n_tp * seqs // 2
        pair = jnp.concatenate([seg[:seqs], seg[middle : middle + seqs]], axis=0)
        allowed.append(attn_mask(pair))

        x_all, _ = fence(x_all, w_m)
        _, scale_x, mamba_in = rms_forward(x_all, gain_mamba)
        total_rows = mamba_in.shape[0]
        proj = nn(mamba_in, w_in_here, bf16)
        dt_raw = nn(mamba_in, w_dt_here)
        proj_all.append(proj)
        pars = (seg_col, seg_row, conv_par, chan_par, head_par)
        gained, square = scan_forward(heads, length, proj, dt_raw, *pars)
        partial = nt(gained, w_mix_t)
        high = square.astype(bf16).astype(f32)
        lane = lax.broadcasted_iota(jnp.int32, square.shape, 1)
        extra = jnp.where(lane == 0, high, jnp.where(lane == 1, square - high, 0.0))
        back = return_rows(jnp.concatenate([partial, extra], axis=1))
        gate_scale = lax.rsqrt((back[:, D : D + 1] + back[:, D + 1 : D + 2]) / DI + epsilon)
        mix_branch = back[:, :D] * gate_scale
        hidden_one.append(x_own[m] + mix_branch)
        mamba_kept.append((rows_all, scale_x[:own_rows], mamba_in, (proj, dt_raw, *pars), gained))
        mix_kept.append((mix_branch, gate_scale))

    attn_pack = jnp.concatenate(
        [
            by_owner(w_qkv[:, :q_all], 2),
            by_owner(w_qkv[:, q_all : q_all + kv_all], 2),
            by_owner(w_qkv[:, q_all + kv_all :], 2),
            by_owner(w_out.T, 2),
        ],
        axis=2,
    ).transpose(1, 0, 2)
    attn_pack, _ = fence(attn_pack, moved_s)
    attn_pack = lax.all_to_all(attn_pack, "core", split_axis=0, concat_axis=0, tiled=True)
    own = attn_pack.reshape(2 * rows, -1)
    n_z = lax.axis_size("z")
    parts = [send(own, "z", ring(s)) for s in range(n_z - 1, 0, -1)] + [own]
    parts, _ = fence(parts, mamba_kept[-1][-1])
    twice = jnp.concatenate(parts + parts, axis=0)
    start = (n_z - 1 - lax.axis_index("z")) * 2 * rows
    attn_w = lax.dynamic_slice(twice, (start, 0), (n_z * 2 * rows, own.shape[1]))
    attn_w = lax.all_gather(attn_w, FS, axis=0, tiled=True)
    w_qkv_here = attn_w[:, : q_width + 2 * kv_width]
    w_out_t = attn_w[:, q_width + 2 * kv_width :]

    one_kept, layer_one = [], []
    for m in each:
        normed, scale, own = rms_forward(hidden_one[m], gain_moe_m)
        total, kept = moe_forward(own, masks[m][0], moe_m)
        layer_one.append(hidden_one[m] + return_rows(narrow(total)))
        one_kept.append((normed, scale, kept))
    attn_kept, hidden_two = [], []
    for m in each:
        cot, _ = fence(cotangent[m], layer_one[m])
        cot_all.append(gather_rows(cot))
        normed, scale, own = rms_forward(layer_one[m], gain_attn)
        branch, kept = attn_forward(own, allowed[m], w_qkv_here, w_out_t)
        hidden_two.append(layer_one[m] + branch)
        attn_kept.append((normed, scale, kept))
    two_kept, results = [], []
    for m in each:
        hidden_two[m], cot_all[m] = fence(hidden_two[m], cot_all[m])
        normed, scale, own = rms_forward(hidden_two[m], gain_moe)
        total, kept = moe_forward(own, masks[m][1], moe_a)
        results.append(total)
        two_kept.append((normed, scale, kept))

    gains = [0.0, 0.0, 0.0, 0.0]

    def up_over_dp(g):
        return lax.psum_scatter(g, "dp", scatter_dimension=0, tiled=True)

    def low_over_dp(g):
        g = g.reshape(local_experts, EXP_FF, D)
        return lax.psum_scatter(g, "dp", scatter_dimension=1, tiled=True)

    def expert_out(g_up, g_low):
        units = local_experts * EXP_FF
        cols = []
        for e in range(local_experts):
            low, high = e * EXP_FF, (e + 1) * EXP_FF
            pair = [g_up[:, low:high], g_up[:, units + low : units + high]]
            cols.append(jnp.concatenate(pair, axis=1).astype(f32))
        return jnp.stack(cols), g_low.astype(f32)

    saving = lax.axis_size("w") > 1

    def moe_stage(grads, kept_all, w, gain, *before):
        grads = list(grads)
        backs, sides, first_rows = [], [], []
        for m in each:
            back, side = moe_backward(grads[m], kept_all[m][2], w, experts_total)
            backs.append(back)
            sides.append(side)
            first_rows.append(side[6][:own_rows])
            if saving:
                newer = moe_weight_grads(sides[-1:])
                hold = (back, newer, grads[m + 1 :])
                backs[-1], newer, grads[m + 1 :] = lax.optimization_barrier(hold)
                weights = newer if m == 0 else [a + b for a, b in zip(weights, newer)]
        if not saving:
            weights = moe_weight_grads(sides)
            backs[-1], weights = lax.optimization_barrier((backs[-1], weights))
        backs[-1], before = fence(backs[-1], before)
        grad_gain = 0.0
        values, logits = [], []
        for m in each:
            normed, scale, kept = kept_all[m]
            grad_in, grad_logits = moe_finish(backs[m], kept, w, experts_total)
            logits.append(grad_logits)
            grad_values, part = rms_backward(grad_in, normed, scale, gain)
            grad_gain = grad_gain + part
            values.append(grad_values)
        g_router = tn_sum(list(zip(first_rows, logits)), f32)
        return values, weights, grad_gain, g_router, before

    values, (g_in_a, g_down_a, g_sin_a, g_sdown_a), gains[3], g_router, _ = moe_stage(
        cot_all, two_kept, moe_a, gain_moe
    )
    sum_in_a = up_over_dp(g_in_a)
    sum_down_a = low_over_dp(g_down_a)
    grad_two = [cotangent[m].astype(f32) + values[m] for m in each]
    for m in each:
        total, _ = fence(results[m], grad_two[m])
        results[m] = (hidden_two[m] + return_rows(narrow(total))).astype(bf16)

    grad_layer, sides = [], []
    attn_back = []
    for m in each:
        grad_in, side = attn_backward(
            grad_two[m].astype(bf16), attn_kept[m][2], w_qkv_here, w_out_t
        )
        attn_back.append(grad_in)
        sides.append(side)
    g_attn = by_rows(
        jnp.concatenate(
            [
                by_rows(tn_sum([(s[0], s[1]) for s in sides])),
                by_rows(tn_sum([(s[3], s[2]) for s in sides])),
            ],
            axis=1,
        )
    )
    attn_back[-1], g_attn = lax.optimization_barrier((attn_back[-1], g_attn))
    g_attn = lax.psum_scatter(g_attn, FS, scatter_dimension=0, tiled=True)
    g_part = g_attn
    for m in each:
        normed, scale, _ = attn_kept[m]
        grad_values, part = rms_backward(attn_back[m], normed, scale, gain_attn)
        gains[2] = gains[2] + part
        grad_layer.append(grad_two[m] + grad_values)

    values, (g_in_m, g_down_m, g_sin_m, g_sdown_m), gains[1], g_router_m, before = moe_stage(
        [gather_rows(g.astype(bf16)) for g in grad_layer],
        one_kept,
        moe_m,
        gain_moe_m,
        sum_in_a,
        sum_down_a,
        g_part,
    )
    sum_in_a, sum_down_a, g_part = before
    out_expert_in, out_expert_down = expert_out(sum_in_a, sum_down_a)
    sum_in_m = up_over_dp(g_in_m)
    sum_down_m = low_over_dp(g_down_m)
    grad_one = [grad_layer[m] + values[m] for m in each]

    def attn_owner(g_part, *after):
        blocks = fence(g_part, *after)[0].reshape(n_z, 2 * rows, -1)
        here = lax.axis_index("z")
        own = lax.dynamic_index_in_dim(blocks, here, 0, keepdims=False)
        sent = []
        for shift in range(1, n_z):
            block = lax.dynamic_index_in_dim(blocks, (here + shift) % n_z, 0, keepdims=False)
            sent.append(send(block, "z", ring(shift)))
        return own, sent

    def attn_total(own, sent):
        total = own.astype(f32)
        for block in sent:
            total = total + block.astype(f32)
        return lax.all_to_all(
            total.astype(bf16).reshape(2, rows, -1), "core", split_axis=0, concat_axis=0, tiled=True
        ).astype(f32)

    small = None
    mamba_sides, mamba_back, mixes, own_normed = [], [], [], []
    for m in each:
        mix_branch, gate_scale = mix_kept[m]
        x_rows, _, mamba_in, scan_args, _ = mamba_kept[m]
        x_rows, _ = fence(x_rows, grad_one[m])
        x_rows = x_rows[:, :D].astype(f32)
        normed_x = x_rows * row_scale(x_rows)
        own_normed.append(normed_x[:own_rows])
        grad_mix = grad_one[m].astype(bf16)
        mean_term = jnp.sum(grad_mix.astype(f32) * mix_branch, axis=-1, keepdims=True) / DI
        extra = lanes(split_two(gate_scale) + split_two(mean_term), 128)
        rows_all = gather_rows(jnp.concatenate([grad_mix, extra], axis=1))
        if m == micro - 1:
            rows_all, out_expert_in, out_expert_down = fence(
                rows_all, out_expert_in, out_expert_down
            )
        mix_all = rows_all[:, :D]
        extra_all = rows_all[:, D:]
        scale_all = extra_all[:, 0:1].astype(f32) + extra_all[:, 1:2].astype(f32)
        scaled_mix = (mix_all.astype(f32) * scale_all).astype(bf16)
        mixes.append(scaled_mix)
        if m == micro - 1:
            g_mix = tn_sum([(x, k[4]) for x, k in zip(mixes, mamba_kept)])
            mix_all, g_mix = fence(mix_all, by_rows(g_mix))
        if m == micro - 1:
            attn_sent = attn_owner(g_part, mix_all)
        grad_gated = nn(mix_all, w_mix_t, bf16)
        grad_scan, *grads = scan_backward(
            heads, length, *scan_args, grad_gated, extra_all
        )
        if m == micro - 1:
            grad_scan, attn_sent = fence(grad_scan, attn_sent)
        mamba_sides.append((mamba_in, grad_scan))
        small = grads if small is None else [a + b for a, b in zip(small, grads)]
        total = nt(grad_scan, w_scan)
        gains[0] = gains[0] + jnp.sum(total * normed_x, axis=0)
        mamba_back.append(return_rows(total))

    g_attn = attn_total(*attn_sent)

    def rows_back(packed):
        packed = lax.psum_scatter(packed, FS, scatter_dimension=0, tiled=True)
        return lax.all_to_all(
            packed.reshape(n_tp, rows, -1), TP, split_axis=0, concat_axis=0, tiled=True
        ).astype(f32)

    def owned(block):
        return block.transpose(1, 0, 2).reshape(rows, -1)

    g_s = rows_back(
        jnp.concatenate([g_mix, g_sin_m, g_sdown_m, g_sin_a, g_sdown_a], axis=1)
    )

    g_scan = by_rows(tn_sum(mamba_sides, f32))
    g_scan, sum_in_m, sum_down_m = fence(g_scan, sum_in_m, sum_down_m)
    out_expert_in_m, out_expert_down_m = expert_out(sum_in_m, sum_down_m)

    conv_sums, chan_sums, head_sums = small
    g_gate = chan_sums[0]
    g_skip = jnp.sum(chan_sums[1].reshape(heads, HP), axis=1)
    head_grad = jnp.stack([head_sums[0, :heads], head_sums[1, :heads], g_skip])

    def spread(part, width):
        zeros = jnp.zeros(part.shape[:-1] + (width,), f32)
        return lax.dynamic_update_slice_in_dim(zeros, part[..., :chan], slot * chan, axis=-1)

    conv_grad = jnp.concatenate([conv_sums[CK : CK + 1], conv_sums[:CK]], axis=0)
    conv_grad = spread(conv_grad, conv_total) + jnp.pad(conv_grad[:, chan:], ((0, 0), (DI, 0)))
    conv_grad = conv_grad.reshape(CK + 1, n_all, conv_here).transpose(1, 0, 2).reshape(n_all, -1)
    vec_grad = jnp.concatenate([spread(g_gate, DI).reshape(n_all, gate_here), conv_grad], axis=1)
    vec_grad = jnp.pad(vec_grad, ((0, 0), (0, rows * vec_cols - vec_len))).reshape(D, vec_cols)
    little = jnp.concatenate([g[:, None] for g in gains] + [g_router_m, g_router, vec_grad], axis=1)
    after = step_width - heads - small_cols
    g_scan = jnp.pad(g_scan, ((0, 0), (0, step_width - 128)))
    g_m = rows_back((g_scan + jnp.pad(little, ((0, 0), (in_width + heads, after)))).astype(bf16))
    mamba_back[-1], g_s = fence(mamba_back[-1], g_s)
    grads_in = []
    for m in each:
        scale_x = mamba_kept[m][1]
        grad_values, _ = rms_backward(mamba_back[m], own_normed[m], scale_x, gain_mamba)
        grads_in.append(grad_one[m] + grad_values)

    out_w_in = jnp.concatenate(
        [
            owned(g_m[:, :, :chan]),
            owned(g_m[:, :, chan : 2 * chan]),
            jnp.sum(g_m[:, :, 2 * chan : in_width], axis=0),
        ],
        axis=1,
    )
    out_mix = owned(g_s[:, :, :chan]).T
    out_w_dt = owned(g_m[:, :, in_width : in_width + heads])
    little = jnp.sum(g_m[:, :, in_width + heads : in_width + heads + small_cols], axis=0)
    vec = little[:, 4 + 2 * experts_total :].reshape(-1)
    out_gate = vec[:gate_here]
    out_conv_b = vec[gate_here : gate_here + conv_here]
    out_conv_w = vec[gate_here + conv_here : vec_len].reshape(CK, conv_here)

    head_grad = lax.dynamic_update_slice(jnp.zeros((8, 128), f32), head_grad, (0, slot * heads))
    for axis in ALL:
        size = lax.axis_size(axis)
        step = 1
        while step < size:
            pairs = [(i, i ^ step) for i in range(size)]
            head_grad = head_grad + send(head_grad, axis, pairs)
            step *= 2
    head_grad = head_grad[:3, :MH]

    cuts = (q_width, q_width + kv_width, q_width + 2 * kv_width)
    out_w_qkv = jnp.concatenate(
        [
            owned(g_attn[:, :, : cuts[0]]),
            owned(g_attn[:, :, cuts[0] : cuts[1]]),
            owned(g_attn[:, :, cuts[1] : cuts[2]]),
        ],
        axis=1,
    )
    out_w_out = owned(g_attn[:, :, cuts[2] :]).T

    def shared_out(block):
        g_sin = jnp.concatenate([owned(block[:, :, :ff]), owned(block[:, :, ff : 2 * ff])], axis=1)
        return g_sin, owned(block[:, :, 2 * ff :]).T

    out_sin_m, out_sdown_m = shared_out(g_s[:, :, chan : chan + 3 * ff])
    out_sin, out_sdown = shared_out(g_s[:, :, chan + 3 * ff :])

    return (
        jnp.stack(results).reshape(batches, length, D),
        jnp.stack(grads_in).reshape(batches, length, D),
        little[:, 0],
        out_w_in,
        out_w_dt,
        out_conv_w,
        out_conv_b,
        head_grad[0],
        head_grad[1],
        head_grad[2],
        out_gate,
        out_mix,
        little[:, 1],
        little[:, 4 : 4 + experts_total],
        out_sin_m,
        out_sdown_m,
        out_expert_in_m,
        out_expert_down_m,
        little[:, 2],
        out_w_qkv,
        out_w_out,
        little[:, 3],
        little[:, 4 + experts_total : 4 + 2 * experts_total],
        out_sin,
        out_sdown,
        out_expert_in,
        out_expert_down,
    )


def solution(mesh):
    n_dp, n_ex = mesh.shape["dp"], mesh.shape["expert"]
    outer = n_ex // 8
    fine = Mesh(mesh.devices.reshape(n_dp, outer, 4, 2), ALL)
    split = P(ALL)
    row = P(ALL, None)
    col = P(None, ALL)
    mid = P(None, ALL, None)
    part = P(EX, "dp", None)
    same = P()
    return jax.shard_map(
        body,
        mesh=fine,
        in_specs=(
            mid,
            mid,
            P(None, None, ALL, None),
            split,
            row,
            row,
            col,
            split,
            same,
            same,
            same,
            split,
            col,
            split,
            row,
            row,
            col,
            part,
            part,
            split,
            row,
            col,
            split,
            row,
            row,
            col,
            part,
            part,
            mid,
        ),
        out_specs=(
            mid,
            mid,
            split,
            row,
            row,
            col,
            split,
            same,
            same,
            same,
            split,
            col,
            split,
            row,
            row,
            col,
            part,
            part,
            split,
            row,
            col,
            split,
            row,
            row,
            col,
            part,
            part,
        ),
        check_vma=False,
    )
```

```python
import functools

import jax
import jax.numpy as jnp
from jax import lax
from jax.experimental import pallas as pl
from jax.experimental.pallas import tpu as pltpu
from jax.experimental.layout import Layout, with_layout_constraint
from jax.sharding import Mesh, PartitionSpec as P

D = 1536
QH = 12
KVH = 4
HEAD = 128
EXP_FF = 512
SH_FF = 1024
TOP = 6
MH = 48
HP = 64
STATE = 128
CK = 4
DI = 3072

bf16 = jnp.bfloat16
f32 = jnp.float32
epsilon = 1e-05
masked_value = -1e30
highest = lax.Precision.HIGHEST
ALL = ("dp", "w", "z", "core")
EX = ("w", "z", "core")
TP = ("z", "core")
FS = ("dp", "w")
SWAP = [(0, 1), (1, 0)]


def dot(a, b, dims, out=f32):
    r = lax.dot_general(a, b, (dims, ((), ())), preferred_element_type=f32)
    return r if out == f32 else r.astype(out)


def nn(a, b, out=f32):
    return dot(a, b, ((1,), (0,)), out)


def nt(a, b, out=f32):
    return dot(a, b, ((1,), (1,)), out)


def tn(a, b, out=f32):
    return dot(a, b, ((0,), (0,)), out)


def ring(shift, axis="z"):
    n = lax.axis_size(axis)
    return [(i, (i + shift) % n) for i in range(n)]


def wide(x):
    parts = [x] + [lax.ppermute(x, "w", ring(s, "w")) for s in range(1, lax.axis_size("w"))]
    return parts[0] if len(parts) == 1 else jnp.concatenate(parts, axis=0)


def narrow(total):
    n = lax.axis_size("w")
    rows = total.shape[0] // n
    out = total[:rows]
    for s in range(1, n):
        part = total[s * rows : (s + 1) * rows].astype(bf16)
        out = out + lax.ppermute(part, "w", ring(-s, "w")).astype(f32)
    return out


def add_first(total, part):
    rows = part.shape[0]
    if rows == total.shape[0]:
        return total + part
    return jnp.concatenate([total[:rows] + part, total[rows:]], axis=0)


def fence(*trees):
    if lax.axis_size("w") > 1:
        return trees
    return lax.optimization_barrier(trees)


def by_rows(x):
    if lax.axis_size("w") > 1:
        return x
    return with_layout_constraint(x, Layout(major_to_minor=tuple(range(x.ndim))))


def send(x, axis, pairs):
    return by_rows(lax.ppermute(by_rows(x), axis, pairs))


def gather_start(x):
    return [x] + [send(x, "z", ring(s)) for s in range(1, lax.axis_size("z"))]


def gather_finish(parts):
    mine = by_rows(jnp.concatenate(parts, axis=0))
    return by_rows(jnp.concatenate([mine, send(mine, "core", SWAP)], axis=0))


def gather_rows(x):
    return gather_finish(gather_start(x))


def return_start(total):
    n = lax.axis_size("z")
    half = total.shape[0] // 2
    rows = half // n
    recv = send(total[half:].astype(bf16), "core", SWAP)
    mine = total[:half] + recv.astype(f32)
    sent = [
        send(mine[s * rows : (s + 1) * rows].astype(bf16), "z", ring(-s)) for s in range(1, n)
    ]
    return mine[:rows], sent


def return_finish(own, sent):
    for part in sent:
        own = own + part.astype(f32)
    return own


def return_rows(total):
    return return_finish(*return_start(total))


def pair_gather(x):
    return by_rows(jnp.concatenate([x, send(x, "core", SWAP)], axis=0))


def pair_return(total):
    half = total.shape[0] // 2
    recv = send(total[half:].astype(bf16), "core", SWAP)
    return total[:half] + recv.astype(f32)


def split_two(x):
    high = x.astype(bf16)
    return [high, (x - high.astype(f32)).astype(bf16)]


def row_scale(values):
    return lax.rsqrt(jnp.mean(values * values, axis=-1, keepdims=True) + epsilon)


def rms_forward(values, gain):
    scale = row_scale(values)
    normed = values * scale
    return normed, scale, (normed * gain).astype(bf16)


def rms_backward(grad_result, normed, scale, gain):
    grad_gain = jnp.sum(grad_result * normed, axis=0)
    grad_normed = grad_result * gain
    grad_values = scale * (
        grad_normed - normed * jnp.mean(grad_normed * normed, axis=-1, keepdims=True)
    )
    return grad_values, grad_gain


def lanes(parts, width):
    used = sum(p.shape[-1] for p in parts)
    rows = parts[0].shape[0]
    if used < width:
        parts = parts + [jnp.zeros((rows, width - used), bf16)]
    return jnp.concatenate(parts, axis=1)


def scan_core(proj, step_raw, seg_col, seg_row, taps, bias, heads_par):
    length = proj.shape[0]
    chan = proj.shape[1] - 2 * STATE
    chan = chan // 2
    z = proj[:, :chan].astype(f32)
    conv_in = proj[:, chan:].astype(f32)
    place = lax.broadcasted_iota(jnp.int32, (length, 1), 0)
    shifted, masks = [], []
    conv_sum = bias
    for k in range(CK):
        if k == 0:
            moved, mask = conv_in, None
            conv_sum = conv_sum + taps[0:1] * moved
        else:
            same = pltpu.roll(seg_col, k, 0) == seg_col
            mask = jnp.where(same & (place >= k), 1.0, 0.0)
            moved = pltpu.roll(conv_in, k, 0) * mask
            conv_sum = conv_sum + taps[k : k + 1] * moved
        shifted.append(moved)
        masks.append(mask)
    logistic = jax.nn.sigmoid(conv_sum)
    act = conv_sum * logistic
    pre = step_raw + heads_par[0:1]
    step = jnp.maximum(pre, 0.0) + jnp.log1p(jnp.exp(-jnp.abs(pre)))
    decay_rate = heads_par[1:2]
    rows_pos = lax.broadcasted_iota(jnp.int32, (length, length), 0)
    cols_pos = lax.broadcasted_iota(jnp.int32, (length, length), 1)
    lower = jnp.where(cols_pos <= rows_pos, 1.0, 0.0)
    cum = lax.dot_general(
        lower, step * decay_rate, (((1,), (0,)), ((), ())), precision=highest, preferred_element_type=f32
    )
    allowed = (seg_col == seg_row) & (cols_pos <= rows_pos)
    b_low = act[:, chan : chan + STATE].astype(bf16)
    c_low = act[:, chan + STATE :].astype(bf16)
    cb = nt(c_low, b_low)
    return dict(
        chan=chan, z=z, conv_in=conv_in, shifted=shifted, masks=masks, conv_sum=conv_sum,
        logistic=logistic, act=act, pre=pre, step=step, rate=decay_rate, lower=lower, cum=cum,
        cum_t=cum.T, step_t=step.T, allowed=allowed, b=b_low, c=c_low, cb=cb,
    )


def head_table(s, h):
    gap = s["cum"][:, h : h + 1] - s["cum_t"][h : h + 1, :]
    decay = jnp.exp(jnp.where(s["allowed"], gap, masked_value))
    return decay, s["step_t"][h : h + 1, :]


def pair_scan(s, heads, low):
    lane = lax.broadcasted_iota(jnp.int32, (1, 2 * HP), 1)
    blocks, mixes, tables = [], [], []
    for j in range(heads // 2):
        both = low[:, j * 2 * HP : (j + 1) * 2 * HP]
        outs = []
        for h in (2 * j, 2 * j + 1):
            decay, step_row = head_table(s, h)
            mix = (decay * s["cb"] * step_row).astype(bf16)
            outs.append(nn(mix, both))
            mixes.append(mix)
            tables.append((decay, step_row))
        blocks.append(jnp.where(lane < HP, outs[0], outs[1]))
    return jnp.concatenate(blocks, axis=1), mixes, tables


def scan_forward_kernel(heads, proj_ref, step_ref, col_ref, row_ref, conv_ref, chan_ref, head_ref, gained_ref, square_ref):
    s = scan_core(
        proj_ref[...], step_ref[...], col_ref[...], row_ref[0], conv_ref[0:CK], conv_ref[CK : CK + 1], head_ref[...]
    )
    chan = s["chan"]
    inputs = s["act"][:, :chan]
    scan, _, _ = pair_scan(s, heads, inputs.astype(bf16))
    scan = scan + chan_ref[1:2] * inputs
    gated = scan * s["z"] * jax.nn.sigmoid(s["z"])
    gained_ref[...] = (gated * chan_ref[0:1]).astype(bf16)
    square_ref[...] = jnp.broadcast_to(jnp.sum(gated * gated, axis=1, keepdims=True), square_ref.shape)


def scan_backward_kernel(
    heads, proj_ref, step_ref, col_ref, row_ref, conv_ref, chan_ref, head_ref, grad_ref, extra_ref,
    dproj_ref, dconv_ref, dchan_ref, dhead_ref, flat_ref,
):
    @pl.when(pl.program_id(0) == 0)
    def _():
        dconv_ref[...] = jnp.zeros_like(dconv_ref)
        dchan_ref[...] = jnp.zeros_like(dchan_ref)
        dhead_ref[...] = jnp.zeros_like(dhead_ref)

    taps = conv_ref[0:CK]
    s = scan_core(proj_ref[...], step_ref[...], col_ref[...], row_ref[0], taps, conv_ref[CK : CK + 1], head_ref[...])
    chan, length = s["chan"], s["z"].shape[0]
    gain, skip = chan_ref[0:1], chan_ref[1:2]
    inputs = s["act"][:, :chan]
    low = inputs.astype(bf16)
    scan, mixes, tables = pair_scan(s, heads, low)
    scan = scan + skip * inputs
    z = s["z"]
    sig = jax.nn.sigmoid(z)
    silu = z * sig
    gated = scan * silu
    extra = extra_ref[...].astype(f32)
    scale = extra[:, 0:1] + extra[:, 1:2]
    mean = extra[:, 2:3] + extra[:, 3:4]
    grad = grad_ref[...].astype(f32)
    normed = gated * scale
    d_gated = scale * (grad * gain - normed * mean)
    d_scan = d_gated * silu
    d_z = d_gated * scan * sig * (1.0 + z * (1.0 - sig))
    d_low = d_scan.astype(bf16)
    lane = lax.broadcasted_iota(jnp.int32, (1, 2 * HP), 1)
    spot = lax.broadcasted_iota(jnp.int32, (1, s["step"].shape[1]), 1)
    d_cb = jnp.zeros((length, length), f32)
    d_cum = jnp.zeros(s["step"].shape, f32)
    flat_ref[...] = jnp.zeros_like(flat_ref)
    blocks = []
    for j in range(heads // 2):
        cut = slice(j * 2 * HP, (j + 1) * 2 * HP)
        both, d_both = low[:, cut], d_low[:, cut]
        outs = []
        for i, h in enumerate((2 * j, 2 * j + 1)):
            decay, step_row = tables[h]
            outs.append(tn(mixes[h], d_both))
            keep = (lane < HP) if i == 0 else (lane >= HP)
            d_mix = nt(jnp.where(keep, d_both, jnp.zeros_like(d_both)), both)
            part = d_mix * decay
            d_cb = d_cb + part * step_row
            part = part * s["cb"]
            flat_ref[h : h + 1, 0:length] = jnp.sum(part, axis=0, keepdims=True)
            column = jnp.sum(part * step_row, axis=1, keepdims=True)
            d_cum = d_cum + jnp.where(spot == h, column, 0.0)
        blocks.append(jnp.where(lane < HP, outs[0], outs[1]))
    d_inputs = jnp.concatenate(blocks, axis=1) + skip * d_scan
    from_rows = flat_ref[...].T[0:length]
    d_cum = d_cum - s["step"] * from_rows
    d_rate = lax.dot_general(
        s["lower"], d_cum, (((0,), (0,)), ((), ())), precision=highest, preferred_element_type=f32
    )
    d_step = from_rows + d_rate * s["rate"]
    d_pre = jnp.where(spot < heads, d_step * jax.nn.sigmoid(s["pre"]), 0.0)
    d_cb_low = d_cb.astype(bf16)
    d_act = jnp.concatenate([d_inputs, tn(d_cb_low, s["c"]), nn(d_cb_low, s["b"])], axis=1)
    logistic = s["logistic"]
    d_sum = d_act * logistic * (1.0 + s["conv_sum"] * (1.0 - logistic))
    d_in = taps[0:1] * d_sum
    for k in range(1, CK):
        back = d_sum * s["masks"][k] * taps[k : k + 1]
        d_in = d_in + pltpu.roll(back, length - k, 0)
    dproj_ref[...] = jnp.concatenate([d_z, d_in, d_pre], axis=1).astype(bf16)
    for k in range(CK):
        dconv_ref[k : k + 1] += jnp.sum(d_sum * s["shifted"][k], axis=0, keepdims=True)
    dconv_ref[CK : CK + 1] += jnp.sum(d_sum, axis=0, keepdims=True)
    dchan_ref[0:1] += jnp.sum(grad * normed, axis=0, keepdims=True)
    dchan_ref[1:2] += jnp.sum(d_scan * inputs, axis=0, keepdims=True)
    dhead_ref[0:1] += jnp.sum(d_pre, axis=0, keepdims=True)
    dhead_ref[1:2] += jnp.sum(d_rate * s["step"] * s["rate"], axis=0, keepdims=True)


def scan_specs(length, width, lanes_, conv, chan):
    def whole(shape):
        return pl.BlockSpec(shape, lambda i: (0,) * len(shape))

    rows = lambda w: pl.BlockSpec((length, w), lambda i: (i, 0))
    return rows, whole, [
        rows(width), rows(lanes_), rows(1), pl.BlockSpec((1, 1, length), lambda i: (i, 0, 0)),
        whole((8, conv)), whole((8, chan)), whole((8, lanes_)),
    ]


def scan_forward(heads, length, proj, step, seg_col, seg_row, conv_par, chan_par, head_par):
    total, width = proj.shape
    chan = heads * HP
    rows, whole, specs = scan_specs(length, width, step.shape[1], width - chan, chan)
    return pl.pallas_call(
        functools.partial(scan_forward_kernel, heads),
        grid=(total // length,),
        in_specs=specs,
        out_specs=[rows(chan), rows(128)],
        out_shape=[jax.ShapeDtypeStruct((total, chan), bf16), jax.ShapeDtypeStruct((total, 128), f32)],
        compiler_params=pltpu.CompilerParams(vmem_limit_bytes=32 << 20),
        name="scan_forward",
    )(proj, step, seg_col, seg_row, conv_par, chan_par, head_par)


def scan_backward(heads, length, proj, step, seg_col, seg_row, conv_par, chan_par, head_par, grad, extra):
    total, width = proj.shape
    chan = heads * HP
    lanes_ = step.shape[1]
    rows, whole, specs = scan_specs(length, width, lanes_, width - chan, chan)
    return pl.pallas_call(
        functools.partial(scan_backward_kernel, heads),
        grid=(total // length,),
        in_specs=specs + [rows(chan), rows(128)],
        out_specs=[rows(width + lanes_), whole((8, width - chan)), whole((8, chan)), whole((8, lanes_))],
        out_shape=[
            jax.ShapeDtypeStruct((total, width + lanes_), bf16),
            jax.ShapeDtypeStruct((8, width - chan), f32),
            jax.ShapeDtypeStruct((8, chan), f32),
            jax.ShapeDtypeStruct((8, lanes_), f32),
        ],
        scratch_shapes=[pltpu.VMEM((128, 128), f32)],
        compiler_params=pltpu.CompilerParams(vmem_limit_bytes=32 << 20),
        name="scan_backward",
    )(proj, step, seg_col, seg_row, conv_par, chan_par, head_par, grad, extra)


def swiglu(gate, up):
    return gate * jax.nn.sigmoid(gate) * up


def swiglu_back(grad, gate, up):
    logistic = jax.nn.sigmoid(gate)
    grad_gate = grad * up * logistic * (1.0 + gate * (1.0 - logistic))
    return grad_gate.astype(bf16), (grad * gate * logistic).astype(bf16)


def gate_table(moe_in, mask, router):
    logits = nn(moe_in, router)
    picked = jnp.where(mask, logits, masked_value)
    peak = jnp.max(picked, axis=-1, keepdims=True)
    ex = jnp.where(mask, jnp.exp(picked - peak), 0.0)
    return ex / jnp.sum(ex, axis=-1, keepdims=True)


def unit_gates(local, units):
    count = local.shape[1]
    owner = lax.broadcasted_iota(jnp.int32, (1, units), 1) // EXP_FF
    spread = local[:, count - 1 :]
    for e in range(count - 1):
        spread = jnp.where(owner == e, local[:, e : e + 1], spread)
    return spread, owner


def moe_forward(own_in, mask, w, riders=None):
    rows = own_in.shape[0]
    base_in = gather_rows(own_in)
    moe_in = wide(base_in)
    gates = gate_table(moe_in, mask, w["router"])
    units = w["expert_down"].shape[0]
    count = units // EXP_FF
    first = lax.axis_index(EX) * count
    local = lax.dynamic_slice(gates, (0, first), (gates.shape[0], count))
    pre = nn(moe_in, w["expert_in"], bf16)
    pre_s = nn(base_in, w["shared_in"], bf16)
    if riders is not None:
        riders = gather_start(riders)
        riders[1], pre = fence(riders[1], pre)
    pre, pre_s = lax.optimization_barrier((pre, pre_s))
    p = pre.astype(f32)
    spread, _ = unit_gates(local, units)
    hid = (swiglu(p[:, :units], p[:, units:]) * spread).astype(bf16)
    half = pre_s.shape[1] // 2
    p = pre_s.astype(f32)
    hid_s = swiglu(p[:, :half], p[:, half:]).astype(bf16)
    low = nn(hid, w["expert_down"])
    if riders is not None:
        riders[2:], low = fence(riders[2:], low)
    total = add_first(low, nt(hid_s, w["shared_down_t"]))
    kept = (moe_in, base_in, gates[:rows], local, pre, pre_s)
    return (total, kept) if riders is None else (total, kept, riders)


def moe_backward(base_z, kept, w, experts_total):
    moe_in, base_in, own_gates, local, pre, pre_s = kept
    pre, pre_s, _ = lax.optimization_barrier((pre, pre_s, base_z))
    grad_z = wide(base_z)
    units = w["expert_down"].shape[0]
    count = units // EXP_FF
    first = lax.axis_index(EX) * count
    spread, owner = unit_gates(local, units)
    p = pre.astype(f32)
    gate, up = p[:, :units], p[:, units:]
    grad_hid = nt(grad_z, w["expert_down"])
    act = swiglu(gate, up)
    hidden = (act * spread).astype(bf16)
    product = grad_hid * act
    lane = lax.broadcasted_iota(jnp.int32, (1, experts_total), 1)
    table = jnp.zeros((grad_z.shape[0], experts_total), f32)
    for e in range(count):
        mine = jnp.sum(jnp.where(owner == e, product, 0.0), axis=-1, keepdims=True)
        table = table + local[:, e : e + 1] * mine * (lane == first + e).astype(f32)
    g_gate, g_up = swiglu_back(grad_hid * spread, gate, up)
    g_pre = jnp.concatenate([g_gate, g_up], axis=1)
    total = nt(g_pre, w["expert_in"])
    half = pre_s.shape[1] // 2
    p = pre_s.astype(f32)
    grad_hid = nn(base_z, w["shared_down_t"])
    hid_s = swiglu(p[:, :half], p[:, half:]).astype(bf16)
    g_gate, g_up = swiglu_back(grad_hid, p[:, :half], p[:, half:])
    g_pre_s = jnp.concatenate([g_gate, g_up], axis=1)
    total = add_first(total, nt(g_pre_s, w["shared_in"]))
    extra = -(-experts_total // 128) * 128
    table = jnp.pad(table, ((0, 0), (0, extra - experts_total)))
    total = jnp.concatenate([total, table], axis=1)
    side = (moe_in, grad_z, hidden, hid_s, g_pre, g_pre_s, base_in, base_z)
    return total, side


def moe_finish(back, kept, w, experts_total):
    own_gates = kept[2]
    weighted = back[:, D : D + experts_total]
    grad_logits = weighted - own_gates * jnp.sum(weighted, axis=-1, keepdims=True)
    grad_logits = grad_logits.astype(bf16)
    return back[:, :D] + nt(grad_logits, w["router"]), grad_logits


def tn_sum(pairs, out=bf16):
    if lax.axis_size("w") > 1:
        return tn(*[jnp.concatenate(side, axis=0) for side in zip(*pairs)], out)
    total = None
    for a, b in pairs:
        part = tn(a, b)
        total = part if total is None else total + part
    return total.astype(out)


def moe_weight_grads(sides):
    g_down = tn_sum([(s[2], s[1]) for s in sides])
    g_in = tn_sum([(s[0], s[4]) for s in sides])
    g_sin = tn_sum([(s[6], s[5]) for s in sides])
    g_sdown_t = tn_sum([(s[7], s[3]) for s in sides])
    return g_in, g_down, g_sin, g_sdown_t


def attn_mask(seg):
    length = seg.shape[1]
    rows_pos = lax.broadcasted_iota(jnp.int32, (length, length), 0)
    cols_pos = lax.broadcasted_iota(jnp.int32, (length, length), 1)
    return (seg[:, :, None] == seg[:, None, :]) & (cols_pos <= rows_pos)[None]


def attn_forward(own_in, allowed, w_qkv, w_out_t):
    seqs, length, _ = allowed.shape
    kv = KVH // 2
    group = QH // KVH
    q_width = kv * group * HEAD
    kv_width = kv * HEAD
    attn_in = pair_gather(own_in)
    packed = nn(attn_in, w_qkv, bf16)
    q = packed[:, :q_width].reshape(seqs, length, kv, group, HEAD)
    k = packed[:, q_width : q_width + kv_width].reshape(seqs, length, kv, HEAD)
    v = packed[:, q_width + kv_width :].reshape(seqs, length, kv, HEAD)
    scores = jnp.einsum("bqhgd,bkhd->bhgqk", q, k, preferred_element_type=f32) * HEAD**-0.5
    scores = jnp.where(allowed[:, None, None], scores, masked_value)
    peak = jnp.max(scores, axis=-1, keepdims=True)
    ex = jnp.exp(scores - peak)
    probs = ex / jnp.sum(ex, axis=-1, keepdims=True)
    context = jnp.einsum("bhgqk,bkhd->bqhgd", probs.astype(bf16), v, preferred_element_type=f32)
    context = context.reshape(seqs * length, q_width).astype(bf16)
    branch = pair_return(nt(context, w_out_t))
    return branch, (attn_in, q, k, v, probs, context)


def attn_backward(own_grad, kept, w_qkv, w_out_t):
    attn_in, q, k, v, probs, context = kept
    seqs, length, kv, group, _ = q.shape
    grad = pair_gather(own_grad)
    grad_context = nn(grad, w_out_t, bf16).reshape(seqs, length, kv, group, HEAD)
    probs_low = probs.astype(bf16)
    grad_v = jnp.einsum("bhgqk,bqhgd->bkhd", probs_low, grad_context, preferred_element_type=f32)
    grad_p = jnp.einsum("bqhgd,bkhd->bhgqk", grad_context, v, preferred_element_type=f32)
    delta = jnp.sum(probs * grad_p, axis=-1, keepdims=True)
    grad_s = (probs * (grad_p - delta)).astype(bf16)
    scale = HEAD**-0.5
    grad_q = jnp.einsum("bhgqk,bkhd->bqhgd", grad_s, k, preferred_element_type=f32) * scale
    grad_k = jnp.einsum("bhgqk,bqhgd->bkhd", grad_s, q, preferred_element_type=f32) * scale
    rows = seqs * length
    grad_packed = jnp.concatenate(
        [grad_q.reshape(rows, -1), grad_k.reshape(rows, -1), grad_v.reshape(rows, -1)], axis=1
    ).astype(bf16)
    grad_in = pair_return(nt(grad_packed, w_qkv))
    return grad_in, (attn_in, grad_packed, context, grad)


def by_owner(x, count):
    return x.reshape(x.shape[0], count, x.shape[1] // count)


def body(
    tokens,
    segments,
    routes,
    norm_mamba,
    w_in,
    w_dt,
    conv_w,
    conv_b,
    dt_bias,
    a_log,
    skip_scale,
    gate_norm,
    w_mix_out,
    norm_moe_m,
    router_m,
    shared_in_m,
    shared_down_m,
    expert_in_m,
    expert_down_m,
    norm_attn,
    w_qkv,
    w_out,
    norm_moe,
    router,
    shared_in,
    shared_down,
    expert_in,
    expert_down,
    cotangent,
):
    batches, length, _ = tokens.shape
    micro = batches if lax.axis_size("w") > 1 else 1
    seqs = batches // micro
    own_rows = seqs * length
    tokens = tokens.reshape(micro, own_rows, D)
    cotangent = cotangent.reshape(micro, own_rows, D)
    routes = routes.reshape(2, micro, own_rows, TOP)
    segments = segments.reshape(micro, own_rows)
    n_tp = lax.axis_size("z") * lax.axis_size("core")
    n_ex = lax.axis_size("w") * n_tp
    n_all = lax.axis_size("dp") * n_ex
    rows = w_in.shape[0]
    local_experts = expert_in.shape[0]
    experts_total = local_experts * n_ex
    heads = MH // n_tp
    chan = heads * HP
    ff = SH_FF // n_tp
    slot = lax.axis_index(TP)
    conv_total = DI + 2 * STATE
    conv_here = conv_w.shape[1]
    gate_here = gate_norm.shape[0]
    vec_len = gate_here + (CK + 1) * conv_here
    vec_cols = -(-vec_len // rows)
    small_cols = 4 + 2 * experts_total + vec_cols
    step_width = -(-(heads + small_cols) // 128) * 128

    vec = jnp.concatenate([gate_norm, conv_b, conv_w.reshape(-1)])
    vec = jnp.pad(vec, (0, rows * vec_cols - vec_len)).reshape(rows, vec_cols)
    gains_own = jnp.stack([norm_mamba, norm_moe_m, norm_attn, norm_moe], axis=1)
    little = jnp.concatenate([gains_own, router_m, router, vec], axis=1)

    def for_all(x):
        return jnp.broadcast_to(x[:, None], (rows, n_tp, x.shape[1]))

    def packed_columns(parts):
        return jnp.concatenate(parts, axis=2).transpose(1, 0, 2)

    def moved_columns(packed):
        moved = lax.all_to_all(packed, TP, split_axis=0, concat_axis=0, tiled=True)
        return moved.reshape(n_tp * rows, -1)

    def whole_rows(moved):
        return lax.all_gather(moved, FS, axis=0, tiled=True)

    def shared_pack(w_sin, w_sdown):
        return [
            by_owner(w_sin[:, :SH_FF], n_tp),
            by_owner(w_sin[:, SH_FF:], n_tp),
            by_owner(w_sdown.T, n_tp),
        ]

    blank = jnp.zeros((rows, n_tp, step_width - heads - small_cols), bf16)
    packed_m = packed_columns(
        [
            by_owner(w_in[:, :DI], n_tp),
            by_owner(w_in[:, DI : 2 * DI], n_tp),
            for_all(w_in[:, 2 * DI :]),
            by_owner(w_dt, n_tp),
            for_all(little),
            blank,
            by_owner(w_mix_out.T, n_tp),
        ]
    )
    moved_m = moved_columns(packed_m)

    expert_ids = jnp.arange(experts_total, dtype=jnp.int32)
    info_width = -(-(2 * experts_total + 1) // 128) * 128
    each = range(micro)
    rows_in = []
    for m in each:
        hot = [
            jnp.any(routes[b, m][:, :, None] == expert_ids, axis=1).astype(bf16) for b in range(2)
        ]
        info = lanes(hot + [segments[m][:, None].astype(bf16)], info_width)
        x_info, moved_m = fence(jnp.concatenate([tokens[m], info], axis=1), moved_m)
        rows_in.append(gather_rows(x_info))
    w_m = whole_rows(moved_m)
    in_width = 2 * chan + 2 * STATE
    w_in_here = w_m[:, :in_width]
    at = in_width + step_width
    w_step = w_m[:, in_width:at]
    w_dt_here = w_step[:, :128]
    small_all = w_step[:, heads : heads + small_cols]
    pick = (jnp.arange(128)[None, :] == heads + jnp.arange(8)[:, None]).astype(bf16)
    gain_rows = nt(pick, w_dt_here)
    gain_mamba, gain_moe_m, gain_attn, gain_moe = [gain_rows[i] for i in range(4)]
    router_m_full = small_all[:, 4 : 4 + experts_total]
    router_full = small_all[:, 4 + experts_total : 4 + 2 * experts_total]
    vec_all = small_all[:, 4 + 2 * experts_total :].reshape(n_all, rows * vec_cols).astype(f32)
    gain_gate = vec_all[:, :gate_here].reshape(DI)
    bias_all = vec_all[:, gate_here : gate_here + conv_here].reshape(conv_total)
    taps_all = vec_all[:, gate_here + conv_here : vec_len].reshape(n_all, CK, conv_here)
    taps_all = taps_all.transpose(1, 0, 2).reshape(CK, conv_total)

    def channels(full_row):
        mine = lax.dynamic_slice_in_dim(full_row, slot * chan, chan, axis=-1)
        return jnp.concatenate([mine, full_row[..., DI:]], axis=-1)

    taps = channels(taps_all)
    bias = channels(bias_all)
    gain_here = lax.dynamic_slice_in_dim(gain_gate, slot * chan, chan)
    dt_here = lax.dynamic_slice_in_dim(dt_bias, slot * heads, heads)
    log_here = lax.dynamic_slice_in_dim(a_log, slot * heads, heads)
    skip_here = lax.dynamic_slice_in_dim(skip_scale, slot * heads, heads)

    w_scan = w_m[:, : in_width + 128]
    w_mix_t = w_m[:, at:]

    def expert_weights(w_up, w_low):
        count = w_up.shape[0]
        cols = [w_up[e, :, :EXP_FF] for e in range(count)] + [w_up[e, :, EXP_FF:] for e in range(count)]
        cols = by_rows(jnp.concatenate(cols, axis=1))
        return (
            by_rows(lax.all_gather(cols, "dp", axis=0, tiled=True)),
            lax.all_gather(w_low, "dp", axis=1, tiled=True).reshape(-1, D),
        )

    up_m, low_m = expert_weights(expert_in_m, expert_down_m)
    kv = KVH // 2
    q_width = QH // 2 * HEAD
    kv_width = kv * HEAD
    q_all, kv_all = QH * HEAD, KVH * HEAD
    attn_pack = jnp.concatenate(
        [
            by_owner(w_qkv[:, :q_all], 2),
            by_owner(w_qkv[:, q_all : q_all + kv_all], 2),
            by_owner(w_qkv[:, q_all + kv_all :], 2),
            by_owner(w_out.T, 2),
        ],
        axis=2,
    ).transpose(1, 0, 2)
    packed_s = shared_pack(shared_in_m, shared_down_m) + shared_pack(shared_in, shared_down)
    packed_s, rows_in = fence(packed_columns(packed_s), rows_in)
    moved_s = moved_columns(packed_s)
    attn_pack, moved_s = fence(attn_pack, moved_s)
    attn_pack = lax.all_to_all(attn_pack, "core", split_axis=0, concat_axis=0, tiled=True)
    own = attn_pack.reshape(2 * rows, -1)
    n_z = lax.axis_size("z")
    attn_parts = [send(own, "z", ring(s)) for s in range(n_z - 1, 0, -1)] + [own]
    def eight(parts):
        block = jnp.concatenate([p.reshape(-1, p.shape[-1]) for p in parts], axis=0)
        return jnp.pad(block, ((0, 8 - block.shape[0]), (0, 0)))

    conv_par = eight([taps, bias])
    chan_par = eight([gain_here, jnp.repeat(skip_here, HP)])
    head_par = jnp.pad(eight([dt_here, -jnp.exp(log_here)]), ((0, 0), (0, 128 - heads)))
    x_own = [tokens[m].astype(f32) for m in each]
    masks, allowed, mamba_kept, mix_kept, hidden_one = [], [], [], [], []
    proj_all, cot_all = [], []
    for m in each:
        rows_all = rows_in[m]
        x_all = rows_all[:, :D].astype(f32)
        marks = wide(rows_all[:, D : D + 2 * experts_total]) > 0.5
        masks.append([marks[:, :experts_total], marks[:, experts_total:]])
        seg_col = rows_all[:, D + 2 * experts_total :][:, :1].astype(f32)
        seg_row = seg_col.reshape(n_tp * seqs, 1, length)
        seg = seg_row[:, 0].astype(jnp.int32)
        middle = n_tp * seqs // 2
        pair = jnp.concatenate([seg[:seqs], seg[middle : middle + seqs]], axis=0)
        allowed.append(attn_mask(pair))

        _, scale_x, mamba_in = rms_forward(x_all, gain_mamba)
        total_rows = mamba_in.shape[0]
        proj = nn(mamba_in, w_in_here, bf16)
        dt_raw = nn(mamba_in, w_dt_here)
        proj_all.append(proj)
        pars = (seg_col, seg_row, conv_par, chan_par, head_par)
        gained, square = scan_forward(heads, length, proj, dt_raw, *pars)
        if m == micro - 1:
            attn_parts, gained = fence(attn_parts, gained)
        partial = nt(gained, w_mix_t)
        high = square.astype(bf16).astype(f32)
        lane = lax.broadcasted_iota(jnp.int32, square.shape, 1)
        extra = jnp.where(lane == 0, high, jnp.where(lane == 1, square - high, 0.0))
        own, sent = return_start(jnp.concatenate([partial, extra], axis=1))
        back = return_finish(own, sent)
        gate_scale = lax.rsqrt((back[:, D : D + 1] + back[:, D + 1 : D + 2]) / DI + epsilon)
        mix_branch = back[:, :D] * gate_scale
        hidden_one.append(x_own[m] + mix_branch)
        mamba_kept.append((rows_all, scale_x[:own_rows], mamba_in, (proj, dt_raw, *pars), gained))
        mix_kept.append((mix_branch, gate_scale))

    twice = jnp.concatenate(attn_parts + attn_parts, axis=0)
    start = (n_z - 1 - lax.axis_index("z")) * 2 * rows
    attn_w = lax.dynamic_slice(twice, (start, 0), (n_z * 2 * rows, twice.shape[1]))
    attn_w = lax.all_gather(attn_w, FS, axis=0, tiled=True)
    w_qkv_here = attn_w[:, : q_width + 2 * kv_width]
    w_out_t = attn_w[:, q_width + 2 * kv_width :]

    w_s = whole_rows(moved_s)
    moe_m = {
        "router": router_m_full,
        "shared_in": w_s[:, : 2 * ff],
        "shared_down_t": w_s[:, 2 * ff : 3 * ff],
        "expert_in": up_m,
        "expert_down": low_m,
    }

    up_a, low_a = fence(*expert_weights(expert_in, expert_down))
    moe_a = {
        "router": router_full,
        "shared_in": w_s[:, 3 * ff : 5 * ff],
        "shared_down_t": w_s[:, 5 * ff :],
        "expert_in": up_a,
        "expert_down": low_a,
    }

    one_kept, layer_one = [], []
    for m in each:
        normed, scale, own = rms_forward(hidden_one[m], gain_moe_m)
        total, kept, riders = moe_forward(own, masks[m][0], moe_m, cotangent[m])
        cot_all.append(riders)
        layer_one.append(hidden_one[m] + return_rows(narrow(total)))
        one_kept.append((normed, scale, kept))
    attn_kept, hidden_two = [], []
    for m in each:
        normed, scale, own = rms_forward(layer_one[m], gain_attn)
        branch, kept = attn_forward(own, allowed[m], w_qkv_here, w_out_t)
        hidden_two.append(layer_one[m] + branch)
        attn_kept.append((normed, scale, kept))
    two_kept, results = [], []
    for m in each:
        cot_all[m] = gather_finish(cot_all[m])
        normed, scale, own = rms_forward(hidden_two[m], gain_moe)
        total, kept = moe_forward(own, masks[m][1], moe_a)
        results.append(total)
        two_kept.append((normed, scale, kept))

    gains = [0.0, 0.0, 0.0, 0.0]

    def up_over_dp(g):
        return lax.psum_scatter(g, "dp", scatter_dimension=0, tiled=True)

    def low_over_dp(g):
        g = g.reshape(local_experts, EXP_FF, D)
        return lax.psum_scatter(g, "dp", scatter_dimension=1, tiled=True)

    def expert_out(g_up, g_low):
        units = local_experts * EXP_FF
        cols = []
        for e in range(local_experts):
            low, high = e * EXP_FF, (e + 1) * EXP_FF
            pair = [g_up[:, low:high], g_up[:, units + low : units + high]]
            cols.append(jnp.concatenate(pair, axis=1).astype(f32))
        return jnp.stack(cols), g_low.astype(f32)

    saving = lax.axis_size("w") > 1

    def moe_stage(grads, kept_all, w, gain, *before):
        grads = list(grads)
        backs, first_rows = [], []
        for m in each:
            total, side = moe_backward(grads[m], kept_all[m][2], w, experts_total)
            own, sent = return_start(narrow(total))
            first_rows.append(side[6][:own_rows])
            if saving:
                back = return_finish(own, sent)
                hold = (back, moe_weight_grads([side]), grads[m + 1 :])
                back, newer, grads[m + 1 :] = lax.optimization_barrier(hold)
                weights = newer if m == 0 else [a + b for a, b in zip(weights, newer)]
            else:
                hidden, g_pre, own = fence(side[2], side[4], own)
                weights = moe_weight_grads([(*side[:2], hidden, side[3], g_pre, *side[5:])])
                sent, weights = fence(sent, weights)
                back = return_finish(own, sent)
            backs.append(back)
        backs[-1], before = fence(backs[-1], before)
        grad_gain = 0.0
        values, logits = [], []
        for m in each:
            normed, scale, kept = kept_all[m]
            grad_in, grad_logits = moe_finish(backs[m], kept, w, experts_total)
            logits.append(grad_logits)
            grad_values, part = rms_backward(grad_in, normed, scale, gain)
            grad_gain = grad_gain + part
            values.append(grad_values)
        g_router = tn_sum(list(zip(first_rows, logits)), f32)
        return values, weights, grad_gain, g_router, before

    values, (g_in_a, g_down_a, g_sin_a, g_sdown_a), gains[3], g_router, _ = moe_stage(
        cot_all, two_kept, moe_a, gain_moe
    )
    sum_in_a = up_over_dp(g_in_a)
    sum_down_a = low_over_dp(g_down_a)
    grad_two = [cotangent[m].astype(f32) + values[m] for m in each]
    for m in each:
        total, grad_two[m] = fence(results[m], grad_two[m])
        results[m] = (hidden_two[m] + return_rows(narrow(total))).astype(bf16)

    grad_layer, sides = [], []
    attn_back = []
    for m in each:
        grad_in, side = attn_backward(
            grad_two[m].astype(bf16), attn_kept[m][2], w_qkv_here, w_out_t
        )
        attn_back.append(grad_in)
        sides.append(side)
    g_attn = by_rows(
        jnp.concatenate(
            [
                by_rows(tn_sum([(s[0], s[1]) for s in sides])),
                by_rows(tn_sum([(s[3], s[2]) for s in sides])),
            ],
            axis=1,
        )
    )
    attn_back[-1], g_attn = lax.optimization_barrier((attn_back[-1], g_attn))
    g_attn = lax.psum_scatter(g_attn, FS, scatter_dimension=0, tiled=True)
    g_part = g_attn
    for m in each:
        normed, scale, _ = attn_kept[m]
        grad_values, part = rms_backward(attn_back[m], normed, scale, gain_attn)
        gains[2] = gains[2] + part
        grad_layer.append(grad_two[m] + grad_values)

    values, (g_in_m, g_down_m, g_sin_m, g_sdown_m), gains[1], g_router_m, before = moe_stage(
        [gather_rows(g.astype(bf16)) for g in grad_layer],
        one_kept,
        moe_m,
        gain_moe_m,
        sum_in_a,
        sum_down_a,
    )
    sum_in_a, sum_down_a = before
    out_expert_in, out_expert_down = expert_out(sum_in_a, sum_down_a)
    sum_in_m = up_over_dp(g_in_m)
    sum_down_m = low_over_dp(g_down_m)
    grad_one = [grad_layer[m] + values[m] for m in each]

    def attn_owner(g_part):
        blocks = g_part.reshape(n_z, 2 * rows, -1)
        here = lax.axis_index("z")
        own = lax.dynamic_index_in_dim(blocks, here, 0, keepdims=False)
        sent = []
        for shift in range(1, n_z):
            block = lax.dynamic_index_in_dim(blocks, (here + shift) % n_z, 0, keepdims=False)
            sent.append(send(block, "z", ring(shift)))
        return own, sent

    def attn_total(own, sent):
        total = own.astype(f32)
        for block in sent:
            total = total + block.astype(f32)
        return lax.all_to_all(
            total.astype(bf16).reshape(2, rows, -1), "core", split_axis=0, concat_axis=0, tiled=True
        ).astype(f32)

    small = None
    mamba_sides, mamba_back, mixes, own_normed = [], [], [], []
    for m in each:
        mix_branch, gate_scale = mix_kept[m]
        x_rows, _, mamba_in, scan_args, _ = mamba_kept[m]
        x_rows, _ = fence(x_rows, grad_one[m])
        x_rows = x_rows[:, :D].astype(f32)
        normed_x = x_rows * row_scale(x_rows)
        own_normed.append(normed_x[:own_rows])
        grad_mix = grad_one[m].astype(bf16)
        mean_term = jnp.sum(grad_mix.astype(f32) * mix_branch, axis=-1, keepdims=True) / DI
        extra = lanes(split_two(gate_scale) + split_two(mean_term), 128)
        rows_all = gather_rows(jnp.concatenate([grad_mix, extra], axis=1))
        if m == micro - 1:
            rows_all, out_expert_in, out_expert_down = fence(
                rows_all, out_expert_in, out_expert_down
            )
        mix_all = rows_all[:, :D]
        extra_all = rows_all[:, D:]
        scale_all = extra_all[:, 0:1].astype(f32) + extra_all[:, 1:2].astype(f32)
        scaled_mix = (mix_all.astype(f32) * scale_all).astype(bf16)
        mixes.append(scaled_mix)
        if m == micro - 1:
            g_mix = tn_sum([(x, k[4]) for x, k in zip(mixes, mamba_kept)])
            mix_all, g_mix = fence(mix_all, by_rows(g_mix))
        if m == micro - 1:
            g_part, mix_all = fence(g_part, mix_all)
            attn_sent = attn_owner(g_part)
        grad_gated = nn(mix_all, w_mix_t, bf16)
        grad_scan, *grads = scan_backward(
            heads, length, *scan_args, grad_gated, extra_all
        )
        small = grads if small is None else [a + b for a, b in zip(small, grads)]
        total = nt(grad_scan, w_scan)
        gains[0] = gains[0] + jnp.sum(total * normed_x, axis=0)
        own, sent = return_start(total)
        grad_scan, own = fence(grad_scan, own)
        mamba_sides.append((mamba_in, grad_scan))
        mamba_back.append((own, sent))

    def rows_sum(packed):
        return lax.psum_scatter(packed, FS, scatter_dimension=0, tiled=True)

    def rows_back(packed):
        return lax.all_to_all(
            packed.reshape(n_tp, rows, -1), TP, split_axis=0, concat_axis=0, tiled=True
        ).astype(f32)

    def owned(block):
        return block.transpose(1, 0, 2).reshape(rows, -1)

    g_s = rows_sum(
        jnp.concatenate([g_mix, g_sin_m, g_sdown_m, g_sin_a, g_sdown_a], axis=1)
    )

    g_scan = by_rows(tn_sum(mamba_sides, f32))
    mamba_back, g_scan, attn_sent = fence(mamba_back, g_scan, attn_sent)
    mamba_back = [return_finish(*pair) for pair in mamba_back]
    g_attn = attn_total(*attn_sent)
    g_s, mamba_back[-1] = fence(g_s, mamba_back[-1])
    g_s = rows_back(g_s)
    out_expert_in_m, out_expert_down_m = expert_out(sum_in_m, sum_down_m)

    conv_sums, chan_sums, head_sums = small
    g_gate = chan_sums[0]
    g_skip = jnp.sum(chan_sums[1].reshape(heads, HP), axis=1)
    head_grad = jnp.stack([head_sums[0, :heads], head_sums[1, :heads], g_skip])

    def spread(part, width):
        zeros = jnp.zeros(part.shape[:-1] + (width,), f32)
        return lax.dynamic_update_slice_in_dim(zeros, part[..., :chan], slot * chan, axis=-1)

    conv_grad = jnp.concatenate([conv_sums[CK : CK + 1], conv_sums[:CK]], axis=0)
    conv_grad = spread(conv_grad, conv_total) + jnp.pad(conv_grad[:, chan:], ((0, 0), (DI, 0)))
    conv_grad = conv_grad.reshape(CK + 1, n_all, conv_here).transpose(1, 0, 2).reshape(n_all, -1)
    vec_grad = jnp.concatenate([spread(g_gate, DI).reshape(n_all, gate_here), conv_grad], axis=1)
    vec_grad = jnp.pad(vec_grad, ((0, 0), (0, rows * vec_cols - vec_len))).reshape(D, vec_cols)
    little = jnp.concatenate([g[:, None] for g in gains] + [g_router_m, g_router, vec_grad], axis=1)
    spare = step_width - heads - small_cols
    g_scan = jnp.pad(g_scan, ((0, 0), (0, step_width - 128)))
    g_m = rows_sum((g_scan + jnp.pad(little, ((0, 0), (in_width + heads, spare)))).astype(bf16))
    g_m, g_s = fence(g_m, g_s)
    g_m = rows_back(g_m)
    grads_in = []
    for m in each:
        scale_x = mamba_kept[m][1]
        grad_values, _ = rms_backward(mamba_back[m], own_normed[m], scale_x, gain_mamba)
        grads_in.append(grad_one[m] + grad_values)

    out_w_in = jnp.concatenate(
        [
            owned(g_m[:, :, :chan]),
            owned(g_m[:, :, chan : 2 * chan]),
            jnp.sum(g_m[:, :, 2 * chan : in_width], axis=0),
        ],
        axis=1,
    )
    out_mix = owned(g_s[:, :, :chan]).T
    out_w_dt = owned(g_m[:, :, in_width : in_width + heads])
    little = jnp.sum(g_m[:, :, in_width + heads : in_width + heads + small_cols], axis=0)
    vec = little[:, 4 + 2 * experts_total :].reshape(-1)
    out_gate = vec[:gate_here]
    out_conv_b = vec[gate_here : gate_here + conv_here]
    out_conv_w = vec[gate_here + conv_here : vec_len].reshape(CK, conv_here)

    head_grad = lax.dynamic_update_slice(jnp.zeros((8, 128), f32), head_grad, (0, slot * heads))
    head_grad, mamba_back[-1] = fence(head_grad, mamba_back[-1])
    for axis in ALL:
        size = lax.axis_size(axis)
        step = 1
        while step < size:
            pairs = [(i, i ^ step) for i in range(size)]
            head_grad = head_grad + send(head_grad, axis, pairs)
            step *= 2
    head_grad = head_grad[:3, :MH]

    cuts = (q_width, q_width + kv_width, q_width + 2 * kv_width)
    out_w_qkv = jnp.concatenate(
        [
            owned(g_attn[:, :, : cuts[0]]),
            owned(g_attn[:, :, cuts[0] : cuts[1]]),
            owned(g_attn[:, :, cuts[1] : cuts[2]]),
        ],
        axis=1,
    )
    out_w_out = owned(g_attn[:, :, cuts[2] :]).T

    def shared_out(block):
        g_sin = jnp.concatenate([owned(block[:, :, :ff]), owned(block[:, :, ff : 2 * ff])], axis=1)
        return g_sin, owned(block[:, :, 2 * ff :]).T

    out_sin_m, out_sdown_m = shared_out(g_s[:, :, chan : chan + 3 * ff])
    out_sin, out_sdown = shared_out(g_s[:, :, chan + 3 * ff :])

    return (
        jnp.stack(results).reshape(batches, length, D),
        jnp.stack(grads_in).reshape(batches, length, D),
        little[:, 0],
        out_w_in,
        out_w_dt,
        out_conv_w,
        out_conv_b,
        head_grad[0],
        head_grad[1],
        head_grad[2],
        out_gate,
        out_mix,
        little[:, 1],
        little[:, 4 : 4 + experts_total],
        out_sin_m,
        out_sdown_m,
        out_expert_in_m,
        out_expert_down_m,
        little[:, 2],
        out_w_qkv,
        out_w_out,
        little[:, 3],
        little[:, 4 + experts_total : 4 + 2 * experts_total],
        out_sin,
        out_sdown,
        out_expert_in,
        out_expert_down,
    )


def solution(mesh):
    n_dp, n_ex = mesh.shape["dp"], mesh.shape["expert"]
    outer = n_ex // 8
    fine = Mesh(mesh.devices.reshape(n_dp, outer, 4, 2), ALL)
    split = P(ALL)
    row = P(ALL, None)
    col = P(None, ALL)
    mid = P(None, ALL, None)
    part = P(EX, "dp", None)
    same = P()
    return jax.shard_map(
        body,
        mesh=fine,
        in_specs=(
            mid,
            mid,
            P(None, None, ALL, None),
            split,
            row,
            row,
            col,
            split,
            same,
            same,
            same,
            split,
            col,
            split,
            row,
            row,
            col,
            part,
            part,
            split,
            row,
            col,
            split,
            row,
            row,
            col,
            part,
            part,
            mid,
        ),
        out_specs=(
            mid,
            mid,
            split,
            row,
            row,
            col,
            split,
            same,
            same,
            same,
            split,
            col,
            split,
            row,
            row,
            col,
            part,
            part,
            split,
            row,
            col,
            split,
            row,
            row,
            col,
            part,
            part,
        ),
        check_vma=False,
    )
```

```python
import functools

import jax
import jax.numpy as jnp
from jax import lax
from jax.experimental import pallas as pl
from jax.experimental.pallas import tpu as pltpu
from jax.experimental.layout import Layout, with_layout_constraint
from jax.sharding import Mesh, PartitionSpec as P

D = 1536
QH = 12
KVH = 4
HEAD = 128
EXP_FF = 512
SH_FF = 1024
TOP = 6
MH = 48
HP = 64
STATE = 128
CK = 4
DI = 3072

bf16 = jnp.bfloat16
f32 = jnp.float32
epsilon = 1e-05
masked_value = -1e30
highest = lax.Precision.HIGHEST
ALL = ("dp", "w", "z", "core")
EX = ("w", "z", "core")
TP = ("z", "core")
FS = ("dp", "w")
SWAP = [(0, 1), (1, 0)]


def dot(a, b, dims, out=f32):
    r = lax.dot_general(a, b, (dims, ((), ())), preferred_element_type=f32)
    return r if out == f32 else r.astype(out)


def nn(a, b, out=f32):
    return dot(a, b, ((1,), (0,)), out)


def nt(a, b, out=f32):
    return dot(a, b, ((1,), (1,)), out)


def tn(a, b, out=f32):
    return dot(a, b, ((0,), (0,)), out)


def ring(shift, axis="z"):
    n = lax.axis_size(axis)
    return [(i, (i + shift) % n) for i in range(n)]


def wide(x):
    parts = [x] + [lax.ppermute(x, "w", ring(s, "w")) for s in range(1, lax.axis_size("w"))]
    return parts[0] if len(parts) == 1 else jnp.concatenate(parts, axis=0)


def narrow(total):
    n = lax.axis_size("w")
    rows = total.shape[0] // n
    out = total[:rows]
    for s in range(1, n):
        part = total[s * rows : (s + 1) * rows].astype(bf16)
        out = out + lax.ppermute(part, "w", ring(-s, "w")).astype(f32)
    return out


def add_first(total, part):
    rows = part.shape[0]
    if rows == total.shape[0]:
        return total + part
    return jnp.concatenate([total[:rows] + part, total[rows:]], axis=0)


def fence(*trees):
    if lax.axis_size("w") > 1:
        return trees
    return lax.optimization_barrier(trees)


def by_rows(x):
    if lax.axis_size("w") > 1:
        return x
    return with_layout_constraint(x, Layout(major_to_minor=tuple(range(x.ndim))))


def send(x, axis, pairs):
    return by_rows(lax.ppermute(by_rows(x), axis, pairs))


def gather_start(x):
    return [x] + [send(x, "z", ring(s)) for s in range(1, lax.axis_size("z"))]


def gather_finish(parts):
    mine = by_rows(jnp.concatenate(parts, axis=0))
    return by_rows(jnp.concatenate([mine, send(mine, "core", SWAP)], axis=0))


def gather_rows(x):
    return gather_finish(gather_start(x))


def return_start(total):
    n = lax.axis_size("z")
    half = total.shape[0] // 2
    rows = half // n
    recv = send(total[half:].astype(bf16), "core", SWAP)
    mine = total[:half] + recv.astype(f32)
    sent = [
        send(mine[s * rows : (s + 1) * rows].astype(bf16), "z", ring(-s)) for s in range(1, n)
    ]
    return mine[:rows], sent


def return_finish(own, sent):
    for part in sent:
        own = own + part.astype(f32)
    return own


def return_rows(total):
    return return_finish(*return_start(total))


def pair_gather(x):
    return by_rows(jnp.concatenate([x, send(x, "core", SWAP)], axis=0))


def pair_return(total):
    half = total.shape[0] // 2
    recv = send(total[half:].astype(bf16), "core", SWAP)
    return total[:half] + recv.astype(f32)


def split_two(x):
    high = x.astype(bf16)
    return [high, (x - high.astype(f32)).astype(bf16)]


def row_scale(values):
    return lax.rsqrt(jnp.mean(values * values, axis=-1, keepdims=True) + epsilon)


def rms_forward(values, gain):
    scale = row_scale(values)
    normed = values * scale
    return normed, scale, (normed * gain).astype(bf16)


def rms_backward(grad_result, normed, scale, gain):
    grad_gain = jnp.sum(grad_result * normed, axis=0)
    grad_normed = grad_result * gain
    grad_values = scale * (
        grad_normed - normed * jnp.mean(grad_normed * normed, axis=-1, keepdims=True)
    )
    return grad_values, grad_gain


def lanes(parts, width):
    used = sum(p.shape[-1] for p in parts)
    rows = parts[0].shape[0]
    if used < width:
        parts = parts + [jnp.zeros((rows, width - used), bf16)]
    return jnp.concatenate(parts, axis=1)


def scan_core(proj, step_raw, seg_col, seg_row, taps, bias, heads_par):
    length = proj.shape[0]
    chan = proj.shape[1] - 2 * STATE
    chan = chan // 2
    z = proj[:, :chan].astype(f32)
    conv_in = proj[:, chan:].astype(f32)
    place = lax.broadcasted_iota(jnp.int32, (length, 1), 0)
    shifted, masks = [], []
    conv_sum = bias
    for k in range(CK):
        if k == 0:
            moved, mask = conv_in, None
            conv_sum = conv_sum + taps[0:1] * moved
        else:
            same = pltpu.roll(seg_col, k, 0) == seg_col
            mask = jnp.where(same & (place >= k), 1.0, 0.0)
            moved = pltpu.roll(conv_in, k, 0) * mask
            conv_sum = conv_sum + taps[k : k + 1] * moved
        shifted.append(moved)
        masks.append(mask)
    logistic = jax.nn.sigmoid(conv_sum)
    act = conv_sum * logistic
    pre = step_raw + heads_par[0:1]
    step = jnp.maximum(pre, 0.0) + jnp.log1p(jnp.exp(-jnp.abs(pre)))
    decay_rate = heads_par[1:2]
    rows_pos = lax.broadcasted_iota(jnp.int32, (length, length), 0)
    cols_pos = lax.broadcasted_iota(jnp.int32, (length, length), 1)
    lower = jnp.where(cols_pos <= rows_pos, 1.0, 0.0)
    cum = lax.dot_general(
        lower, step * decay_rate, (((1,), (0,)), ((), ())), precision=highest, preferred_element_type=f32
    )
    allowed = (seg_col == seg_row) & (cols_pos <= rows_pos)
    b_low = act[:, chan : chan + STATE].astype(bf16)
    c_low = act[:, chan + STATE :].astype(bf16)
    cb = nt(c_low, b_low)
    return dict(
        chan=chan, z=z, conv_in=conv_in, shifted=shifted, masks=masks, conv_sum=conv_sum,
        logistic=logistic, act=act, pre=pre, step=step, rate=decay_rate, lower=lower, cum=cum,
        cum_t=cum.T, step_t=step.T, allowed=allowed, b=b_low, c=c_low, cb=cb,
    )


def head_table(s, h):
    gap = s["cum"][:, h : h + 1] - s["cum_t"][h : h + 1, :]
    decay = jnp.exp(jnp.where(s["allowed"], gap, masked_value))
    return decay, s["step_t"][h : h + 1, :]


def pair_scan(s, heads, low):
    lane = lax.broadcasted_iota(jnp.int32, (1, 2 * HP), 1)
    blocks, mixes, tables = [], [], []
    for j in range(heads // 2):
        both = low[:, j * 2 * HP : (j + 1) * 2 * HP]
        outs = []
        for h in (2 * j, 2 * j + 1):
            decay, step_row = head_table(s, h)
            mix = (decay * s["cb"] * step_row).astype(bf16)
            outs.append(nn(mix, both))
            mixes.append(mix)
            tables.append((decay, step_row))
        blocks.append(jnp.where(lane < HP, outs[0], outs[1]))
    return jnp.concatenate(blocks, axis=1), mixes, tables


def scan_forward_kernel(heads, proj_ref, step_ref, col_ref, row_ref, conv_ref, chan_ref, head_ref, gained_ref, square_ref):
    s = scan_core(
        proj_ref[...], step_ref[...], col_ref[...], row_ref[0], conv_ref[0:CK], conv_ref[CK : CK + 1], head_ref[...]
    )
    chan = s["chan"]
    inputs = s["act"][:, :chan]
    scan, _, _ = pair_scan(s, heads, inputs.astype(bf16))
    scan = scan + chan_ref[1:2] * inputs
    gated = scan * s["z"] * jax.nn.sigmoid(s["z"])
    gained_ref[...] = (gated * chan_ref[0:1]).astype(bf16)
    square_ref[...] = jnp.broadcast_to(jnp.sum(gated * gated, axis=1, keepdims=True), square_ref.shape)


def scan_backward_kernel(
    heads, proj_ref, step_ref, col_ref, row_ref, conv_ref, chan_ref, head_ref, grad_ref, extra_ref,
    dproj_ref, dconv_ref, dchan_ref, dhead_ref, flat_ref,
):
    @pl.when(pl.program_id(0) == 0)
    def _():
        dconv_ref[...] = jnp.zeros_like(dconv_ref)
        dchan_ref[...] = jnp.zeros_like(dchan_ref)
        dhead_ref[...] = jnp.zeros_like(dhead_ref)

    taps = conv_ref[0:CK]
    s = scan_core(proj_ref[...], step_ref[...], col_ref[...], row_ref[0], taps, conv_ref[CK : CK + 1], head_ref[...])
    chan, length = s["chan"], s["z"].shape[0]
    gain, skip = chan_ref[0:1], chan_ref[1:2]
    inputs = s["act"][:, :chan]
    low = inputs.astype(bf16)
    scan, mixes, tables = pair_scan(s, heads, low)
    scan = scan + skip * inputs
    z = s["z"]
    sig = jax.nn.sigmoid(z)
    silu = z * sig
    gated = scan * silu
    extra = extra_ref[...].astype(f32)
    scale = extra[:, 0:1] + extra[:, 1:2]
    mean = extra[:, 2:3] + extra[:, 3:4]
    grad = grad_ref[...].astype(f32)
    normed = gated * scale
    d_gated = scale * (grad * gain - normed * mean)
    d_scan = d_gated * silu
    d_z = d_gated * scan * sig * (1.0 + z * (1.0 - sig))
    d_low = d_scan.astype(bf16)
    lane = lax.broadcasted_iota(jnp.int32, (1, 2 * HP), 1)
    spot = lax.broadcasted_iota(jnp.int32, (1, s["step"].shape[1]), 1)
    d_cb = jnp.zeros((length, length), f32)
    d_cum = jnp.zeros(s["step"].shape, f32)
    flat_ref[...] = jnp.zeros_like(flat_ref)
    blocks = []
    for j in range(heads // 2):
        cut = slice(j * 2 * HP, (j + 1) * 2 * HP)
        both, d_both = low[:, cut], d_low[:, cut]
        outs = []
        for i, h in enumerate((2 * j, 2 * j + 1)):
            decay, step_row = tables[h]
            outs.append(tn(mixes[h], d_both))
            keep = (lane < HP) if i == 0 else (lane >= HP)
            d_mix = nt(jnp.where(keep, d_both, jnp.zeros_like(d_both)), both)
            part = d_mix * decay
            d_cb = d_cb + part * step_row
            part = part * s["cb"]
            flat_ref[h : h + 1, 0:length] = jnp.sum(part, axis=0, keepdims=True)
            column = jnp.sum(part * step_row, axis=1, keepdims=True)
            d_cum = d_cum + jnp.where(spot == h, column, 0.0)
        blocks.append(jnp.where(lane < HP, outs[0], outs[1]))
    d_inputs = jnp.concatenate(blocks, axis=1) + skip * d_scan
    from_rows = flat_ref[...].T[0:length]
    d_cum = d_cum - s["step"] * from_rows
    d_rate = lax.dot_general(
        s["lower"], d_cum, (((0,), (0,)), ((), ())), precision=highest, preferred_element_type=f32
    )
    d_step = from_rows + d_rate * s["rate"]
    d_pre = jnp.where(spot < heads, d_step * jax.nn.sigmoid(s["pre"]), 0.0)
    d_cb_low = d_cb.astype(bf16)
    d_act = jnp.concatenate([d_inputs, tn(d_cb_low, s["c"]), nn(d_cb_low, s["b"])], axis=1)
    logistic = s["logistic"]
    d_sum = d_act * logistic * (1.0 + s["conv_sum"] * (1.0 - logistic))
    d_in = taps[0:1] * d_sum
    for k in range(1, CK):
        back = d_sum * s["masks"][k] * taps[k : k + 1]
        d_in = d_in + pltpu.roll(back, length - k, 0)
    dproj_ref[...] = jnp.concatenate([d_z, d_in, d_pre], axis=1).astype(bf16)
    for k in range(CK):
        dconv_ref[k : k + 1] += jnp.sum(d_sum * s["shifted"][k], axis=0, keepdims=True)
    dconv_ref[CK : CK + 1] += jnp.sum(d_sum, axis=0, keepdims=True)
    dchan_ref[0:1] += jnp.sum(grad * normed, axis=0, keepdims=True)
    dchan_ref[1:2] += jnp.sum(d_scan * inputs, axis=0, keepdims=True)
    dhead_ref[0:1] += jnp.sum(d_pre, axis=0, keepdims=True)
    dhead_ref[1:2] += jnp.sum(d_rate * s["step"] * s["rate"], axis=0, keepdims=True)


def scan_specs(length, width, lanes_, conv, chan):
    def whole(shape):
        return pl.BlockSpec(shape, lambda i: (0,) * len(shape))

    rows = lambda w: pl.BlockSpec((length, w), lambda i: (i, 0))
    return rows, whole, [
        rows(width), rows(lanes_), rows(1), pl.BlockSpec((1, 1, length), lambda i: (i, 0, 0)),
        whole((8, conv)), whole((8, chan)), whole((8, lanes_)),
    ]


def scan_forward(heads, length, proj, step, seg_col, seg_row, conv_par, chan_par, head_par):
    total, width = proj.shape
    chan = heads * HP
    rows, whole, specs = scan_specs(length, width, step.shape[1], width - chan, chan)
    return pl.pallas_call(
        functools.partial(scan_forward_kernel, heads),
        grid=(total // length,),
        in_specs=specs,
        out_specs=[rows(chan), rows(128)],
        out_shape=[jax.ShapeDtypeStruct((total, chan), bf16), jax.ShapeDtypeStruct((total, 128), f32)],
        compiler_params=pltpu.CompilerParams(vmem_limit_bytes=32 << 20),
        name="scan_forward",
    )(proj, step, seg_col, seg_row, conv_par, chan_par, head_par)


def scan_backward(heads, length, proj, step, seg_col, seg_row, conv_par, chan_par, head_par, grad, extra):
    total, width = proj.shape
    chan = heads * HP
    lanes_ = step.shape[1]
    rows, whole, specs = scan_specs(length, width, lanes_, width - chan, chan)
    return pl.pallas_call(
        functools.partial(scan_backward_kernel, heads),
        grid=(total // length,),
        in_specs=specs + [rows(chan), rows(128)],
        out_specs=[rows(width + lanes_), whole((8, width - chan)), whole((8, chan)), whole((8, lanes_))],
        out_shape=[
            jax.ShapeDtypeStruct((total, width + lanes_), bf16),
            jax.ShapeDtypeStruct((8, width - chan), f32),
            jax.ShapeDtypeStruct((8, chan), f32),
            jax.ShapeDtypeStruct((8, lanes_), f32),
        ],
        scratch_shapes=[pltpu.VMEM((128, 128), f32)],
        compiler_params=pltpu.CompilerParams(vmem_limit_bytes=32 << 20),
        name="scan_backward",
    )(proj, step, seg_col, seg_row, conv_par, chan_par, head_par, grad, extra)


def swiglu(gate, up):
    return gate * jax.nn.sigmoid(gate) * up


def swiglu_back(grad, gate, up):
    logistic = jax.nn.sigmoid(gate)
    grad_gate = grad * up * logistic * (1.0 + gate * (1.0 - logistic))
    return grad_gate.astype(bf16), (grad * gate * logistic).astype(bf16)


def gate_table(moe_in, mask, router):
    logits = nn(moe_in, router)
    picked = jnp.where(mask, logits, masked_value)
    peak = jnp.max(picked, axis=-1, keepdims=True)
    ex = jnp.where(mask, jnp.exp(picked - peak), 0.0)
    return ex / jnp.sum(ex, axis=-1, keepdims=True)


def unit_gates(local, units):
    count = local.shape[1]
    owner = lax.broadcasted_iota(jnp.int32, (1, units), 1) // EXP_FF
    spread = local[:, count - 1 :]
    for e in range(count - 1):
        spread = jnp.where(owner == e, local[:, e : e + 1], spread)
    return spread, owner


def moe_forward(own_in, mask, w, riders=None):
    rows = own_in.shape[0]
    base_in = gather_rows(own_in)
    moe_in = wide(base_in)
    gates = gate_table(moe_in, mask, w["router"])
    units = w["expert_down"].shape[0]
    count = units // EXP_FF
    first = lax.axis_index(EX) * count
    local = lax.dynamic_slice(gates, (0, first), (gates.shape[0], count))
    pre = nn(moe_in, w["expert_in"], bf16)
    pre_s = nn(base_in, w["shared_in"], bf16)
    if riders is not None:
        riders = gather_start(riders)
        riders[1], pre = fence(riders[1], pre)
    pre, pre_s = lax.optimization_barrier((pre, pre_s))
    p = pre.astype(f32)
    spread, _ = unit_gates(local, units)
    hid = (swiglu(p[:, :units], p[:, units:]) * spread).astype(bf16)
    half = pre_s.shape[1] // 2
    p = pre_s.astype(f32)
    hid_s = swiglu(p[:, :half], p[:, half:]).astype(bf16)
    low = nn(hid, w["expert_down"])
    if riders is not None:
        riders[2:], low = fence(riders[2:], low)
    total = add_first(low, nt(hid_s, w["shared_down_t"]))
    kept = (moe_in, base_in, gates[:rows], local, pre, pre_s)
    return (total, kept) if riders is None else (total, kept, riders)


def moe_backward(base_z, kept, w, experts_total, riders=None):
    moe_in, base_in, own_gates, local, pre, pre_s = kept
    pre, pre_s, _ = lax.optimization_barrier((pre, pre_s, base_z))
    grad_z = wide(base_z)
    units = w["expert_down"].shape[0]
    count = units // EXP_FF
    first = lax.axis_index(EX) * count
    spread, owner = unit_gates(local, units)
    p = pre.astype(f32)
    gate, up = p[:, :units], p[:, units:]
    grad_hid = nt(grad_z, w["expert_down"])
    if riders is not None:
        riders[:1], grad_hid = fence(riders[:1], grad_hid)
    act = swiglu(gate, up)
    hidden = (act * spread).astype(bf16)
    product = grad_hid * act
    lane = lax.broadcasted_iota(jnp.int32, (1, experts_total), 1)
    table = jnp.zeros((grad_z.shape[0], experts_total), f32)
    for e in range(count):
        mine = jnp.sum(jnp.where(owner == e, product, 0.0), axis=-1, keepdims=True)
        table = table + local[:, e : e + 1] * mine * (lane == first + e).astype(f32)
    g_gate, g_up = swiglu_back(grad_hid * spread, gate, up)
    g_pre = jnp.concatenate([g_gate, g_up], axis=1)
    total = nt(g_pre, w["expert_in"])
    if riders is not None:
        riders[1:], total = fence(riders[1:], total)
    half = pre_s.shape[1] // 2
    p = pre_s.astype(f32)
    grad_hid = nn(base_z, w["shared_down_t"])
    hid_s = swiglu(p[:, :half], p[:, half:]).astype(bf16)
    g_gate, g_up = swiglu_back(grad_hid, p[:, :half], p[:, half:])
    g_pre_s = jnp.concatenate([g_gate, g_up], axis=1)
    total = add_first(total, nt(g_pre_s, w["shared_in"]))
    extra = -(-experts_total // 128) * 128
    table = jnp.pad(table, ((0, 0), (0, extra - experts_total)))
    total = jnp.concatenate([total, table], axis=1)
    side = (moe_in, grad_z, hidden, hid_s, g_pre, g_pre_s, base_in, base_z)
    return total, side


def moe_finish(back, kept, w, experts_total):
    own_gates = kept[2]
    weighted = back[:, D : D + experts_total]
    grad_logits = weighted - own_gates * jnp.sum(weighted, axis=-1, keepdims=True)
    grad_logits = grad_logits.astype(bf16)
    return back[:, :D] + nt(grad_logits, w["router"]), grad_logits


def tn_sum(pairs, out=bf16):
    if lax.axis_size("w") > 1:
        return tn(*[jnp.concatenate(side, axis=0) for side in zip(*pairs)], out)
    total = None
    for a, b in pairs:
        part = tn(a, b)
        total = part if total is None else total + part
    return total.astype(out)


def moe_weight_grads(sides):
    g_down = tn_sum([(s[2], s[1]) for s in sides])
    g_in = tn_sum([(s[0], s[4]) for s in sides])
    g_sin = tn_sum([(s[6], s[5]) for s in sides])
    g_sdown_t = tn_sum([(s[7], s[3]) for s in sides])
    return g_in, g_down, g_sin, g_sdown_t


def attn_mask(seg):
    length = seg.shape[1]
    rows_pos = lax.broadcasted_iota(jnp.int32, (length, length), 0)
    cols_pos = lax.broadcasted_iota(jnp.int32, (length, length), 1)
    return (seg[:, :, None] == seg[:, None, :]) & (cols_pos <= rows_pos)[None]


def attn_forward(own_in, allowed, w_qkv, w_out_t):
    seqs, length, _ = allowed.shape
    kv = KVH // 2
    group = QH // KVH
    q_width = kv * group * HEAD
    kv_width = kv * HEAD
    attn_in = pair_gather(own_in)
    packed = nn(attn_in, w_qkv, bf16)
    q = packed[:, :q_width].reshape(seqs, length, kv, group, HEAD)
    k = packed[:, q_width : q_width + kv_width].reshape(seqs, length, kv, HEAD)
    v = packed[:, q_width + kv_width :].reshape(seqs, length, kv, HEAD)
    scores = jnp.einsum("bqhgd,bkhd->bhgqk", q, k, preferred_element_type=f32) * HEAD**-0.5
    scores = jnp.where(allowed[:, None, None], scores, masked_value)
    peak = jnp.max(scores, axis=-1, keepdims=True)
    ex = jnp.exp(scores - peak)
    probs = ex / jnp.sum(ex, axis=-1, keepdims=True)
    context = jnp.einsum("bhgqk,bkhd->bqhgd", probs.astype(bf16), v, preferred_element_type=f32)
    context = context.reshape(seqs * length, q_width).astype(bf16)
    branch = pair_return(nt(context, w_out_t))
    return branch, (attn_in, q, k, v, probs, context)


def attn_backward(own_grad, kept, w_qkv, w_out_t):
    attn_in, q, k, v, probs, context = kept
    seqs, length, kv, group, _ = q.shape
    grad = pair_gather(own_grad)
    grad_context = nn(grad, w_out_t, bf16).reshape(seqs, length, kv, group, HEAD)
    probs_low = probs.astype(bf16)
    grad_v = jnp.einsum("bhgqk,bqhgd->bkhd", probs_low, grad_context, preferred_element_type=f32)
    grad_p = jnp.einsum("bqhgd,bkhd->bhgqk", grad_context, v, preferred_element_type=f32)
    delta = jnp.sum(probs * grad_p, axis=-1, keepdims=True)
    grad_s = (probs * (grad_p - delta)).astype(bf16)
    scale = HEAD**-0.5
    grad_q = jnp.einsum("bhgqk,bkhd->bqhgd", grad_s, k, preferred_element_type=f32) * scale
    grad_k = jnp.einsum("bhgqk,bqhgd->bkhd", grad_s, q, preferred_element_type=f32) * scale
    rows = seqs * length
    grad_packed = jnp.concatenate(
        [grad_q.reshape(rows, -1), grad_k.reshape(rows, -1), grad_v.reshape(rows, -1)], axis=1
    ).astype(bf16)
    grad_in = pair_return(nt(grad_packed, w_qkv))
    return grad_in, (attn_in, grad_packed, context, grad)


def by_owner(x, count):
    return x.reshape(x.shape[0], count, x.shape[1] // count)


def body(
    tokens,
    segments,
    routes,
    norm_mamba,
    w_in,
    w_dt,
    conv_w,
    conv_b,
    dt_bias,
    a_log,
    skip_scale,
    gate_norm,
    w_mix_out,
    norm_moe_m,
    router_m,
    shared_in_m,
    shared_down_m,
    expert_in_m,
    expert_down_m,
    norm_attn,
    w_qkv,
    w_out,
    norm_moe,
    router,
    shared_in,
    shared_down,
    expert_in,
    expert_down,
    cotangent,
):
    batches, length, _ = tokens.shape
    micro = batches if lax.axis_size("w") > 1 else 1
    seqs = batches // micro
    own_rows = seqs * length
    tokens = tokens.reshape(micro, own_rows, D)
    cotangent = cotangent.reshape(micro, own_rows, D)
    routes = routes.reshape(2, micro, own_rows, TOP)
    segments = segments.reshape(micro, own_rows)
    n_tp = lax.axis_size("z") * lax.axis_size("core")
    n_ex = lax.axis_size("w") * n_tp
    n_all = lax.axis_size("dp") * n_ex
    rows = w_in.shape[0]
    local_experts = expert_in.shape[0]
    experts_total = local_experts * n_ex
    heads = MH // n_tp
    chan = heads * HP
    ff = SH_FF // n_tp
    slot = lax.axis_index(TP)
    conv_total = DI + 2 * STATE
    conv_here = conv_w.shape[1]
    gate_here = gate_norm.shape[0]
    vec_len = gate_here + (CK + 1) * conv_here
    vec_cols = -(-vec_len // rows)
    small_cols = 4 + 2 * experts_total + vec_cols
    step_width = -(-(heads + small_cols) // 128) * 128

    vec = jnp.concatenate([gate_norm, conv_b, conv_w.reshape(-1)])
    vec = jnp.pad(vec, (0, rows * vec_cols - vec_len)).reshape(rows, vec_cols)
    gains_own = jnp.stack([norm_mamba, norm_moe_m, norm_attn, norm_moe], axis=1)
    little = jnp.concatenate([gains_own, router_m, router, vec], axis=1)

    def for_all(x):
        return jnp.broadcast_to(x[:, None], (rows, n_tp, x.shape[1]))

    def packed_columns(parts):
        return jnp.concatenate(parts, axis=2).transpose(1, 0, 2)

    def moved_columns(packed):
        moved = lax.all_to_all(packed, TP, split_axis=0, concat_axis=0, tiled=True)
        return moved.reshape(n_tp * rows, -1)

    def whole_rows(moved):
        return lax.all_gather(moved, FS, axis=0, tiled=True)

    def shared_pack(w_sin, w_sdown):
        return [
            by_owner(w_sin[:, :SH_FF], n_tp),
            by_owner(w_sin[:, SH_FF:], n_tp),
            by_owner(w_sdown.T, n_tp),
        ]

    blank = jnp.zeros((rows, n_tp, step_width - heads - small_cols), bf16)
    packed_m = packed_columns(
        [
            by_owner(w_in[:, :DI], n_tp),
            by_owner(w_in[:, DI : 2 * DI], n_tp),
            for_all(w_in[:, 2 * DI :]),
            by_owner(w_dt, n_tp),
            for_all(little),
            blank,
            by_owner(w_mix_out.T, n_tp),
        ]
    )
    moved_m = moved_columns(packed_m)

    expert_ids = jnp.arange(experts_total, dtype=jnp.int32)
    info_width = -(-(2 * experts_total + 1) // 128) * 128
    each = range(micro)
    rows_in = []
    for m in each:
        hot = [
            jnp.any(routes[b, m][:, :, None] == expert_ids, axis=1).astype(bf16) for b in range(2)
        ]
        info = lanes(hot + [segments[m][:, None].astype(bf16)], info_width)
        x_info, moved_m = fence(jnp.concatenate([tokens[m], info], axis=1), moved_m)
        rows_in.append(gather_rows(x_info))
    def low_weights(w_low):
        return lax.all_gather(w_low, "dp", axis=1, tiled=True).reshape(-1, D)

    low_m = low_weights(expert_down_m)
    moved_m, low_m = fence(moved_m, low_m)
    w_m = whole_rows(moved_m)
    in_width = 2 * chan + 2 * STATE
    w_in_here = w_m[:, :in_width]
    at = in_width + step_width
    w_step = w_m[:, in_width:at]
    w_dt_here = w_step[:, :128]
    small_all = w_step[:, heads : heads + small_cols]
    pick = (jnp.arange(128)[None, :] == heads + jnp.arange(8)[:, None]).astype(bf16)
    gain_rows = nt(pick, w_dt_here)
    gain_mamba, gain_moe_m, gain_attn, gain_moe = [gain_rows[i] for i in range(4)]
    router_m_full = small_all[:, 4 : 4 + experts_total]
    router_full = small_all[:, 4 + experts_total : 4 + 2 * experts_total]
    vec_all = small_all[:, 4 + 2 * experts_total :].reshape(n_all, rows * vec_cols).astype(f32)
    gain_gate = vec_all[:, :gate_here].reshape(DI)
    bias_all = vec_all[:, gate_here : gate_here + conv_here].reshape(conv_total)
    taps_all = vec_all[:, gate_here + conv_here : vec_len].reshape(n_all, CK, conv_here)
    taps_all = taps_all.transpose(1, 0, 2).reshape(CK, conv_total)

    def channels(full_row):
        mine = lax.dynamic_slice_in_dim(full_row, slot * chan, chan, axis=-1)
        return jnp.concatenate([mine, full_row[..., DI:]], axis=-1)

    taps = channels(taps_all)
    bias = channels(bias_all)
    gain_here = lax.dynamic_slice_in_dim(gain_gate, slot * chan, chan)
    dt_here = lax.dynamic_slice_in_dim(dt_bias, slot * heads, heads)
    log_here = lax.dynamic_slice_in_dim(a_log, slot * heads, heads)
    skip_here = lax.dynamic_slice_in_dim(skip_scale, slot * heads, heads)

    w_scan = w_m[:, : in_width + 128]
    w_mix_t = w_m[:, at:]

    def up_weights(w_up):
        count = w_up.shape[0]
        cols = [w_up[e, :, :EXP_FF] for e in range(count)] + [w_up[e, :, EXP_FF:] for e in range(count)]
        cols = by_rows(jnp.concatenate(cols, axis=1))
        return by_rows(lax.all_gather(cols, "dp", axis=0, tiled=True))

    up_m = up_weights(expert_in_m)
    kv = KVH // 2
    q_width = QH // 2 * HEAD
    kv_width = kv * HEAD
    q_all, kv_all = QH * HEAD, KVH * HEAD
    attn_pack = jnp.concatenate(
        [
            by_owner(w_qkv[:, :q_all], 2),
            by_owner(w_qkv[:, q_all : q_all + kv_all], 2),
            by_owner(w_qkv[:, q_all + kv_all :], 2),
            by_owner(w_out.T, 2),
        ],
        axis=2,
    ).transpose(1, 0, 2)
    packed_s = shared_pack(shared_in_m, shared_down_m) + shared_pack(shared_in, shared_down)
    packed_s, rows_in = fence(packed_columns(packed_s), rows_in)
    moved_s = moved_columns(packed_s)
    attn_pack, moved_s = fence(attn_pack, moved_s)
    attn_pack = lax.all_to_all(attn_pack, "core", split_axis=0, concat_axis=0, tiled=True)
    own = attn_pack.reshape(2 * rows, -1)
    n_z = lax.axis_size("z")
    attn_parts = [send(own, "z", ring(s)) for s in range(n_z - 1, 0, -1)] + [own]
    def eight(parts):
        block = jnp.concatenate([p.reshape(-1, p.shape[-1]) for p in parts], axis=0)
        return jnp.pad(block, ((0, 8 - block.shape[0]), (0, 0)))

    conv_par = eight([taps, bias])
    chan_par = eight([gain_here, jnp.repeat(skip_here, HP)])
    head_par = jnp.pad(eight([dt_here, -jnp.exp(log_here)]), ((0, 0), (0, 128 - heads)))
    x_own = [tokens[m].astype(f32) for m in each]
    masks, allowed, mamba_kept, mix_kept, hidden_one = [], [], [], [], []
    proj_all, cot_all = [], []
    for m in each:
        rows_all = rows_in[m]
        x_all = rows_all[:, :D].astype(f32)
        marks = wide(rows_all[:, D : D + 2 * experts_total]) > 0.5
        masks.append([marks[:, :experts_total], marks[:, experts_total:]])
        seg_col = rows_all[:, D + 2 * experts_total :][:, :1].astype(f32)
        seg_row = seg_col.reshape(n_tp * seqs, 1, length)
        seg = seg_row[:, 0].astype(jnp.int32)
        middle = n_tp * seqs // 2
        pair = jnp.concatenate([seg[:seqs], seg[middle : middle + seqs]], axis=0)
        allowed.append(attn_mask(pair))

        _, scale_x, mamba_in = rms_forward(x_all, gain_mamba)
        total_rows = mamba_in.shape[0]
        proj = nn(mamba_in, w_in_here, bf16)
        dt_raw = nn(mamba_in, w_dt_here)
        proj_all.append(proj)
        pars = (seg_col, seg_row, conv_par, chan_par, head_par)
        gained, square = scan_forward(heads, length, proj, dt_raw, *pars)
        if m == micro - 1:
            attn_parts, gained = fence(attn_parts, gained)
        partial = nt(gained, w_mix_t)
        high = square.astype(bf16).astype(f32)
        lane = lax.broadcasted_iota(jnp.int32, square.shape, 1)
        extra = jnp.where(lane == 0, high, jnp.where(lane == 1, square - high, 0.0))
        own, sent = return_start(jnp.concatenate([partial, extra], axis=1))
        back = return_finish(own, sent)
        gate_scale = lax.rsqrt((back[:, D : D + 1] + back[:, D + 1 : D + 2]) / DI + epsilon)
        mix_branch = back[:, :D] * gate_scale
        hidden_one.append(x_own[m] + mix_branch)
        mamba_kept.append((rows_all, scale_x[:own_rows], mamba_in, (proj, dt_raw, *pars), gained))
        mix_kept.append((mix_branch, gate_scale))

    twice = jnp.concatenate(attn_parts + attn_parts, axis=0)
    start = (n_z - 1 - lax.axis_index("z")) * 2 * rows
    attn_w = lax.dynamic_slice(twice, (start, 0), (n_z * 2 * rows, twice.shape[1]))
    attn_w = lax.all_gather(attn_w, FS, axis=0, tiled=True)
    w_qkv_here = attn_w[:, : q_width + 2 * kv_width]
    w_out_t = attn_w[:, q_width + 2 * kv_width :]

    w_s = whole_rows(moved_s)
    moe_m = {
        "router": router_m_full,
        "shared_in": w_s[:, : 2 * ff],
        "shared_down_t": w_s[:, 2 * ff : 3 * ff],
        "expert_in": up_m,
        "expert_down": low_m,
    }

    up_a, low_a = fence(up_weights(expert_in), low_weights(expert_down))
    moe_a = {
        "router": router_full,
        "shared_in": w_s[:, 3 * ff : 5 * ff],
        "shared_down_t": w_s[:, 5 * ff :],
        "expert_in": up_a,
        "expert_down": low_a,
    }

    one_kept, layer_one = [], []
    for m in each:
        normed, scale, own = rms_forward(hidden_one[m], gain_moe_m)
        total, kept, riders = moe_forward(own, masks[m][0], moe_m, cotangent[m])
        cot_all.append(riders)
        layer_one.append(hidden_one[m] + return_rows(narrow(total)))
        one_kept.append((normed, scale, kept))
    attn_kept, hidden_two = [], []
    for m in each:
        normed, scale, own = rms_forward(layer_one[m], gain_attn)
        branch, kept = attn_forward(own, allowed[m], w_qkv_here, w_out_t)
        hidden_two.append(layer_one[m] + branch)
        attn_kept.append((normed, scale, kept))
    two_kept, results = [], []
    for m in each:
        cot_all[m] = gather_finish(cot_all[m])
        normed, scale, own = rms_forward(hidden_two[m], gain_moe)
        total, kept = moe_forward(own, masks[m][1], moe_a)
        results.append(total)
        two_kept.append((normed, scale, kept))

    gains = [0.0, 0.0, 0.0, 0.0]

    def up_over_dp(g):
        return lax.psum_scatter(g, "dp", scatter_dimension=0, tiled=True)

    def low_over_dp(g):
        g = g.reshape(local_experts, EXP_FF, D)
        return lax.psum_scatter(g, "dp", scatter_dimension=1, tiled=True)

    def expert_out(g_up, g_low):
        units = local_experts * EXP_FF
        cols = []
        for e in range(local_experts):
            low, high = e * EXP_FF, (e + 1) * EXP_FF
            pair = [g_up[:, low:high], g_up[:, units + low : units + high]]
            cols.append(jnp.concatenate(pair, axis=1).astype(f32))
        return jnp.stack(cols), g_low.astype(f32)

    saving = lax.axis_size("w") > 1

    def moe_stage(grads, kept_all, w, gain, *before, riders=None):
        grads = list(grads)
        backs, first_rows = [], []
        for m in each:
            rider = None if riders is None else riders[m][1]
            total, side = moe_backward(grads[m], kept_all[m][2], w, experts_total, rider)
            own, sent = return_start(narrow(total))
            first_rows.append(side[6][:own_rows])
            if saving:
                back = return_finish(own, sent)
                hold = (back, moe_weight_grads([side]), grads[m + 1 :])
                back, newer, grads[m + 1 :] = lax.optimization_barrier(hold)
                weights = newer if m == 0 else [a + b for a, b in zip(weights, newer)]
            else:
                hidden, g_pre, own = fence(side[2], side[4], own)
                g_low = tn_sum([(hidden, side[1])])
                g_up = tn_sum([(side[0], g_pre)])
                g_pre_s, g_low, g_up = fence(side[5], g_low, g_up)
                g_sin = tn_sum([(side[6], g_pre_s)])
                sent, g_sin = fence(sent, g_sin)
                weights = (g_up, g_low, g_sin, tn_sum([(side[7], side[3])]))
                back = return_finish(own, sent)
            backs.append(back)
        backs[-1], before = fence(backs[-1], before)
        grad_gain = 0.0
        values, logits = [], []
        for m in each:
            normed, scale, kept = kept_all[m]
            grad_in, grad_logits = moe_finish(backs[m], kept, w, experts_total)
            logits.append(grad_logits)
            grad_values, part = rms_backward(grad_in, normed, scale, gain)
            grad_gain = grad_gain + part
            values.append(grad_values)
        g_router = tn_sum(list(zip(first_rows, logits)), f32)
        return values, weights, grad_gain, g_router, before

    values, (g_in_a, g_down_a, g_sin_a, g_sdown_a), gains[3], g_router, _ = moe_stage(
        cot_all, two_kept, moe_a, gain_moe
    )
    sum_in_a = up_over_dp(g_in_a)
    sum_down_a = low_over_dp(g_down_a)
    grad_two = [cotangent[m].astype(f32) + values[m] for m in each]
    for m in each:
        total, grad_two[m] = fence(results[m], grad_two[m])
        results[m] = return_start(narrow(total))

    grad_layer, sides = [], []
    attn_back = []
    for m in each:
        grad_in, side = attn_backward(
            grad_two[m].astype(bf16), attn_kept[m][2], w_qkv_here, w_out_t
        )
        attn_back.append(grad_in)
        sides.append(side)
    g_attn = by_rows(
        jnp.concatenate(
            [
                by_rows(tn_sum([(s[0], s[1]) for s in sides])),
                by_rows(tn_sum([(s[3], s[2]) for s in sides])),
            ],
            axis=1,
        )
    )
    attn_back[-1], g_attn = lax.optimization_barrier((attn_back[-1], g_attn))
    g_attn = lax.psum_scatter(g_attn, FS, scatter_dimension=0, tiled=True)
    g_part = g_attn
    for m in each:
        normed, scale, _ = attn_kept[m]
        grad_values, part = rms_backward(attn_back[m], normed, scale, gain_attn)
        gains[2] = gains[2] + part
        grad_layer.append(grad_two[m] + grad_values)

    values, (g_in_m, g_down_m, g_sin_m, g_sdown_m), gains[1], g_router_m, before = moe_stage(
        [gather_rows(g.astype(bf16)) for g in grad_layer],
        one_kept,
        moe_m,
        gain_moe_m,
        sum_in_a,
        sum_down_a,
        riders=results,
    )
    sum_in_a, sum_down_a = before
    for m in each:
        results[m] = (hidden_two[m] + return_finish(*results[m])).astype(bf16)
    out_expert_in, out_expert_down = expert_out(sum_in_a, sum_down_a)
    sum_in_m = up_over_dp(g_in_m)
    sum_down_m = low_over_dp(g_down_m)
    grad_one = [grad_layer[m] + values[m] for m in each]

    def attn_owner(g_part):
        blocks = g_part.reshape(n_z, 2 * rows, -1)
        here = lax.axis_index("z")
        own = lax.dynamic_index_in_dim(blocks, here, 0, keepdims=False)
        sent = []
        for shift in range(1, n_z):
            block = lax.dynamic_index_in_dim(blocks, (here + shift) % n_z, 0, keepdims=False)
            sent.append(send(block, "z", ring(shift)))
        return own, sent

    def attn_total(own, sent):
        total = own.astype(f32)
        for block in sent:
            total = total + block.astype(f32)
        return lax.all_to_all(
            total.astype(bf16).reshape(2, rows, -1), "core", split_axis=0, concat_axis=0, tiled=True
        ).astype(f32)

    small = None
    mamba_sides, mamba_back, mixes, own_normed = [], [], [], []
    for m in each:
        mix_branch, gate_scale = mix_kept[m]
        x_rows, _, mamba_in, scan_args, _ = mamba_kept[m]
        x_rows, _ = fence(x_rows, grad_one[m])
        x_rows = x_rows[:, :D].astype(f32)
        normed_x = x_rows * row_scale(x_rows)
        own_normed.append(normed_x[:own_rows])
        grad_mix = grad_one[m].astype(bf16)
        mean_term = jnp.sum(grad_mix.astype(f32) * mix_branch, axis=-1, keepdims=True) / DI
        extra = lanes(split_two(gate_scale) + split_two(mean_term), 128)
        rows_all = gather_rows(jnp.concatenate([grad_mix, extra], axis=1))
        if m == micro - 1:
            rows_all, out_expert_in, out_expert_down = fence(
                rows_all, out_expert_in, out_expert_down
            )
        mix_all = rows_all[:, :D]
        extra_all = rows_all[:, D:]
        scale_all = extra_all[:, 0:1].astype(f32) + extra_all[:, 1:2].astype(f32)
        scaled_mix = (mix_all.astype(f32) * scale_all).astype(bf16)
        mixes.append(scaled_mix)
        if m == micro - 1:
            g_mix = tn_sum([(x, k[4]) for x, k in zip(mixes, mamba_kept)])
            mix_all, g_mix = fence(mix_all, by_rows(g_mix))
        if m == micro - 1:
            g_part, mix_all = fence(g_part, mix_all)
            attn_sent = attn_owner(g_part)
        grad_gated = nn(mix_all, w_mix_t, bf16)
        grad_scan, *grads = scan_backward(
            heads, length, *scan_args, grad_gated, extra_all
        )
        small = grads if small is None else [a + b for a, b in zip(small, grads)]
        own_part, sent_part = attn_sent if m == micro - 1 else (None, [])
        if m == micro - 1:
            sent_part[:2], grad_scan = fence(sent_part[:2], grad_scan)
        total = nt(grad_scan, w_scan)
        if m == micro - 1:
            sent_part[2:], total = fence(sent_part[2:], total)
            total, sum_in_m = fence(total, sum_in_m)
            attn_sent = (own_part, sent_part)
        gains[0] = gains[0] + jnp.sum(total * normed_x, axis=0)
        own, sent = return_start(total)
        grad_scan, own = fence(grad_scan, own)
        mamba_sides.append((mamba_in, grad_scan))
        mamba_back.append((own, sent))

    def rows_sum(packed):
        return lax.psum_scatter(packed, FS, scatter_dimension=0, tiled=True)

    def rows_back(packed):
        return lax.all_to_all(
            packed.reshape(n_tp, rows, -1), TP, split_axis=0, concat_axis=0, tiled=True
        ).astype(f32)

    def owned(block):
        return block.transpose(1, 0, 2).reshape(rows, -1)

    g_s = rows_sum(
        jnp.concatenate([g_mix, g_sin_m, g_sdown_m, g_sin_a, g_sdown_a], axis=1)
    )

    g_scan = by_rows(tn_sum(mamba_sides, f32))
    mamba_back, g_scan = fence(mamba_back, g_scan)
    mamba_back = [return_finish(*pair) for pair in mamba_back]
    g_attn = attn_total(*attn_sent)
    g_s, mamba_back[-1] = fence(g_s, mamba_back[-1])
    g_s = rows_back(g_s)
    out_expert_in_m, out_expert_down_m = expert_out(sum_in_m, sum_down_m)

    conv_sums, chan_sums, head_sums = small
    g_gate = chan_sums[0]
    g_skip = jnp.sum(chan_sums[1].reshape(heads, HP), axis=1)
    head_grad = jnp.stack([head_sums[0, :heads], head_sums[1, :heads], g_skip])

    def spread(part, width):
        zeros = jnp.zeros(part.shape[:-1] + (width,), f32)
        return lax.dynamic_update_slice_in_dim(zeros, part[..., :chan], slot * chan, axis=-1)

    conv_grad = jnp.concatenate([conv_sums[CK : CK + 1], conv_sums[:CK]], axis=0)
    conv_grad = spread(conv_grad, conv_total) + jnp.pad(conv_grad[:, chan:], ((0, 0), (DI, 0)))
    conv_grad = conv_grad.reshape(CK + 1, n_all, conv_here).transpose(1, 0, 2).reshape(n_all, -1)
    vec_grad = jnp.concatenate([spread(g_gate, DI).reshape(n_all, gate_here), conv_grad], axis=1)
    vec_grad = jnp.pad(vec_grad, ((0, 0), (0, rows * vec_cols - vec_len))).reshape(D, vec_cols)
    little = jnp.concatenate([g[:, None] for g in gains] + [g_router_m, g_router, vec_grad], axis=1)
    spare = step_width - heads - small_cols
    g_scan = jnp.pad(g_scan, ((0, 0), (0, step_width - 128)))
    g_m = rows_sum((g_scan + jnp.pad(little, ((0, 0), (in_width + heads, spare)))).astype(bf16))
    g_m, g_s = fence(g_m, g_s)
    g_m = rows_back(g_m)
    grads_in = []
    for m in each:
        scale_x = mamba_kept[m][1]
        grad_values, _ = rms_backward(mamba_back[m], own_normed[m], scale_x, gain_mamba)
        grads_in.append(grad_one[m] + grad_values)

    out_w_in = jnp.concatenate(
        [
            owned(g_m[:, :, :chan]),
            owned(g_m[:, :, chan : 2 * chan]),
            jnp.sum(g_m[:, :, 2 * chan : in_width], axis=0),
        ],
        axis=1,
    )
    out_mix = owned(g_s[:, :, :chan]).T
    out_w_dt = owned(g_m[:, :, in_width : in_width + heads])
    little = jnp.sum(g_m[:, :, in_width + heads : in_width + heads + small_cols], axis=0)
    vec = little[:, 4 + 2 * experts_total :].reshape(-1)
    out_gate = vec[:gate_here]
    out_conv_b = vec[gate_here : gate_here + conv_here]
    out_conv_w = vec[gate_here + conv_here : vec_len].reshape(CK, conv_here)

    head_grad = lax.dynamic_update_slice(jnp.zeros((8, 128), f32), head_grad, (0, slot * heads))
    head_grad, mamba_back[-1] = fence(head_grad, mamba_back[-1])
    for axis in ALL:
        size = lax.axis_size(axis)
        step = 1
        while step < size:
            pairs = [(i, i ^ step) for i in range(size)]
            head_grad = head_grad + send(head_grad, axis, pairs)
            step *= 2
    head_grad = head_grad[:3, :MH]

    cuts = (q_width, q_width + kv_width, q_width + 2 * kv_width)
    out_w_qkv = jnp.concatenate(
        [
            owned(g_attn[:, :, : cuts[0]]),
            owned(g_attn[:, :, cuts[0] : cuts[1]]),
            owned(g_attn[:, :, cuts[1] : cuts[2]]),
        ],
        axis=1,
    )
    out_w_out = owned(g_attn[:, :, cuts[2] :]).T

    def shared_out(block):
        g_sin = jnp.concatenate([owned(block[:, :, :ff]), owned(block[:, :, ff : 2 * ff])], axis=1)
        return g_sin, owned(block[:, :, 2 * ff :]).T

    out_sin_m, out_sdown_m = shared_out(g_s[:, :, chan : chan + 3 * ff])
    out_sin, out_sdown = shared_out(g_s[:, :, chan + 3 * ff :])

    return (
        jnp.stack(results).reshape(batches, length, D),
        jnp.stack(grads_in).reshape(batches, length, D),
        little[:, 0],
        out_w_in,
        out_w_dt,
        out_conv_w,
        out_conv_b,
        head_grad[0],
        head_grad[1],
        head_grad[2],
        out_gate,
        out_mix,
        little[:, 1],
        little[:, 4 : 4 + experts_total],
        out_sin_m,
        out_sdown_m,
        out_expert_in_m,
        out_expert_down_m,
        little[:, 2],
        out_w_qkv,
        out_w_out,
        little[:, 3],
        little[:, 4 + experts_total : 4 + 2 * experts_total],
        out_sin,
        out_sdown,
        out_expert_in,
        out_expert_down,
    )


def solution(mesh):
    n_dp, n_ex = mesh.shape["dp"], mesh.shape["expert"]
    outer = n_ex // 8
    fine = Mesh(mesh.devices.reshape(n_dp, outer, 4, 2), ALL)
    split = P(ALL)
    row = P(ALL, None)
    col = P(None, ALL)
    mid = P(None, ALL, None)
    part = P(EX, "dp", None)
    same = P()
    return jax.shard_map(
        body,
        mesh=fine,
        in_specs=(
            mid,
            mid,
            P(None, None, ALL, None),
            split,
            row,
            row,
            col,
            split,
            same,
            same,
            same,
            split,
            col,
            split,
            row,
            row,
            col,
            part,
            part,
            split,
            row,
            col,
            split,
            row,
            row,
            col,
            part,
            part,
            mid,
        ),
        out_specs=(
            mid,
            mid,
            split,
            row,
            row,
            col,
            split,
            same,
            same,
            same,
            split,
            col,
            split,
            row,
            row,
            col,
            part,
            part,
            split,
            row,
            col,
            split,
            row,
            row,
            col,
            part,
            part,
        ),
        check_vma=False,
    )
```

```python
import functools

import jax
import jax.numpy as jnp
from jax import lax
from jax.experimental import pallas as pl
from jax.experimental.pallas import tpu as pltpu
from jax.experimental.layout import Layout, with_layout_constraint
from jax.sharding import Mesh, PartitionSpec as P

D = 1536
QH = 12
KVH = 4
HEAD = 128
EXP_FF = 512
SH_FF = 1024
TOP = 6
MH = 48
HP = 64
STATE = 128
CK = 4
DI = 3072

bf16 = jnp.bfloat16
f32 = jnp.float32
epsilon = 1e-05
masked_value = -1e30
highest = lax.Precision.HIGHEST
ALL = ("dp", "w", "z", "core")
EX = ("w", "z", "core")
TP = ("z", "core")
FS = ("dp", "w")
SWAP = [(0, 1), (1, 0)]


def dot(a, b, dims, out=f32):
    r = lax.dot_general(a, b, (dims, ((), ())), preferred_element_type=f32)
    return r if out == f32 else r.astype(out)


def nn(a, b, out=f32):
    return dot(a, b, ((1,), (0,)), out)


def nt(a, b, out=f32):
    return dot(a, b, ((1,), (1,)), out)


def tn(a, b, out=f32):
    return dot(a, b, ((0,), (0,)), out)


def ring(shift, axis="z"):
    n = lax.axis_size(axis)
    return [(i, (i + shift) % n) for i in range(n)]


def wide(x):
    parts = [x] + [lax.ppermute(x, "w", ring(s, "w")) for s in range(1, lax.axis_size("w"))]
    return parts[0] if len(parts) == 1 else jnp.concatenate(parts, axis=0)


def narrow(total):
    n = lax.axis_size("w")
    rows = total.shape[0] // n
    out = total[:rows]
    for s in range(1, n):
        part = total[s * rows : (s + 1) * rows].astype(bf16)
        out = out + lax.ppermute(part, "w", ring(-s, "w")).astype(f32)
    return out


def add_first(total, part):
    rows = part.shape[0]
    if rows == total.shape[0]:
        return total + part
    return jnp.concatenate([total[:rows] + part, total[rows:]], axis=0)


def fence(*trees):
    if lax.axis_size("w") > 1:
        return trees
    return lax.optimization_barrier(trees)


def by_rows(x):
    if lax.axis_size("w") > 1:
        return x
    return with_layout_constraint(x, Layout(major_to_minor=tuple(range(x.ndim))))


def send(x, axis, pairs):
    return by_rows(lax.ppermute(by_rows(x), axis, pairs))


def gather_start(x):
    return [x] + [send(x, "z", ring(s)) for s in range(1, lax.axis_size("z"))]


def gather_finish(parts):
    mine = by_rows(jnp.concatenate(parts, axis=0))
    return by_rows(jnp.concatenate([mine, send(mine, "core", SWAP)], axis=0))


def gather_rows(x):
    return gather_finish(gather_start(x))


def return_start(total):
    n = lax.axis_size("z")
    half = total.shape[0] // 2
    rows = half // n
    recv = send(total[half:].astype(bf16), "core", SWAP)
    mine = total[:half] + recv.astype(f32)
    sent = [
        send(mine[s * rows : (s + 1) * rows].astype(bf16), "z", ring(-s)) for s in range(1, n)
    ]
    return mine[:rows], sent


def return_finish(own, sent):
    for part in sent:
        own = own + part.astype(f32)
    return own


def return_rows(total):
    return return_finish(*return_start(total))


def pair_gather(x):
    return by_rows(jnp.concatenate([x, send(x, "core", SWAP)], axis=0))


def pair_return(total):
    half = total.shape[0] // 2
    recv = send(total[half:].astype(bf16), "core", SWAP)
    return total[:half] + recv.astype(f32)


def split_two(x):
    high = x.astype(bf16)
    return [high, (x - high.astype(f32)).astype(bf16)]


def row_scale(values):
    return lax.rsqrt(jnp.mean(values * values, axis=-1, keepdims=True) + epsilon)


def rms_forward(values, gain):
    scale = row_scale(values)
    normed = values * scale
    return normed, scale, (normed * gain).astype(bf16)


def rms_backward(grad_result, normed, scale, gain):
    grad_gain = jnp.sum(grad_result * normed, axis=0)
    grad_normed = grad_result * gain
    grad_values = scale * (
        grad_normed - normed * jnp.mean(grad_normed * normed, axis=-1, keepdims=True)
    )
    return grad_values, grad_gain


def lanes(parts, width):
    used = sum(p.shape[-1] for p in parts)
    rows = parts[0].shape[0]
    if used < width:
        parts = parts + [jnp.zeros((rows, width - used), bf16)]
    return jnp.concatenate(parts, axis=1)


def scan_core(proj, step_raw, seg_col, seg_row, taps, bias, heads_par):
    length = proj.shape[0]
    chan = proj.shape[1] - 2 * STATE
    chan = chan // 2
    z = proj[:, :chan].astype(f32)
    conv_in = proj[:, chan:].astype(f32)
    place = lax.broadcasted_iota(jnp.int32, (length, 1), 0)
    shifted, masks = [], []
    conv_sum = bias
    for k in range(CK):
        if k == 0:
            moved, mask = conv_in, None
            conv_sum = conv_sum + taps[0:1] * moved
        else:
            same = pltpu.roll(seg_col, k, 0) == seg_col
            mask = jnp.where(same & (place >= k), 1.0, 0.0)
            moved = pltpu.roll(conv_in, k, 0) * mask
            conv_sum = conv_sum + taps[k : k + 1] * moved
        shifted.append(moved)
        masks.append(mask)
    logistic = jax.nn.sigmoid(conv_sum)
    act = conv_sum * logistic
    pre = step_raw + heads_par[0:1]
    step = jnp.maximum(pre, 0.0) + jnp.log1p(jnp.exp(-jnp.abs(pre)))
    decay_rate = heads_par[1:2]
    rows_pos = lax.broadcasted_iota(jnp.int32, (length, length), 0)
    cols_pos = lax.broadcasted_iota(jnp.int32, (length, length), 1)
    lower = jnp.where(cols_pos <= rows_pos, 1.0, 0.0)
    cum = lax.dot_general(
        lower, step * decay_rate, (((1,), (0,)), ((), ())), precision=highest, preferred_element_type=f32
    )
    allowed = (seg_col == seg_row) & (cols_pos <= rows_pos)
    b_low = act[:, chan : chan + STATE].astype(bf16)
    c_low = act[:, chan + STATE :].astype(bf16)
    cb = nt(c_low, b_low)
    return dict(
        chan=chan, z=z, conv_in=conv_in, shifted=shifted, masks=masks, conv_sum=conv_sum,
        logistic=logistic, act=act, pre=pre, step=step, rate=decay_rate, lower=lower, cum=cum,
        cum_t=cum.T, step_t=step.T, allowed=allowed, b=b_low, c=c_low, cb=cb,
    )


def head_table(s, h):
    gap = s["cum"][:, h : h + 1] - s["cum_t"][h : h + 1, :]
    decay = jnp.exp(jnp.where(s["allowed"], gap, masked_value))
    return decay, s["step_t"][h : h + 1, :]


def pair_scan(s, heads, low):
    lane = lax.broadcasted_iota(jnp.int32, (1, 2 * HP), 1)
    blocks, mixes, tables = [], [], []
    for j in range(heads // 2):
        both = low[:, j * 2 * HP : (j + 1) * 2 * HP]
        outs = []
        for h in (2 * j, 2 * j + 1):
            decay, step_row = head_table(s, h)
            mix = (decay * s["cb"] * step_row).astype(bf16)
            outs.append(nn(mix, both))
            mixes.append(mix)
            tables.append((decay, step_row))
        blocks.append(jnp.where(lane < HP, outs[0], outs[1]))
    return jnp.concatenate(blocks, axis=1), mixes, tables


def scan_forward_kernel(heads, proj_ref, step_ref, col_ref, row_ref, conv_ref, chan_ref, head_ref, gained_ref, square_ref):
    s = scan_core(
        proj_ref[...], step_ref[...], col_ref[...], row_ref[0], conv_ref[0:CK], conv_ref[CK : CK + 1], head_ref[...]
    )
    chan = s["chan"]
    inputs = s["act"][:, :chan]
    scan, _, _ = pair_scan(s, heads, inputs.astype(bf16))
    scan = scan + chan_ref[1:2] * inputs
    gated = scan * s["z"] * jax.nn.sigmoid(s["z"])
    gained_ref[...] = (gated * chan_ref[0:1]).astype(bf16)
    square_ref[...] = jnp.broadcast_to(jnp.sum(gated * gated, axis=1, keepdims=True), square_ref.shape)


def scan_backward_kernel(
    heads, proj_ref, step_ref, col_ref, row_ref, conv_ref, chan_ref, head_ref, grad_ref, extra_ref,
    dproj_ref, dconv_ref, dchan_ref, dhead_ref, flat_ref,
):
    @pl.when(pl.program_id(0) == 0)
    def _():
        dconv_ref[...] = jnp.zeros_like(dconv_ref)
        dchan_ref[...] = jnp.zeros_like(dchan_ref)
        dhead_ref[...] = jnp.zeros_like(dhead_ref)

    taps = conv_ref[0:CK]
    s = scan_core(proj_ref[...], step_ref[...], col_ref[...], row_ref[0], taps, conv_ref[CK : CK + 1], head_ref[...])
    chan, length = s["chan"], s["z"].shape[0]
    gain, skip = chan_ref[0:1], chan_ref[1:2]
    inputs = s["act"][:, :chan]
    low = inputs.astype(bf16)
    scan, mixes, tables = pair_scan(s, heads, low)
    scan = scan + skip * inputs
    z = s["z"]
    sig = jax.nn.sigmoid(z)
    silu = z * sig
    gated = scan * silu
    extra = extra_ref[...].astype(f32)
    scale = extra[:, 0:1] + extra[:, 1:2]
    mean = extra[:, 2:3] + extra[:, 3:4]
    grad = grad_ref[...].astype(f32)
    normed = gated * scale
    d_gated = scale * (grad * gain - normed * mean)
    d_scan = d_gated * silu
    d_z = d_gated * scan * sig * (1.0 + z * (1.0 - sig))
    d_low = d_scan.astype(bf16)
    lane = lax.broadcasted_iota(jnp.int32, (1, 2 * HP), 1)
    spot = lax.broadcasted_iota(jnp.int32, (1, s["step"].shape[1]), 1)
    d_cb = jnp.zeros((length, length), f32)
    d_cum = jnp.zeros(s["step"].shape, f32)
    flat_ref[...] = jnp.zeros_like(flat_ref)
    blocks = []
    for j in range(heads // 2):
        cut = slice(j * 2 * HP, (j + 1) * 2 * HP)
        both, d_both = low[:, cut], d_low[:, cut]
        outs = []
        for i, h in enumerate((2 * j, 2 * j + 1)):
            decay, step_row = tables[h]
            outs.append(tn(mixes[h], d_both))
            keep = (lane < HP) if i == 0 else (lane >= HP)
            d_mix = nt(jnp.where(keep, d_both, jnp.zeros_like(d_both)), both)
            part = d_mix * decay
            d_cb = d_cb + part * step_row
            part = part * s["cb"]
            flat_ref[h : h + 1, 0:length] = jnp.sum(part, axis=0, keepdims=True)
            column = jnp.sum(part * step_row, axis=1, keepdims=True)
            d_cum = d_cum + jnp.where(spot == h, column, 0.0)
        blocks.append(jnp.where(lane < HP, outs[0], outs[1]))
    d_inputs = jnp.concatenate(blocks, axis=1) + skip * d_scan
    from_rows = flat_ref[...].T[0:length]
    d_cum = d_cum - s["step"] * from_rows
    d_rate = lax.dot_general(
        s["lower"], d_cum, (((0,), (0,)), ((), ())), precision=highest, preferred_element_type=f32
    )
    d_step = from_rows + d_rate * s["rate"]
    d_pre = jnp.where(spot < heads, d_step * jax.nn.sigmoid(s["pre"]), 0.0)
    d_cb_low = d_cb.astype(bf16)
    d_act = jnp.concatenate([d_inputs, tn(d_cb_low, s["c"]), nn(d_cb_low, s["b"])], axis=1)
    logistic = s["logistic"]
    d_sum = d_act * logistic * (1.0 + s["conv_sum"] * (1.0 - logistic))
    d_in = taps[0:1] * d_sum
    for k in range(1, CK):
        back = d_sum * s["masks"][k] * taps[k : k + 1]
        d_in = d_in + pltpu.roll(back, length - k, 0)
    dproj_ref[...] = jnp.concatenate([d_z, d_in, d_pre], axis=1).astype(bf16)
    for k in range(CK):
        dconv_ref[k : k + 1] += jnp.sum(d_sum * s["shifted"][k], axis=0, keepdims=True)
    dconv_ref[CK : CK + 1] += jnp.sum(d_sum, axis=0, keepdims=True)
    dchan_ref[0:1] += jnp.sum(grad * normed, axis=0, keepdims=True)
    dchan_ref[1:2] += jnp.sum(d_scan * inputs, axis=0, keepdims=True)
    dhead_ref[0:1] += jnp.sum(d_pre, axis=0, keepdims=True)
    dhead_ref[1:2] += jnp.sum(d_rate * s["step"] * s["rate"], axis=0, keepdims=True)


def scan_specs(length, width, lanes_, conv, chan):
    def whole(shape):
        return pl.BlockSpec(shape, lambda i: (0,) * len(shape))

    rows = lambda w: pl.BlockSpec((length, w), lambda i: (i, 0))
    return rows, whole, [
        rows(width), rows(lanes_), rows(1), pl.BlockSpec((1, 1, length), lambda i: (i, 0, 0)),
        whole((8, conv)), whole((8, chan)), whole((8, lanes_)),
    ]


def scan_forward(heads, length, proj, step, seg_col, seg_row, conv_par, chan_par, head_par):
    total, width = proj.shape
    chan = heads * HP
    rows, whole, specs = scan_specs(length, width, step.shape[1], width - chan, chan)
    return pl.pallas_call(
        functools.partial(scan_forward_kernel, heads),
        grid=(total // length,),
        in_specs=specs,
        out_specs=[rows(chan), rows(128)],
        out_shape=[jax.ShapeDtypeStruct((total, chan), bf16), jax.ShapeDtypeStruct((total, 128), f32)],
        compiler_params=pltpu.CompilerParams(vmem_limit_bytes=32 << 20),
        name="scan_forward",
    )(proj, step, seg_col, seg_row, conv_par, chan_par, head_par)


def scan_backward(heads, length, proj, step, seg_col, seg_row, conv_par, chan_par, head_par, grad, extra):
    total, width = proj.shape
    chan = heads * HP
    lanes_ = step.shape[1]
    rows, whole, specs = scan_specs(length, width, lanes_, width - chan, chan)
    return pl.pallas_call(
        functools.partial(scan_backward_kernel, heads),
        grid=(total // length,),
        in_specs=specs + [rows(chan), rows(128)],
        out_specs=[rows(width + lanes_), whole((8, width - chan)), whole((8, chan)), whole((8, lanes_))],
        out_shape=[
            jax.ShapeDtypeStruct((total, width + lanes_), bf16),
            jax.ShapeDtypeStruct((8, width - chan), f32),
            jax.ShapeDtypeStruct((8, chan), f32),
            jax.ShapeDtypeStruct((8, lanes_), f32),
        ],
        scratch_shapes=[pltpu.VMEM((128, 128), f32)],
        compiler_params=pltpu.CompilerParams(vmem_limit_bytes=32 << 20),
        name="scan_backward",
    )(proj, step, seg_col, seg_row, conv_par, chan_par, head_par, grad, extra)


def swiglu(gate, up):
    return gate * jax.nn.sigmoid(gate) * up


def swiglu_back(grad, gate, up):
    logistic = jax.nn.sigmoid(gate)
    grad_gate = grad * up * logistic * (1.0 + gate * (1.0 - logistic))
    return grad_gate.astype(bf16), (grad * gate * logistic).astype(bf16)


def gate_table(moe_in, mask, router):
    logits = nn(moe_in, router)
    picked = jnp.where(mask, logits, masked_value)
    peak = jnp.max(picked, axis=-1, keepdims=True)
    ex = jnp.where(mask, jnp.exp(picked - peak), 0.0)
    return ex / jnp.sum(ex, axis=-1, keepdims=True)


def unit_gates(local, units):
    count = local.shape[1]
    owner = lax.broadcasted_iota(jnp.int32, (1, units), 1) // EXP_FF
    spread = local[:, count - 1 :]
    for e in range(count - 1):
        spread = jnp.where(owner == e, local[:, e : e + 1], spread)
    return spread, owner


def moe_forward(own_in, mask, w, riders=None):
    rows = own_in.shape[0]
    base_in = gather_rows(own_in)
    moe_in = wide(base_in)
    gates = gate_table(moe_in, mask, w["router"])
    units = w["expert_down"].shape[0]
    count = units // EXP_FF
    first = lax.axis_index(EX) * count
    local = lax.dynamic_slice(gates, (0, first), (gates.shape[0], count))
    pre = nn(moe_in, w["expert_in"], bf16)
    pre_s = nn(base_in, w["shared_in"], bf16)
    if riders is not None:
        riders = gather_start(riders)
        riders[1], pre = fence(riders[1], pre)
    pre, pre_s = lax.optimization_barrier((pre, pre_s))
    p = pre.astype(f32)
    spread, _ = unit_gates(local, units)
    hid = (swiglu(p[:, :units], p[:, units:]) * spread).astype(bf16)
    half = pre_s.shape[1] // 2
    p = pre_s.astype(f32)
    hid_s = swiglu(p[:, :half], p[:, half:]).astype(bf16)
    low = nn(hid, w["expert_down"])
    if riders is not None:
        riders[2:], low = fence(riders[2:], low)
    total = add_first(low, nt(hid_s, w["shared_down_t"]))
    kept = (moe_in, base_in, gates[:rows], local, pre, pre_s)
    return (total, kept) if riders is None else (total, kept, riders)


def moe_backward(base_z, kept, w, experts_total, riders=None):
    moe_in, base_in, own_gates, local, pre, pre_s = kept
    pre, pre_s, _ = lax.optimization_barrier((pre, pre_s, base_z))
    grad_z = wide(base_z)
    units = w["expert_down"].shape[0]
    count = units // EXP_FF
    first = lax.axis_index(EX) * count
    spread, owner = unit_gates(local, units)
    p = pre.astype(f32)
    gate, up = p[:, :units], p[:, units:]
    grad_hid = nt(grad_z, w["expert_down"])
    if riders is not None:
        riders[:1], grad_hid = fence(riders[:1], grad_hid)
    act = swiglu(gate, up)
    hidden = (act * spread).astype(bf16)
    product = grad_hid * act
    lane = lax.broadcasted_iota(jnp.int32, (1, experts_total), 1)
    table = jnp.zeros((grad_z.shape[0], experts_total), f32)
    for e in range(count):
        mine = jnp.sum(jnp.where(owner == e, product, 0.0), axis=-1, keepdims=True)
        table = table + local[:, e : e + 1] * mine * (lane == first + e).astype(f32)
    g_gate, g_up = swiglu_back(grad_hid * spread, gate, up)
    g_pre = jnp.concatenate([g_gate, g_up], axis=1)
    total = nt(g_pre, w["expert_in"])
    if riders is not None:
        riders[1:], total = fence(riders[1:], total)
    half = pre_s.shape[1] // 2
    p = pre_s.astype(f32)
    grad_hid = nn(base_z, w["shared_down_t"])
    hid_s = swiglu(p[:, :half], p[:, half:]).astype(bf16)
    g_gate, g_up = swiglu_back(grad_hid, p[:, :half], p[:, half:])
    g_pre_s = jnp.concatenate([g_gate, g_up], axis=1)
    total = add_first(total, nt(g_pre_s, w["shared_in"]))
    extra = -(-experts_total // 128) * 128
    table = jnp.pad(table, ((0, 0), (0, extra - experts_total)))
    total = jnp.concatenate([total, table], axis=1)
    side = (moe_in, grad_z, hidden, hid_s, g_pre, g_pre_s, base_in, base_z)
    return total, side


def moe_finish(back, kept, w, experts_total):
    own_gates = kept[2]
    weighted = back[:, D : D + experts_total]
    grad_logits = weighted - own_gates * jnp.sum(weighted, axis=-1, keepdims=True)
    grad_logits = grad_logits.astype(bf16)
    return back[:, :D] + nt(grad_logits, w["router"]), grad_logits


def tn_sum(pairs, out=bf16):
    if lax.axis_size("w") > 1:
        return tn(*[jnp.concatenate(side, axis=0) for side in zip(*pairs)], out)
    total = None
    for a, b in pairs:
        part = tn(a, b)
        total = part if total is None else total + part
    return total.astype(out)


def moe_weight_grads(sides):
    g_down = tn_sum([(s[2], s[1]) for s in sides])
    g_in = tn_sum([(s[0], s[4]) for s in sides])
    g_sin = tn_sum([(s[6], s[5]) for s in sides])
    g_sdown_t = tn_sum([(s[7], s[3]) for s in sides])
    return g_in, g_down, g_sin, g_sdown_t


def attn_mask(seg):
    length = seg.shape[1]
    rows_pos = lax.broadcasted_iota(jnp.int32, (length, length), 0)
    cols_pos = lax.broadcasted_iota(jnp.int32, (length, length), 1)
    return (seg[:, :, None] == seg[:, None, :]) & (cols_pos <= rows_pos)[None]


def attn_forward(own_in, allowed, w_qkv, w_out_t):
    seqs, length, _ = allowed.shape
    kv = KVH // 2
    group = QH // KVH
    q_width = kv * group * HEAD
    kv_width = kv * HEAD
    attn_in = pair_gather(own_in)
    packed = nn(attn_in, w_qkv, bf16)
    q = packed[:, :q_width].reshape(seqs, length, kv, group, HEAD)
    k = packed[:, q_width : q_width + kv_width].reshape(seqs, length, kv, HEAD)
    v = packed[:, q_width + kv_width :].reshape(seqs, length, kv, HEAD)
    scores = jnp.einsum("bqhgd,bkhd->bhgqk", q, k, preferred_element_type=f32) * HEAD**-0.5
    scores = jnp.where(allowed[:, None, None], scores, masked_value)
    peak = jnp.max(scores, axis=-1, keepdims=True)
    ex = jnp.exp(scores - peak)
    probs = ex / jnp.sum(ex, axis=-1, keepdims=True)
    context = jnp.einsum("bhgqk,bkhd->bqhgd", probs.astype(bf16), v, preferred_element_type=f32)
    context = context.reshape(seqs * length, q_width).astype(bf16)
    branch = pair_return(nt(context, w_out_t))
    return branch, (attn_in, q, k, v, probs, context)


def attn_backward(own_grad, kept, w_qkv, w_out_t):
    attn_in, q, k, v, probs, context = kept
    seqs, length, kv, group, _ = q.shape
    grad = pair_gather(own_grad)
    grad_context = nn(grad, w_out_t, bf16).reshape(seqs, length, kv, group, HEAD)
    probs_low = probs.astype(bf16)
    grad_v = jnp.einsum("bhgqk,bqhgd->bkhd", probs_low, grad_context, preferred_element_type=f32)
    grad_p = jnp.einsum("bqhgd,bkhd->bhgqk", grad_context, v, preferred_element_type=f32)
    delta = jnp.sum(probs * grad_p, axis=-1, keepdims=True)
    grad_s = (probs * (grad_p - delta)).astype(bf16)
    scale = HEAD**-0.5
    grad_q = jnp.einsum("bhgqk,bkhd->bqhgd", grad_s, k, preferred_element_type=f32) * scale
    grad_k = jnp.einsum("bhgqk,bqhgd->bkhd", grad_s, q, preferred_element_type=f32) * scale
    rows = seqs * length
    grad_packed = jnp.concatenate(
        [grad_q.reshape(rows, -1), grad_k.reshape(rows, -1), grad_v.reshape(rows, -1)], axis=1
    ).astype(bf16)
    grad_in = pair_return(nt(grad_packed, w_qkv))
    return grad_in, (attn_in, grad_packed, context, grad)


def by_owner(x, count):
    return x.reshape(x.shape[0], count, x.shape[1] // count)


def body(
    tokens,
    segments,
    routes,
    norm_mamba,
    w_in,
    w_dt,
    conv_w,
    conv_b,
    dt_bias,
    a_log,
    skip_scale,
    gate_norm,
    w_mix_out,
    norm_moe_m,
    router_m,
    shared_in_m,
    shared_down_m,
    expert_in_m,
    expert_down_m,
    norm_attn,
    w_qkv,
    w_out,
    norm_moe,
    router,
    shared_in,
    shared_down,
    expert_in,
    expert_down,
    cotangent,
):
    batches, length, _ = tokens.shape
    micro = batches if lax.axis_size("w") > 1 else 1
    seqs = batches // micro
    own_rows = seqs * length
    tokens = tokens.reshape(micro, own_rows, D)
    cotangent = cotangent.reshape(micro, own_rows, D)
    routes = routes.reshape(2, micro, own_rows, TOP)
    segments = segments.reshape(micro, own_rows)
    n_tp = lax.axis_size("z") * lax.axis_size("core")
    n_ex = lax.axis_size("w") * n_tp
    n_all = lax.axis_size("dp") * n_ex
    rows = w_in.shape[0]
    local_experts = expert_in.shape[0]
    experts_total = local_experts * n_ex
    heads = MH // n_tp
    chan = heads * HP
    ff = SH_FF // n_tp
    slot = lax.axis_index(TP)
    conv_total = DI + 2 * STATE
    conv_here = conv_w.shape[1]
    gate_here = gate_norm.shape[0]
    vec_len = gate_here + (CK + 1) * conv_here
    vec_cols = -(-vec_len // rows)
    small_cols = 4 + 2 * experts_total + vec_cols
    step_width = -(-(heads + small_cols) // 128) * 128

    vec = jnp.concatenate([gate_norm, conv_b, conv_w.reshape(-1)])
    vec = jnp.pad(vec, (0, rows * vec_cols - vec_len)).reshape(rows, vec_cols)
    gains_own = jnp.stack([norm_mamba, norm_moe_m, norm_attn, norm_moe], axis=1)
    little = jnp.concatenate([gains_own, router_m, router, vec], axis=1)

    def for_all(x):
        return jnp.broadcast_to(x[:, None], (rows, n_tp, x.shape[1]))

    def packed_columns(parts):
        return jnp.concatenate(parts, axis=2).transpose(1, 0, 2)

    def moved_columns(packed):
        moved = lax.all_to_all(packed, TP, split_axis=0, concat_axis=0, tiled=True)
        return moved.reshape(n_tp * rows, -1)

    def whole_rows(moved):
        return lax.all_gather(moved, FS, axis=0, tiled=True)

    def shared_pack(w_sin, w_sdown):
        return [
            by_owner(w_sin[:, :SH_FF], n_tp),
            by_owner(w_sin[:, SH_FF:], n_tp),
            by_owner(w_sdown.T, n_tp),
        ]

    blank = jnp.zeros((rows, n_tp, step_width - heads - small_cols), bf16)
    packed_m = packed_columns(
        [
            by_owner(w_in[:, :DI], n_tp),
            by_owner(w_in[:, DI : 2 * DI], n_tp),
            for_all(w_in[:, 2 * DI :]),
            by_owner(w_dt, n_tp),
            for_all(little),
            blank,
            by_owner(w_mix_out.T, n_tp),
        ]
    )
    moved_m = moved_columns(packed_m)

    expert_ids = jnp.arange(experts_total, dtype=jnp.int32)
    info_width = -(-(2 * experts_total + 1) // 128) * 128
    each = range(micro)
    rows_in = []
    for m in each:
        hot = [
            jnp.any(routes[b, m][:, :, None] == expert_ids, axis=1).astype(bf16) for b in range(2)
        ]
        info = lanes(hot + [segments[m][:, None].astype(bf16)], info_width)
        x_info, moved_m = fence(jnp.concatenate([tokens[m], info], axis=1), moved_m)
        rows_in.append(gather_rows(x_info))
    def low_weights(w_low):
        return lax.all_gather(w_low, "dp", axis=1, tiled=True).reshape(-1, D)

    low_m = low_weights(expert_down_m)
    moved_m, low_m = fence(moved_m, low_m)
    w_m = whole_rows(moved_m)
    in_width = 2 * chan + 2 * STATE
    w_in_here = w_m[:, :in_width]
    at = in_width + step_width
    w_step = w_m[:, in_width:at]
    w_dt_here = w_step[:, :128]
    small_all = w_step[:, heads : heads + small_cols]
    pick = (jnp.arange(128)[None, :] == heads + jnp.arange(8)[:, None]).astype(bf16)
    gain_rows = nt(pick, w_dt_here)
    gain_mamba, gain_moe_m, gain_attn, gain_moe = [gain_rows[i] for i in range(4)]
    router_m_full = small_all[:, 4 : 4 + experts_total]
    router_full = small_all[:, 4 + experts_total : 4 + 2 * experts_total]
    vec_all = small_all[:, 4 + 2 * experts_total :].reshape(n_all, rows * vec_cols).astype(f32)
    gain_gate = vec_all[:, :gate_here].reshape(DI)
    bias_all = vec_all[:, gate_here : gate_here + conv_here].reshape(conv_total)
    taps_all = vec_all[:, gate_here + conv_here : vec_len].reshape(n_all, CK, conv_here)
    taps_all = taps_all.transpose(1, 0, 2).reshape(CK, conv_total)

    def channels(full_row):
        mine = lax.dynamic_slice_in_dim(full_row, slot * chan, chan, axis=-1)
        return jnp.concatenate([mine, full_row[..., DI:]], axis=-1)

    taps = channels(taps_all)
    bias = channels(bias_all)
    gain_here = lax.dynamic_slice_in_dim(gain_gate, slot * chan, chan)
    dt_here = lax.dynamic_slice_in_dim(dt_bias, slot * heads, heads)
    log_here = lax.dynamic_slice_in_dim(a_log, slot * heads, heads)
    skip_here = lax.dynamic_slice_in_dim(skip_scale, slot * heads, heads)

    w_scan = w_m[:, : in_width + 128]
    w_mix_t = w_m[:, at:]

    def up_weights(w_up):
        count = w_up.shape[0]
        cols = [w_up[e, :, :EXP_FF] for e in range(count)] + [w_up[e, :, EXP_FF:] for e in range(count)]
        cols = by_rows(jnp.concatenate(cols, axis=1))
        return by_rows(lax.all_gather(cols, "dp", axis=0, tiled=True))

    up_m = up_weights(expert_in_m)
    kv = KVH // 2
    q_width = QH // 2 * HEAD
    kv_width = kv * HEAD
    q_all, kv_all = QH * HEAD, KVH * HEAD
    attn_pack = jnp.concatenate(
        [
            by_owner(w_qkv[:, :q_all], 2),
            by_owner(w_qkv[:, q_all : q_all + kv_all], 2),
            by_owner(w_qkv[:, q_all + kv_all :], 2),
            by_owner(w_out.T, 2),
        ],
        axis=2,
    ).transpose(1, 0, 2)
    packed_s = shared_pack(shared_in_m, shared_down_m) + shared_pack(shared_in, shared_down)
    packed_s, rows_in = fence(packed_columns(packed_s), rows_in)
    moved_s = moved_columns(packed_s)
    attn_pack, moved_s = fence(attn_pack, moved_s)
    attn_pack = lax.all_to_all(attn_pack, "core", split_axis=0, concat_axis=0, tiled=True)
    own = attn_pack.reshape(2 * rows, -1)
    n_z = lax.axis_size("z")
    attn_parts = [send(own, "z", ring(s)) for s in range(n_z - 1, 0, -1)] + [own]
    def eight(parts):
        block = jnp.concatenate([p.reshape(-1, p.shape[-1]) for p in parts], axis=0)
        return jnp.pad(block, ((0, 8 - block.shape[0]), (0, 0)))

    conv_par = eight([taps, bias])
    chan_par = eight([gain_here, jnp.repeat(skip_here, HP)])
    head_par = jnp.pad(eight([dt_here, -jnp.exp(log_here)]), ((0, 0), (0, 128 - heads)))
    x_own = [tokens[m].astype(f32) for m in each]
    masks, allowed, mamba_kept, mix_kept, hidden_one = [], [], [], [], []
    proj_all, cot_all = [], []
    for m in each:
        rows_all = rows_in[m]
        x_all = rows_all[:, :D].astype(f32)
        marks = wide(rows_all[:, D : D + 2 * experts_total]) > 0.5
        masks.append([marks[:, :experts_total], marks[:, experts_total:]])
        seg_col = rows_all[:, D + 2 * experts_total :][:, :1].astype(f32)
        seg_row = seg_col.reshape(n_tp * seqs, 1, length)
        seg = seg_row[:, 0].astype(jnp.int32)
        middle = n_tp * seqs // 2
        pair = jnp.concatenate([seg[:seqs], seg[middle : middle + seqs]], axis=0)
        allowed.append(attn_mask(pair))

        _, scale_x, mamba_in = rms_forward(x_all, gain_mamba)
        total_rows = mamba_in.shape[0]
        proj = nn(mamba_in, w_in_here, bf16)
        dt_raw = nn(mamba_in, w_dt_here)
        proj_all.append(proj)
        pars = (seg_col, seg_row, conv_par, chan_par, head_par)
        gained, square = scan_forward(heads, length, proj, dt_raw, *pars)
        if m == micro - 1:
            attn_parts, gained = fence(attn_parts, gained)
        partial = nt(gained, w_mix_t)
        high = square.astype(bf16).astype(f32)
        lane = lax.broadcasted_iota(jnp.int32, square.shape, 1)
        extra = jnp.where(lane == 0, high, jnp.where(lane == 1, square - high, 0.0))
        own, sent = return_start(jnp.concatenate([partial, extra], axis=1))
        back = return_finish(own, sent)
        gate_scale = lax.rsqrt((back[:, D : D + 1] + back[:, D + 1 : D + 2]) / DI + epsilon)
        mix_branch = back[:, :D] * gate_scale
        hidden_one.append(x_own[m] + mix_branch)
        mamba_kept.append((rows_all, scale_x[:own_rows], mamba_in, (proj, dt_raw, *pars), gained))
        mix_kept.append((mix_branch, gate_scale))

    twice = jnp.concatenate(attn_parts + attn_parts, axis=0)
    start = (n_z - 1 - lax.axis_index("z")) * 2 * rows
    attn_w = lax.dynamic_slice(twice, (start, 0), (n_z * 2 * rows, twice.shape[1]))
    attn_w = lax.all_gather(attn_w, FS, axis=0, tiled=True)
    w_qkv_here = attn_w[:, : q_width + 2 * kv_width]
    w_out_t = attn_w[:, q_width + 2 * kv_width :]

    w_s = whole_rows(moved_s)
    moe_m = {
        "router": router_m_full,
        "shared_in": w_s[:, : 2 * ff],
        "shared_down_t": w_s[:, 2 * ff : 3 * ff],
        "expert_in": up_m,
        "expert_down": low_m,
    }

    up_a, low_a = fence(up_weights(expert_in), low_weights(expert_down))
    moe_a = {
        "router": router_full,
        "shared_in": w_s[:, 3 * ff : 5 * ff],
        "shared_down_t": w_s[:, 5 * ff :],
        "expert_in": up_a,
        "expert_down": low_a,
    }

    one_kept, layer_one = [], []
    for m in each:
        normed, scale, own = rms_forward(hidden_one[m], gain_moe_m)
        total, kept, riders = moe_forward(own, masks[m][0], moe_m, cotangent[m])
        cot_all.append(riders)
        layer_one.append(hidden_one[m] + return_rows(narrow(total)))
        one_kept.append((normed, scale, kept))
    attn_kept, hidden_two = [], []
    for m in each:
        normed, scale, own = rms_forward(layer_one[m], gain_attn)
        branch, kept = attn_forward(own, allowed[m], w_qkv_here, w_out_t)
        hidden_two.append(layer_one[m] + branch)
        attn_kept.append((normed, scale, kept))
    two_kept, results = [], []
    for m in each:
        cot_all[m] = gather_finish(cot_all[m])
        normed, scale, own = rms_forward(hidden_two[m], gain_moe)
        total, kept = moe_forward(own, masks[m][1], moe_a)
        results.append(total)
        two_kept.append((normed, scale, kept))

    gains = [0.0, 0.0, 0.0, 0.0]

    def up_over_dp(g):
        return lax.psum_scatter(g, "dp", scatter_dimension=0, tiled=True)

    def low_over_dp(g):
        g = g.reshape(local_experts, EXP_FF, D)
        return lax.psum_scatter(g, "dp", scatter_dimension=1, tiled=True)

    def expert_out(g_up, g_low):
        units = local_experts * EXP_FF
        cols = []
        for e in range(local_experts):
            low, high = e * EXP_FF, (e + 1) * EXP_FF
            pair = [g_up[:, low:high], g_up[:, units + low : units + high]]
            cols.append(jnp.concatenate(pair, axis=1).astype(f32))
        return jnp.stack(cols), g_low.astype(f32)

    saving = lax.axis_size("w") > 1

    def moe_stage(grads, kept_all, w, gain, *before, riders=None):
        grads = list(grads)
        backs, first_rows = [], []
        for m in each:
            rider = None if riders is None else riders[m][1]
            total, side = moe_backward(grads[m], kept_all[m][2], w, experts_total, rider)
            own, sent = return_start(narrow(total))
            first_rows.append(side[6][:own_rows])
            if saving:
                back = return_finish(own, sent)
                hold = (back, moe_weight_grads([side]), grads[m + 1 :])
                back, newer, grads[m + 1 :] = lax.optimization_barrier(hold)
                weights = newer if m == 0 else [a + b for a, b in zip(weights, newer)]
            else:
                hidden, g_pre, own = fence(side[2], side[4], own)
                g_low = tn_sum([(hidden, side[1])])
                g_up = tn_sum([(side[0], g_pre)])
                sent[:1], g_low = fence(sent[:1], g_low)
                sent[1:], g_up = fence(sent[1:], g_up)
                g_sin = tn_sum([(side[6], side[5])])
                weights = (g_up, g_low, g_sin, tn_sum([(side[7], side[3])]))
                back = return_finish(own, sent)
            backs.append(back)
        backs[-1], before = fence(backs[-1], before)
        grad_gain = 0.0
        values, logits = [], []
        for m in each:
            normed, scale, kept = kept_all[m]
            grad_in, grad_logits = moe_finish(backs[m], kept, w, experts_total)
            logits.append(grad_logits)
            grad_values, part = rms_backward(grad_in, normed, scale, gain)
            grad_gain = grad_gain + part
            values.append(grad_values)
        g_router = tn_sum(list(zip(first_rows, logits)), f32)
        return values, weights, grad_gain, g_router, before

    values, (g_in_a, g_down_a, g_sin_a, g_sdown_a), gains[3], g_router, _ = moe_stage(
        cot_all, two_kept, moe_a, gain_moe
    )
    sum_in_a = up_over_dp(g_in_a)
    sum_down_a = low_over_dp(g_down_a)
    grad_two = [cotangent[m].astype(f32) + values[m] for m in each]
    for m in each:
        total, grad_two[m] = fence(results[m], grad_two[m])
        results[m] = return_start(narrow(total))

    grad_layer, sides = [], []
    attn_back = []
    for m in each:
        grad_in, side = attn_backward(
            grad_two[m].astype(bf16), attn_kept[m][2], w_qkv_here, w_out_t
        )
        attn_back.append(grad_in)
        sides.append(side)
    g_attn = by_rows(
        jnp.concatenate(
            [
                by_rows(tn_sum([(s[0], s[1]) for s in sides])),
                by_rows(tn_sum([(s[3], s[2]) for s in sides])),
            ],
            axis=1,
        )
    )
    attn_back[-1], g_attn = lax.optimization_barrier((attn_back[-1], g_attn))
    g_attn = lax.psum_scatter(g_attn, FS, scatter_dimension=0, tiled=True)
    g_part = g_attn
    for m in each:
        normed, scale, _ = attn_kept[m]
        grad_values, part = rms_backward(attn_back[m], normed, scale, gain_attn)
        gains[2] = gains[2] + part
        grad_layer.append(grad_two[m] + grad_values)

    values, (g_in_m, g_down_m, g_sin_m, g_sdown_m), gains[1], g_router_m, before = moe_stage(
        [gather_rows(g.astype(bf16)) for g in grad_layer],
        one_kept,
        moe_m,
        gain_moe_m,
        sum_in_a,
        sum_down_a,
        riders=results,
    )
    sum_in_a, sum_down_a = before
    for m in each:
        results[m] = (hidden_two[m] + return_finish(*results[m])).astype(bf16)
    out_expert_in, out_expert_down = expert_out(sum_in_a, sum_down_a)
    sum_in_m = up_over_dp(g_in_m)
    sum_down_m = low_over_dp(g_down_m)
    grad_one = [grad_layer[m] + values[m] for m in each]

    def attn_owner(g_part):
        blocks = g_part.reshape(n_z, 2 * rows, -1)
        here = lax.axis_index("z")
        own = lax.dynamic_index_in_dim(blocks, here, 0, keepdims=False)
        sent = []
        for shift in range(1, n_z):
            block = lax.dynamic_index_in_dim(blocks, (here + shift) % n_z, 0, keepdims=False)
            sent.append(send(block, "z", ring(shift)))
        return own, sent

    def attn_total(own, sent):
        total = own.astype(f32)
        for block in sent:
            total = total + block.astype(f32)
        return lax.all_to_all(
            total.astype(bf16).reshape(2, rows, -1), "core", split_axis=0, concat_axis=0, tiled=True
        ).astype(f32)

    small = None
    mamba_sides, mamba_back, mixes, own_normed = [], [], [], []
    for m in each:
        mix_branch, gate_scale = mix_kept[m]
        x_rows, _, mamba_in, scan_args, _ = mamba_kept[m]
        x_rows, _ = fence(x_rows, grad_one[m])
        x_rows = x_rows[:, :D].astype(f32)
        normed_x = x_rows * row_scale(x_rows)
        own_normed.append(normed_x[:own_rows])
        grad_mix = grad_one[m].astype(bf16)
        mean_term = jnp.sum(grad_mix.astype(f32) * mix_branch, axis=-1, keepdims=True) / DI
        extra = lanes(split_two(gate_scale) + split_two(mean_term), 128)
        rows_all = gather_rows(jnp.concatenate([grad_mix, extra], axis=1))
        if m == micro - 1:
            rows_all, out_expert_in, out_expert_down = fence(
                rows_all, out_expert_in, out_expert_down
            )
        mix_all = rows_all[:, :D]
        extra_all = rows_all[:, D:]
        scale_all = extra_all[:, 0:1].astype(f32) + extra_all[:, 1:2].astype(f32)
        scaled_mix = (mix_all.astype(f32) * scale_all).astype(bf16)
        mixes.append(scaled_mix)
        if m == micro - 1:
            g_mix = tn_sum([(x, k[4]) for x, k in zip(mixes, mamba_kept)])
            mix_all, g_mix = fence(mix_all, by_rows(g_mix))
        if m == micro - 1:
            g_part, mix_all = fence(g_part, mix_all)
            attn_sent = attn_owner(g_part)
        grad_gated = nn(mix_all, w_mix_t, bf16)
        grad_scan, *grads = scan_backward(
            heads, length, *scan_args, grad_gated, extra_all
        )
        small = grads if small is None else [a + b for a, b in zip(small, grads)]
        own_part, sent_part = attn_sent if m == micro - 1 else (None, [])
        if m == micro - 1:
            sent_part[:2], grad_scan = fence(sent_part[:2], grad_scan)
        total = nt(grad_scan, w_scan)
        if m == micro - 1:
            sent_part[2:], total = fence(sent_part[2:], total)
            total, sum_in_m = fence(total, sum_in_m)
            attn_sent = (own_part, sent_part)
        gains[0] = gains[0] + jnp.sum(total * normed_x, axis=0)
        own, sent = return_start(total)
        grad_scan, own = fence(grad_scan, own)
        mamba_sides.append((mamba_in, grad_scan))
        mamba_back.append((own, sent))

    def rows_sum(packed):
        return lax.psum_scatter(packed, FS, scatter_dimension=0, tiled=True)

    def rows_back(packed):
        return lax.all_to_all(
            packed.reshape(n_tp, rows, -1), TP, split_axis=0, concat_axis=0, tiled=True
        ).astype(f32)

    def owned(block):
        return block.transpose(1, 0, 2).reshape(rows, -1)

    g_s = rows_sum(
        jnp.concatenate([g_mix, g_sin_m, g_sdown_m, g_sin_a, g_sdown_a], axis=1)
    )

    g_scan = by_rows(tn_sum(mamba_sides, f32))
    last_own, last_sent = mamba_back[-1]
    last_sent[:1], g_scan = fence(last_sent[:1], g_scan)
    mamba_back = [return_finish(*pair) for pair in mamba_back]
    g_attn = attn_total(*attn_sent)
    g_s, mamba_back[-1] = fence(g_s, mamba_back[-1])
    g_s = rows_back(g_s)
    out_expert_in_m, out_expert_down_m = expert_out(sum_in_m, sum_down_m)

    conv_sums, chan_sums, head_sums = small
    g_gate = chan_sums[0]
    g_skip = jnp.sum(chan_sums[1].reshape(heads, HP), axis=1)
    head_grad = jnp.stack([head_sums[0, :heads], head_sums[1, :heads], g_skip])

    def spread(part, width):
        zeros = jnp.zeros(part.shape[:-1] + (width,), f32)
        return lax.dynamic_update_slice_in_dim(zeros, part[..., :chan], slot * chan, axis=-1)

    conv_grad = jnp.concatenate([conv_sums[CK : CK + 1], conv_sums[:CK]], axis=0)
    conv_grad = spread(conv_grad, conv_total) + jnp.pad(conv_grad[:, chan:], ((0, 0), (DI, 0)))
    conv_grad = conv_grad.reshape(CK + 1, n_all, conv_here).transpose(1, 0, 2).reshape(n_all, -1)
    vec_grad = jnp.concatenate([spread(g_gate, DI).reshape(n_all, gate_here), conv_grad], axis=1)
    vec_grad = jnp.pad(vec_grad, ((0, 0), (0, rows * vec_cols - vec_len))).reshape(D, vec_cols)
    little = jnp.concatenate([g[:, None] for g in gains] + [g_router_m, g_router, vec_grad], axis=1)
    spare = step_width - heads - small_cols
    g_scan = jnp.pad(g_scan, ((0, 0), (0, step_width - 128)))
    g_m = rows_sum((g_scan + jnp.pad(little, ((0, 0), (in_width + heads, spare)))).astype(bf16))
    g_m, g_s = fence(g_m, g_s)
    g_m = rows_back(g_m)
    grads_in = []
    for m in each:
        scale_x = mamba_kept[m][1]
        grad_values, _ = rms_backward(mamba_back[m], own_normed[m], scale_x, gain_mamba)
        grads_in.append(grad_one[m] + grad_values)

    out_w_in = jnp.concatenate(
        [
            owned(g_m[:, :, :chan]),
            owned(g_m[:, :, chan : 2 * chan]),
            jnp.sum(g_m[:, :, 2 * chan : in_width], axis=0),
        ],
        axis=1,
    )
    out_mix = owned(g_s[:, :, :chan]).T
    out_w_dt = owned(g_m[:, :, in_width : in_width + heads])
    little = jnp.sum(g_m[:, :, in_width + heads : in_width + heads + small_cols], axis=0)
    vec = little[:, 4 + 2 * experts_total :].reshape(-1)
    out_gate = vec[:gate_here]
    out_conv_b = vec[gate_here : gate_here + conv_here]
    out_conv_w = vec[gate_here + conv_here : vec_len].reshape(CK, conv_here)

    head_grad = lax.dynamic_update_slice(jnp.zeros((8, 128), f32), head_grad, (0, slot * heads))
    head_grad, mamba_back[-1] = fence(head_grad, mamba_back[-1])
    for axis in ALL:
        size = lax.axis_size(axis)
        step = 1
        while step < size:
            pairs = [(i, i ^ step) for i in range(size)]
            head_grad = head_grad + send(head_grad, axis, pairs)
            step *= 2
    head_grad = head_grad[:3, :MH]

    cuts = (q_width, q_width + kv_width, q_width + 2 * kv_width)
    out_w_qkv = jnp.concatenate(
        [
            owned(g_attn[:, :, : cuts[0]]),
            owned(g_attn[:, :, cuts[0] : cuts[1]]),
            owned(g_attn[:, :, cuts[1] : cuts[2]]),
        ],
        axis=1,
    )
    out_w_out = owned(g_attn[:, :, cuts[2] :]).T

    def shared_out(block):
        g_sin = jnp.concatenate([owned(block[:, :, :ff]), owned(block[:, :, ff : 2 * ff])], axis=1)
        return g_sin, owned(block[:, :, 2 * ff :]).T

    out_sin_m, out_sdown_m = shared_out(g_s[:, :, chan : chan + 3 * ff])
    out_sin, out_sdown = shared_out(g_s[:, :, chan + 3 * ff :])

    return (
        jnp.stack(results).reshape(batches, length, D),
        jnp.stack(grads_in).reshape(batches, length, D),
        little[:, 0],
        out_w_in,
        out_w_dt,
        out_conv_w,
        out_conv_b,
        head_grad[0],
        head_grad[1],
        head_grad[2],
        out_gate,
        out_mix,
        little[:, 1],
        little[:, 4 : 4 + experts_total],
        out_sin_m,
        out_sdown_m,
        out_expert_in_m,
        out_expert_down_m,
        little[:, 2],
        out_w_qkv,
        out_w_out,
        little[:, 3],
        little[:, 4 + experts_total : 4 + 2 * experts_total],
        out_sin,
        out_sdown,
        out_expert_in,
        out_expert_down,
    )


def solution(mesh):
    n_dp, n_ex = mesh.shape["dp"], mesh.shape["expert"]
    outer = n_ex // 8
    fine = Mesh(mesh.devices.reshape(n_dp, outer, 4, 2), ALL)
    split = P(ALL)
    row = P(ALL, None)
    col = P(None, ALL)
    mid = P(None, ALL, None)
    part = P(EX, "dp", None)
    same = P()
    return jax.shard_map(
        body,
        mesh=fine,
        in_specs=(
            mid,
            mid,
            P(None, None, ALL, None),
            split,
            row,
            row,
            col,
            split,
            same,
            same,
            same,
            split,
            col,
            split,
            row,
            row,
            col,
            part,
            part,
            split,
            row,
            col,
            split,
            row,
            row,
            col,
            part,
            part,
            mid,
        ),
        out_specs=(
            mid,
            mid,
            split,
            row,
            row,
            col,
            split,
            same,
            same,
            same,
            split,
            col,
            split,
            row,
            row,
            col,
            part,
            part,
            split,
            row,
            col,
            split,
            row,
            row,
            col,
            part,
            part,
        ),
        check_vma=False,
    )
```

```python
import functools

import jax
import jax.numpy as jnp
from jax import lax
from jax.experimental import pallas as pl
from jax.experimental.pallas import tpu as pltpu
from jax.experimental.layout import Layout, with_layout_constraint
from jax.sharding import Mesh, PartitionSpec as P

D = 1536
QH = 12
KVH = 4
HEAD = 128
EXP_FF = 512
SH_FF = 1024
TOP = 6
MH = 48
HP = 64
STATE = 128
CK = 4
DI = 3072

bf16 = jnp.bfloat16
f32 = jnp.float32
epsilon = 1e-05
masked_value = -1e30
highest = lax.Precision.HIGHEST
ALL = ("dp", "w", "z", "core")
EX = ("w", "z", "core")
TP = ("z", "core")
FS = ("dp", "w")
SWAP = [(0, 1), (1, 0)]


def dot(a, b, dims, out=f32):
    r = lax.dot_general(a, b, (dims, ((), ())), preferred_element_type=f32)
    return r if out == f32 else r.astype(out)


def nn(a, b, out=f32):
    return dot(a, b, ((1,), (0,)), out)


def nt(a, b, out=f32):
    return dot(a, b, ((1,), (1,)), out)


def tn(a, b, out=f32):
    return dot(a, b, ((0,), (0,)), out)


def ring(shift, axis="z"):
    n = lax.axis_size(axis)
    return [(i, (i + shift) % n) for i in range(n)]


def wide(x):
    parts = [x] + [lax.ppermute(x, "w", ring(s, "w")) for s in range(1, lax.axis_size("w"))]
    return parts[0] if len(parts) == 1 else jnp.concatenate(parts, axis=0)


def narrow(total):
    n = lax.axis_size("w")
    rows = total.shape[0] // n
    out = total[:rows]
    for s in range(1, n):
        part = total[s * rows : (s + 1) * rows].astype(bf16)
        out = out + lax.ppermute(part, "w", ring(-s, "w")).astype(f32)
    return out


def add_first(total, part):
    rows = part.shape[0]
    if rows == total.shape[0]:
        return total + part
    return jnp.concatenate([total[:rows] + part, total[rows:]], axis=0)


def fence(*trees):
    if lax.axis_size("w") > 1:
        return trees
    return lax.optimization_barrier(trees)


def by_rows(x):
    if lax.axis_size("w") > 1:
        return x
    return with_layout_constraint(x, Layout(major_to_minor=tuple(range(x.ndim))))


def send(x, axis, pairs):
    return by_rows(lax.ppermute(by_rows(x), axis, pairs))


def gather_start(x):
    return [x] + [send(x, "z", ring(s)) for s in range(1, lax.axis_size("z"))]


def gather_finish(parts):
    mine = by_rows(jnp.concatenate(parts, axis=0))
    return by_rows(jnp.concatenate([mine, send(mine, "core", SWAP)], axis=0))


def gather_rows(x):
    return gather_finish(gather_start(x))


def return_start(total):
    n = lax.axis_size("z")
    half = total.shape[0] // 2
    rows = half // n
    recv = send(total[half:].astype(bf16), "core", SWAP)
    mine = total[:half] + recv.astype(f32)
    sent = [
        send(mine[s * rows : (s + 1) * rows].astype(bf16), "z", ring(-s)) for s in range(1, n)
    ]
    return mine[:rows], sent


def return_finish(own, sent):
    for part in sent:
        own = own + part.astype(f32)
    return own


def return_rows(total):
    return return_finish(*return_start(total))


def pair_gather(x):
    return by_rows(jnp.concatenate([x, send(x, "core", SWAP)], axis=0))


def pair_return(total):
    half = total.shape[0] // 2
    recv = send(total[half:].astype(bf16), "core", SWAP)
    return total[:half] + recv.astype(f32)


def split_two(x):
    high = x.astype(bf16)
    return [high, (x - high.astype(f32)).astype(bf16)]


def row_scale(values):
    return lax.rsqrt(jnp.mean(values * values, axis=-1, keepdims=True) + epsilon)


def rms_forward(values, gain):
    scale = row_scale(values)
    normed = values * scale
    return normed, scale, (normed * gain).astype(bf16)


def rms_backward(grad_result, normed, scale, gain):
    grad_gain = jnp.sum(grad_result * normed, axis=0)
    grad_normed = grad_result * gain
    grad_values = scale * (
        grad_normed - normed * jnp.mean(grad_normed * normed, axis=-1, keepdims=True)
    )
    return grad_values, grad_gain


def lanes(parts, width):
    used = sum(p.shape[-1] for p in parts)
    rows = parts[0].shape[0]
    if used < width:
        parts = parts + [jnp.zeros((rows, width - used), bf16)]
    return jnp.concatenate(parts, axis=1)


def scan_core(proj, step_raw, seg_col, seg_row, taps, bias, heads_par):
    length = proj.shape[0]
    chan = proj.shape[1] - 2 * STATE
    chan = chan // 2
    z = proj[:, :chan].astype(f32)
    conv_in = proj[:, chan:].astype(f32)
    place = lax.broadcasted_iota(jnp.int32, (length, 1), 0)
    shifted, masks = [], []
    conv_sum = bias
    for k in range(CK):
        if k == 0:
            moved, mask = conv_in, None
            conv_sum = conv_sum + taps[0:1] * moved
        else:
            same = pltpu.roll(seg_col, k, 0) == seg_col
            mask = jnp.where(same & (place >= k), 1.0, 0.0)
            moved = pltpu.roll(conv_in, k, 0) * mask
            conv_sum = conv_sum + taps[k : k + 1] * moved
        shifted.append(moved)
        masks.append(mask)
    logistic = jax.nn.sigmoid(conv_sum)
    act = conv_sum * logistic
    pre = step_raw + heads_par[0:1]
    step = jnp.maximum(pre, 0.0) + jnp.log1p(jnp.exp(-jnp.abs(pre)))
    decay_rate = heads_par[1:2]
    rows_pos = lax.broadcasted_iota(jnp.int32, (length, length), 0)
    cols_pos = lax.broadcasted_iota(jnp.int32, (length, length), 1)
    lower = jnp.where(cols_pos <= rows_pos, 1.0, 0.0)
    cum = lax.dot_general(
        lower, step * decay_rate, (((1,), (0,)), ((), ())), precision=highest, preferred_element_type=f32
    )
    allowed = (seg_col == seg_row) & (cols_pos <= rows_pos)
    b_low = act[:, chan : chan + STATE].astype(bf16)
    c_low = act[:, chan + STATE :].astype(bf16)
    cb = nt(c_low, b_low)
    return dict(
        chan=chan, z=z, conv_in=conv_in, shifted=shifted, masks=masks, conv_sum=conv_sum,
        logistic=logistic, act=act, pre=pre, step=step, rate=decay_rate, lower=lower, cum=cum,
        cum_t=cum.T, step_t=step.T, allowed=allowed, b=b_low, c=c_low, cb=cb,
    )


def head_table(s, h):
    gap = s["cum"][:, h : h + 1] - s["cum_t"][h : h + 1, :]
    decay = jnp.exp(jnp.where(s["allowed"], gap, masked_value))
    return decay, s["step_t"][h : h + 1, :]


def pair_scan(s, heads, low):
    lane = lax.broadcasted_iota(jnp.int32, (1, 2 * HP), 1)
    blocks, mixes, tables = [], [], []
    for j in range(heads // 2):
        both = low[:, j * 2 * HP : (j + 1) * 2 * HP]
        outs = []
        for h in (2 * j, 2 * j + 1):
            decay, step_row = head_table(s, h)
            mix = (decay * s["cb"] * step_row).astype(bf16)
            outs.append(nn(mix, both))
            mixes.append(mix)
            tables.append((decay, step_row))
        blocks.append(jnp.where(lane < HP, outs[0], outs[1]))
    return jnp.concatenate(blocks, axis=1), mixes, tables


def scan_forward_kernel(heads, proj_ref, step_ref, col_ref, row_ref, conv_ref, chan_ref, head_ref, gained_ref, square_ref):
    s = scan_core(
        proj_ref[...], step_ref[...], col_ref[...], row_ref[0], conv_ref[0:CK], conv_ref[CK : CK + 1], head_ref[...]
    )
    chan = s["chan"]
    inputs = s["act"][:, :chan]
    scan, _, _ = pair_scan(s, heads, inputs.astype(bf16))
    scan = scan + chan_ref[1:2] * inputs
    gated = scan * s["z"] * jax.nn.sigmoid(s["z"])
    gained_ref[...] = (gated * chan_ref[0:1]).astype(bf16)
    square_ref[...] = jnp.broadcast_to(jnp.sum(gated * gated, axis=1, keepdims=True), square_ref.shape)


def scan_backward_kernel(
    heads, proj_ref, step_ref, col_ref, row_ref, conv_ref, chan_ref, head_ref, grad_ref, extra_ref,
    dproj_ref, dconv_ref, dchan_ref, dhead_ref, flat_ref,
):
    @pl.when(pl.program_id(0) == 0)
    def _():
        dconv_ref[...] = jnp.zeros_like(dconv_ref)
        dchan_ref[...] = jnp.zeros_like(dchan_ref)
        dhead_ref[...] = jnp.zeros_like(dhead_ref)

    taps = conv_ref[0:CK]
    s = scan_core(proj_ref[...], step_ref[...], col_ref[...], row_ref[0], taps, conv_ref[CK : CK + 1], head_ref[...])
    chan, length = s["chan"], s["z"].shape[0]
    gain, skip = chan_ref[0:1], chan_ref[1:2]
    inputs = s["act"][:, :chan]
    low = inputs.astype(bf16)
    scan, mixes, tables = pair_scan(s, heads, low)
    scan = scan + skip * inputs
    z = s["z"]
    sig = jax.nn.sigmoid(z)
    silu = z * sig
    gated = scan * silu
    extra = extra_ref[...].astype(f32)
    scale = extra[:, 0:1] + extra[:, 1:2]
    mean = extra[:, 2:3] + extra[:, 3:4]
    grad = grad_ref[...].astype(f32)
    normed = gated * scale
    d_gated = scale * (grad * gain - normed * mean)
    d_scan = d_gated * silu
    d_z = d_gated * scan * sig * (1.0 + z * (1.0 - sig))
    d_low = d_scan.astype(bf16)
    lane = lax.broadcasted_iota(jnp.int32, (1, 2 * HP), 1)
    spot = lax.broadcasted_iota(jnp.int32, (1, s["step"].shape[1]), 1)
    d_cb = jnp.zeros((length, length), f32)
    d_cum = jnp.zeros(s["step"].shape, f32)
    flat_ref[...] = jnp.zeros_like(flat_ref)
    blocks = []
    for j in range(heads // 2):
        cut = slice(j * 2 * HP, (j + 1) * 2 * HP)
        both, d_both = low[:, cut], d_low[:, cut]
        outs = []
        for i, h in enumerate((2 * j, 2 * j + 1)):
            decay, step_row = tables[h]
            outs.append(tn(mixes[h], d_both))
            keep = (lane < HP) if i == 0 else (lane >= HP)
            d_mix = nt(jnp.where(keep, d_both, jnp.zeros_like(d_both)), both)
            part = d_mix * decay
            d_cb = d_cb + part * step_row
            part = part * s["cb"]
            flat_ref[h : h + 1, 0:length] = jnp.sum(part, axis=0, keepdims=True)
            column = jnp.sum(part * step_row, axis=1, keepdims=True)
            d_cum = d_cum + jnp.where(spot == h, column, 0.0)
        blocks.append(jnp.where(lane < HP, outs[0], outs[1]))
    d_inputs = jnp.concatenate(blocks, axis=1) + skip * d_scan
    from_rows = flat_ref[...].T[0:length]
    d_cum = d_cum - s["step"] * from_rows
    d_rate = lax.dot_general(
        s["lower"], d_cum, (((0,), (0,)), ((), ())), precision=highest, preferred_element_type=f32
    )
    d_step = from_rows + d_rate * s["rate"]
    d_pre = jnp.where(spot < heads, d_step * jax.nn.sigmoid(s["pre"]), 0.0)
    d_cb_low = d_cb.astype(bf16)
    d_act = jnp.concatenate([d_inputs, tn(d_cb_low, s["c"]), nn(d_cb_low, s["b"])], axis=1)
    logistic = s["logistic"]
    d_sum = d_act * logistic * (1.0 + s["conv_sum"] * (1.0 - logistic))
    d_in = taps[0:1] * d_sum
    for k in range(1, CK):
        back = d_sum * s["masks"][k] * taps[k : k + 1]
        d_in = d_in + pltpu.roll(back, length - k, 0)
    dproj_ref[...] = jnp.concatenate([d_z, d_in, d_pre], axis=1).astype(bf16)
    for k in range(CK):
        dconv_ref[k : k + 1] += jnp.sum(d_sum * s["shifted"][k], axis=0, keepdims=True)
    dconv_ref[CK : CK + 1] += jnp.sum(d_sum, axis=0, keepdims=True)
    dchan_ref[0:1] += jnp.sum(grad * normed, axis=0, keepdims=True)
    dchan_ref[1:2] += jnp.sum(d_scan * inputs, axis=0, keepdims=True)
    dhead_ref[0:1] += jnp.sum(d_pre, axis=0, keepdims=True)
    dhead_ref[1:2] += jnp.sum(d_rate * s["step"] * s["rate"], axis=0, keepdims=True)


def scan_specs(length, width, lanes_, conv, chan):
    def whole(shape):
        return pl.BlockSpec(shape, lambda i: (0,) * len(shape))

    rows = lambda w: pl.BlockSpec((length, w), lambda i: (i, 0))
    return rows, whole, [
        rows(width), rows(lanes_), rows(1), pl.BlockSpec((1, 1, length), lambda i: (i, 0, 0)),
        whole((8, conv)), whole((8, chan)), whole((8, lanes_)),
    ]


def scan_forward(heads, length, proj, step, seg_col, seg_row, conv_par, chan_par, head_par):
    total, width = proj.shape
    chan = heads * HP
    rows, whole, specs = scan_specs(length, width, step.shape[1], width - chan, chan)
    return pl.pallas_call(
        functools.partial(scan_forward_kernel, heads),
        grid=(total // length,),
        in_specs=specs,
        out_specs=[rows(chan), rows(128)],
        out_shape=[jax.ShapeDtypeStruct((total, chan), bf16), jax.ShapeDtypeStruct((total, 128), f32)],
        compiler_params=pltpu.CompilerParams(vmem_limit_bytes=32 << 20),
        name="scan_forward",
    )(proj, step, seg_col, seg_row, conv_par, chan_par, head_par)


def scan_backward(heads, length, proj, step, seg_col, seg_row, conv_par, chan_par, head_par, grad, extra):
    total, width = proj.shape
    chan = heads * HP
    lanes_ = step.shape[1]
    rows, whole, specs = scan_specs(length, width, lanes_, width - chan, chan)
    return pl.pallas_call(
        functools.partial(scan_backward_kernel, heads),
        grid=(total // length,),
        in_specs=specs + [rows(chan), rows(128)],
        out_specs=[rows(width + lanes_), whole((8, width - chan)), whole((8, chan)), whole((8, lanes_))],
        out_shape=[
            jax.ShapeDtypeStruct((total, width + lanes_), bf16),
            jax.ShapeDtypeStruct((8, width - chan), f32),
            jax.ShapeDtypeStruct((8, chan), f32),
            jax.ShapeDtypeStruct((8, lanes_), f32),
        ],
        scratch_shapes=[pltpu.VMEM((128, 128), f32)],
        compiler_params=pltpu.CompilerParams(vmem_limit_bytes=32 << 20),
        name="scan_backward",
    )(proj, step, seg_col, seg_row, conv_par, chan_par, head_par, grad, extra)


def swiglu(gate, up):
    return gate * jax.nn.sigmoid(gate) * up


def swiglu_back(grad, gate, up):
    logistic = jax.nn.sigmoid(gate)
    grad_gate = grad * up * logistic * (1.0 + gate * (1.0 - logistic))
    return grad_gate.astype(bf16), (grad * gate * logistic).astype(bf16)


def gate_table(moe_in, mask, router):
    logits = nn(moe_in, router)
    picked = jnp.where(mask, logits, masked_value)
    peak = jnp.max(picked, axis=-1, keepdims=True)
    ex = jnp.where(mask, jnp.exp(picked - peak), 0.0)
    return ex / jnp.sum(ex, axis=-1, keepdims=True)


def unit_gates(local, units):
    count = local.shape[1]
    owner = lax.broadcasted_iota(jnp.int32, (1, units), 1) // EXP_FF
    spread = local[:, count - 1 :]
    for e in range(count - 1):
        spread = jnp.where(owner == e, local[:, e : e + 1], spread)
    return spread, owner


def moe_forward(own_in, mask, w, riders=None):
    rows = own_in.shape[0]
    base_in = gather_rows(own_in)
    moe_in = wide(base_in)
    gates = gate_table(moe_in, mask, w["router"])
    units = w["expert_down"].shape[0]
    count = units // EXP_FF
    first = lax.axis_index(EX) * count
    local = lax.dynamic_slice(gates, (0, first), (gates.shape[0], count))
    pre = nn(moe_in, w["expert_in"], bf16)
    pre_s = nn(base_in, w["shared_in"], bf16)
    if riders is not None:
        riders = gather_start(riders)
        riders[1], pre = fence(riders[1], pre)
    pre, pre_s = lax.optimization_barrier((pre, pre_s))
    p = pre.astype(f32)
    spread, _ = unit_gates(local, units)
    hid = (swiglu(p[:, :units], p[:, units:]) * spread).astype(bf16)
    half = pre_s.shape[1] // 2
    p = pre_s.astype(f32)
    hid_s = swiglu(p[:, :half], p[:, half:]).astype(bf16)
    low = nn(hid, w["expert_down"])
    if riders is not None:
        riders[2:], low = fence(riders[2:], low)
    total = add_first(low, nt(hid_s, w["shared_down_t"]))
    kept = (moe_in, base_in, gates[:rows], local, pre, pre_s)
    return (total, kept) if riders is None else (total, kept, riders)


def moe_backward(base_z, kept, w, experts_total, riders=None):
    moe_in, base_in, own_gates, local, pre, pre_s = kept
    pre, pre_s, _ = lax.optimization_barrier((pre, pre_s, base_z))
    grad_z = wide(base_z)
    units = w["expert_down"].shape[0]
    count = units // EXP_FF
    first = lax.axis_index(EX) * count
    spread, owner = unit_gates(local, units)
    p = pre.astype(f32)
    gate, up = p[:, :units], p[:, units:]
    grad_hid = nt(grad_z, w["expert_down"])
    if riders is not None:
        riders[:1], grad_hid = fence(riders[:1], grad_hid)
    act = swiglu(gate, up)
    hidden = (act * spread).astype(bf16)
    product = grad_hid * act
    lane = lax.broadcasted_iota(jnp.int32, (1, experts_total), 1)
    table = jnp.zeros((grad_z.shape[0], experts_total), f32)
    for e in range(count):
        mine = jnp.sum(jnp.where(owner == e, product, 0.0), axis=-1, keepdims=True)
        table = table + local[:, e : e + 1] * mine * (lane == first + e).astype(f32)
    g_gate, g_up = swiglu_back(grad_hid * spread, gate, up)
    g_pre = jnp.concatenate([g_gate, g_up], axis=1)
    total = nt(g_pre, w["expert_in"])
    if riders is not None:
        riders[1:], total = fence(riders[1:], total)
    half = pre_s.shape[1] // 2
    p = pre_s.astype(f32)
    grad_hid = nn(base_z, w["shared_down_t"])
    hid_s = swiglu(p[:, :half], p[:, half:]).astype(bf16)
    g_gate, g_up = swiglu_back(grad_hid, p[:, :half], p[:, half:])
    g_pre_s = jnp.concatenate([g_gate, g_up], axis=1)
    total = add_first(total, nt(g_pre_s, w["shared_in"]))
    extra = -(-experts_total // 128) * 128
    table = jnp.pad(table, ((0, 0), (0, extra - experts_total)))
    total = jnp.concatenate([total, table], axis=1)
    side = (moe_in, grad_z, hidden, hid_s, g_pre, g_pre_s, base_in, base_z)
    return total, side


def moe_finish(back, kept, w, experts_total):
    own_gates = kept[2]
    weighted = back[:, D : D + experts_total]
    grad_logits = weighted - own_gates * jnp.sum(weighted, axis=-1, keepdims=True)
    grad_logits = grad_logits.astype(bf16)
    return back[:, :D] + nt(grad_logits, w["router"]), grad_logits


def tn_sum(pairs, out=bf16):
    if lax.axis_size("w") > 1:
        return tn(*[jnp.concatenate(side, axis=0) for side in zip(*pairs)], out)
    total = None
    for a, b in pairs:
        part = tn(a, b)
        total = part if total is None else total + part
    return total.astype(out)


def moe_weight_grads(sides):
    g_down = tn_sum([(s[2], s[1]) for s in sides])
    g_in = tn_sum([(s[0], s[4]) for s in sides])
    g_sin = tn_sum([(s[6], s[5]) for s in sides])
    g_sdown_t = tn_sum([(s[7], s[3]) for s in sides])
    return g_in, g_down, g_sin, g_sdown_t


def attn_mask(seg):
    length = seg.shape[1]
    rows_pos = lax.broadcasted_iota(jnp.int32, (length, length), 0)
    cols_pos = lax.broadcasted_iota(jnp.int32, (length, length), 1)
    return (seg[:, :, None] == seg[:, None, :]) & (cols_pos <= rows_pos)[None]


def attn_forward(own_in, allowed, w_qkv, w_out_t):
    seqs, length, _ = allowed.shape
    kv = KVH // 2
    group = QH // KVH
    q_width = kv * group * HEAD
    kv_width = kv * HEAD
    attn_in = pair_gather(own_in)
    packed = nn(attn_in, w_qkv, bf16)
    q = packed[:, :q_width].reshape(seqs, length, kv, group, HEAD)
    k = packed[:, q_width : q_width + kv_width].reshape(seqs, length, kv, HEAD)
    v = packed[:, q_width + kv_width :].reshape(seqs, length, kv, HEAD)
    scores = jnp.einsum("bqhgd,bkhd->bhgqk", q, k, preferred_element_type=f32) * HEAD**-0.5
    scores = jnp.where(allowed[:, None, None], scores, masked_value)
    peak = jnp.max(scores, axis=-1, keepdims=True)
    ex = jnp.exp(scores - peak)
    probs = ex / jnp.sum(ex, axis=-1, keepdims=True)
    context = jnp.einsum("bhgqk,bkhd->bqhgd", probs.astype(bf16), v, preferred_element_type=f32)
    context = context.reshape(seqs * length, q_width).astype(bf16)
    branch = pair_return(nt(context, w_out_t))
    return branch, (attn_in, q, k, v, probs, context)


def attn_backward(own_grad, kept, w_qkv, w_out_t):
    attn_in, q, k, v, probs, context = kept
    seqs, length, kv, group, _ = q.shape
    grad = pair_gather(own_grad)
    grad_context = nn(grad, w_out_t, bf16).reshape(seqs, length, kv, group, HEAD)
    probs_low = probs.astype(bf16)
    grad_v = jnp.einsum("bhgqk,bqhgd->bkhd", probs_low, grad_context, preferred_element_type=f32)
    grad_p = jnp.einsum("bqhgd,bkhd->bhgqk", grad_context, v, preferred_element_type=f32)
    delta = jnp.sum(probs * grad_p, axis=-1, keepdims=True)
    grad_s = (probs * (grad_p - delta)).astype(bf16)
    scale = HEAD**-0.5
    grad_q = jnp.einsum("bhgqk,bkhd->bqhgd", grad_s, k, preferred_element_type=f32) * scale
    grad_k = jnp.einsum("bhgqk,bqhgd->bkhd", grad_s, q, preferred_element_type=f32) * scale
    rows = seqs * length
    grad_packed = jnp.concatenate(
        [grad_q.reshape(rows, -1), grad_k.reshape(rows, -1), grad_v.reshape(rows, -1)], axis=1
    ).astype(bf16)
    grad_in = pair_return(nt(grad_packed, w_qkv))
    return grad_in, (attn_in, grad_packed, context, grad)


def by_owner(x, count):
    return x.reshape(x.shape[0], count, x.shape[1] // count)


def body(
    tokens,
    segments,
    routes,
    norm_mamba,
    w_in,
    w_dt,
    conv_w,
    conv_b,
    dt_bias,
    a_log,
    skip_scale,
    gate_norm,
    w_mix_out,
    norm_moe_m,
    router_m,
    shared_in_m,
    shared_down_m,
    expert_in_m,
    expert_down_m,
    norm_attn,
    w_qkv,
    w_out,
    norm_moe,
    router,
    shared_in,
    shared_down,
    expert_in,
    expert_down,
    cotangent,
):
    batches, length, _ = tokens.shape
    micro = batches if lax.axis_size("w") > 1 else 1
    seqs = batches // micro
    own_rows = seqs * length
    tokens = tokens.reshape(micro, own_rows, D)
    cotangent = cotangent.reshape(micro, own_rows, D)
    routes = routes.reshape(2, micro, own_rows, TOP)
    segments = segments.reshape(micro, own_rows)
    n_tp = lax.axis_size("z") * lax.axis_size("core")
    n_ex = lax.axis_size("w") * n_tp
    n_all = lax.axis_size("dp") * n_ex
    rows = w_in.shape[0]
    local_experts = expert_in.shape[0]
    experts_total = local_experts * n_ex
    heads = MH // n_tp
    chan = heads * HP
    ff = SH_FF // n_tp
    slot = lax.axis_index(TP)
    conv_total = DI + 2 * STATE
    conv_here = conv_w.shape[1]
    gate_here = gate_norm.shape[0]
    vec_len = gate_here + (CK + 1) * conv_here
    vec_cols = -(-vec_len // rows)
    small_cols = 4 + 2 * experts_total + vec_cols
    step_width = -(-(heads + small_cols) // 128) * 128

    vec = jnp.concatenate([gate_norm, conv_b, conv_w.reshape(-1)])
    vec = jnp.pad(vec, (0, rows * vec_cols - vec_len)).reshape(rows, vec_cols)
    gains_own = jnp.stack([norm_mamba, norm_moe_m, norm_attn, norm_moe], axis=1)
    little = jnp.concatenate([gains_own, router_m, router, vec], axis=1)

    def for_all(x):
        return jnp.broadcast_to(x[:, None], (rows, n_tp, x.shape[1]))

    def packed_columns(parts):
        return jnp.concatenate(parts, axis=2).transpose(1, 0, 2)

    def moved_columns(packed):
        moved = lax.all_to_all(packed, TP, split_axis=0, concat_axis=0, tiled=True)
        return moved.reshape(n_tp * rows, -1)

    def whole_rows(moved):
        return lax.all_gather(moved, FS, axis=0, tiled=True)

    def shared_pack(w_sin, w_sdown):
        return [
            by_owner(w_sin[:, :SH_FF], n_tp),
            by_owner(w_sin[:, SH_FF:], n_tp),
            by_owner(w_sdown.T, n_tp),
        ]

    blank = jnp.zeros((rows, n_tp, step_width - heads - small_cols), bf16)
    packed_m = packed_columns(
        [
            by_owner(w_in[:, :DI], n_tp),
            by_owner(w_in[:, DI : 2 * DI], n_tp),
            for_all(w_in[:, 2 * DI :]),
            by_owner(w_dt, n_tp),
            for_all(little),
            blank,
            by_owner(w_mix_out.T, n_tp),
        ]
    )
    moved_m = moved_columns(packed_m)

    expert_ids = jnp.arange(experts_total, dtype=jnp.int32)
    info_width = -(-(2 * experts_total + 1) // 128) * 128
    each = range(micro)
    rows_in = []
    for m in each:
        hot = [
            jnp.any(routes[b, m][:, :, None] == expert_ids, axis=1).astype(bf16) for b in range(2)
        ]
        info = lanes(hot + [segments[m][:, None].astype(bf16)], info_width)
        x_info, moved_m = fence(jnp.concatenate([tokens[m], info], axis=1), moved_m)
        rows_in.append(gather_rows(x_info))
    def low_weights(w_low):
        return lax.all_gather(w_low, "dp", axis=1, tiled=True).reshape(-1, D)

    low_m = low_weights(expert_down_m)
    moved_m, low_m = fence(moved_m, low_m)
    w_m = whole_rows(moved_m)
    in_width = 2 * chan + 2 * STATE
    w_in_here = w_m[:, :in_width]
    at = in_width + step_width
    w_step = w_m[:, in_width:at]
    w_dt_here = w_step[:, :128]
    small_all = w_step[:, heads : heads + small_cols]
    pick = (jnp.arange(128)[None, :] == heads + jnp.arange(8)[:, None]).astype(bf16)
    gain_rows = nt(pick, w_dt_here)
    gain_mamba, gain_moe_m, gain_attn, gain_moe = [gain_rows[i] for i in range(4)]
    router_m_full = small_all[:, 4 : 4 + experts_total]
    router_full = small_all[:, 4 + experts_total : 4 + 2 * experts_total]
    vec_all = small_all[:, 4 + 2 * experts_total :].reshape(n_all, rows * vec_cols).astype(f32)
    gain_gate = vec_all[:, :gate_here].reshape(DI)
    bias_all = vec_all[:, gate_here : gate_here + conv_here].reshape(conv_total)
    taps_all = vec_all[:, gate_here + conv_here : vec_len].reshape(n_all, CK, conv_here)
    taps_all = taps_all.transpose(1, 0, 2).reshape(CK, conv_total)

    def channels(full_row):
        mine = lax.dynamic_slice_in_dim(full_row, slot * chan, chan, axis=-1)
        return jnp.concatenate([mine, full_row[..., DI:]], axis=-1)

    taps = channels(taps_all)
    bias = channels(bias_all)
    gain_here = lax.dynamic_slice_in_dim(gain_gate, slot * chan, chan)
    dt_here = lax.dynamic_slice_in_dim(dt_bias, slot * heads, heads)
    log_here = lax.dynamic_slice_in_dim(a_log, slot * heads, heads)
    skip_here = lax.dynamic_slice_in_dim(skip_scale, slot * heads, heads)

    w_scan = w_m[:, : in_width + 128]
    w_mix_t = w_m[:, at:]

    def up_weights(w_up):
        count = w_up.shape[0]
        cols = [w_up[e, :, :EXP_FF] for e in range(count)] + [w_up[e, :, EXP_FF:] for e in range(count)]
        cols = by_rows(jnp.concatenate(cols, axis=1))
        return by_rows(lax.all_gather(cols, "dp", axis=0, tiled=True))

    up_m = up_weights(expert_in_m)
    kv = KVH // 2
    q_width = QH // 2 * HEAD
    kv_width = kv * HEAD
    q_all, kv_all = QH * HEAD, KVH * HEAD
    attn_pack = jnp.concatenate(
        [
            by_owner(w_qkv[:, :q_all], 2),
            by_owner(w_qkv[:, q_all : q_all + kv_all], 2),
            by_owner(w_qkv[:, q_all + kv_all :], 2),
            by_owner(w_out.T, 2),
        ],
        axis=2,
    ).transpose(1, 0, 2)
    packed_s = shared_pack(shared_in_m, shared_down_m) + shared_pack(shared_in, shared_down)
    packed_s, rows_in = fence(packed_columns(packed_s), rows_in)
    moved_s = moved_columns(packed_s)
    attn_pack, moved_s = fence(attn_pack, moved_s)
    attn_pack = lax.all_to_all(attn_pack, "core", split_axis=0, concat_axis=0, tiled=True)
    own = attn_pack.reshape(2 * rows, -1)
    n_z = lax.axis_size("z")
    attn_parts = [send(own, "z", ring(s)) for s in range(n_z - 1, 0, -1)] + [own]
    def eight(parts):
        block = jnp.concatenate([p.reshape(-1, p.shape[-1]) for p in parts], axis=0)
        return jnp.pad(block, ((0, 8 - block.shape[0]), (0, 0)))

    conv_par = eight([taps, bias])
    chan_par = eight([gain_here, jnp.repeat(skip_here, HP)])
    head_par = jnp.pad(eight([dt_here, -jnp.exp(log_here)]), ((0, 0), (0, 128 - heads)))
    x_own = [tokens[m].astype(f32) for m in each]
    masks, allowed, mamba_kept, mix_kept, hidden_one = [], [], [], [], []
    proj_all, cot_all = [], []
    for m in each:
        rows_all = rows_in[m]
        x_all = rows_all[:, :D].astype(f32)
        marks = wide(rows_all[:, D : D + 2 * experts_total]) > 0.5
        masks.append([marks[:, :experts_total], marks[:, experts_total:]])
        seg_col = rows_all[:, D + 2 * experts_total :][:, :1].astype(f32)
        seg_row = seg_col.reshape(n_tp * seqs, 1, length)
        seg = seg_row[:, 0].astype(jnp.int32)
        middle = n_tp * seqs // 2
        pair = jnp.concatenate([seg[:seqs], seg[middle : middle + seqs]], axis=0)
        allowed.append(attn_mask(pair))

        _, scale_x, mamba_in = rms_forward(x_all, gain_mamba)
        total_rows = mamba_in.shape[0]
        proj = nn(mamba_in, w_in_here, bf16)
        dt_raw = nn(mamba_in, w_dt_here)
        proj_all.append(proj)
        pars = (seg_col, seg_row, conv_par, chan_par, head_par)
        gained, square = scan_forward(heads, length, proj, dt_raw, *pars)
        if m == micro - 1:
            attn_parts, gained = fence(attn_parts, gained)
        partial = nt(gained, w_mix_t)
        high = square.astype(bf16).astype(f32)
        lane = lax.broadcasted_iota(jnp.int32, square.shape, 1)
        extra = jnp.where(lane == 0, high, jnp.where(lane == 1, square - high, 0.0))
        own, sent = return_start(jnp.concatenate([partial, extra], axis=1))
        back = return_finish(own, sent)
        gate_scale = lax.rsqrt((back[:, D : D + 1] + back[:, D + 1 : D + 2]) / DI + epsilon)
        mix_branch = back[:, :D] * gate_scale
        hidden_one.append(x_own[m] + mix_branch)
        mamba_kept.append((rows_all, scale_x[:own_rows], mamba_in, (proj, dt_raw, *pars), gained))
        mix_kept.append((mix_branch, gate_scale))

    twice = jnp.concatenate(attn_parts + attn_parts, axis=0)
    start = (n_z - 1 - lax.axis_index("z")) * 2 * rows
    attn_w = lax.dynamic_slice(twice, (start, 0), (n_z * 2 * rows, twice.shape[1]))
    attn_w = lax.all_gather(attn_w, FS, axis=0, tiled=True)
    w_qkv_here = attn_w[:, : q_width + 2 * kv_width]
    w_out_t = attn_w[:, q_width + 2 * kv_width :]

    w_s = whole_rows(moved_s)
    moe_m = {
        "router": router_m_full,
        "shared_in": w_s[:, : 2 * ff],
        "shared_down_t": w_s[:, 2 * ff : 3 * ff],
        "expert_in": up_m,
        "expert_down": low_m,
    }

    up_a, low_a = fence(up_weights(expert_in), low_weights(expert_down))
    moe_a = {
        "router": router_full,
        "shared_in": w_s[:, 3 * ff : 5 * ff],
        "shared_down_t": w_s[:, 5 * ff :],
        "expert_in": up_a,
        "expert_down": low_a,
    }

    one_kept, layer_one = [], []
    for m in each:
        normed, scale, own = rms_forward(hidden_one[m], gain_moe_m)
        total, kept, riders = moe_forward(own, masks[m][0], moe_m, cotangent[m])
        cot_all.append(riders)
        layer_one.append(hidden_one[m] + return_rows(narrow(total)))
        one_kept.append((normed, scale, kept))
    attn_kept, hidden_two = [], []
    for m in each:
        normed, scale, own = rms_forward(layer_one[m], gain_attn)
        branch, kept = attn_forward(own, allowed[m], w_qkv_here, w_out_t)
        hidden_two.append(layer_one[m] + branch)
        attn_kept.append((normed, scale, kept))
    two_kept, results = [], []
    for m in each:
        cot_all[m] = gather_finish(cot_all[m])
        normed, scale, own = rms_forward(hidden_two[m], gain_moe)
        total, kept = moe_forward(own, masks[m][1], moe_a)
        results.append(total)
        two_kept.append((normed, scale, kept))

    gains = [0.0, 0.0, 0.0, 0.0]

    def up_over_dp(g):
        return lax.psum_scatter(g, "dp", scatter_dimension=0, tiled=True)

    def low_over_dp(g):
        g = g.reshape(local_experts, EXP_FF, D)
        return lax.psum_scatter(g, "dp", scatter_dimension=1, tiled=True)

    def expert_out(g_up, g_low):
        units = local_experts * EXP_FF
        cols = []
        for e in range(local_experts):
            low, high = e * EXP_FF, (e + 1) * EXP_FF
            pair = [g_up[:, low:high], g_up[:, units + low : units + high]]
            cols.append(jnp.concatenate(pair, axis=1).astype(f32))
        return jnp.stack(cols), g_low.astype(f32)

    saving = lax.axis_size("w") > 1

    def moe_stage(grads, kept_all, w, gain, *before, riders=None):
        grads = list(grads)
        backs, first_rows = [], []
        for m in each:
            rider = None if riders is None else riders[m][1]
            total, side = moe_backward(grads[m], kept_all[m][2], w, experts_total, rider)
            own, sent = return_start(narrow(total))
            first_rows.append(side[6][:own_rows])
            if saving:
                back = return_finish(own, sent)
                hold = (back, moe_weight_grads([side]), grads[m + 1 :])
                back, newer, grads[m + 1 :] = lax.optimization_barrier(hold)
                weights = newer if m == 0 else [a + b for a, b in zip(weights, newer)]
            else:
                hidden, g_pre, own = fence(side[2], side[4], own)
                g_low = tn_sum([(hidden, side[1])])
                g_up = tn_sum([(side[0], g_pre)])
                sent[:1], g_low = fence(sent[:1], g_low)
                sent[1:], g_up = fence(sent[1:], g_up)
                g_sin = tn_sum([(side[6], side[5])])
                weights = (g_up, g_low, g_sin, tn_sum([(side[7], side[3])]))
                back = return_finish(own, sent)
            backs.append(back)
        backs[-1], before = fence(backs[-1], before)
        grad_gain = 0.0
        values, logits = [], []
        for m in each:
            normed, scale, kept = kept_all[m]
            grad_in, grad_logits = moe_finish(backs[m], kept, w, experts_total)
            logits.append(grad_logits)
            grad_values, part = rms_backward(grad_in, normed, scale, gain)
            grad_gain = grad_gain + part
            values.append(grad_values)
        g_router = tn_sum(list(zip(first_rows, logits)), f32)
        return values, weights, grad_gain, g_router, before

    values, (g_in_a, g_down_a, g_sin_a, g_sdown_a), gains[3], g_router, _ = moe_stage(
        cot_all, two_kept, moe_a, gain_moe
    )
    sum_in_a = up_over_dp(g_in_a)
    sum_down_a = low_over_dp(g_down_a)
    grad_two = [cotangent[m].astype(f32) + values[m] for m in each]
    for m in each:
        total, grad_two[m] = fence(results[m], grad_two[m])
        results[m] = return_start(narrow(total))

    grad_layer, sides = [], []
    attn_back = []
    for m in each:
        grad_in, side = attn_backward(
            grad_two[m].astype(bf16), attn_kept[m][2], w_qkv_here, w_out_t
        )
        attn_back.append(grad_in)
        sides.append(side)
    g_attn = by_rows(
        jnp.concatenate(
            [
                by_rows(tn_sum([(s[0], s[1]) for s in sides])),
                by_rows(tn_sum([(s[3], s[2]) for s in sides])),
            ],
            axis=1,
        )
    )
    attn_back[-1], g_attn = lax.optimization_barrier((attn_back[-1], g_attn))
    g_attn = lax.psum_scatter(g_attn, FS, scatter_dimension=0, tiled=True)
    g_part = g_attn
    for m in each:
        normed, scale, _ = attn_kept[m]
        grad_values, part = rms_backward(attn_back[m], normed, scale, gain_attn)
        gains[2] = gains[2] + part
        grad_layer.append(grad_two[m] + grad_values)

    values, (g_in_m, g_down_m, g_sin_m, g_sdown_m), gains[1], g_router_m, before = moe_stage(
        [gather_rows(g.astype(bf16)) for g in grad_layer],
        one_kept,
        moe_m,
        gain_moe_m,
        sum_in_a,
        sum_down_a,
        riders=results,
    )
    sum_in_a, sum_down_a = before
    for m in each:
        results[m] = (hidden_two[m] + return_finish(*results[m])).astype(bf16)
    out_expert_in, out_expert_down = expert_out(sum_in_a, sum_down_a)
    sum_in_m = up_over_dp(g_in_m)
    sum_down_m = low_over_dp(g_down_m)
    grad_one = [grad_layer[m] + values[m] for m in each]

    def attn_owner(g_part):
        blocks = g_part.reshape(n_z, 2 * rows, -1)
        here = lax.axis_index("z")
        own = lax.dynamic_index_in_dim(blocks, here, 0, keepdims=False)
        sent = []
        for shift in range(1, n_z):
            block = lax.dynamic_index_in_dim(blocks, (here + shift) % n_z, 0, keepdims=False)
            sent.append(send(block, "z", ring(shift)))
        return own, sent

    def attn_total(own, sent):
        total = own.astype(f32)
        for block in sent:
            total = total + block.astype(f32)
        return lax.all_to_all(
            total.astype(bf16).reshape(2, rows, -1), "core", split_axis=0, concat_axis=0, tiled=True
        ).astype(f32)

    small = None
    mamba_sides, mamba_back, mixes, own_normed = [], [], [], []
    for m in each:
        mix_branch, gate_scale = mix_kept[m]
        x_rows, _, mamba_in, scan_args, _ = mamba_kept[m]
        x_rows, _ = fence(x_rows, grad_one[m])
        x_rows = x_rows[:, :D].astype(f32)
        normed_x = x_rows * row_scale(x_rows)
        own_normed.append(normed_x[:own_rows])
        grad_mix = grad_one[m].astype(bf16)
        mean_term = jnp.sum(grad_mix.astype(f32) * mix_branch, axis=-1, keepdims=True) / DI
        extra = lanes(split_two(gate_scale) + split_two(mean_term), 128)
        rows_all = gather_rows(jnp.concatenate([grad_mix, extra], axis=1))
        if m == micro - 1:
            rows_all, out_expert_in, out_expert_down = fence(
                rows_all, out_expert_in, out_expert_down
            )
        mix_all = rows_all[:, :D]
        extra_all = rows_all[:, D:]
        scale_all = extra_all[:, 0:1].astype(f32) + extra_all[:, 1:2].astype(f32)
        scaled_mix = (mix_all.astype(f32) * scale_all).astype(bf16)
        mixes.append(scaled_mix)
        if m == micro - 1:
            g_mix = tn_sum([(x, k[4]) for x, k in zip(mixes, mamba_kept)])
            mix_all, g_mix = fence(mix_all, by_rows(g_mix))
        if m == micro - 1:
            g_part, mix_all = fence(g_part, mix_all)
            attn_sent = attn_owner(g_part)
        grad_gated = nn(mix_all, w_mix_t, bf16)
        grad_scan, *grads = scan_backward(
            heads, length, *scan_args, grad_gated, extra_all
        )
        small = grads if small is None else [a + b for a, b in zip(small, grads)]
        own_part, sent_part = attn_sent if m == micro - 1 else (None, [])
        if m == micro - 1:
            sent_part[:2], grad_scan = fence(sent_part[:2], grad_scan)
        total = nt(grad_scan, w_scan)
        if m == micro - 1:
            sent_part[2:], total = fence(sent_part[2:], total)
            total, sum_in_m = fence(total, sum_in_m)
            attn_sent = (own_part, sent_part)
        gains[0] = gains[0] + jnp.sum(total * normed_x, axis=0)
        own, sent = return_start(total)
        grad_scan, own = fence(grad_scan, own)
        mamba_sides.append((mamba_in, grad_scan))
        mamba_back.append((own, sent))

    def rows_sum(packed):
        return lax.psum_scatter(packed, FS, scatter_dimension=0, tiled=True)

    def rows_back(packed):
        return lax.all_to_all(
            packed.reshape(n_tp, rows, -1), TP, split_axis=0, concat_axis=0, tiled=True
        ).astype(f32)

    def owned(block):
        return block.transpose(1, 0, 2).reshape(rows, -1)

    g_s = rows_sum(
        jnp.concatenate([g_mix, g_sin_m, g_sdown_m, g_sin_a, g_sdown_a], axis=1)
    )

    g_scan = by_rows(tn_sum(mamba_sides, f32))
    last_own, last_sent = mamba_back[-1]
    last_sent[:1], g_scan = fence(last_sent[:1], g_scan)
    mamba_back = [return_finish(*pair) for pair in mamba_back]
    g_attn = attn_total(*attn_sent)
    g_s, mamba_back[-1] = fence(g_s, mamba_back[-1])
    g_s = rows_back(g_s)
    out_expert_in_m, out_expert_down_m = expert_out(sum_in_m, sum_down_m)

    conv_sums, chan_sums, head_sums = small
    g_gate = chan_sums[0]
    g_skip = jnp.sum(chan_sums[1].reshape(heads, HP), axis=1)
    head_grad = jnp.stack([head_sums[0, :heads], head_sums[1, :heads], g_skip])

    def spread(part, width):
        zeros = jnp.zeros(part.shape[:-1] + (width,), f32)
        return lax.dynamic_update_slice_in_dim(zeros, part[..., :chan], slot * chan, axis=-1)

    conv_grad = jnp.concatenate([conv_sums[CK : CK + 1], conv_sums[:CK]], axis=0)
    conv_grad = spread(conv_grad, conv_total) + jnp.pad(conv_grad[:, chan:], ((0, 0), (DI, 0)))
    conv_grad = conv_grad.reshape(CK + 1, n_all, conv_here).transpose(1, 0, 2).reshape(n_all, -1)
    vec_grad = jnp.concatenate([spread(g_gate, DI).reshape(n_all, gate_here), conv_grad], axis=1)
    vec_grad = jnp.pad(vec_grad, ((0, 0), (0, rows * vec_cols - vec_len))).reshape(D, vec_cols)
    little = jnp.concatenate([g[:, None] for g in gains] + [g_router_m, g_router, vec_grad], axis=1)
    spare = step_width - heads - small_cols
    g_scan = jnp.pad(g_scan, ((0, 0), (0, step_width - 128)))
    g_m = rows_sum((g_scan + jnp.pad(little, ((0, 0), (in_width + heads, spare)))).astype(bf16))
    g_m, g_s, head_grad = fence(g_m, g_s, head_grad)
    g_m = rows_back(g_m)
    grads_in = []
    for m in each:
        scale_x = mamba_kept[m][1]
        grad_values, _ = rms_backward(mamba_back[m], own_normed[m], scale_x, gain_mamba)
        grads_in.append(grad_one[m] + grad_values)

    out_w_in = jnp.concatenate(
        [
            owned(g_m[:, :, :chan]),
            owned(g_m[:, :, chan : 2 * chan]),
            jnp.sum(g_m[:, :, 2 * chan : in_width], axis=0),
        ],
        axis=1,
    )
    out_mix = owned(g_s[:, :, :chan]).T
    out_w_dt = owned(g_m[:, :, in_width : in_width + heads])
    little = jnp.sum(g_m[:, :, in_width + heads : in_width + heads + small_cols], axis=0)
    vec = little[:, 4 + 2 * experts_total :].reshape(-1)
    out_gate = vec[:gate_here]
    out_conv_b = vec[gate_here : gate_here + conv_here]
    out_conv_w = vec[gate_here + conv_here : vec_len].reshape(CK, conv_here)

    head_grad = lax.dynamic_update_slice(jnp.zeros((8, 128), f32), head_grad, (0, slot * heads))
    for axis in ALL:
        size = lax.axis_size(axis)
        step = 1
        while step < size:
            pairs = [(i, i ^ step) for i in range(size)]
            head_grad = head_grad + send(head_grad, axis, pairs)
            step *= 2
    head_grad = head_grad[:3, :MH]

    cuts = (q_width, q_width + kv_width, q_width + 2 * kv_width)
    out_w_qkv = jnp.concatenate(
        [
            owned(g_attn[:, :, : cuts[0]]),
            owned(g_attn[:, :, cuts[0] : cuts[1]]),
            owned(g_attn[:, :, cuts[1] : cuts[2]]),
        ],
        axis=1,
    )
    out_w_out = owned(g_attn[:, :, cuts[2] :]).T

    def shared_out(block):
        g_sin = jnp.concatenate([owned(block[:, :, :ff]), owned(block[:, :, ff : 2 * ff])], axis=1)
        return g_sin, owned(block[:, :, 2 * ff :]).T

    out_sin_m, out_sdown_m = shared_out(g_s[:, :, chan : chan + 3 * ff])
    out_sin, out_sdown = shared_out(g_s[:, :, chan + 3 * ff :])

    return (
        jnp.stack(results).reshape(batches, length, D),
        jnp.stack(grads_in).reshape(batches, length, D),
        little[:, 0],
        out_w_in,
        out_w_dt,
        out_conv_w,
        out_conv_b,
        head_grad[0],
        head_grad[1],
        head_grad[2],
        out_gate,
        out_mix,
        little[:, 1],
        little[:, 4 : 4 + experts_total],
        out_sin_m,
        out_sdown_m,
        out_expert_in_m,
        out_expert_down_m,
        little[:, 2],
        out_w_qkv,
        out_w_out,
        little[:, 3],
        little[:, 4 + experts_total : 4 + 2 * experts_total],
        out_sin,
        out_sdown,
        out_expert_in,
        out_expert_down,
    )


def solution(mesh):
    n_dp, n_ex = mesh.shape["dp"], mesh.shape["expert"]
    outer = n_ex // 8
    fine = Mesh(mesh.devices.reshape(n_dp, outer, 4, 2), ALL)
    split = P(ALL)
    row = P(ALL, None)
    col = P(None, ALL)
    mid = P(None, ALL, None)
    part = P(EX, "dp", None)
    same = P()
    return jax.shard_map(
        body,
        mesh=fine,
        in_specs=(
            mid,
            mid,
            P(None, None, ALL, None),
            split,
            row,
            row,
            col,
            split,
            same,
            same,
            same,
            split,
            col,
            split,
            row,
            row,
            col,
            part,
            part,
            split,
            row,
            col,
            split,
            row,
            row,
            col,
            part,
            part,
            mid,
        ),
        out_specs=(
            mid,
            mid,
            split,
            row,
            row,
            col,
            split,
            same,
            same,
            same,
            split,
            col,
            split,
            row,
            row,
            col,
            part,
            part,
            split,
            row,
            col,
            split,
            row,
            row,
            col,
            part,
            part,
        ),
        check_vma=False,
    )
```
